32 devices in a mesh: grp: 4 (over x, core), seq: 8 (over z, y).
Axes of the slice: x: 2, y: 2, z: 4, core: 2. Of those that a mesh axis runs over, the one named last changes fastest.
Arguments:
- signal: float32 [64, 2048, 768], P('grp', 'seq'), may hold values from -36 to 36
- entry_gain: float32 [768], replicated
- entry_shift: float32 [768], replicated, may hold values from -3 to 3
- dilated_kernel: float32 [3, 768, 384], replicated
- middle_gain: float32 [384], replicated
- middle_shift: float32 [384], replicated, may hold values from -3 to 3
- pointwise_kernel: float32 [384, 768], replicated
- pointwise_bias: float32 [768], replicated, may hold values from -3 to 3
- lengths: int32 [64], replicated, may hold values from 128 to 1024, as said below
- assignment: int32 [4, 16], P('grp'), may hold values from 0 to 15, as said below
- cotangent: float32 [65536, 768], P(('grp', 'seq')), may hold values from -6 to 6
Outputs:
- activations: float32 [65536, 768], P(('grp', 'seq'))
- signal_gradient: float32 [64, 2048, 768], P('grp', 'seq')
- entry_gain_gradient: float32 [768], replicated
- entry_shift_gradient: float32 [768], replicated
- dilated_kernel_gradient: float32 [3, 768, 384], replicated
- middle_gain_gradient: float32 [384], replicated
- middle_shift_gradient: float32 [384], replicated
- pointwise_kernel_gradient: float32 [384, 768], replicated
- pointwise_bias_gradient: float32 [768], replicated
The draws below stay inside these ranges and needn't reach their ends.
Inputs may be any that keep to these rules, and one draw needn't show every extreme that they name: `lengths`: valid rows of a window come first; some window is full with 1024 rows and some has exactly 128. `assignment`: each row lists the 16 windows of one group once.
All inputs are finite; a program needn't handle non-finite values.
Results may differ from the reference program's by a relative error of at most 0.0066.
Values may be sent and summed in bfloat16 or wider, within the bound.
No kernel may reach another device: no remote copies, remote signals or barrier semaphores. Data moves between devices by JAX's collectives and lax.ppermute only.
A program may use at most 128 MiB of HBM per device.

```python
import math
from functools import partial
import jax
import jax.numpy as jnp
from jax import lax

D = 768
F = 384
WIN_HI = 2048
DILATION_STEP = 38
MINLEN = 128
WIN_DEV = 2
WINDOW_SPAN = 1024
HALF_WINDOW_ROWS = 512
WPG = 16
GROUPS = 4
WINDOWS = 64
OUT_ROWS = 65536
N_GRP = 4
N_SEQ = 8


EPSILON = 0.001


HIGHEST = lax.Precision.HIGHEST


def signal_values(key):
    base_key = jax.random.fold_in(key, 11)
    noise_key, window_key, channel_key, offset_key = jax.random.split(base_key, 4)
    window_scale = jnp.exp(jax.random.uniform(window_key, (WINDOWS, 1, 1), jnp.float32, math.log(0.3), math.log(3.0)))
    channel_scale = jnp.exp(jax.random.uniform(channel_key, (1, 1, D), jnp.float32, math.log(0.5), math.log(2.0)))
    noise = jnp.clip(jax.random.normal(noise_key, (WINDOWS, WIN_HI, D), jnp.float32), -6.0, 6.0)
    return noise * window_scale * channel_scale


def length_values(key):
    base_key = jax.random.fold_in(key, 12)
    start_key, full_key, short_key = jax.random.split(base_key, 3)
    lengths_drawn = jax.random.randint(start_key, (WINDOWS,), MINLEN, WINDOW_SPAN + WINDOW_SPAN // 2, jnp.int32)
    lengths_drawn = jnp.minimum(lengths_drawn, WINDOW_SPAN)
    full_place = jax.random.randint(full_key, (), 0, WINDOWS, jnp.int32)
    short_place = (full_place + 1 + jax.random.randint(short_key, (), 0, WINDOWS - 1, jnp.int32)) % WINDOWS
    return lengths_drawn.at[full_place].set(WINDOW_SPAN).at[short_place].set(MINLEN)


def group_order(group_key):
    return jax.random.permutation(group_key, WPG)


def order_values(key):
    group_keys = jax.random.split(jax.random.fold_in(key, 13), GROUPS)
    return jax.vmap(group_order)(group_keys).astype(jnp.int32)


def gain_values(key, salt, width):
    drawn = jax.random.normal(jax.random.fold_in(key, salt), (width,), jnp.float32)
    return 1.0 + 0.15 * jnp.clip(drawn, -5.0, 5.0)


def shift_values(key, salt, width):
    drawn = jax.random.normal(jax.random.fold_in(key, salt), (width,), jnp.float32)
    return 0.5 * jnp.clip(drawn, -6.0, 6.0)


def kernel_values(key, salt, shape, fan_in):
    drawn = jax.random.normal(jax.random.fold_in(key, salt), shape, jnp.float32)
    return jnp.clip(drawn, -6.0, 6.0) * (1.0 / math.sqrt(fan_in))


def draw_signal(key, part):
    return signal_values(key)


def draw_lengths(key, part):
    return length_values(key)


def draw_assignment(key, part):
    return order_values(key)


def draw_entry_gain(key, part):
    return gain_values(key, 21, D)


def draw_entry_shift(key, part):
    return shift_values(key, 22, D)


def draw_dilated_kernel(key, part):
    return kernel_values(key, 23, (3, D, F), 3 * D)


def draw_middle_gain(key, part):
    return gain_values(key, 24, F)


def draw_middle_shift(key, part):
    return shift_values(key, 25, F)


def draw_pointwise_kernel(key, part):
    return kernel_values(key, 26, (F, D), F)


def draw_pointwise_bias(key, part):
    return shift_values(key, 27, D)


def norm_apply(values, valid_mask, row_count, gain_vector, shift_vector):
    channel_mean = jnp.sum(values * valid_mask, axis=(0, 1)) / row_count
    spread = jnp.sum(valid_mask * (values - channel_mean) ** 2, axis=(0, 1)) / row_count
    return (values - channel_mean) * lax.rsqrt(spread + EPSILON) * gain_vector + shift_vector


def block_rows(key):
    signal = signal_values(key)
    lengths = length_values(key)
    assignment = order_values(key)
    bin_pairs = signal.reshape(WINDOWS, WINDOW_SPAN, 2, D)
    first_bin = bin_pairs[:, :, 0]
    second_bin = bin_pairs[:, :, 1]
    raw_pool = jnp.where(first_bin >= second_bin, first_bin, second_bin)
    position = jnp.arange(WINDOW_SPAN, dtype=jnp.int32)
    valid_mask = (position[None, :] < lengths[:, None]).astype(jnp.float32)[:, :, None]
    pooled = raw_pool * valid_mask
    row_count = jnp.sum(lengths.astype(jnp.float32))
    entry_activation = jax.nn.gelu(norm_apply(pooled, valid_mask, row_count, draw_entry_gain(key, 0), draw_entry_shift(key, 0)), approximate=True) * valid_mask
    kernel = draw_dilated_kernel(key, 0)
    padded_input = jnp.pad(entry_activation, ((0, 0), (DILATION_STEP, DILATION_STEP), (0, 0)))
    dilated_out = jnp.zeros((WINDOWS, WINDOW_SPAN, F), jnp.float32)
    for kernel_tap_index in range(3):
        shifted_rows = padded_input[:, kernel_tap_index * DILATION_STEP:kernel_tap_index * DILATION_STEP + WINDOW_SPAN]
        dilated_out = dilated_out + jnp.einsum('wrc,cf->wrf', shifted_rows, kernel[kernel_tap_index], precision=HIGHEST)
    middle_act = jax.nn.gelu(norm_apply(dilated_out, valid_mask, row_count, draw_middle_gain(key, 0), draw_middle_shift(key, 0)), approximate=True) * valid_mask
    mixed_out = jnp.einsum('wrf,fd->wrd', middle_act, draw_pointwise_kernel(key, 0), precision=HIGHEST)
    block_out = valid_mask * (pooled + mixed_out + draw_pointwise_bias(key, 0))
    groups_index = jnp.arange(GROUPS, dtype=jnp.int32)[:, None, None, None]
    places = jnp.arange(WPG // WIN_DEV, dtype=jnp.int32)[None, :, None, None]
    slot_index = jnp.arange(WIN_DEV, dtype=jnp.int32)[None, None, :, None]
    half_index = jnp.arange(2, dtype=jnp.int32)[None, None, None, :]
    column = jnp.bitwise_xor(places, half_index) * WIN_DEV + slot_index
    chosen = assignment[groups_index, column]
    window_index = groups_index * WPG + chosen
    half_full = jnp.broadcast_to(half_index, chosen.shape)
    halves = block_out.reshape(WINDOWS, 2, HALF_WINDOW_ROWS, D)
    return halves[window_index, half_full].reshape(OUT_ROWS, D)


def draw_cotangent(key, part):
    noise_key = jax.random.fold_in(key, 31)
    noise = jnp.clip(jax.random.normal(noise_key, (OUT_ROWS, D), jnp.float32), -6.0, 6.0)
    return jnp.clip(0.5 * block_rows(key) + noise, -6.0, 6.0)


def setup_inputs(seed: int = 0) -> dict:
    keys = jax.random.split(jax.random.key(seed), 12)
    signal = draw_signal(jax.random.fold_in(keys[11], 71), 0)
    entry_gain = draw_entry_gain(jax.random.fold_in(keys[11], 71), 0)
    entry_shift = draw_entry_shift(jax.random.fold_in(keys[11], 71), 0)
    dilated_kernel = draw_dilated_kernel(jax.random.fold_in(keys[11], 71), 0)
    middle_gain = draw_middle_gain(jax.random.fold_in(keys[11], 71), 0)
    middle_shift = draw_middle_shift(jax.random.fold_in(keys[11], 71), 0)
    pointwise_kernel = draw_pointwise_kernel(jax.random.fold_in(keys[11], 71), 0)
    pointwise_bias = draw_pointwise_bias(jax.random.fold_in(keys[11], 71), 0)
    lengths = draw_lengths(jax.random.fold_in(keys[11], 71), 0)
    assignment = draw_assignment(jax.random.fold_in(keys[11], 71), 0)
    cotangent = draw_cotangent(jax.random.fold_in(keys[11], 71), 0)
    return {"signal": signal, "entry_gain": entry_gain, "entry_shift": entry_shift, "dilated_kernel": dilated_kernel, "middle_gain": middle_gain, "middle_shift": middle_shift, "pointwise_kernel": pointwise_kernel, "pointwise_bias": pointwise_bias, "lengths": lengths, "assignment": assignment, "cotangent": cotangent}


EPSILON = 0.001
HIGHEST = lax.Precision.HIGHEST

@jax.custom_vjp
def low(v):
    return lax.optimization_barrier(v.astype(jnp.bfloat16)).astype(jnp.float32)

@jax.custom_vjp
def low_back(v):
    return v

def low_keep(v):
    return (low(v), None)

def low_pass(kept, grad):
    return (grad,)

def back_keep(v):
    return (v, None)

def back_low(kept, grad):
    return (low(grad),)
low.defvjp(low_keep, low_pass)
low_back.defvjp(back_keep, back_low)

def smooth(values):
    return jax.nn.gelu(values, approximate=True)

def normalize(values, valid_mask, row_count, gain_vector, shift_vector):
    channel_mean = lax.optimization_barrier(jnp.sum(values * valid_mask, axis=(0, 1))) / row_count
    spread = lax.optimization_barrier(jnp.sum(valid_mask * (values - channel_mean) ** 2, axis=(0, 1))) / row_count
    return (values - channel_mean) * lax.rsqrt(spread + EPSILON) * gain_vector + shift_vector

def target_windows(assignment):
    groups_index = jnp.arange(N_GRP, dtype=jnp.int32)[:, None, None, None]
    places = jnp.arange(N_SEQ, dtype=jnp.int32)[None, :, None, None]
    slot_index = jnp.arange(WIN_DEV, dtype=jnp.int32)[None, None, :, None]
    half_index = jnp.arange(2, dtype=jnp.int32)[None, None, None, :]
    column = jnp.bitwise_xor(places, half_index) * WIN_DEV + slot_index
    chosen = assignment[groups_index, column]
    return (groups_index * WPG + chosen, jnp.broadcast_to(half_index, chosen.shape))

def forward(signal, entry_gain, entry_shift, dilated_kernel, middle_gain, middle_shift, pointwise_kernel, pointwise_bias, lengths, assignment):
    window_total = signal.shape[0]
    bin_pairs = signal.reshape(window_total, WINDOW_SPAN, 2, D)
    first_bin = bin_pairs[:, :, 0]
    second_bin = bin_pairs[:, :, 1]
    raw_pool = jnp.where(first_bin >= second_bin, first_bin, second_bin)
    position = jnp.arange(WINDOW_SPAN, dtype=jnp.int32)
    valid_mask = (position[None, :] < lengths[:, None]).astype(jnp.float32)[:, :, None]
    pooled = low_back(low(raw_pool * valid_mask))
    row_count = jnp.sum(lengths.astype(jnp.float32))
    entry_activation = low(smooth(normalize(pooled, valid_mask, row_count, entry_gain, entry_shift)) * valid_mask)
    kernel = low(dilated_kernel)
    padded_input = jnp.pad(entry_activation, ((0, 0), (DILATION_STEP, DILATION_STEP), (0, 0)))
    dilated_out = jnp.zeros((window_total, WINDOW_SPAN, F), jnp.float32)
    for kernel_tap_index in range(3):
        rows_per_window = padded_input[:, kernel_tap_index * DILATION_STEP:kernel_tap_index * DILATION_STEP + WINDOW_SPAN]
        dilated_out = dilated_out + jnp.einsum('wrc,cf->wrf', rows_per_window, kernel[kernel_tap_index], precision=HIGHEST)
    dilated_out = low_back(dilated_out)
    middle_act = low(smooth(normalize(dilated_out, valid_mask, row_count, middle_gain, middle_shift)) * valid_mask)
    mixed_out = low_back(jnp.einsum('wrf,fd->wrd', middle_act, low(pointwise_kernel), precision=HIGHEST))
    block_out = valid_mask * (pooled + mixed_out + pointwise_bias)
    window_index, half_index = target_windows(assignment)
    halves = block_out.reshape(window_total, 2, HALF_WINDOW_ROWS, D)
    placed = halves[window_index, half_index]
    return placed.reshape(-1, D)

def reference(signal, entry_gain, entry_shift, dilated_kernel, middle_gain, middle_shift, pointwise_kernel, pointwise_bias, lengths, assignment, cotangent):
    function = partial(forward, lengths=lengths, assignment=assignment)
    output, pullback = jax.vjp(function, signal, entry_gain, entry_shift, dilated_kernel, middle_gain, middle_shift, pointwise_kernel, pointwise_bias)
    slopes = pullback(cotangent)
    return (output, slopes[0], slopes[1], slopes[2], slopes[3], slopes[4], slopes[5], slopes[6], slopes[7])
```

```python
import jax
import jax.numpy as jnp
from jax import lax
from jax.experimental import pallas as pl
from jax.experimental.pallas import tpu as pltpu
from jax.sharding import PartitionSpec as P

DILATION_STEP = 38
WINDOW_SPAN = 1024
HALF_WINDOW_ROWS = 512


EPSILON = 0.001


def from_partner(block, axis, mask):
    count = lax.axis_size(axis)
    return lax.ppermute(block, axis, [(place, place ^ mask) for place in range(count)])


def exchange_steps():
    steps = []
    for axis in ("grp", "seq"):
        mask = 1
        while mask < lax.axis_size(axis):
            steps.append((axis, mask))
            mask *= 2
    return steps


def total(values):
    for axis, mask in exchange_steps():
        values = values + from_partner(values, axis, mask)
    return values


def merge_moments(left, right):
    left_count, right_count = left[2:3], right[2:3]
    gap = left[0:1] / jnp.maximum(left_count, 1.0) - right[0:1] / jnp.maximum(right_count, 1.0)
    weight = left_count * right_count / jnp.maximum(left_count + right_count, 1.0)
    spread = left[1:2] + right[1:2] + gap * gap * weight
    return jnp.concatenate([left[0:1] + right[0:1], spread, left_count + right_count], axis=0)


def global_moments(local_sum, local_spread, local_count, row_count):
    packed = jnp.stack(
        [local_sum, local_spread, jnp.broadcast_to(local_count, local_sum.shape)], axis=0
    )
    for axis, mask in exchange_steps():
        packed = merge_moments(packed, from_partner(packed, axis, mask))
    return packed[0] / row_count, lax.rsqrt(packed[1] / row_count + EPSILON)


def total_of_large(buffer):
    steps = exchange_steps()
    marks = []
    for axis, mask in steps:
        half = buffer.shape[0] // 2
        upper = (lax.axis_index(axis) // mask) % 2
        kept = lax.dynamic_slice_in_dim(buffer, upper * half, half)
        sent = lax.dynamic_slice_in_dim(buffer, (1 - upper) * half, half)
        buffer = kept + from_partner(sent, axis, mask)
        marks.append(upper)
    for (axis, mask), upper in zip(reversed(steps), reversed(marks)):
        other = from_partner(buffer, axis, mask)
        buffer = jnp.where(
            upper == 0,
            jnp.concatenate([buffer, other], axis=0),
            jnp.concatenate([other, buffer], axis=0),
        )
    return buffer


LANES = 128


def pool_kernel(order_ref, count_ref, before_ref, *refs):
    pooled_ref, first_ref, moments_ref = refs[-3:]
    place = pl.program_id(0)
    rows = pooled_ref.shape[1]
    count = count_ref[place]
    count_f = count.astype(jnp.float32)
    before_f = before_ref[place].astype(jnp.float32)
    weight = before_f * count_f / jnp.maximum(before_f + count_f, 1.0)
    inside = lax.broadcasted_iota(jnp.int32, (rows, LANES), 0) < count

    @pl.when(place == 0)
    def _():
        moments_ref[...] = jnp.zeros_like(moments_ref)

    for column, signal_ref in enumerate(refs[:-3]):
        lanes = slice(column * LANES, (column + 1) * LANES)
        first_bin = signal_ref[0, pl.ds(0, rows, stride=2), :]
        second_bin = signal_ref[0, pl.ds(1, rows, stride=2), :]
        take_first = first_bin >= second_bin
        raw = jnp.where(take_first, first_bin, second_bin)
        first_ref[0, :, lanes] = jnp.where(take_first, 1.0, 0.0).astype(jnp.bfloat16)
        low = jnp.where(inside, raw, 0.0).astype(jnp.bfloat16)
        pooled_ref[0, :, lanes] = low
        values = low.astype(jnp.float32)
        block_sum = jnp.sum(values, axis=0, keepdims=True)
        block_mean = block_sum / jnp.maximum(count_f, 1.0)
        deviation = jnp.where(inside, values - block_mean, 0.0)
        block_spread = jnp.sum(deviation * deviation, axis=0, keepdims=True)
        held_sum = moments_ref[0:1, lanes]
        gap = held_sum / jnp.maximum(before_f, 1.0) - block_mean
        moments_ref[0:1, lanes] = held_sum + block_sum
        moments_ref[1:2, lanes] = moments_ref[1:2, lanes] + block_spread + gap * gap * weight


def pool(signal, picked, counts, before):
    windows, segment, width = signal.shape
    rows = segment // 2
    columns = width // LANES
    return pl.pallas_call(
        pool_kernel,
        grid_spec=pltpu.PrefetchScalarGridSpec(
            num_scalar_prefetch=3,
            grid=(windows,),
            in_specs=[
                pl.BlockSpec((1, segment, LANES), lambda p, o, c, b, column=column: (o[p], 0, column))
                for column in range(columns)
            ],
            out_specs=[
                pl.BlockSpec((1, rows, width), lambda p, o, c, b: (p, 0, 0)),
                pl.BlockSpec((1, rows, width), lambda p, o, c, b: (p, 0, 0)),
                pl.BlockSpec((2, width), lambda p, o, c, b: (0, 0)),
            ],
        ),
        out_shape=[
            jax.ShapeDtypeStruct((windows, rows, width), jnp.bfloat16),
            jax.ShapeDtypeStruct((windows, rows, width), jnp.bfloat16),
            jax.ShapeDtypeStruct((2, width), jnp.float32),
        ],
        compiler_params=pltpu.CompilerParams(vmem_limit_bytes=16 << 20),
        cost_estimate=pl.CostEstimate(
            flops=10 * windows * rows * width,
            bytes_accessed=windows * rows * width * 12,
            transcendentals=0,
        ),
        name="pool",
    )(picked, counts, before, *([signal] * columns))


def unpool_kernel(
    order_ref, count_ref, returned_ref, pooled_ref, first_ref, terms_ref, out_ref
):
    place = pl.program_id(0)
    rows, width = pooled_ref.shape[1:]
    inside = lax.broadcasted_iota(jnp.int32, (rows, width), 0) < count_ref[place]
    centred = pooled_ref[0].astype(jnp.float32) - terms_ref[0:1]
    gradient = returned_ref[0].astype(jnp.float32) - (terms_ref[1:2] + centred * terms_ref[2:3])
    gradient = jnp.where(inside, gradient, 0.0)
    chosen = first_ref[0].astype(jnp.float32) > 0.5
    pair = jnp.concatenate(
        [
            jnp.where(chosen, gradient, 0.0).astype(jnp.bfloat16),
            jnp.where(chosen, 0.0, gradient).astype(jnp.bfloat16),
        ],
        axis=0,
    )
    bin_index = lax.broadcasted_iota(jnp.int32, (2 * rows, 2 * rows), 0)
    pair_index = lax.broadcasted_iota(jnp.int32, (2 * rows, 2 * rows), 1)
    source = bin_index // 2 + (bin_index % 2) * rows
    spread = jnp.where(pair_index == source, 1.0, 0.0).astype(jnp.bfloat16)
    out_ref[0] = jnp.dot(spread, pair, preferred_element_type=jnp.float32)


def unpool(returned, pooled, first, terms, picked, counts):
    windows, rows, width = returned.shape
    block = pl.BlockSpec((1, rows, width), lambda p, o, c: (p, 0, 0))
    return pl.pallas_call(
        unpool_kernel,
        grid_spec=pltpu.PrefetchScalarGridSpec(
            num_scalar_prefetch=2,
            grid=(windows,),
            in_specs=[block, block, block, pl.BlockSpec((3, width), lambda p, o, c: (0, 0))],
            out_specs=pl.BlockSpec((1, 2 * rows, width), lambda p, o, c: (o[p], 0, 0)),
        ),
        out_shape=jax.ShapeDtypeStruct((windows, 2 * rows, width), jnp.float32),
        compiler_params=pltpu.CompilerParams(vmem_limit_bytes=16 << 20),
        cost_estimate=pl.CostEstimate(
            flops=10 * windows * rows * width,
            bytes_accessed=windows * rows * width * 14,
            transcendentals=0,
        ),
        name="unpool",
    )(picked, counts, returned, pooled, first, terms)


def smooth(values):
    return jax.nn.gelu(values, approximate=True)


def extended(resident_rows, neighbour_border):
    position_count = resident_rows.shape[0]
    channel_width = resident_rows.shape[2]
    empty_row_block = jnp.zeros((position_count, DILATION_STEP, channel_width), resident_rows.dtype)
    bottom_portion = jnp.concatenate(
        [empty_row_block, resident_rows[:, :HALF_WINDOW_ROWS], neighbour_border[:, DILATION_STEP:]],
        axis=1,
    )
    top_portion = jnp.concatenate(
        [neighbour_border[:, :DILATION_STEP], resident_rows[:, HALF_WINDOW_ROWS:], empty_row_block],
        axis=1,
    )
    return jnp.stack([bottom_portion, top_portion], axis=1).reshape(
        2 * position_count, HALF_WINDOW_ROWS + 2 * DILATION_STEP, channel_width
    )


def per_device(
    signal,
    entry_gain,
    entry_shift,
    dilated_kernel,
    middle_gain,
    middle_shift,
    pointwise_kernel,
    pointwise_bias,
    lengths,
    assignment,
    cotangent,
):
    seq_count = lax.axis_size("seq")
    seq_place = lax.axis_index("seq")
    grp_place = lax.axis_index("grp")
    group_windows, segment, channel_width = signal.shape
    source_rows = segment // 2
    position_count = group_windows // seq_count
    group_lengths = lax.dynamic_slice_in_dim(lengths, grp_place * group_windows, group_windows)
    window_order = assignment[0]
    upper_source = (seq_place >= seq_count // 2).astype(jnp.int32)
    targets = jnp.arange(seq_count, dtype=jnp.int32)
    slot_range = jnp.arange(position_count, dtype=jnp.int32)
    picked = window_order[
        (
            jnp.bitwise_xor(targets, upper_source)[:, None] * position_count + slot_range[None, :]
        ).reshape(-1)
    ]
    counts = jnp.clip(group_lengths[picked] - seq_place * source_rows, 0, source_rows)
    before = jnp.cumsum(counts) - counts
    row_count = jnp.sum(lengths.astype(jnp.float32))

    outgoing, first_chosen, entry_local = pool(signal, picked, counts, before)
    arrived = lax.all_to_all(outgoing, "seq", split_axis=0, concat_axis=1, tiled=True)
    entry_centre, entry_scale = global_moments(
        entry_local[0], entry_local[1], jnp.sum(counts).astype(jnp.float32), row_count
    )

    partner_place = jnp.bitwise_xor(seq_place, 1)
    own_windows = lax.dynamic_slice_in_dim(window_order, seq_place * position_count, position_count)
    partner_windows = lax.dynamic_slice_in_dim(
        window_order, partner_place * position_count, position_count
    )
    row_position = jnp.arange(WINDOW_SPAN, dtype=jnp.int32)
    limit_rows = jnp.where(
        row_position[None, :] < HALF_WINDOW_ROWS,
        jnp.take(group_lengths, own_windows)[:, None],
        jnp.take(group_lengths, partner_windows)[:, None],
    )
    valid_mask = (row_position[None, :] < limit_rows).astype(jnp.float32)[:, :, None]
    resident_count = jnp.sum(valid_mask)
    pooled = arrived.astype(jnp.float32)
    entry_norm = (pooled - entry_centre) * entry_scale
    entry_smooth, entry_back = jax.vjp(smooth, entry_norm * entry_gain + entry_shift)
    entry_activation = (entry_smooth * valid_mask).astype(jnp.bfloat16)
    kernel_low = dilated_kernel.astype(jnp.bfloat16)
    entry_border = from_partner(
        entry_activation[:, HALF_WINDOW_ROWS - DILATION_STEP : HALF_WINDOW_ROWS + DILATION_STEP],
        "seq",
        1,
    )
    entry_widened = extended(entry_activation, entry_border)
    dilated_out = jnp.zeros(
        (2 * position_count, HALF_WINDOW_ROWS, kernel_low.shape[2]), jnp.float32
    )
    for kernel_tap_index in range(3):
        displaced_rows = entry_widened[
            :,
            kernel_tap_index * DILATION_STEP : kernel_tap_index * DILATION_STEP + HALF_WINDOW_ROWS,
        ]
        dilated_out = dilated_out + jnp.einsum(
            "hrc,cf->hrf",
            displaced_rows,
            kernel_low[kernel_tap_index],
            preferred_element_type=jnp.float32,
        )
    dilated_out = dilated_out.reshape(position_count, WINDOW_SPAN, -1)
    middle_sum = jnp.sum(dilated_out * valid_mask, axis=(0, 1))
    middle_deviation = (dilated_out - middle_sum / jnp.maximum(resident_count, 1.0)) * valid_mask
    middle_centre, middle_scale = global_moments(
        middle_sum,
        jnp.sum(middle_deviation * middle_deviation, axis=(0, 1)),
        resident_count,
        row_count,
    )
    middle_norm = (dilated_out - middle_centre) * middle_scale
    middle_smooth, middle_back = jax.vjp(smooth, middle_norm * middle_gain + middle_shift)
    middle_act = (middle_smooth * valid_mask).astype(jnp.bfloat16)
    pointwise_low = pointwise_kernel.astype(jnp.bfloat16)
    mixed_out = jnp.einsum(
        "krf,fd->krd", middle_act, pointwise_low, preferred_element_type=jnp.float32
    )
    activations = (valid_mask * (pooled + mixed_out + pointwise_bias)).reshape(-1, channel_width)
    grad_block = cotangent.reshape(position_count, WINDOW_SPAN, channel_width) * valid_mask
    grad_mixed = grad_block.astype(jnp.bfloat16)
    bias_part = jnp.sum(grad_block, axis=(0, 1))
    pointwise_part = jnp.einsum(
        "krd,krf->df", grad_mixed, middle_act, preferred_element_type=jnp.float32
    )
    grad_middle = jnp.einsum(
        "krd,fd->krf", grad_mixed, pointwise_low, preferred_element_type=jnp.float32
    )
    grad_middle_pre = middle_back(grad_middle * valid_mask)[0]
    middle_sums = total(
        jnp.stack(
            [
                jnp.sum(grad_middle_pre * middle_norm, axis=(0, 1)),
                jnp.sum(grad_middle_pre, axis=(0, 1)),
            ]
        )
    )
    middle_gain_gradient, middle_shift_gradient = middle_sums[0], middle_sums[1]
    dilated_gradient = (
        middle_gain
        * middle_scale
        * (
            grad_middle_pre
            - (middle_shift_gradient + middle_norm * middle_gain_gradient) / row_count
        )
        * valid_mask
    )
    dilated_gradient = dilated_gradient.astype(jnp.bfloat16)
    border_gradient = from_partner(
        dilated_gradient[:, HALF_WINDOW_ROWS - DILATION_STEP : HALF_WINDOW_ROWS + DILATION_STEP],
        "seq",
        1,
    )
    grad_wide = extended(dilated_gradient, border_gradient)
    grad_halves = dilated_gradient.reshape(2 * position_count, HALF_WINDOW_ROWS, -1)
    kernel_pieces = []
    grad_entry = jnp.zeros((2 * position_count, HALF_WINDOW_ROWS, channel_width), jnp.float32)
    for kernel_tap_index in range(3):
        displaced_rows = entry_widened[
            :,
            kernel_tap_index * DILATION_STEP : kernel_tap_index * DILATION_STEP + HALF_WINDOW_ROWS,
        ]
        kernel_pieces.append(
            jnp.einsum(
                "hrc,hrf->cf", displaced_rows, grad_halves, preferred_element_type=jnp.float32
            )
        )
        backward_offset = (2 - kernel_tap_index) * DILATION_STEP
        grad_shifted = grad_wide[:, backward_offset : backward_offset + HALF_WINDOW_ROWS]
        grad_entry = grad_entry + jnp.einsum(
            "hrf,cf->hrc",
            grad_shifted,
            kernel_low[kernel_tap_index],
            preferred_element_type=jnp.float32,
        )
    grad_entry = grad_entry.reshape(position_count, WINDOW_SPAN, channel_width)
    grad_entry_pre = entry_back(grad_entry * valid_mask)[0]
    entry_sums = total(
        jnp.stack(
            [
                jnp.sum(grad_entry_pre * entry_norm, axis=(0, 1)),
                jnp.sum(grad_entry_pre, axis=(0, 1)),
                bias_part,
            ]
        )
    )
    entry_gain_gradient, entry_shift_gradient = entry_sums[0], entry_sums[1]
    pointwise_bias_gradient = entry_sums[2]
    sent_back = (entry_gain * entry_scale * grad_entry_pre + grad_block).astype(jnp.bfloat16)
    sent_back = sent_back.reshape(position_count, seq_count, source_rows, channel_width)
    sent_back = jnp.swapaxes(sent_back, 0, 1).reshape(group_windows, source_rows, channel_width)
    returned = lax.all_to_all(sent_back, "seq", split_axis=0, concat_axis=0, tiled=True)
    factor = entry_gain * entry_scale / row_count
    terms = jnp.stack(
        [entry_centre, factor * entry_shift_gradient, factor * entry_scale * entry_gain_gradient]
    )
    signal_gradient = unpool(returned, outgoing, first_chosen, terms, picked, counts)
    tap_rows = 3 * channel_width
    weight_sums = total_of_large(jnp.concatenate(kernel_pieces + [pointwise_part], axis=0))
    dilated_kernel_gradient = weight_sums[:tap_rows].reshape(dilated_kernel.shape)
    pointwise_kernel_gradient = weight_sums[tap_rows:].T
    return (
        activations,
        signal_gradient,
        entry_gain_gradient,
        entry_shift_gradient,
        dilated_kernel_gradient,
        middle_gain_gradient,
        middle_shift_gradient,
        pointwise_kernel_gradient,
        pointwise_bias_gradient,
    )


def solution(mesh):
    return jax.shard_map(
        per_device,
        mesh=mesh,
        in_specs=(
            P("grp", "seq", None),
            P(),
            P(),
            P(),
            P(),
            P(),
            P(),
            P(),
            P(),
            P("grp", None),
            P(("grp", "seq"), None),
        ),
        out_specs=(
            P(("grp", "seq"), None),
            P("grp", "seq", None),
            P(),
            P(),
            P(),
            P(),
            P(),
            P(),
            P(),
        ),
        check_vma=False,
    )
```

```python
import functools
import math

import jax
import jax.numpy as jnp
from jax import lax
from jax.experimental import pallas as pl
from jax.experimental.pallas import tpu as pltpu
from jax.sharding import PartitionSpec as P

DILATION_STEP = 38
WINDOW_SPAN = 1024
HALF_WINDOW_ROWS = 512


EPSILON = 0.001

LANES = 128
BORDER = 48
STRIP = 64
PAD = 40
PADDED_ROWS = HALF_WINDOW_ROWS + 2 * PAD
GELU_SLOPE = math.sqrt(2.0 / math.pi)
GELU_CUBE = 0.044715

VMEM = pl.BlockSpec(memory_space=pltpu.VMEM)
SMEM = pl.BlockSpec(memory_space=pltpu.SMEM)
HBM = pl.BlockSpec(memory_space=pltpu.HBM)


def from_partner(block, axis, mask):
    count = lax.axis_size(axis)
    return lax.ppermute(block, axis, [(place, place ^ mask) for place in range(count)])


def exchange_steps():
    steps = []
    for axis in ("grp", "seq"):
        mask = 1
        while mask < lax.axis_size(axis):
            steps.append((axis, mask))
            mask *= 2
    return steps


def total(values):
    for axis, mask in exchange_steps():
        values = values + from_partner(values, axis, mask)
    return values


def merged(left, right):
    left_sum, left_spread, left_count = left
    right_sum, right_spread, right_count = right
    gap = left_sum / jnp.maximum(left_count, 1.0) - right_sum / jnp.maximum(right_count, 1.0)
    weight = left_count * right_count / jnp.maximum(left_count + right_count, 1.0)
    return (
        left_sum + right_sum,
        left_spread + right_spread + gap * gap * weight,
        left_count + right_count,
    )


def total_moments(packed):
    for axis, mask in exchange_steps():
        other = from_partner(packed, axis, mask)
        packed = jnp.concatenate(
            merged(
                (packed[0:1], packed[1:2], packed[2:3]), (other[0:1], other[1:2], other[2:3])
            ),
            axis=0,
        )
    return packed


class Facts:
    def __init__(self, ref, windows, slots):
        self.ref, self.windows, self.slots = ref, windows, slots

    def slot_window(self, slot):
        upper = (2 * self.ref[1]) // self.ref[2]
        target = jnp.bitwise_xor(slot // self.slots, upper)
        return self.ref[3 + target * self.slots + slot % self.slots]

    def length(self, window):
        return self.ref[3 + self.windows + self.ref[0] * self.windows + window]

    def slot_count(self, slot, rows):
        return jnp.clip(self.length(self.slot_window(slot)) - self.ref[1] * rows, 0, rows)

    def half_limit(self, slot, half):
        place = jnp.bitwise_xor(self.ref[1], half)
        window = self.ref[3 + place * self.slots + slot]
        return jnp.clip(self.length(window) - half * HALF_WINDOW_ROWS, 0, HALF_WINDOW_ROWS)

    def row_count(self):
        start = 3 + self.windows
        count = self.ref.shape[0] - start
        added = lax.fori_loop(0, count, lambda i, held: held + self.ref[start + i], jnp.int32(0))
        return added.astype(jnp.float32)


def kernel_call(body, name, inputs, specs, outputs, out_specs, scratch=(), flops=0, bytes_moved=0, grant=8 << 20):
    return pl.pallas_call(
        body,
        in_specs=specs,
        out_specs=out_specs,
        out_shape=outputs,
        scratch_shapes=list(scratch),
        compiler_params=pltpu.CompilerParams(vmem_limit_bytes=grant),
        cost_estimate=pl.CostEstimate(
            flops=flops, bytes_accessed=bytes_moved, transcendentals=0
        ),
        name=name,
    )(*inputs)


def shape(dims, dtype):
    return jax.ShapeDtypeStruct(dims, dtype)


def in_hbm(array):
    return pltpu.with_memory_space_constraint(array, pltpu.HBM)


def column_slices(width):
    return [slice(start, start + LANES) for start in range(0, width, LANES)]


def pool_body(
    slots, facts_ref, signal_ref, pooled_ref, first_ref, moments_ref,
    held, low, mark, arrivals, departures,
):
    windows, columns = held.shape[:2]
    rows = low.shape[1]
    facts = Facts(facts_ref, windows, slots)

    def arrival(place, column):
        return pltpu.make_async_copy(
            signal_ref.at[facts.slot_window(place), :, pl.ds(column * LANES, LANES)],
            held.at[place, column],
            arrivals.at[place, column],
        )

    def departure(place):
        return [
            pltpu.make_async_copy(low.at[place], pooled_ref.at[place], departures.at[place, 0]),
            pltpu.make_async_copy(mark.at[place], first_ref.at[place], departures.at[place, 1]),
        ]

    def begin(place, carry):
        for column in range(columns):
            arrival(place, column).start()
        return carry

    lax.fori_loop(0, windows, begin, 0)
    moments_ref[...] = jnp.zeros_like(moments_ref)

    def work(place, before):
        count = facts.slot_count(place, rows)
        count_f = count.astype(jnp.float32)
        before_f = before.astype(jnp.float32)
        weight = before_f * count_f / jnp.maximum(before_f + count_f, 1.0)
        inside = lax.broadcasted_iota(jnp.int32, (rows, LANES), 0) < count
        for column, lanes in enumerate(column_slices(columns * LANES)):
            arrival(place, column).wait()
            first_bin = held[place, column, pl.ds(0, rows, stride=2), :]
            second_bin = held[place, column, pl.ds(1, rows, stride=2), :]
            take_first = first_bin >= second_bin
            raw = jnp.maximum(first_bin, second_bin)
            mark[place, :, lanes] = jnp.where(take_first, 1.0, 0.0).astype(jnp.bfloat16)
            pooled = jnp.where(inside, raw, 0.0).astype(jnp.bfloat16)
            low[place, :, lanes] = pooled
            values = pooled.astype(jnp.float32)
            block_sum = jnp.sum(values, axis=0, keepdims=True)
            block_mean = block_sum / jnp.maximum(count_f, 1.0)
            deviation = jnp.where(inside, values - block_mean, 0.0)
            block_spread = jnp.sum(deviation * deviation, axis=0, keepdims=True)
            held_sum = moments_ref[0:1, lanes]
            gap = held_sum / jnp.maximum(before_f, 1.0) - block_mean
            moments_ref[0:1, lanes] = held_sum + block_sum
            moments_ref[1:2, lanes] = (
                moments_ref[1:2, lanes] + block_spread + gap * gap * weight
            )
            moments_ref[2:3, lanes] = moments_ref[2:3, lanes] + count_f
        for copy in departure(place):
            copy.start()
        return before + count

    lax.fori_loop(0, windows, work, jnp.int32(0))

    def finish(place, carry):
        for copy in departure(place):
            copy.wait()
        return carry

    lax.fori_loop(0, windows, finish, 0)


def pool(facts, signal, slots):
    windows, segment, width = signal.shape
    rows, columns = segment // 2, width // LANES
    block = (windows, rows, width)
    return kernel_call(
        functools.partial(pool_body, slots),
        "pool",
        (facts, in_hbm(signal)),
        [SMEM, HBM],
        [
            pltpu.HBM(block, jnp.bfloat16),
            pltpu.HBM(block, jnp.bfloat16),
            shape((3, width), jnp.float32),
        ],
        [HBM, HBM, VMEM],
        [
            pltpu.VMEM((windows, columns, segment, LANES), jnp.float32),
            pltpu.VMEM(block, jnp.bfloat16),
            pltpu.VMEM(block, jnp.bfloat16),
            pltpu.SemaphoreType.DMA((windows, columns)),
            pltpu.SemaphoreType.DMA((windows, 2)),
        ],
        flops=10 * windows * rows * width,
        bytes_moved=windows * rows * width * 12,
        grant=24 << 20,
    )


def unpool_body(
    slots, slot, windows, facts_ref, returned_ref, pooled_ref, first_ref, moments_ref, sums_ref,
    params_ref, *refs,
):
    out_ref, back, low, mark, held, arrivals, departures = refs[-7:]
    targets, rows, width = back.shape
    columns = held.shape[1]
    facts = Facts(facts_ref, windows, slots)

    def arrival(target):
        place = target * slots + slot
        return [
            pltpu.make_async_copy(returned_ref.at[target], back.at[target], arrivals.at[target, 0]),
            pltpu.make_async_copy(pooled_ref.at[place], low.at[target], arrivals.at[target, 1]),
            pltpu.make_async_copy(first_ref.at[place], mark.at[target], arrivals.at[target, 2]),
        ]

    def departure(target, column):
        window = facts.slot_window(target * slots + slot)
        return pltpu.make_async_copy(
            held.at[target, column],
            out_ref.at[window, :, pl.ds(column * LANES, LANES)],
            departures.at[target, column],
        )

    def begin(target, carry):
        for copy in arrival(target):
            copy.start()
        return carry

    lax.fori_loop(0, targets, begin, 0)
    rows_total = facts.row_count()
    centre = moments_ref[0:1] / rows_total
    scale = lax.rsqrt(moments_ref[1:2] / rows_total + EPSILON)
    factor = params_ref[0:1] * scale / rows_total
    level = factor * sums_ref[1:2]
    tilt = factor * scale * sums_ref[0:1]

    def work(target, carry):
        for copy in arrival(target):
            copy.wait()
        inside = lax.broadcasted_iota(jnp.int32, (rows, LANES), 0) < facts.slot_count(
            target * slots + slot, rows
        )
        for column, lanes in enumerate(column_slices(width)):
            centred = low[target, :, lanes].astype(jnp.float32) - centre[:, lanes]
            gradient = back[target, :, lanes].astype(jnp.float32) - (
                level[:, lanes] + centred * tilt[:, lanes]
            )
            gradient = jnp.where(inside, gradient, 0.0).astype(jnp.bfloat16).astype(jnp.float32)
            first = gradient * mark[target, :, lanes].astype(jnp.float32)
            held[target, column, pl.ds(0, rows, stride=2), :] = first
            held[target, column, pl.ds(1, rows, stride=2), :] = gradient - first
            departure(target, column).start()
        return carry

    lax.fori_loop(0, targets, work, 0)

    def finish(target, carry):
        for column in range(columns):
            departure(target, column).wait()
        return carry

    lax.fori_loop(0, targets, finish, 0)


def unpool(facts, returned, pooled, first, moments, sums, params, slots, slot, held_output):
    targets, rows, width = returned.shape
    windows, columns = targets * slots, width // LANES
    inputs = [facts, in_hbm(returned), in_hbm(pooled), in_hbm(first), moments, sums, params]
    specs = [SMEM, HBM, HBM, HBM, VMEM, VMEM, VMEM]
    aliases = {}
    if held_output is not None:
        aliases = {len(inputs): 0}
        inputs.append(in_hbm(held_output))
        specs.append(HBM)
    block = (targets, rows, width)
    return pl.pallas_call(
        functools.partial(unpool_body, slots, slot, windows),
        in_specs=specs,
        out_specs=HBM,
        out_shape=pltpu.HBM((windows, 2 * rows, width), jnp.float32),
        input_output_aliases=aliases,
        scratch_shapes=[
            pltpu.VMEM(block, jnp.bfloat16),
            pltpu.VMEM(block, jnp.bfloat16),
            pltpu.VMEM(block, jnp.bfloat16),
            pltpu.VMEM((targets, columns, 2 * rows, LANES), jnp.float32),
            pltpu.SemaphoreType.DMA((targets, 3)),
            pltpu.SemaphoreType.DMA((targets, columns)),
        ],
        compiler_params=pltpu.CompilerParams(vmem_limit_bytes=16 << 20),
        cost_estimate=pl.CostEstimate(
            flops=10 * targets * rows * width,
            bytes_accessed=targets * rows * width * 14,
            transcendentals=0,
        ),
        name="unpool",
    )(*inputs)


def prepare_body(slots, windows, facts_ref, cot_ref, weight_ref, low_ref, middle_ref, bias_ref):
    step = pl.program_id(0)
    rows = cot_ref.shape[0]
    facts = Facts(facts_ref, windows, slots)
    first_row = step * rows
    piece = first_row // HALF_WINDOW_ROWS
    limit = facts.half_limit(piece // 2, piece % 2) - first_row % HALF_WINDOW_ROWS

    @pl.when(step == 0)
    def _():
        bias_ref[...] = jnp.zeros_like(bias_ref)

    inside = lax.broadcasted_iota(jnp.int32, (rows, 1), 0) < limit
    block = jnp.where(inside, cot_ref[...], 0.0)
    bias_ref[...] = bias_ref[...] + jnp.sum(block, axis=0, keepdims=True)
    low = block.astype(jnp.bfloat16)
    low_ref[...] = low
    middle_ref[...] = lax.dot_general(
        low, weight_ref[...], (((1,), (1,)), ((), ())), preferred_element_type=jnp.float32
    )


def prepare(facts, cotangent, weight, slots, windows):
    total_rows, width = cotangent.shape
    inner = weight.shape[0]
    rows = 256
    return pl.pallas_call(
        functools.partial(prepare_body, slots, windows),
        grid=(total_rows // rows,),
        in_specs=[
            SMEM,
            pl.BlockSpec((rows, width), lambda i: (i, 0)),
            pl.BlockSpec((inner, width), lambda i: (0, 0)),
        ],
        out_specs=[
            pl.BlockSpec((rows, width), lambda i: (i, 0)),
            pl.BlockSpec((rows, inner), lambda i: (i, 0)),
            pl.BlockSpec((1, width), lambda i: (0, 0)),
        ],
        out_shape=[
            shape((total_rows, width), jnp.bfloat16),
            shape((total_rows, inner), jnp.float32),
            shape((1, width), jnp.float32),
        ],
        compiler_params=pltpu.CompilerParams(vmem_limit_bytes=16 << 20),
        cost_estimate=pl.CostEstimate(
            flops=2 * total_rows * width * inner,
            bytes_accessed=total_rows * (width * 6 + inner * 4),
            transcendentals=0,
        ),
        name="prepare_cotangent",
    )(facts, cotangent, weight)


def norm_terms(moments_ref, params_ref, rows_total):
    centre = moments_ref[0:1] / rows_total
    scale = lax.rsqrt(moments_ref[1:2] / rows_total + EPSILON)
    return centre, scale, params_ref[0:1] * scale, params_ref[1:2]


def half_terms(moments_ref, params_ref, rows_total):
    centre, _, slope, offset = norm_terms(moments_ref, params_ref, rows_total)
    return 0.5 * slope, 0.5 * (offset - centre * slope)


def bent(half):
    square = half * half
    return jnp.tanh(half * (2.0 * GELU_SLOPE + (8.0 * GELU_SLOPE * GELU_CUBE) * square)), square


def gelu_slope(half, bend, square):
    inner = GELU_SLOPE + (12.0 * GELU_SLOPE * GELU_CUBE) * square
    return (0.5 + 0.5 * bend) + (half - half * bend * bend) * inner


def activate_body(
    slots, windows, facts_ref, arrived_ref, moments_ref, params_ref, act_ref, border_ref
):
    blocks, rows, width = arrived_ref.shape
    facts = Facts(facts_ref, windows, slots)
    per_half = HALF_WINDOW_ROWS // rows
    slope, offset = half_terms(moments_ref, params_ref, facts.row_count())

    def work(block, carry):
        source, slot = block // slots, block % slots
        half, start = source // per_half, (source % per_half) * rows
        inside = lax.broadcasted_iota(jnp.int32, (rows, 1), 0) < (
            facts.half_limit(slot, half) - start
        )
        for lanes in column_slices(width):
            values = arrived_ref[block, :, lanes].astype(jnp.float32)
            half_pre = values * slope[:, lanes] + offset[:, lanes]
            bend, _ = bent(half_pre)
            act = jnp.where(inside, half_pre + half_pre * bend, 0.0)
            act_ref[slot * 2 + half, pl.ds(pl.multiple_of(start, rows), rows), lanes] = act.astype(
                jnp.bfloat16
            )
        return carry

    lax.fori_loop(0, blocks, work, 0)
    for piece in range(act_ref.shape[0]):
        start = 0 if piece % 2 else HALF_WINDOW_ROWS - BORDER
        border_ref[piece] = act_ref[piece, start : start + BORDER]


def activate(facts, arrived, moments, params, slots, windows):
    width = arrived.shape[2]
    return kernel_call(
        functools.partial(activate_body, slots, windows),
        "activate",
        (facts, arrived, moments, params),
        [SMEM, VMEM, VMEM, VMEM],
        [
            shape((2 * slots, HALF_WINDOW_ROWS, width), jnp.bfloat16),
            shape((2 * slots, BORDER, width), jnp.bfloat16),
        ],
        [VMEM, VMEM],
        flops=20 * arrived.size,
        bytes_moved=4 * arrived.size,
    )


def slope_body(slots, windows, piece, facts_ref, arrived_ref, moments_ref, params_ref, slope_ref):
    blocks, rows, width = arrived_ref.shape
    facts = Facts(facts_ref, windows, slots)
    per_half = HALF_WINDOW_ROWS // rows
    slope, offset = half_terms(moments_ref, params_ref, facts.row_count())
    slot, half = piece // 2, piece % 2
    limit = facts.half_limit(slot, half)

    def work(part, carry):
        start = part * rows
        inside = lax.broadcasted_iota(jnp.int32, (rows, 1), 0) < limit - start
        for lanes in column_slices(width):
            values = arrived_ref[(half * per_half + part) * slots + slot, :, lanes]
            half_pre = values.astype(jnp.float32) * slope[:, lanes] + offset[:, lanes]
            found = jnp.where(inside, gelu_slope(half_pre, *bent(half_pre)), 0.0)
            slope_ref[pl.ds(pl.multiple_of(start, rows), rows), lanes] = found
        return carry

    lax.fori_loop(0, per_half, work, 0)


def entry_slope(facts, arrived, moments, params, slots, windows, piece):
    width = arrived.shape[2]
    return kernel_call(
        functools.partial(slope_body, slots, windows, piece),
        "entry_slope",
        (facts, arrived, moments, params),
        [SMEM, VMEM, VMEM, VMEM],
        shape((HALF_WINDOW_ROWS, width), jnp.float32),
        VMEM,
        flops=25 * HALF_WINDOW_ROWS * width,
        bytes_moved=6 * HALF_WINDOW_ROWS * width,
    )


def block_moments(values, inside, count):
    block_sum = jnp.sum(jnp.where(inside, values, 0.0), axis=0, keepdims=True)
    deviation = jnp.where(inside, values - block_sum / jnp.maximum(count, 1.0), 0.0)
    return block_sum, jnp.sum(deviation * deviation, axis=0, keepdims=True), count


def convolve_body(slots, windows, facts_ref, act_ref, weight_ref, out_ref, moments_ref, wide):
    facts = Facts(facts_ref, windows, slots)
    pieces, rows, inner = out_ref.shape
    tiles = inner // LANES
    for tile in range(3 * tiles):
        wide[tile, 0:PAD] = jnp.zeros((PAD, LANES), jnp.float32)
        wide[tile, PAD + rows : PADDED_ROWS] = jnp.zeros((PAD, LANES), jnp.float32)
    moments_ref[...] = jnp.zeros_like(moments_ref)
    below, above = PAD - DILATION_STEP, PAD + DILATION_STEP

    def work(piece, carry):
        product = jnp.dot(act_ref[piece], weight_ref[...], preferred_element_type=jnp.float32)
        for tile, lanes in enumerate(column_slices(3 * inner)):
            wide[tile, PAD : PAD + rows] = product[:, lanes]
        half = piece % 2
        limit = facts.half_limit(piece // 2, half)
        start = half * STRIP
        row = lax.broadcasted_iota(jnp.int32, (rows, 1), 0)
        end = jnp.minimum(limit, rows - STRIP + start)
        inside = jnp.logical_and(row >= start, row < end)
        count = jnp.maximum(end - start, 0).astype(jnp.float32)
        for tile, lanes in enumerate(column_slices(inner)):
            out = (
                wide[tiles + tile, PAD : PAD + rows]
                + wide[tile, below : below + rows]
                + wide[2 * tiles + tile, above : above + rows]
            )
            out_ref[piece, :, lanes] = out
            held = (moments_ref[0:1, lanes], moments_ref[1:2, lanes], moments_ref[2:3, lanes])
            moments_ref[0:1, lanes], moments_ref[1:2, lanes], moments_ref[2:3, lanes] = merged(
                held, block_moments(out, inside, count)
            )
        return carry

    lax.fori_loop(0, pieces, work, 0)


def convolve(facts, act, weight, slots, windows):
    pieces, rows, width = act.shape
    inner = weight.shape[1] // 3
    return kernel_call(
        functools.partial(convolve_body, slots, windows),
        "convolve",
        (facts, act, weight),
        [SMEM, VMEM, VMEM],
        [shape((pieces, rows, inner), jnp.float32), shape((3, inner), jnp.float32)],
        [VMEM, VMEM],
        [pltpu.VMEM((3 * inner // LANES, PADDED_ROWS, LANES), jnp.float32)],
        flops=6 * pieces * rows * width * inner,
        bytes_moved=pieces * rows * (width * 2 + inner * 4),
    )


def join_body(
    slots, windows, facts_ref, out_ref, border_ref, weight_ref, held_ref, strip_ref, moments_ref,
    moved,
):
    facts = Facts(facts_ref, windows, slots)
    pieces, rows, inner = out_ref.shape
    found = (held_ref[0:1], held_ref[1:2], held_ref[2:3])
    gap = STRIP - DILATION_STEP
    skip = BORDER - DILATION_STEP
    for piece in range(pieces):
        half = piece % 2
        other = piece + 1 - 2 * half
        moved[...] = jnp.zeros_like(moved)
        if half == 0:
            moved[gap : gap + BORDER] = jnp.dot(
                border_ref[other], weight_ref[:, 2 * inner :], preferred_element_type=jnp.float32
            )
            strip = out_ref[piece, rows - STRIP : rows] + moved[0:STRIP]
        else:
            moved[0:BORDER] = jnp.dot(
                border_ref[other], weight_ref[:, :inner], preferred_element_type=jnp.float32
            )
            strip = out_ref[piece, 0:STRIP] + moved[skip : skip + STRIP]
        strip_ref[piece] = strip
        limit = facts.half_limit(piece // 2, half) - (1 - half) * (rows - STRIP)
        count = jnp.clip(limit, 0, STRIP)
        inside = lax.broadcasted_iota(jnp.int32, (STRIP, 1), 0) < count
        found = merged(found, block_moments(strip, inside, count.astype(jnp.float32)))
    for number, value in enumerate(found):
        moments_ref[number : number + 1] = jnp.broadcast_to(value, (1, inner))


def join(facts, out, border, weight, held, slots, windows):
    pieces, rows, inner = out.shape
    return kernel_call(
        functools.partial(join_body, slots, windows),
        "join_halves",
        (facts, out, border, weight, held),
        [SMEM, VMEM, VMEM, VMEM, VMEM],
        [shape((pieces, STRIP, inner), jnp.float32), shape((3, inner), jnp.float32)],
        [VMEM, VMEM],
        [pltpu.VMEM((2 * STRIP, inner), jnp.float32)],
        flops=2 * pieces * BORDER * border.shape[2] * inner,
        bytes_moved=pieces * STRIP * inner * 8,
    )


def middle_body(
    slots, windows, facts_ref, out_ref, strip_ref, moments_ref, params_ref, grad_ref,
    act_ref, slope_ref, norm_ref, sums_ref,
):
    facts = Facts(facts_ref, windows, slots)
    pieces, rows, inner = out_ref.shape
    centre, scale, _, _ = norm_terms(moments_ref, params_ref, facts.row_count())
    gain, offset = 0.5 * params_ref[0:1], 0.5 * params_ref[1:2]
    sums_ref[...] = jnp.zeros_like(sums_ref)

    def chunk(piece, start, values):
        size = values.shape[0]
        limit = facts.half_limit(piece // 2, piece % 2)
        inside = lax.broadcasted_iota(jnp.int32, (size, 1), 0) < limit - start
        here = pl.ds(start, size)
        for lanes in column_slices(inner):
            norm = (values[:, lanes] - centre[:, lanes]) * scale[:, lanes]
            half_pre = norm * gain[:, lanes] + offset[:, lanes]
            bend, square = bent(half_pre)
            act = jnp.where(inside, half_pre + half_pre * bend, 0.0)
            act_ref[piece, here, lanes] = act.astype(jnp.bfloat16)
            grad = grad_ref[piece, here, lanes] * gelu_slope(half_pre, bend, square)
            grad = jnp.where(inside, grad, 0.0)
            slope_ref[piece, here, lanes] = grad
            norm_ref[piece, here, lanes] = norm
            sums_ref[0:1, lanes] = sums_ref[0:1, lanes] + jnp.sum(
                grad * norm, axis=0, keepdims=True
            )
            sums_ref[1:2, lanes] = sums_ref[1:2, lanes] + jnp.sum(grad, axis=0, keepdims=True)

    size = 2 * STRIP
    steps = rows // size - 1

    def main(step, carry):
        piece = step // steps
        start = pl.multiple_of((step % steps + piece % 2) * size, size)
        chunk(piece, start, out_ref[piece, pl.ds(start, size), :])
        return carry

    lax.fori_loop(0, pieces * steps, main, 0)

    def edge(slot, carry):
        low, high = 2 * slot, 2 * slot + 1
        start = rows - size
        values = jnp.concatenate([out_ref[low, start : start + STRIP], strip_ref[low]], axis=0)
        chunk(low, start, values)
        chunk(high, 0, jnp.concatenate([strip_ref[high], out_ref[high, STRIP:size]], axis=0))
        return carry

    lax.fori_loop(0, slots, edge, 0)


def middle(facts, out, strip, moments, params, grad, slots, windows):
    dims = out.shape
    return kernel_call(
        functools.partial(middle_body, slots, windows),
        "middle_norm",
        (facts, out, strip, moments, params, grad),
        [SMEM] + [VMEM] * 5,
        [
            shape(dims, jnp.bfloat16),
            shape(dims, jnp.float32),
            shape(dims, jnp.float32),
            shape((2, dims[2]), jnp.float32),
        ],
        [VMEM] * 4,
        flops=40 * out.size,
        bytes_moved=18 * out.size,
    )


def middle_grad_body(
    slots, windows, facts_ref, grad_ref, norm_ref, moments_ref, params_ref, sums_ref,
    padded_ref, border_ref,
):
    facts = Facts(facts_ref, windows, slots)
    pieces, rows, inner = grad_ref.shape
    rows_total = facts.row_count()
    _, _, slope, _ = norm_terms(moments_ref, params_ref, rows_total)
    level, tilt = sums_ref[1:2] / rows_total, sums_ref[0:1] / rows_total
    tiles = inner // LANES
    for piece in range(pieces):
        for tile in range(tiles):
            padded_ref[piece, tile, 0:PAD] = jnp.zeros((PAD, LANES), jnp.float32)
            padded_ref[piece, tile, PAD + rows : PADDED_ROWS] = jnp.zeros(
                (PAD, LANES), jnp.float32
            )
    size = 2 * STRIP

    def work(step, carry):
        piece, part = step // (rows // size), step % (rows // size)
        start = pl.multiple_of(part * size, size)
        limit = facts.half_limit(piece // 2, piece % 2)
        inside = lax.broadcasted_iota(jnp.int32, (size, 1), 0) < limit - start
        for tile, lanes in enumerate(column_slices(inner)):
            norm = norm_ref[piece, pl.ds(start, size), lanes]
            grad = slope[:, lanes] * (
                grad_ref[piece, pl.ds(start, size), lanes]
                - (level[:, lanes] + norm * tilt[:, lanes])
            )
            low = jnp.where(inside, grad, 0.0).astype(jnp.bfloat16)
            padded_ref[piece, tile, pl.ds(pl.multiple_of(start + PAD, 8), size), :] = low.astype(
                jnp.float32
            )
        return carry

    lax.fori_loop(0, pieces * (rows // size), work, 0)
    for piece in range(pieces):
        start = PAD + (0 if piece % 2 else rows - BORDER)
        for tile, lanes in enumerate(column_slices(inner)):
            border_ref[piece, :, lanes] = padded_ref[piece, tile, start : start + BORDER].astype(
                jnp.bfloat16
            )


def middle_grad(facts, grad, norm, moments, params, sums, slots, windows):
    pieces, _, inner = grad.shape
    return kernel_call(
        functools.partial(middle_grad_body, slots, windows),
        "middle_grad",
        (facts, grad, norm, moments, params, sums),
        [SMEM] + [VMEM] * 5,
        [
            shape((pieces, inner // LANES, PADDED_ROWS, LANES), jnp.float32),
            shape((pieces, BORDER, inner), jnp.bfloat16),
        ],
        [VMEM, VMEM],
        flops=8 * grad.size,
        bytes_moved=12 * grad.size,
    )


def output_body(
    slots, windows, facts_ref, act_ref, weight_ref, arrived_ref, params_ref, out_ref
):
    source, slot = pl.program_id(0), pl.program_id(1)
    rows = out_ref.shape[0]
    facts = Facts(facts_ref, windows, slots)
    per_half = HALF_WINDOW_ROWS // rows
    half, start = source // per_half, (source % per_half) * rows
    inside = lax.broadcasted_iota(jnp.int32, (rows, 1), 0) < facts.half_limit(slot, half) - start
    mixed = jnp.dot(act_ref[...], weight_ref[...], preferred_element_type=jnp.float32)
    block = arrived_ref[0].astype(jnp.float32) + mixed + params_ref[2:3]
    out_ref[...] = jnp.where(inside, block, 0.0)


def output_rows(facts, act, weight, arrived, params, slots, windows):
    blocks, rows, width = arrived.shape
    inner = act.shape[1]
    sources = blocks // slots
    place = lambda s, j: (j * sources + s, 0)
    return pl.pallas_call(
        functools.partial(output_body, slots, windows),
        grid=(sources, slots),
        in_specs=[
            SMEM,
            pl.BlockSpec((rows, inner), place),
            pl.BlockSpec((inner, width), lambda s, j: (0, 0)),
            pl.BlockSpec((1, rows, width), lambda s, j: (s * slots + j, 0, 0)),
            pl.BlockSpec((3, width), lambda s, j: (0, 0)),
        ],
        out_specs=pl.BlockSpec((rows, width), place),
        out_shape=shape((blocks * rows, width), jnp.float32),
        compiler_params=pltpu.CompilerParams(vmem_limit_bytes=16 << 20),
        cost_estimate=pl.CostEstimate(
            flops=2 * act.size * width, bytes_accessed=8 * arrived.size, transcendentals=0
        ),
        name="output_rows",
    )(facts, act, weight, arrived, params)


def entry_grad_body(
    slots, windows, slot, facts_ref, padded_ref, border_ref, weight_ref, *refs
):
    slope_refs, (arrived_ref, block_ref, moments_ref, params_ref) = refs[:2], refs[2:6]
    sent_ref, taps_ref, sums_ref, wide, packed, departures = refs[6:]
    facts = Facts(facts_ref, windows, slots)
    sources, rows, width = packed.shape
    tiles = padded_ref.shape[1]
    per_half = HALF_WINDOW_ROWS // rows
    centre, scale, slope, _ = norm_terms(moments_ref, params_ref, facts.row_count())
    skip = BORDER - DILATION_STEP
    sums_ref[...] = jnp.zeros_like(sums_ref)

    def departure(source):
        return pltpu.make_async_copy(
            packed.at[source], sent_ref.at[source], departures.at[source]
        )

    for half in range(2):
        piece = slot * 2 + half
        other = slot * 2 + 1 - half
        for tile, lanes in enumerate(column_slices(tiles * LANES)):
            border = border_ref[other, :, lanes].astype(jnp.float32)
            wide[tile] = padded_ref[piece, tile]
            if half == 0:
                end = PAD + HALF_WINDOW_ROWS
                wide[tile, end : end + DILATION_STEP] = border[0:DILATION_STEP]
            else:
                wide[tile, PAD - DILATION_STEP : PAD] = border[skip:BORDER]
            for tap in range(3):
                start = PAD - (tap - 1) * DILATION_STEP
                first = (tap * tiles + tile) * LANES
                taps_ref[half, :, first : first + LANES] = wide[
                    tile, start : start + HALF_WINDOW_ROWS
                ].astype(jnp.bfloat16)
        for column in range(0, width, 2 * LANES):
            grad = jnp.dot(
                taps_ref[half],
                weight_ref[:, column : column + 2 * LANES],
                preferred_element_type=jnp.float32,
            )
            for part in range(per_half):
                source = half * per_half + part
                here = slice(part * rows, (part + 1) * rows)
                for start in (column, column + LANES):
                    lanes = slice(start, start + LANES)
                    pre = grad[here, start - column : start - column + LANES]
                    pre = pre * slope_refs[half][here, lanes]
                    values = arrived_ref[source * slots + slot, :, lanes].astype(jnp.float32)
                    sums_ref[0:1, lanes] = sums_ref[0:1, lanes] + jnp.sum(
                        pre * values, axis=0, keepdims=True
                    )
                    sums_ref[1:2, lanes] = sums_ref[1:2, lanes] + jnp.sum(
                        pre, axis=0, keepdims=True
                    )
                    block = block_ref[piece, here, lanes].astype(jnp.float32)
                    packed[source, :, lanes] = (pre * slope[:, lanes] + block).astype(
                        jnp.bfloat16
                    )
        for part in range(per_half):
            departure(half * per_half + part).start()
    sums_ref[0:1] = (sums_ref[0:1] - centre * sums_ref[1:2]) * scale
    for source in range(sources):
        departure(source).wait()


def entry_grad(
    facts, padded, border, weight, slopes, arrived, block, moments, params, slots, windows, slot
):
    blocks, rows, width = arrived.shape
    inner = border.shape[2]
    sources = blocks // slots
    return kernel_call(
        functools.partial(entry_grad_body, slots, windows, slot),
        "entry_grad",
        (facts, padded, border, weight, *slopes, arrived, block, moments, params),
        [SMEM] + [VMEM] * 9,
        [
            pltpu.HBM((sources, rows, width), jnp.bfloat16),
            shape((2, HALF_WINDOW_ROWS, 3 * inner), jnp.bfloat16),
            shape((2, width), jnp.float32),
        ],
        [HBM, VMEM, VMEM],
        [
            pltpu.VMEM((inner // LANES, PADDED_ROWS, LANES), jnp.float32),
            pltpu.VMEM((sources, rows, width), jnp.bfloat16),
            pltpu.SemaphoreType.DMA((sources,)),
        ],
        flops=2 * 2 * HALF_WINDOW_ROWS * 3 * inner * width,
        bytes_moved=2 * HALF_WINDOW_ROWS * (width * 10 + inner * 10),
    )


def flat_mask(bits):
    return sum(mask * (lax.axis_size("seq") if axis == "grp" else 1) for axis, mask in bits)


def from_flat_partner(block, mask):
    count = lax.axis_size("grp") * lax.axis_size("seq")
    return lax.ppermute(
        block, ("grp", "seq"), [(place, place ^ mask) for place in range(count)]
    )


def bit_of(axis, mask):
    return (lax.axis_index(axis) // mask) % 2


def square_phases():
    steps = exchange_steps()[1:]
    outer = [step for step in steps if step[0] == "grp"]
    inner = [step for step in steps if step[0] == "seq"]
    ordered = []
    while outer and inner:
        ordered += [outer.pop(0), inner.pop(0)]
    ordered += outer + inner
    return [ordered[start : start + 2] for start in range(0, len(ordered), 2)]


def phase_place(phase):
    return sum(bit_of(*step) * 2**number for number, step in enumerate(phase))


def phase_parts(phase):
    parts = 2 ** len(phase)
    masks = [
        flat_mask([step for number, step in enumerate(phase) if part >> number & 1])
        for part in range(parts)
    ]
    return parts, masks


def scatter_starts(phase, rows):
    parts, _ = phase_parts(phase)
    mine = phase_place(phase)
    return [jnp.bitwise_xor(mine, part) * (rows // parts) for part in range(parts)]


def scatter_sum(buffer, phase, starts):
    parts, masks = phase_parts(phase)
    rows = buffer.shape[0] // parts
    kept = lax.dynamic_slice_in_dim(buffer, starts[0], rows)
    for part in range(1, parts):
        sent = lax.dynamic_slice_in_dim(buffer, starts[part], rows).astype(jnp.bfloat16)
        kept = kept + from_flat_partner(sent, masks[part]).astype(jnp.float32)
    return kept


def gather_parts(buffer, phase, mine):
    parts, masks = phase_parts(phase)
    found = [buffer] + [from_flat_partner(buffer, masks[part]) for part in range(1, parts)]
    orders = [
        jnp.concatenate([found[place ^ own] for place in range(parts)], axis=0)
        for own in range(parts)
    ]
    result = orders[0]
    for own in range(1, parts):
        result = jnp.where(mine == own, orders[own], result)
    return result


def finish_body(facts_ref, mine_ref, other_ref, dilated_ref, pointwise_ref):
    inner = dilated_ref.shape[2]

    def write(low_ref, high_ref):
        dilated_ref[0] = low_ref[:, :inner].astype(jnp.float32)
        dilated_ref[1] = low_ref[:, inner:].astype(jnp.float32)
        dilated_ref[2] = high_ref[:, :inner].astype(jnp.float32)
        pointwise_ref[...] = high_ref[:, inner:].astype(jnp.float32).T

    upper = facts_ref[0] % 2

    @pl.when(upper == 0)
    def _():
        write(mine_ref, other_ref)

    @pl.when(upper == 1)
    def _():
        write(other_ref, mine_ref)


def finish_weights(facts, mine, other):
    width, both = mine.shape
    inner = both // 2
    return kernel_call(
        finish_body,
        "finish_weights",
        (facts, mine, other),
        [SMEM, VMEM, VMEM],
        [shape((3, width, inner), jnp.float32), shape((inner, width), jnp.float32)],
        [VMEM, VMEM],
        flops=width * both,
        bytes_moved=12 * width * both,
        grant=16 << 20,
    )


def per_device(
    signal,
    entry_gain,
    entry_shift,
    dilated_kernel,
    middle_gain,
    middle_shift,
    pointwise_kernel,
    pointwise_bias,
    lengths,
    assignment,
    cotangent,
):
    seq_count = lax.axis_size("seq")
    windows, segment, width = signal.shape
    inner = pointwise_kernel.shape[0]
    slots = windows // seq_count
    rows = segment // 2
    pieces = 2 * slots
    places = jnp.stack([lax.axis_index("grp"), lax.axis_index("seq"), jnp.int32(seq_count)])
    facts = jnp.concatenate([places.astype(jnp.int32), assignment[0], lengths])
    entry_params = jnp.stack([entry_gain, entry_shift, pointwise_bias])
    middle_params = jnp.stack([middle_gain, middle_shift])

    outgoing, first_chosen, entry_local = pool(facts, signal, slots)
    arrived = lax.all_to_all(outgoing, "seq", split_axis=0, concat_axis=0, tiled=True)
    entry_moments = total_moments(entry_local)

    kernel_low = dilated_kernel.astype(jnp.bfloat16)
    wide_kernel = jnp.concatenate([kernel_low[tap] for tap in range(3)], axis=1)
    pointwise_low = pointwise_kernel.astype(jnp.bfloat16)
    back_kernel = jnp.swapaxes(kernel_low, 1, 2).reshape(3 * inner, width)
    grad_block, grad_middle, bias_part = prepare(
        facts, cotangent, pointwise_low, slots, windows
    )
    phases = square_phases()
    starts, held_rows = [], width
    for phase in phases:
        starts.append(scatter_starts(phase, held_rows))
        held_rows //= 2 ** len(phase)
    spots = [phase_place(phase) for phase in phases]
    first_axis, first_mask = exchange_steps()[0]
    upper = bit_of(first_axis, first_mask)
    (
        arrived,
        grad_block,
        grad_middle,
        wide_kernel,
        back_kernel,
        pointwise_low,
        starts,
        spots,
        upper,
        middle_params,
        facts,
    ) = lax.optimization_barrier(
        (
            arrived,
            grad_block,
            grad_middle,
            wide_kernel,
            back_kernel,
            pointwise_low,
            starts,
            spots,
            upper,
            middle_params,
            facts,
        )
    )
    upper = upper == 1

    act, act_border = activate(facts, arrived, entry_moments, entry_params, slots, windows)
    act_border = from_partner(act_border, "seq", 1)
    dilated, held_moments = convolve(facts, act, wide_kernel, slots, windows)
    strip, middle_moments = join(
        facts, dilated, act_border, wide_kernel, held_moments, slots, windows
    )
    slopes = []
    for number, (axis, mask) in enumerate(exchange_steps()):
        other = from_partner(middle_moments, axis, mask)
        if number and len(slopes) < pieces:
            tied, middle_moments = lax.optimization_barrier((arrived, middle_moments))
            found = entry_slope(
                facts, tied, entry_moments, entry_params, slots, windows, len(slopes)
            )
            other, found = lax.optimization_barrier((other, found))
            slopes.append(found)
        middle_moments = jnp.concatenate(
            merged(
                (middle_moments[0:1], middle_moments[1:2], middle_moments[2:3]),
                (other[0:1], other[1:2], other[2:3]),
            ),
            axis=0,
        )
    while len(slopes) < pieces:
        slopes.append(
            entry_slope(facts, arrived, entry_moments, entry_params, slots, windows, len(slopes))
        )
    middle_act, middle_slope, middle_norm, middle_sums = middle(
        facts,
        dilated,
        strip,
        middle_moments,
        middle_params,
        grad_middle.reshape(pieces, HALF_WINDOW_ROWS, inner),
        slots,
        windows,
    )
    flat_act = middle_act.reshape(-1, inner)
    for number, (axis, mask) in enumerate(exchange_steps()):
        other = from_partner(middle_sums, axis, mask)
        if number == 1:
            tied, middle_sums = lax.optimization_barrier((flat_act, middle_sums))
            pointwise_part = jnp.einsum(
                "rd,rf->df", grad_block, tied, preferred_element_type=jnp.float32
            )
            other, pointwise_part = lax.optimization_barrier((other, pointwise_part))
        middle_sums = middle_sums + other
    padded, grad_border = middle_grad(
        facts, middle_slope, middle_norm, middle_moments, middle_params, middle_sums, slots, windows
    )
    grad_border = from_partner(grad_border, "seq", 1)
    block_pieces = grad_block.reshape(pieces, HALF_WINDOW_ROWS, width)
    sent, taps, entry_part = [], [], jnp.concatenate([jnp.zeros_like(bias_part)] * 2)
    for slot in range(slots):
        slot_sent, slot_taps, part = entry_grad(
            facts, padded, grad_border, back_kernel, slopes[2 * slot : 2 * slot + 2], arrived,
            block_pieces, entry_moments, entry_params, slots, windows, slot,
        )
        sent.append(slot_sent)
        taps.append(slot_taps)
        entry_part = entry_part + part
    entry_sums = jnp.concatenate([entry_part, bias_part])

    def send_back(block):
        return lax.all_to_all(block, "seq", split_axis=0, concat_axis=0, tiled=True)

    returned = [send_back(sent[0])]
    flat_act, act, *taps = lax.optimization_barrier((flat_act, act, *taps, sent[-1]))[:-1]
    activations = output_rows(
        facts, flat_act, pointwise_low, arrived, entry_params, slots, windows
    )
    dilated_part = sum(
        jnp.einsum(
            "hrc,hrf->cf",
            act[2 * slot : 2 * slot + 2],
            slot_taps,
            preferred_element_type=jnp.float32,
        )
        for slot, slot_taps in enumerate(taps)
    )
    low_half = dilated_part[:, : 2 * inner]
    high_half = jnp.concatenate([dilated_part[:, 2 * inner :], pointwise_part], axis=1)
    other = from_partner(
        jnp.where(upper, low_half, high_half).astype(jnp.bfloat16), first_axis, first_mask
    )
    buffer = jnp.where(upper, high_half, low_half) + other.astype(jnp.float32)
    for number, phase in enumerate(phases):
        if number == len(phases) - 1:
            buffer, entry_sums, returned[0], activations = lax.optimization_barrier(
                (buffer, entry_sums, returned[0], activations)
            )
        buffer = scatter_sum(buffer, phase, starts[number])
    entry_sums = total(entry_sums)
    buffer = buffer.astype(jnp.bfloat16)
    for number, phase in reversed(list(enumerate(phases))):
        buffer = gather_parts(buffer, phase, spots[number])
        if number == len(phases) - 1:
            buffer, entry_sums, *later = lax.optimization_barrier(
                (buffer, entry_sums, *sent[1:])
            )
            returned += [send_back(block) for block in later]
    other = from_partner(buffer, first_axis, first_mask)
    dilated_kernel_gradient, pointwise_kernel_gradient = finish_weights(facts, buffer, other)
    signal_gradient = None
    for slot in range(slots):
        signal_gradient = unpool(
            facts, returned[slot], outgoing, first_chosen, entry_moments, entry_sums,
            entry_params, slots, slot, signal_gradient,
        )
    return (
        activations,
        signal_gradient,
        entry_sums[0],
        entry_sums[1],
        dilated_kernel_gradient,
        middle_sums[0],
        middle_sums[1],
        pointwise_kernel_gradient,
        entry_sums[2],
    )


def solution(mesh):
    return jax.shard_map(
        per_device,
        mesh=mesh,
        in_specs=(
            P("grp", "seq", None),
            P(),
            P(),
            P(),
            P(),
            P(),
            P(),
            P(),
            P(),
            P("grp", None),
            P(("grp", "seq"), None),
        ),
        out_specs=(
            P(("grp", "seq"), None),
            P("grp", "seq", None),
            P(),
            P(),
            P(),
            P(),
            P(),
            P(),
            P(),
        ),
        check_vma=False,
    )
```

```python
import functools
import math

import jax
import jax.numpy as jnp
from jax import lax
from jax.experimental import pallas as pl
from jax.experimental.pallas import tpu as pltpu
from jax.sharding import PartitionSpec as P

DILATION_STEP = 38
WINDOW_SPAN = 1024
HALF_WINDOW_ROWS = 512


EPSILON = 0.001

LANES = 128
BORDER = 48
STRIP = 64
PAD = 40
PADDED_ROWS = HALF_WINDOW_ROWS + 2 * PAD
EXTRA = 8
GELU_SLOPE = math.sqrt(2.0 / math.pi)
GELU_CUBE = 0.044715

VMEM = pl.BlockSpec(memory_space=pltpu.VMEM)
SMEM = pl.BlockSpec(memory_space=pltpu.SMEM)
HBM = pl.BlockSpec(memory_space=pltpu.HBM)


def from_partner(block, axis, mask):
    count = lax.axis_size(axis)
    return lax.ppermute(block, axis, [(place, place ^ mask) for place in range(count)])


def exchange_steps():
    steps = []
    for axis in ("grp", "seq"):
        mask = 1
        while mask < lax.axis_size(axis):
            steps.append((axis, mask))
            mask *= 2
    return steps


def total(values):
    for axis, mask in exchange_steps():
        values = values + from_partner(values, axis, mask)
    return values


def merged(left, right):
    left_sum, left_spread, left_count = left
    right_sum, right_spread, right_count = right
    gap = left_sum / jnp.maximum(left_count, 1.0) - right_sum / jnp.maximum(right_count, 1.0)
    weight = left_count * right_count / jnp.maximum(left_count + right_count, 1.0)
    return (
        left_sum + right_sum,
        left_spread + right_spread + gap * gap * weight,
        left_count + right_count,
    )


def total_moments(packed):
    for axis, mask in exchange_steps():
        other = from_partner(packed, axis, mask)
        packed = jnp.concatenate(
            merged(
                (packed[0:1], packed[1:2], packed[2:3]), (other[0:1], other[1:2], other[2:3])
            ),
            axis=0,
        )
    return packed


class Facts:
    def __init__(self, ref, windows, slots):
        self.ref, self.windows, self.slots = ref, windows, slots

    def slot_window(self, slot):
        upper = (2 * self.ref[1]) // self.ref[2]
        target = jnp.bitwise_xor(slot // self.slots, upper)
        return self.ref[3 + target * self.slots + slot % self.slots]

    def length(self, window):
        return self.ref[3 + self.windows + self.ref[0] * self.windows + window]

    def slot_count(self, slot, rows):
        return jnp.clip(self.length(self.slot_window(slot)) - self.ref[1] * rows, 0, rows)

    def half_limit(self, slot, half):
        place = jnp.bitwise_xor(self.ref[1], half)
        window = self.ref[3 + place * self.slots + slot]
        return jnp.clip(self.length(window) - half * HALF_WINDOW_ROWS, 0, HALF_WINDOW_ROWS)

    def row_count(self):
        start = 3 + self.windows
        count = self.ref.shape[0] - start
        added = lax.fori_loop(0, count, lambda i, held: held + self.ref[start + i], jnp.int32(0))
        return added.astype(jnp.float32)


def kernel_call(body, name, inputs, specs, outputs, out_specs, scratch=(), flops=0, bytes_moved=0, grant=8 << 20):
    return pl.pallas_call(
        body,
        in_specs=specs,
        out_specs=out_specs,
        out_shape=outputs,
        scratch_shapes=list(scratch),
        compiler_params=pltpu.CompilerParams(vmem_limit_bytes=grant),
        cost_estimate=pl.CostEstimate(
            flops=flops, bytes_accessed=bytes_moved, transcendentals=0
        ),
        name=name,
    )(*inputs)


def shape(dims, dtype):
    return jax.ShapeDtypeStruct(dims, dtype)


def in_hbm(array):
    return pltpu.with_memory_space_constraint(array, pltpu.HBM)


def column_slices(width):
    return [slice(start, start + LANES) for start in range(0, width, LANES)]


def pool_body(
    slots, facts_ref, signal_ref, pooled_ref, first_ref, moments_ref,
    held, low, mark, blocks, arrivals, departures,
):
    windows, columns = held.shape[:2]
    rows = low.shape[1]
    facts = Facts(facts_ref, windows, slots)

    def arrival(place, column):
        return pltpu.make_async_copy(
            signal_ref.at[facts.slot_window(place), :, pl.ds(column * LANES, LANES)],
            held.at[place, column],
            arrivals.at[place, column],
        )

    def departure(place):
        return [
            pltpu.make_async_copy(low.at[place], pooled_ref.at[place], departures.at[place, 0]),
            pltpu.make_async_copy(mark.at[place], first_ref.at[place], departures.at[place, 1]),
        ]

    def begin(place, carry):
        for column in range(columns):
            arrival(place, column).start()
        return carry

    lax.fori_loop(0, windows, begin, 0)
    moments_ref[...] = jnp.zeros_like(moments_ref)

    def work(place, carry):
        count = facts.slot_count(place, rows)
        inside = lax.broadcasted_iota(jnp.int32, (rows, LANES), 0) < count
        for column in range(columns):
            arrival(place, column).wait()
        for column, lanes in enumerate(column_slices(columns * LANES)):
            first_bin = held[place, column, pl.ds(0, rows, stride=2), :]
            second_bin = held[place, column, pl.ds(1, rows, stride=2), :]
            mark[place, :, lanes] = jnp.where(first_bin >= second_bin, 1.0, 0.0).astype(
                jnp.bfloat16
            )
            pooled = jnp.where(inside, jnp.maximum(first_bin, second_bin), 0.0)
            pooled = pooled.astype(jnp.bfloat16)
            low[place, :, lanes] = pooled
            found = block_moments(pooled.astype(jnp.float32), inside, count.astype(jnp.float32))
            blocks[place, 0:1, lanes] = found[0]
            blocks[place, 1:2, lanes] = found[1]
        for copy in departure(place):
            copy.start()
        return carry

    lax.fori_loop(0, windows, work, 0)

    def join_blocks(place, carry):
        count = jnp.broadcast_to(
            facts.slot_count(place, rows).astype(jnp.float32), (1, columns * LANES)
        )
        held_moments = (moments_ref[0:1], moments_ref[1:2], moments_ref[2:3])
        moments_ref[0:1], moments_ref[1:2], moments_ref[2:3] = merged(
            held_moments, (blocks[place, 0:1], blocks[place, 1:2], count)
        )
        return carry

    lax.fori_loop(0, windows, join_blocks, 0)

    def finish(place, carry):
        for copy in departure(place):
            copy.wait()
        return carry

    lax.fori_loop(0, windows, finish, 0)


def pool(facts, signal, slots):
    windows, segment, width = signal.shape
    rows, columns = segment // 2, width // LANES
    block = (windows, rows, width)
    return kernel_call(
        functools.partial(pool_body, slots),
        "pool",
        (facts, in_hbm(signal)),
        [SMEM, HBM],
        [
            pltpu.HBM(block, jnp.bfloat16),
            pltpu.HBM(block, jnp.bfloat16),
            shape((3, width), jnp.float32),
        ],
        [HBM, HBM, VMEM],
        [
            pltpu.VMEM((windows, columns, segment, LANES), jnp.float32),
            pltpu.VMEM(block, jnp.bfloat16),
            pltpu.VMEM(block, jnp.bfloat16),
            pltpu.VMEM((windows, 2, width), jnp.float32),
            pltpu.SemaphoreType.DMA((windows, columns)),
            pltpu.SemaphoreType.DMA((windows, 2)),
        ],
        flops=10 * windows * rows * width,
        bytes_moved=windows * rows * width * 12,
        grant=24 << 20,
    )


def unpool_body(
    slots, slot, windows, facts_ref, returned_ref, pooled_ref, first_ref, moments_ref, sums_ref,
    params_ref, *refs,
):
    out_ref, back, low, mark, held, arrivals, departures = refs[-7:]
    targets, rows, width = back.shape
    columns = held.shape[1]
    facts = Facts(facts_ref, windows, slots)

    def arrival(target):
        place = target * slots + slot
        return [
            pltpu.make_async_copy(returned_ref.at[target], back.at[target], arrivals.at[target, 0]),
            pltpu.make_async_copy(pooled_ref.at[place], low.at[target], arrivals.at[target, 1]),
            pltpu.make_async_copy(first_ref.at[place], mark.at[target], arrivals.at[target, 2]),
        ]

    def departure(target, column):
        window = facts.slot_window(target * slots + slot)
        return pltpu.make_async_copy(
            held.at[target, column],
            out_ref.at[window, :, pl.ds(column * LANES, LANES)],
            departures.at[target, column],
        )

    def begin(target, carry):
        for copy in arrival(target):
            copy.start()
        return carry

    lax.fori_loop(0, targets, begin, 0)
    rows_total = facts.row_count()
    centre = moments_ref[0:1] / rows_total
    scale = lax.rsqrt(moments_ref[1:2] / rows_total + EPSILON)
    factor = params_ref[0:1] * scale / rows_total
    level = factor * sums_ref[1:2]
    tilt = factor * scale * sums_ref[0:1]

    def work(target, carry):
        for copy in arrival(target):
            copy.wait()
        inside = lax.broadcasted_iota(jnp.int32, (rows, LANES), 0) < facts.slot_count(
            target * slots + slot, rows
        )
        for column, lanes in enumerate(column_slices(width)):
            centred = low[target, :, lanes].astype(jnp.float32) - centre[:, lanes]
            gradient = back[target, :, lanes].astype(jnp.float32) - (
                level[:, lanes] + centred * tilt[:, lanes]
            )
            gradient = jnp.where(inside, gradient, 0.0).astype(jnp.bfloat16).astype(jnp.float32)
            first = gradient * mark[target, :, lanes].astype(jnp.float32)
            held[target, column, pl.ds(0, rows, stride=2), :] = first
            held[target, column, pl.ds(1, rows, stride=2), :] = gradient - first
        for column in range(columns):
            departure(target, column).start()
        return carry

    lax.fori_loop(0, targets, work, 0)

    def finish(target, carry):
        for column in range(columns):
            departure(target, column).wait()
        return carry

    lax.fori_loop(0, targets, finish, 0)


def unpool(facts, returned, pooled, first, moments, sums, params, slots, slot, held_output):
    targets, rows, width = returned.shape
    windows, columns = targets * slots, width // LANES
    inputs = [facts, in_hbm(returned), in_hbm(pooled), in_hbm(first), moments, sums, params]
    specs = [SMEM, HBM, HBM, HBM, VMEM, VMEM, VMEM]
    aliases = {}
    if held_output is not None:
        aliases = {len(inputs): 0}
        inputs.append(in_hbm(held_output))
        specs.append(HBM)
    block = (targets, rows, width)
    return pl.pallas_call(
        functools.partial(unpool_body, slots, slot, windows),
        in_specs=specs,
        out_specs=HBM,
        out_shape=pltpu.HBM((windows, 2 * rows, width), jnp.float32),
        input_output_aliases=aliases,
        scratch_shapes=[
            pltpu.VMEM(block, jnp.bfloat16),
            pltpu.VMEM(block, jnp.bfloat16),
            pltpu.VMEM(block, jnp.bfloat16),
            pltpu.VMEM((targets, columns, 2 * rows, LANES), jnp.float32),
            pltpu.SemaphoreType.DMA((targets, 3)),
            pltpu.SemaphoreType.DMA((targets, columns)),
        ],
        compiler_params=pltpu.CompilerParams(vmem_limit_bytes=16 << 20),
        cost_estimate=pl.CostEstimate(
            flops=10 * targets * rows * width,
            bytes_accessed=targets * rows * width * 14,
            transcendentals=0,
        ),
        name="unpool",
    )(*inputs)


def prepare_body(slots, windows, facts_ref, cot_ref, weight_ref, low_ref, middle_ref, bias_ref):
    step = pl.program_id(0)
    rows = cot_ref.shape[0]
    facts = Facts(facts_ref, windows, slots)
    first_row = step * rows
    piece = first_row // HALF_WINDOW_ROWS
    limit = facts.half_limit(piece // 2, piece % 2) - first_row % HALF_WINDOW_ROWS

    @pl.when(step == 0)
    def _():
        bias_ref[...] = jnp.zeros_like(bias_ref)

    inside = lax.broadcasted_iota(jnp.int32, (rows, 1), 0) < limit
    block = jnp.where(inside, cot_ref[...], 0.0)
    bias_ref[...] = bias_ref[...] + jnp.sum(block, axis=0, keepdims=True)
    low = block.astype(jnp.bfloat16)
    low_ref[...] = low
    middle_ref[...] = lax.dot_general(
        low, weight_ref[...], (((1,), (1,)), ((), ())), preferred_element_type=jnp.float32
    )


def prepare(facts, cotangent, weight, slots, windows):
    total_rows, width = cotangent.shape
    inner = weight.shape[0]
    rows = 256
    return pl.pallas_call(
        functools.partial(prepare_body, slots, windows),
        grid=(total_rows // rows,),
        in_specs=[
            SMEM,
            pl.BlockSpec((rows, width), lambda i: (i, 0)),
            pl.BlockSpec((inner, width), lambda i: (0, 0)),
        ],
        out_specs=[
            pl.BlockSpec((rows, width), lambda i: (i, 0)),
            pl.BlockSpec((rows, inner), lambda i: (i, 0)),
            pl.BlockSpec((1, width), lambda i: (0, 0)),
        ],
        out_shape=[
            shape((total_rows, width), jnp.bfloat16),
            shape((total_rows, inner), jnp.float32),
            shape((1, width), jnp.float32),
        ],
        compiler_params=pltpu.CompilerParams(vmem_limit_bytes=16 << 20),
        cost_estimate=pl.CostEstimate(
            flops=2 * total_rows * width * inner,
            bytes_accessed=total_rows * (width * 6 + inner * 4),
            transcendentals=0,
        ),
        name="prepare_cotangent",
    )(facts, cotangent, weight)


def norm_terms(moments_ref, params_ref, rows_total):
    centre = moments_ref[0:1] / rows_total
    scale = lax.rsqrt(moments_ref[1:2] / rows_total + EPSILON)
    return centre, scale, params_ref[0:1] * scale, params_ref[1:2]


def half_terms(moments_ref, params_ref, rows_total):
    centre, _, slope, offset = norm_terms(moments_ref, params_ref, rows_total)
    return 0.5 * slope, 0.5 * (offset - centre * slope)


def bent(half):
    square = half * half
    return jnp.tanh(half * (2.0 * GELU_SLOPE + (8.0 * GELU_SLOPE * GELU_CUBE) * square)), square


def gelu_slope(half, bend, square):
    inner = GELU_SLOPE + (12.0 * GELU_SLOPE * GELU_CUBE) * square
    return (0.5 + 0.5 * bend) + (half - half * bend * bend) * inner


def activate_body(
    slots, windows, facts_ref, arrived_ref, moments_ref, params_ref, act_ref, border_ref
):
    blocks, rows, width = arrived_ref.shape
    facts = Facts(facts_ref, windows, slots)
    per_half = HALF_WINDOW_ROWS // rows
    slope, offset = half_terms(moments_ref, params_ref, facts.row_count())

    def work(block, carry):
        source, slot = block // slots, block % slots
        half, start = source // per_half, (source % per_half) * rows
        inside = lax.broadcasted_iota(jnp.int32, (rows, 1), 0) < (
            facts.half_limit(slot, half) - start
        )
        for lanes in column_slices(width):
            values = arrived_ref[block, :, lanes].astype(jnp.float32)
            half_pre = values * slope[:, lanes] + offset[:, lanes]
            bend, _ = bent(half_pre)
            act = jnp.where(inside, half_pre + half_pre * bend, 0.0)
            act_ref[slot * 2 + half, pl.ds(pl.multiple_of(start, rows), rows), lanes] = act.astype(
                jnp.bfloat16
            )
        return carry

    lax.fori_loop(0, blocks, work, 0)
    for piece in range(act_ref.shape[0]):
        start = 0 if piece % 2 else HALF_WINDOW_ROWS - BORDER
        border_ref[piece] = act_ref[piece, start : start + BORDER]


def activate(facts, arrived, moments, params, slots, windows):
    width = arrived.shape[2]
    return kernel_call(
        functools.partial(activate_body, slots, windows),
        "activate",
        (facts, arrived, moments, params),
        [SMEM, VMEM, VMEM, VMEM],
        [
            shape((2 * slots, HALF_WINDOW_ROWS, width), jnp.bfloat16),
            shape((2 * slots, BORDER, width), jnp.bfloat16),
        ],
        [VMEM, VMEM],
        flops=20 * arrived.size,
        bytes_moved=4 * arrived.size,
    )


def slope_body(slots, windows, piece, facts_ref, arrived_ref, moments_ref, params_ref, slope_ref):
    blocks, rows, width = arrived_ref.shape
    facts = Facts(facts_ref, windows, slots)
    per_half = HALF_WINDOW_ROWS // rows
    slope, offset = half_terms(moments_ref, params_ref, facts.row_count())
    slot, half = piece // 2, piece % 2
    limit = facts.half_limit(slot, half)

    def work(part, carry):
        start = part * rows
        inside = lax.broadcasted_iota(jnp.int32, (rows, 1), 0) < limit - start
        for lanes in column_slices(width):
            values = arrived_ref[(half * per_half + part) * slots + slot, :, lanes]
            half_pre = values.astype(jnp.float32) * slope[:, lanes] + offset[:, lanes]
            found = jnp.where(inside, gelu_slope(half_pre, *bent(half_pre)), 0.0)
            slope_ref[pl.ds(pl.multiple_of(start, rows), rows), lanes] = found
        return carry

    lax.fori_loop(0, per_half, work, 0)


def entry_slope(facts, arrived, moments, params, slots, windows, piece):
    width = arrived.shape[2]
    return kernel_call(
        functools.partial(slope_body, slots, windows, piece),
        "entry_slope",
        (facts, arrived, moments, params),
        [SMEM, VMEM, VMEM, VMEM],
        shape((HALF_WINDOW_ROWS, width), jnp.float32),
        VMEM,
        flops=25 * HALF_WINDOW_ROWS * width,
        bytes_moved=6 * HALF_WINDOW_ROWS * width,
    )


def block_moments(values, inside, count):
    block_sum = jnp.sum(jnp.where(inside, values, 0.0), axis=0, keepdims=True)
    deviation = jnp.where(inside, values - block_sum / jnp.maximum(count, 1.0), 0.0)
    return block_sum, jnp.sum(deviation * deviation, axis=0, keepdims=True), count


def convolve_body(slots, windows, facts_ref, act_ref, weight_ref, out_ref, moments_ref, wide):
    facts = Facts(facts_ref, windows, slots)
    pieces, rows, inner = out_ref.shape
    tiles = inner // LANES
    for tile in range(3 * tiles):
        wide[tile, 0:PAD] = jnp.zeros((PAD, LANES), jnp.float32)
        wide[tile, PAD + rows : PADDED_ROWS] = jnp.zeros((PAD, LANES), jnp.float32)
    moments_ref[...] = jnp.zeros_like(moments_ref)
    below, above = PAD - DILATION_STEP, PAD + DILATION_STEP

    def work(piece, carry):
        product = jnp.dot(act_ref[piece], weight_ref[...], preferred_element_type=jnp.float32)
        for tile, lanes in enumerate(column_slices(3 * inner)):
            wide[tile, PAD : PAD + rows] = product[:, lanes]
        half = piece % 2
        limit = facts.half_limit(piece // 2, half)
        start = half * STRIP
        row = lax.broadcasted_iota(jnp.int32, (rows, 1), 0)
        end = jnp.minimum(limit, rows - STRIP + start)
        inside = jnp.logical_and(row >= start, row < end)
        count = jnp.maximum(end - start, 0).astype(jnp.float32)
        for tile, lanes in enumerate(column_slices(inner)):
            out = (
                wide[tiles + tile, PAD : PAD + rows]
                + wide[tile, below : below + rows]
                + wide[2 * tiles + tile, above : above + rows]
            )
            out_ref[piece, :, lanes] = out
            held = (moments_ref[0:1, lanes], moments_ref[1:2, lanes], moments_ref[2:3, lanes])
            moments_ref[0:1, lanes], moments_ref[1:2, lanes], moments_ref[2:3, lanes] = merged(
                held, block_moments(out, inside, count)
            )
        return carry

    lax.fori_loop(0, pieces, work, 0)


def convolve(facts, act, weight, slots, windows):
    pieces, rows, width = act.shape
    inner = weight.shape[1] // 3
    return kernel_call(
        functools.partial(convolve_body, slots, windows),
        "convolve",
        (facts, act, weight),
        [SMEM, VMEM, VMEM],
        [shape((pieces, rows, inner), jnp.float32), shape((3, inner), jnp.float32)],
        [VMEM, VMEM],
        [pltpu.VMEM((3 * inner // LANES, PADDED_ROWS, LANES), jnp.float32)],
        flops=6 * pieces * rows * width * inner,
        bytes_moved=pieces * rows * (width * 2 + inner * 4),
    )


def join_body(
    slots, windows, facts_ref, out_ref, border_ref, weight_ref, held_ref, strip_ref, moments_ref,
    moved,
):
    facts = Facts(facts_ref, windows, slots)
    pieces, rows, inner = out_ref.shape
    found = (held_ref[0:1], held_ref[1:2], held_ref[2:3])
    gap = STRIP - DILATION_STEP
    skip = BORDER - DILATION_STEP
    for piece in range(pieces):
        half = piece % 2
        other = piece + 1 - 2 * half
        moved[...] = jnp.zeros_like(moved)
        if half == 0:
            moved[gap : gap + BORDER] = jnp.dot(
                border_ref[other], weight_ref[:, 2 * inner :], preferred_element_type=jnp.float32
            )
            strip = out_ref[piece, rows - STRIP : rows] + moved[0:STRIP]
        else:
            moved[0:BORDER] = jnp.dot(
                border_ref[other], weight_ref[:, :inner], preferred_element_type=jnp.float32
            )
            strip = out_ref[piece, 0:STRIP] + moved[skip : skip + STRIP]
        strip_ref[piece] = strip
        limit = facts.half_limit(piece // 2, half) - (1 - half) * (rows - STRIP)
        count = jnp.clip(limit, 0, STRIP)
        inside = lax.broadcasted_iota(jnp.int32, (STRIP, 1), 0) < count
        found = merged(found, block_moments(strip, inside, count.astype(jnp.float32)))
    for number, value in enumerate(found):
        moments_ref[number : number + 1] = jnp.broadcast_to(value, (1, inner))


def join(facts, out, border, weight, held, slots, windows):
    pieces, rows, inner = out.shape
    return kernel_call(
        functools.partial(join_body, slots, windows),
        "join_halves",
        (facts, out, border, weight, held),
        [SMEM, VMEM, VMEM, VMEM, VMEM],
        [shape((pieces, STRIP, inner), jnp.float32), shape((3, inner), jnp.float32)],
        [VMEM, VMEM],
        [pltpu.VMEM((2 * STRIP, inner), jnp.float32)],
        flops=2 * pieces * BORDER * border.shape[2] * inner,
        bytes_moved=pieces * STRIP * inner * 8,
    )


def middle_body(
    slots, windows, facts_ref, out_ref, strip_ref, moments_ref, params_ref, grad_ref,
    act_ref, slope_ref, norm_ref, sums_ref,
):
    facts = Facts(facts_ref, windows, slots)
    pieces, rows, inner = out_ref.shape
    centre, scale, _, _ = norm_terms(moments_ref, params_ref, facts.row_count())
    gain, offset = 0.5 * params_ref[0:1], 0.5 * params_ref[1:2]
    sums_ref[...] = jnp.zeros_like(sums_ref)

    def chunk(piece, start, values):
        size = values.shape[0]
        limit = facts.half_limit(piece // 2, piece % 2)
        inside = lax.broadcasted_iota(jnp.int32, (size, 1), 0) < limit - start
        here = pl.ds(start, size)
        for lanes in column_slices(inner):
            norm = (values[:, lanes] - centre[:, lanes]) * scale[:, lanes]
            half_pre = norm * gain[:, lanes] + offset[:, lanes]
            bend, square = bent(half_pre)
            act = jnp.where(inside, half_pre + half_pre * bend, 0.0)
            act_ref[piece, here, lanes] = act.astype(jnp.bfloat16)
            grad = grad_ref[piece, here, lanes] * gelu_slope(half_pre, bend, square)
            grad = jnp.where(inside, grad, 0.0)
            slope_ref[piece, here, lanes] = grad
            norm_ref[piece, here, lanes] = norm
            sums_ref[0:1, lanes] = sums_ref[0:1, lanes] + jnp.sum(
                grad * norm, axis=0, keepdims=True
            )
            sums_ref[1:2, lanes] = sums_ref[1:2, lanes] + jnp.sum(grad, axis=0, keepdims=True)

    size = 2 * STRIP
    steps = rows // size - 1

    def main(step, carry):
        piece = step // steps
        start = pl.multiple_of((step % steps + piece % 2) * size, size)
        chunk(piece, start, out_ref[piece, pl.ds(start, size), :])
        return carry

    lax.fori_loop(0, pieces * steps, main, 0)

    def edge(slot, carry):
        low, high = 2 * slot, 2 * slot + 1
        start = rows - size
        values = jnp.concatenate([out_ref[low, start : start + STRIP], strip_ref[low]], axis=0)
        chunk(low, start, values)
        chunk(high, 0, jnp.concatenate([strip_ref[high], out_ref[high, STRIP:size]], axis=0))
        return carry

    lax.fori_loop(0, slots, edge, 0)


def middle(facts, out, strip, moments, params, grad, slots, windows):
    dims = out.shape
    return kernel_call(
        functools.partial(middle_body, slots, windows),
        "middle_norm",
        (facts, out, strip, moments, params, grad),
        [SMEM] + [VMEM] * 5,
        [
            shape(dims, jnp.bfloat16),
            shape(dims, jnp.float32),
            shape(dims, jnp.float32),
            shape((2, dims[2]), jnp.float32),
        ],
        [VMEM] * 4,
        flops=40 * out.size,
        bytes_moved=18 * out.size,
    )


def middle_grad_body(
    slots, windows, facts_ref, grad_ref, norm_ref, moments_ref, params_ref, sums_ref,
    padded_ref, border_ref,
):
    facts = Facts(facts_ref, windows, slots)
    pieces, rows, inner = grad_ref.shape
    rows_total = facts.row_count()
    _, _, slope, _ = norm_terms(moments_ref, params_ref, rows_total)
    level, tilt = sums_ref[1:2] / rows_total, sums_ref[0:1] / rows_total
    tiles = inner // LANES
    for piece in range(pieces):
        for tile in range(tiles):
            padded_ref[piece, tile, 0:PAD] = jnp.zeros((PAD, LANES), jnp.float32)
            padded_ref[piece, tile, PAD + rows : PADDED_ROWS] = jnp.zeros(
                (PAD, LANES), jnp.float32
            )
    size = 2 * STRIP

    def work(step, carry):
        piece, part = step // (rows // size), step % (rows // size)
        start = pl.multiple_of(part * size, size)
        limit = facts.half_limit(piece // 2, piece % 2)
        inside = lax.broadcasted_iota(jnp.int32, (size, 1), 0) < limit - start
        for tile, lanes in enumerate(column_slices(inner)):
            norm = norm_ref[piece, pl.ds(start, size), lanes]
            grad = slope[:, lanes] * (
                grad_ref[piece, pl.ds(start, size), lanes]
                - (level[:, lanes] + norm * tilt[:, lanes])
            )
            low = jnp.where(inside, grad, 0.0).astype(jnp.bfloat16)
            padded_ref[piece, tile, pl.ds(pl.multiple_of(start + PAD, 8), size), :] = low.astype(
                jnp.float32
            )
        return carry

    lax.fori_loop(0, pieces * (rows // size), work, 0)
    for piece in range(pieces):
        start = PAD + (0 if piece % 2 else rows - BORDER)
        for tile, lanes in enumerate(column_slices(inner)):
            border_ref[piece, :, lanes] = padded_ref[piece, tile, start : start + BORDER].astype(
                jnp.bfloat16
            )


def middle_grad(facts, grad, norm, moments, params, sums, slots, windows):
    pieces, _, inner = grad.shape
    return kernel_call(
        functools.partial(middle_grad_body, slots, windows),
        "middle_grad",
        (facts, grad, norm, moments, params, sums),
        [SMEM] + [VMEM] * 5,
        [
            shape((pieces, inner // LANES, PADDED_ROWS, LANES), jnp.float32),
            shape((pieces, BORDER, inner), jnp.bfloat16),
        ],
        [VMEM, VMEM],
        flops=8 * grad.size,
        bytes_moved=12 * grad.size,
    )


def output_body(
    slots, windows, facts_ref, act_ref, weight_ref, arrived_ref, params_ref, out_ref
):
    source, slot = pl.program_id(0), pl.program_id(1)
    rows = out_ref.shape[0]
    facts = Facts(facts_ref, windows, slots)
    per_half = HALF_WINDOW_ROWS // rows
    half, start = source // per_half, (source % per_half) * rows
    inside = lax.broadcasted_iota(jnp.int32, (rows, 1), 0) < facts.half_limit(slot, half) - start
    mixed = jnp.dot(act_ref[...], weight_ref[...], preferred_element_type=jnp.float32)
    block = arrived_ref[0].astype(jnp.float32) + mixed + params_ref[2:3]
    out_ref[...] = jnp.where(inside, block, 0.0)


def output_rows(facts, act, weight, arrived, params, slots, windows):
    blocks, rows, width = arrived.shape
    inner = act.shape[1]
    sources = blocks // slots
    place = lambda s, j: (j * sources + s, 0)
    return pl.pallas_call(
        functools.partial(output_body, slots, windows),
        grid=(sources, slots),
        in_specs=[
            SMEM,
            pl.BlockSpec((rows, inner), place),
            pl.BlockSpec((inner, width), lambda s, j: (0, 0)),
            pl.BlockSpec((1, rows, width), lambda s, j: (s * slots + j, 0, 0)),
            pl.BlockSpec((3, width), lambda s, j: (0, 0)),
        ],
        out_specs=pl.BlockSpec((rows, width), place),
        out_shape=shape((blocks * rows, width), jnp.float32),
        compiler_params=pltpu.CompilerParams(vmem_limit_bytes=16 << 20),
        cost_estimate=pl.CostEstimate(
            flops=2 * act.size * width, bytes_accessed=8 * arrived.size, transcendentals=0
        ),
        name="output_rows",
    )(facts, act, weight, arrived, params)


def entry_grad_body(
    slots, windows, slot, facts_ref, padded_ref, border_ref, weight_ref, *refs
):
    slope_refs, (arrived_ref, block_ref, moments_ref, params_ref) = refs[:2], refs[2:6]
    sent_ref, kept_ref, sums_ref, wide, packed, taps_ref, departures, kept = refs[-8:]
    facts = Facts(facts_ref, windows, slots)
    sources, rows, width = packed.shape
    tiles = padded_ref.shape[1]
    per_half = HALF_WINDOW_ROWS // rows
    centre, scale, slope, _ = norm_terms(moments_ref, params_ref, facts.row_count())
    skip = BORDER - DILATION_STEP
    sums_ref[...] = jnp.zeros_like(sums_ref)

    def departure(source):
        return pltpu.make_async_copy(
            packed.at[source], sent_ref.at[source], departures.at[source]
        )

    def keeping(half):
        return pltpu.make_async_copy(
            taps_ref.at[half], kept_ref.at[slot * 2 + half], kept.at[half]
        )

    for half in range(2):
        piece = slot * 2 + half
        other = slot * 2 + 1 - half
        for tile, lanes in enumerate(column_slices(tiles * LANES)):
            border = border_ref[other, :, lanes].astype(jnp.float32)
            wide[tile] = padded_ref[piece, tile]
            if half == 0:
                end = PAD + HALF_WINDOW_ROWS
                wide[tile, end : end + DILATION_STEP] = border[0:DILATION_STEP]
            else:
                wide[tile, PAD - DILATION_STEP : PAD] = border[skip:BORDER]
            for tap in range(3):
                start = PAD - (tap - 1) * DILATION_STEP
                first = (tap * tiles + tile) * LANES
                taps_ref[half, :, first : first + LANES] = wide[
                    tile, start : start + HALF_WINDOW_ROWS
                ].astype(jnp.bfloat16)
        keeping(half).start()
        for column in range(0, width, 2 * LANES):
            grad = jnp.dot(
                taps_ref[half],
                weight_ref[:, column : column + 2 * LANES],
                preferred_element_type=jnp.float32,
            )
            for part in range(per_half):
                source = half * per_half + part
                here = slice(part * rows, (part + 1) * rows)
                for start in (column, column + LANES):
                    lanes = slice(start, start + LANES)
                    pre = grad[here, start - column : start - column + LANES]
                    pre = pre * slope_refs[half][here, lanes]
                    values = arrived_ref[source * slots + slot, :, lanes].astype(jnp.float32)
                    sums_ref[0:1, lanes] = sums_ref[0:1, lanes] + jnp.sum(
                        pre * values, axis=0, keepdims=True
                    )
                    sums_ref[1:2, lanes] = sums_ref[1:2, lanes] + jnp.sum(
                        pre, axis=0, keepdims=True
                    )
                    block = block_ref[piece, here, lanes].astype(jnp.float32)
                    packed[source, :, lanes] = (pre * slope[:, lanes] + block).astype(
                        jnp.bfloat16
                    )
        for part in range(per_half):
            departure(half * per_half + part).start()
    sums_ref[0:1] = (sums_ref[0:1] - centre * sums_ref[1:2]) * scale
    for half in range(2):
        keeping(half).wait()
    for source in range(sources):
        departure(source).wait()


def entry_grad(
    facts, padded, border, weight, slopes, arrived, block, moments, params, taps, slots, windows,
    slot,
):
    blocks, rows, width = arrived.shape
    inner, sources = border.shape[2], blocks // slots
    inputs = [facts, padded, border, weight, *slopes, arrived, block, moments, params]
    specs = [SMEM] + [VMEM] * 9
    aliases = {}
    if taps is not None:
        aliases = {len(inputs): 1}
        inputs.append(in_hbm(taps))
        specs.append(HBM)
    taps_shape = (HALF_WINDOW_ROWS, 3 * inner)
    return pl.pallas_call(
        functools.partial(entry_grad_body, slots, windows, slot),
        in_specs=specs,
        out_specs=[HBM, HBM, VMEM],
        out_shape=[
            pltpu.HBM((sources, rows, width), jnp.bfloat16),
            pltpu.HBM((2 * slots, *taps_shape), jnp.bfloat16),
            shape((2, width), jnp.float32),
        ],
        input_output_aliases=aliases,
        scratch_shapes=[
            pltpu.VMEM((inner // LANES, PADDED_ROWS, LANES), jnp.float32),
            pltpu.VMEM((sources, rows, width), jnp.bfloat16),
            pltpu.VMEM((2, *taps_shape), jnp.bfloat16),
            pltpu.SemaphoreType.DMA((sources,)),
            pltpu.SemaphoreType.DMA((2,)),
        ],
        compiler_params=pltpu.CompilerParams(vmem_limit_bytes=10 << 20),
        cost_estimate=pl.CostEstimate(
            flops=2 * 2 * HALF_WINDOW_ROWS * 3 * inner * width,
            bytes_accessed=2 * HALF_WINDOW_ROWS * (width * 10 + inner * 10),
            transcendentals=0,
        ),
        name="entry_grad",
    )(*inputs)


def flat_mask(bits):
    return sum(mask * (lax.axis_size("seq") if axis == "grp" else 1) for axis, mask in bits)


def from_flat_partner(block, mask):
    count = lax.axis_size("grp") * lax.axis_size("seq")
    return lax.ppermute(
        block, ("grp", "seq"), [(place, place ^ mask) for place in range(count)]
    )


def bit_of(axis, mask):
    return (lax.axis_index(axis) // mask) % 2


def square_phases():
    steps = exchange_steps()[1:]
    outer = [step for step in steps if step[0] == "grp"]
    inner = [step for step in steps if step[0] == "seq"]
    ordered = []
    while outer and inner:
        ordered += [outer.pop(0), inner.pop(0)]
    ordered += outer + inner
    return [ordered[start : start + 2] for start in range(0, len(ordered), 2)]


def phase_place(phase):
    return sum(bit_of(*step) * 2**number for number, step in enumerate(phase))


def phase_parts(phase):
    parts = 2 ** len(phase)
    masks = [
        flat_mask([step for number, step in enumerate(phase) if part >> number & 1])
        for part in range(parts)
    ]
    return parts, masks


def exchange_parts(parts, phase):
    _, masks = phase_parts(phase)
    return [from_flat_partner(part, mask) for part, mask in zip(parts, masks[1:])]


def place_in(facts_ref, phase):
    bits = [
        (facts_ref[0 if axis == "grp" else 1] // mask) % 2 * 2**number
        for number, (axis, mask) in enumerate(phase)
    ]
    return sum(bits)


def encoded(sums, rows_ref):
    count = sums.shape[0]
    high = sums.astype(jnp.bfloat16).astype(jnp.float32)
    low = (sums - high).astype(jnp.bfloat16).astype(jnp.float32)
    rows_ref[...] = jnp.zeros_like(rows_ref)
    rows_ref[0:count] = high
    rows_ref[count : 2 * count] = low
    return rows_ref[...].astype(jnp.bfloat16), high + low


def decoded(found_ref, count, rows_ref):
    rows_ref[...] = found_ref[found_ref.shape[0] - EXTRA :, :].astype(jnp.float32)
    return rows_ref[0:count] + rows_ref[count : 2 * count]


def pair_sum(values):
    while len(values) > 1:
        values = [values[i] + values[i + 1] for i in range(0, len(values), 2)]
    return values[0]


def other_half_body(
    facts_ref, dilated_ref, pointwise_ref, sums_ref, sent_ref, held_ref, rows_ref
):
    width, inner = pointwise_ref.shape
    sent_ref[width:, :], held_ref[...] = encoded(sums_ref[...], rows_ref)

    @pl.when(facts_ref[0] % 2 == 0)
    def _():
        sent_ref[:width, :inner] = dilated_ref[:, 2 * inner :].astype(jnp.bfloat16)
        sent_ref[:width, inner:] = pointwise_ref[...].astype(jnp.bfloat16)

    @pl.when(facts_ref[0] % 2 == 1)
    def _():
        sent_ref[:width, :] = dilated_ref[:, : 2 * inner].astype(jnp.bfloat16)


def other_half(facts, dilated, pointwise, sums):
    width, inner = pointwise.shape
    return kernel_call(
        other_half_body,
        "other_half",
        (facts, dilated, pointwise, sums),
        [SMEM, VMEM, VMEM, VMEM],
        [shape((width + EXTRA, 2 * inner), jnp.bfloat16), shape(sums.shape, jnp.float32)],
        [VMEM, VMEM],
        [pltpu.VMEM((EXTRA, 2 * inner), jnp.float32)],
        flops=2 * width * inner,
        bytes_moved=12 * width * inner,
        grant=10 << 20,
    )


def part_rows(mine, part, rows):
    return pl.ds(pl.multiple_of(jnp.bitwise_xor(mine, part) * rows, rows), rows)


def own_half_body(
    phase, facts_ref, dilated_ref, pointwise_ref, sums_ref, other_ref, total_ref, *refs
):
    part_refs, rows_ref = refs[:-1], refs[-1]
    inner = pointwise_ref.shape[1]
    rows = part_refs[0].shape[0]
    mine = place_in(facts_ref, phase)
    sums = sums_ref[...] + decoded(other_ref, sums_ref.shape[0], rows_ref)
    extra, total_ref[...] = encoded(sums, rows_ref)
    for part_ref in part_refs[1:]:
        part_ref[rows:, :] = extra

    def write(low, high):
        for part, part_ref in enumerate(part_refs):
            here = part_rows(mine, part, rows)
            for piece, lanes in ((low, slice(0, inner)), (high, slice(inner, 2 * inner))):
                value = piece(here) + other_ref[here, lanes].astype(jnp.float32)
                part_ref[:rows, lanes] = value.astype(part_ref.dtype)

    @pl.when(facts_ref[0] % 2 == 0)
    def _():
        write(
            lambda here: dilated_ref[here, :inner],
            lambda here: dilated_ref[here, inner : 2 * inner],
        )

    @pl.when(facts_ref[0] % 2 == 1)
    def _():
        write(lambda here: dilated_ref[here, 2 * inner :], lambda here: pointwise_ref[here, :])


def part_shapes(sums, rows, columns, phase):
    parts = 2 ** len(phase)
    rows //= parts
    return [
        shape(sums.shape, jnp.float32),
        shape((rows, columns), jnp.float32),
        *[shape((rows + EXTRA, columns), jnp.bfloat16)] * (parts - 1),
    ]


def own_half(facts, dilated, pointwise, sums, other, phase):
    width, inner = pointwise.shape
    outputs = part_shapes(sums, width, 2 * inner, phase)
    return kernel_call(
        functools.partial(own_half_body, phase),
        "own_half",
        (facts, dilated, pointwise, sums, other),
        [SMEM] + [VMEM] * 4,
        outputs,
        [VMEM] * len(outputs),
        [pltpu.VMEM((EXTRA, 2 * inner), jnp.float32)],
        flops=2 * width * inner,
        bytes_moved=20 * width * inner,
        grant=12 << 20,
    )


def next_parts_body(count, phase, facts_ref, kept_ref, sums_ref, *refs):
    found_refs, total_ref, part_refs, rows_ref = (
        refs[:count],
        refs[count],
        refs[count + 1 : -1],
        refs[-1],
    )
    sums = pair_sum(
        [sums_ref[...]] + [decoded(ref, sums_ref.shape[0], rows_ref) for ref in found_refs]
    )
    total_ref[...] = sums
    rows = part_refs[0].shape[0]
    if phase:
        mine = place_in(facts_ref, phase)
        extra, total_ref[...] = encoded(sums, rows_ref)
        for part_ref in part_refs[1:]:
            part_ref[rows:, :] = extra
    for part, part_ref in enumerate(part_refs):
        here = part_rows(mine, part, rows) if phase else slice(0, rows)
        value = kept_ref[here, :]
        for found_ref in found_refs:
            value = value + found_ref[here, :].astype(jnp.float32)
        part_ref[:rows, :] = value.astype(part_ref.dtype)


def plain_parts(kept, sums, found, phase):
    rows, count = kept.shape[0], sums.shape[0]
    totals = [sums]
    for block in found:
        kept = kept + block[:rows].astype(jnp.float32)
        tail = block[rows:].astype(jnp.float32)
        totals.append(tail[:count] + tail[count : 2 * count])
    sums = pair_sum(totals)
    if not phase:
        return [sums, kept.astype(jnp.bfloat16)]
    high = lax.reduce_precision(sums, 8, 7)
    low = lax.reduce_precision(sums - high, 8, 7)
    rest = jnp.zeros((EXTRA - 2 * count, sums.shape[1]), jnp.float32)
    extra, sums = jnp.concatenate([high, low, rest]).astype(jnp.bfloat16), high + low
    parts = 2 ** len(phase)
    mine, rows = phase_place(phase), rows // parts
    slices = [
        lax.dynamic_slice_in_dim(kept, jnp.bitwise_xor(mine, part) * rows, rows)
        for part in range(parts)
    ]
    return [sums, slices[0]] + [
        jnp.concatenate([block.astype(jnp.bfloat16), extra]) for block in slices[1:]
    ]


def next_parts(facts, kept, sums, found, phase):
    rows, columns = kept.shape
    if rows // 2 ** len(phase) % 16:
        return plain_parts(kept, sums, found, phase)
    outputs = part_shapes(sums, rows, columns, phase)
    if not phase:
        outputs = [outputs[0], shape((rows, columns), jnp.bfloat16)]
    return kernel_call(
        functools.partial(next_parts_body, len(found), phase),
        "next_parts",
        (facts, kept, sums, *found),
        [SMEM] + [VMEM] * (2 + len(found)),
        outputs,
        [VMEM] * len(outputs),
        [pltpu.VMEM((EXTRA, columns), jnp.float32)],
        flops=4 * rows * columns,
        bytes_moved=16 * rows * columns,
    )


def gather_parts(buffer, phase):
    _, masks = phase_parts(phase)
    return [buffer] + [from_flat_partner(buffer, mask) for mask in masks[1:]]


def in_order(found, owners):
    parts = len(found)
    orders = [
        jnp.concatenate([found[place ^ own] for place in range(parts)], axis=0)
        for own in range(parts)
    ]
    result = orders[0]
    for own in range(1, parts):
        result = jnp.where(owners[own], orders[own], result)
    return result


def finish_body(facts_ref, mine_ref, other_ref, dilated_ref, pointwise_ref):
    inner = dilated_ref.shape[2]

    def write(low_ref, high_ref):
        dilated_ref[0] = low_ref[:, :inner].astype(jnp.float32)
        dilated_ref[1] = low_ref[:, inner:].astype(jnp.float32)
        dilated_ref[2] = high_ref[:, :inner].astype(jnp.float32)
        pointwise_ref[...] = high_ref[:, inner:].astype(jnp.float32).T

    upper = facts_ref[0] % 2

    @pl.when(upper == 0)
    def _():
        write(mine_ref, other_ref)

    @pl.when(upper == 1)
    def _():
        write(other_ref, mine_ref)


def finish_weights(facts, mine, other):
    width, both = mine.shape
    inner = both // 2
    return kernel_call(
        finish_body,
        "finish_weights",
        (facts, mine, other),
        [SMEM, VMEM, VMEM],
        [shape((3, width, inner), jnp.float32), shape((inner, width), jnp.float32)],
        [VMEM, VMEM],
        flops=width * both,
        bytes_moved=12 * width * both,
        grant=16 << 20,
    )


def per_device(
    signal,
    entry_gain,
    entry_shift,
    dilated_kernel,
    middle_gain,
    middle_shift,
    pointwise_kernel,
    pointwise_bias,
    lengths,
    assignment,
    cotangent,
):
    seq_count = lax.axis_size("seq")
    windows, segment, width = signal.shape
    inner = pointwise_kernel.shape[0]
    slots = windows // seq_count
    rows = segment // 2
    pieces = 2 * slots
    places = jnp.stack([lax.axis_index("grp"), lax.axis_index("seq"), jnp.int32(seq_count)])
    facts = jnp.concatenate([places.astype(jnp.int32), assignment[0], lengths])
    entry_params = jnp.stack([entry_gain, entry_shift, pointwise_bias])
    middle_params = jnp.stack([middle_gain, middle_shift])

    outgoing, first_chosen, entry_local = pool(facts, signal, slots)
    arrived = lax.all_to_all(outgoing, "seq", split_axis=0, concat_axis=0, tiled=True)
    entry_moments = total_moments(entry_local)

    kernel_low = dilated_kernel.astype(jnp.bfloat16)
    wide_kernel = jnp.concatenate([kernel_low[tap] for tap in range(3)], axis=1)
    pointwise_low = pointwise_kernel.astype(jnp.bfloat16)
    back_kernel = jnp.swapaxes(kernel_low, 1, 2).reshape(3 * inner, width)
    grad_block, grad_middle, bias_part = prepare(
        facts, cotangent, pointwise_low, slots, windows
    )
    phases = square_phases()
    owners = [
        [phase_place(phase) == own for own in range(2 ** len(phase))] for phase in phases
    ]
    first_axis, first_mask = exchange_steps()[0]
    upper = bit_of(first_axis, first_mask) == 1
    (
        arrived,
        grad_block,
        grad_middle,
        wide_kernel,
        back_kernel,
        pointwise_low,
        owners,
        upper,
        middle_params,
        facts,
    ) = lax.optimization_barrier(
        (
            arrived,
            grad_block,
            grad_middle,
            wide_kernel,
            back_kernel,
            pointwise_low,
            owners,
            upper,
            middle_params,
            facts,
        )
    )

    act, act_border = activate(facts, arrived, entry_moments, entry_params, slots, windows)
    act_border = from_partner(act_border, "seq", 1)
    dilated, held_moments = convolve(facts, act, wide_kernel, slots, windows)
    strip, middle_moments = join(
        facts, dilated, act_border, wide_kernel, held_moments, slots, windows
    )
    slopes = []
    for number, (axis, mask) in enumerate(exchange_steps()):
        other = from_partner(middle_moments, axis, mask)
        if number and len(slopes) < pieces:
            tied, middle_moments = lax.optimization_barrier((arrived, middle_moments))
            found = entry_slope(
                facts, tied, entry_moments, entry_params, slots, windows, len(slopes)
            )
            other, found = lax.optimization_barrier((other, found))
            slopes.append(found)
        middle_moments = jnp.concatenate(
            merged(
                (middle_moments[0:1], middle_moments[1:2], middle_moments[2:3]),
                (other[0:1], other[1:2], other[2:3]),
            ),
            axis=0,
        )
    while len(slopes) < pieces:
        slopes.append(
            entry_slope(facts, arrived, entry_moments, entry_params, slots, windows, len(slopes))
        )
    middle_act, middle_slope, middle_norm, middle_sums = middle(
        facts,
        dilated,
        strip,
        middle_moments,
        middle_params,
        grad_middle.reshape(pieces, HALF_WINDOW_ROWS, inner),
        slots,
        windows,
    )
    flat_act = middle_act.reshape(-1, inner)
    for number, (axis, mask) in enumerate(exchange_steps()):
        other = from_partner(middle_sums, axis, mask)
        if number == 1:
            tied, middle_sums = lax.optimization_barrier((flat_act, middle_sums))
            pointwise_part = jnp.einsum(
                "rd,rf->df", grad_block, tied, preferred_element_type=jnp.float32
            )
            other, pointwise_part = lax.optimization_barrier((other, pointwise_part))
        middle_sums = middle_sums + other
    padded, grad_border = middle_grad(
        facts, middle_slope, middle_norm, middle_moments, middle_params, middle_sums, slots, windows
    )
    grad_border = from_partner(grad_border, "seq", 1)
    block_pieces = grad_block.reshape(pieces, HALF_WINDOW_ROWS, width)
    sent, taps, entry_part = [], None, jnp.concatenate([jnp.zeros_like(bias_part)] * 2)
    returned = []

    def send_back(block):
        return lax.all_to_all(block, "seq", split_axis=0, concat_axis=0, tiled=True)

    for slot in range(slots):
        block, taps, part = entry_grad(
            facts, padded, grad_border, back_kernel, slopes[2 * slot : 2 * slot + 2],
            arrived, block_pieces, entry_moments, entry_params, taps, slots, windows, slot,
        )
        sent.append(block)
        entry_part = entry_part + part
    entry_sums = jnp.concatenate([entry_part, bias_part])
    tied = lax.optimization_barrier((*sent, entry_sums))
    sent, entry_sums = list(tied[:-1]), tied[-1]
    returned = [send_back(sent[0])]
    dilated_part = jnp.einsum("hrc,hrf->cf", act, taps, preferred_element_type=jnp.float32)
    other, entry_sums = other_half(facts, dilated_part, pointwise_part, entry_sums)
    other = from_partner(other, first_axis, first_mask)
    entry_sums, *parts = own_half(
        facts, dilated_part, pointwise_part, entry_sums, other, phases[0]
    )
    for held, phase in zip(phases, phases[1:] + [[]]):
        found = exchange_parts(parts[1:], held)
        entry_sums, *parts = next_parts(facts, parts[0], entry_sums, found, phase)
    buffer, signal_gradient, activations = parts[0], None, None
    for number, phase in reversed(list(enumerate(phases))):
        found = gather_parts(buffer, phase)
        if number == 0:
            signal_gradient = unpool(
                facts, returned[0], outgoing, first_chosen, entry_moments, entry_sums,
                entry_params, slots, 0, None,
            )
            activations = output_rows(
                facts, flat_act, pointwise_low, arrived, entry_params, slots, windows
            )
            tied = lax.optimization_barrier((signal_gradient, activations, *found))
            signal_gradient, activations, found = tied[0], tied[1], tied[2:]
        buffer = in_order(found, owners[number])
        if number == len(phases) - 1:
            buffer, flat_act, entry_sums, *later = lax.optimization_barrier(
                (buffer, flat_act, entry_sums, *sent[1:])
            )
            returned += [send_back(block) for block in later]
    other = from_partner(buffer, first_axis, first_mask)
    dilated_kernel_gradient, pointwise_kernel_gradient = finish_weights(facts, buffer, other)
    for slot in range(1, slots):
        signal_gradient = unpool(
            facts, returned[slot], outgoing, first_chosen, entry_moments, entry_sums,
            entry_params, slots, slot, signal_gradient,
        )
    return (
        activations,
        signal_gradient,
        entry_sums[0],
        entry_sums[1],
        dilated_kernel_gradient,
        middle_sums[0],
        middle_sums[1],
        pointwise_kernel_gradient,
        entry_sums[2],
    )


def solution(mesh):
    return jax.shard_map(
        per_device,
        mesh=mesh,
        in_specs=(
            P("grp", "seq", None),
            P(),
            P(),
            P(),
            P(),
            P(),
            P(),
            P(),
            P(),
            P("grp", None),
            P(("grp", "seq"), None),
        ),
        out_specs=(
            P(("grp", "seq"), None),
            P("grp", "seq", None),
            P(),
            P(),
            P(),
            P(),
            P(),
            P(),
            P(),
        ),
        check_vma=False,
    )
```

```python
import functools
import math

import jax
import jax.numpy as jnp
from jax import lax
from jax.experimental import pallas as pl
from jax.experimental.pallas import tpu as pltpu
from jax.sharding import PartitionSpec as P

DILATION_STEP = 38
WINDOW_SPAN = 1024
HALF_WINDOW_ROWS = 512


EPSILON = 0.001

LANES = 128
BORDER = 48
STRIP = 64
PAD = 40
PADDED_ROWS = HALF_WINDOW_ROWS + 2 * PAD
EXTRA = 8
GELU_SLOPE = math.sqrt(2.0 / math.pi)
GELU_CUBE = 0.044715

VMEM = pl.BlockSpec(memory_space=pltpu.VMEM)
SMEM = pl.BlockSpec(memory_space=pltpu.SMEM)
HBM = pl.BlockSpec(memory_space=pltpu.HBM)


def from_partner(block, axis, mask):
    count = lax.axis_size(axis)
    return lax.ppermute(block, axis, [(place, place ^ mask) for place in range(count)])


def exchange_steps():
    steps = []
    for axis in ("grp", "seq"):
        mask = 1
        while mask < lax.axis_size(axis):
            steps.append((axis, mask))
            mask *= 2
    return steps


def total(values):
    for axis, mask in exchange_steps():
        values = values + from_partner(values, axis, mask)
    return values


def merged(left, right):
    left_sum, left_spread, left_count = left
    right_sum, right_spread, right_count = right
    gap = left_sum / jnp.maximum(left_count, 1.0) - right_sum / jnp.maximum(right_count, 1.0)
    weight = left_count * right_count / jnp.maximum(left_count + right_count, 1.0)
    return (
        left_sum + right_sum,
        left_spread + right_spread + gap * gap * weight,
        left_count + right_count,
    )


def total_moments(packed, others):
    steps = exchange_steps()
    for number, (axis, mask) in enumerate(steps):
        if number == len(steps) - 1:
            packed, *others = lax.optimization_barrier((packed, *others))
        other = from_partner(packed, axis, mask)
        packed = jnp.concatenate(
            merged(
                (packed[0:1], packed[1:2], packed[2:3]), (other[0:1], other[1:2], other[2:3])
            ),
            axis=0,
        )
    return packed, others


class Facts:
    def __init__(self, ref, windows, slots):
        self.ref, self.windows, self.slots = ref, windows, slots

    def slot_window(self, slot):
        upper = (2 * self.ref[1]) // self.ref[2]
        target = jnp.bitwise_xor(slot // self.slots, upper)
        return self.ref[3 + target * self.slots + slot % self.slots]

    def length(self, window):
        return self.ref[3 + self.windows + self.ref[0] * self.windows + window]

    def slot_count(self, slot, rows):
        return jnp.clip(self.length(self.slot_window(slot)) - self.ref[1] * rows, 0, rows)

    def half_limit(self, slot, half):
        place = jnp.bitwise_xor(self.ref[1], half)
        window = self.ref[3 + place * self.slots + slot]
        return jnp.clip(self.length(window) - half * HALF_WINDOW_ROWS, 0, HALF_WINDOW_ROWS)

    def row_count(self):
        start = 3 + self.windows
        count = self.ref.shape[0] - start
        added = lax.fori_loop(0, count, lambda i, held: held + self.ref[start + i], jnp.int32(0))
        return added.astype(jnp.float32)


def kernel_call(body, name, inputs, specs, outputs, out_specs, scratch=(), flops=0, bytes_moved=0, grant=8 << 20):
    return pl.pallas_call(
        body,
        in_specs=specs,
        out_specs=out_specs,
        out_shape=outputs,
        scratch_shapes=list(scratch),
        compiler_params=pltpu.CompilerParams(vmem_limit_bytes=grant),
        cost_estimate=pl.CostEstimate(
            flops=flops, bytes_accessed=bytes_moved, transcendentals=0
        ),
        name=name,
    )(*inputs)


def shape(dims, dtype):
    return jax.ShapeDtypeStruct(dims, dtype)


def in_hbm(array):
    return pltpu.with_memory_space_constraint(array, pltpu.HBM)


def column_slices(width):
    return [slice(start, start + LANES) for start in range(0, width, LANES)]


def bin_copy(facts, signal_ref, held, arrivals, place, column):
    return pltpu.make_async_copy(
        signal_ref.at[facts.slot_window(place), :, pl.ds(column * LANES, LANES)],
        held.at[place, column],
        arrivals.at[place, column],
    )


def begin_bins(facts, signal_ref, held, arrivals):
    windows, columns = held.shape[:2]

    def begin(place, carry):
        for column in range(columns):
            bin_copy(facts, signal_ref, held, arrivals, place, column).start()
        return carry

    lax.fori_loop(0, windows, begin, 0)


def bins_of(facts, signal_ref, held, arrivals, place, rows):
    columns = held.shape[1]
    for column in range(columns):
        bin_copy(facts, signal_ref, held, arrivals, place, column).wait()
    return [
        (
            lanes,
            held[place, column, pl.ds(0, rows, stride=2), :],
            held[place, column, pl.ds(1, rows, stride=2), :],
        )
        for column, lanes in enumerate(column_slices(columns * LANES))
    ]


def finish_copies(copy_of, count):
    def finish(place, carry):
        copy_of(place).wait()
        return carry

    lax.fori_loop(0, count, finish, 0)


def pool_body(
    slots, facts_ref, signal_ref, pooled_ref, moments_ref, held, low, blocks, arrivals, departures
):
    windows, columns = held.shape[:2]
    rows = low.shape[1]
    facts = Facts(facts_ref, windows, slots)

    def departure(place):
        return pltpu.make_async_copy(low.at[place], pooled_ref.at[place], departures.at[place])

    begin_bins(facts, signal_ref, held, arrivals)
    moments_ref[...] = jnp.zeros_like(moments_ref)

    def work(place, carry):
        count = facts.slot_count(place, rows)
        inside = lax.broadcasted_iota(jnp.int32, (rows, LANES), 0) < count
        for lanes, first_bin, second_bin in bins_of(
            facts, signal_ref, held, arrivals, place, rows
        ):
            pooled = jnp.where(inside, jnp.maximum(first_bin, second_bin), 0.0)
            pooled = pooled.astype(jnp.bfloat16)
            low[place, :, lanes] = pooled
            found = block_moments(pooled.astype(jnp.float32), inside, count.astype(jnp.float32))
            blocks[place, 0:1, lanes] = found[0]
            blocks[place, 1:2, lanes] = found[1]
        departure(place).start()
        return carry

    lax.fori_loop(0, windows, work, 0)

    def join_blocks(place, carry):
        count = jnp.broadcast_to(
            facts.slot_count(place, rows).astype(jnp.float32), (1, columns * LANES)
        )
        held_moments = (moments_ref[0:1], moments_ref[1:2], moments_ref[2:3])
        moments_ref[0:1], moments_ref[1:2], moments_ref[2:3] = merged(
            held_moments, (blocks[place, 0:1], blocks[place, 1:2], count)
        )
        return carry

    lax.fori_loop(0, windows, join_blocks, 0)
    finish_copies(departure, windows)


def pool(facts, signal, slots):
    windows, segment, width = signal.shape
    rows, columns = segment // 2, width // LANES
    block = (windows, rows, width)
    return kernel_call(
        functools.partial(pool_body, slots),
        "pool",
        (facts, in_hbm(signal)),
        [SMEM, HBM],
        [pltpu.HBM(block, jnp.bfloat16), shape((3, width), jnp.float32)],
        [HBM, VMEM],
        [
            pltpu.VMEM((windows, columns, segment, LANES), jnp.float32),
            pltpu.VMEM(block, jnp.bfloat16),
            pltpu.VMEM((windows, 2, width), jnp.float32),
            pltpu.SemaphoreType.DMA((windows, columns)),
            pltpu.SemaphoreType.DMA((windows,)),
        ],
        flops=10 * windows * rows * width,
        bytes_moved=windows * rows * width * 10,
        grant=24 << 20,
    )


def marks_body(slots, facts_ref, signal_ref, first_ref, held, mark, arrivals, departures):
    windows = held.shape[0]
    rows = mark.shape[1]
    facts = Facts(facts_ref, windows, slots)

    def departure(place):
        return pltpu.make_async_copy(mark.at[place], first_ref.at[place], departures.at[place])

    begin_bins(facts, signal_ref, held, arrivals)

    def work(place, carry):
        for lanes, first_bin, second_bin in bins_of(
            facts, signal_ref, held, arrivals, place, rows
        ):
            mark[place, :, lanes] = jnp.where(first_bin >= second_bin, 1.0, 0.0).astype(
                jnp.bfloat16
            )
        departure(place).start()
        return carry

    lax.fori_loop(0, windows, work, 0)
    finish_copies(departure, windows)


def first_marks(facts, signal, slots):
    windows, segment, width = signal.shape
    rows, columns = segment // 2, width // LANES
    block = (windows, rows, width)
    return kernel_call(
        functools.partial(marks_body, slots),
        "first_marks",
        (facts, in_hbm(signal)),
        [SMEM, HBM],
        pltpu.HBM(block, jnp.bfloat16),
        HBM,
        [
            pltpu.VMEM((windows, columns, segment, LANES), jnp.float32),
            pltpu.VMEM(block, jnp.bfloat16),
            pltpu.SemaphoreType.DMA((windows, columns)),
            pltpu.SemaphoreType.DMA((windows,)),
        ],
        flops=3 * windows * rows * width,
        bytes_moved=windows * rows * width * 10,
        grant=24 << 20,
    )


def unpool_body(
    slots, slot, windows, facts_ref, returned_ref, pooled_ref, first_ref, moments_ref, sums_ref,
    params_ref, *refs,
):
    out_ref, back, low, mark, held, arrivals, departures = refs[-7:]
    targets, rows, width = back.shape
    columns = held.shape[1]
    facts = Facts(facts_ref, windows, slots)

    def arrival(target):
        place = target * slots + slot
        return [
            pltpu.make_async_copy(returned_ref.at[target], back.at[target], arrivals.at[target, 0]),
            pltpu.make_async_copy(pooled_ref.at[place], low.at[target], arrivals.at[target, 1]),
            pltpu.make_async_copy(first_ref.at[place], mark.at[target], arrivals.at[target, 2]),
        ]

    def departure(target, column):
        window = facts.slot_window(target * slots + slot)
        return pltpu.make_async_copy(
            held.at[target, column],
            out_ref.at[window, :, pl.ds(column * LANES, LANES)],
            departures.at[target, column],
        )

    def begin(target, carry):
        for copy in arrival(target):
            copy.start()
        return carry

    lax.fori_loop(0, targets, begin, 0)
    rows_total = facts.row_count()
    centre = moments_ref[0:1] / rows_total
    scale = lax.rsqrt(moments_ref[1:2] / rows_total + EPSILON)
    factor = params_ref[0:1] * scale / rows_total
    level = factor * sums_ref[1:2]
    tilt = factor * scale * sums_ref[0:1]

    def work(target, carry):
        for copy in arrival(target):
            copy.wait()
        inside = lax.broadcasted_iota(jnp.int32, (rows, LANES), 0) < facts.slot_count(
            target * slots + slot, rows
        )
        for column, lanes in enumerate(column_slices(width)):
            centred = low[target, :, lanes].astype(jnp.float32) - centre[:, lanes]
            gradient = back[target, :, lanes].astype(jnp.float32) - (
                level[:, lanes] + centred * tilt[:, lanes]
            )
            gradient = jnp.where(inside, gradient, 0.0).astype(jnp.bfloat16).astype(jnp.float32)
            first = gradient * mark[target, :, lanes].astype(jnp.float32)
            held[target, column, pl.ds(0, rows, stride=2), :] = first
            held[target, column, pl.ds(1, rows, stride=2), :] = gradient - first
        for column in range(columns):
            departure(target, column).start()
        return carry

    lax.fori_loop(0, targets, work, 0)

    def finish(target, carry):
        for column in range(columns):
            departure(target, column).wait()
        return carry

    lax.fori_loop(0, targets, finish, 0)


def unpool(facts, returned, pooled, first, moments, sums, params, slots, slot, held_output):
    targets, rows, width = returned.shape
    windows, columns = targets * slots, width // LANES
    inputs = [facts, in_hbm(returned), in_hbm(pooled), in_hbm(first), moments, sums, params]
    specs = [SMEM, HBM, HBM, HBM, VMEM, VMEM, VMEM]
    aliases = {}
    if held_output is not None:
        aliases = {len(inputs): 0}
        inputs.append(in_hbm(held_output))
        specs.append(HBM)
    block = (targets, rows, width)
    return pl.pallas_call(
        functools.partial(unpool_body, slots, slot, windows),
        in_specs=specs,
        out_specs=HBM,
        out_shape=pltpu.HBM((windows, 2 * rows, width), jnp.float32),
        input_output_aliases=aliases,
        scratch_shapes=[
            pltpu.VMEM(block, jnp.bfloat16),
            pltpu.VMEM(block, jnp.bfloat16),
            pltpu.VMEM(block, jnp.bfloat16),
            pltpu.VMEM((targets, columns, 2 * rows, LANES), jnp.float32),
            pltpu.SemaphoreType.DMA((targets, 3)),
            pltpu.SemaphoreType.DMA((targets, columns)),
        ],
        compiler_params=pltpu.CompilerParams(vmem_limit_bytes=16 << 20),
        cost_estimate=pl.CostEstimate(
            flops=10 * targets * rows * width,
            bytes_accessed=targets * rows * width * 14,
            transcendentals=0,
        ),
        name="unpool",
    )(*inputs)


def prepare_body(slots, windows, facts_ref, cot_ref, weight_ref, low_ref, middle_ref, bias_ref):
    step = pl.program_id(0)
    rows = cot_ref.shape[0]
    facts = Facts(facts_ref, windows, slots)
    first_row = step * rows
    piece = first_row // HALF_WINDOW_ROWS
    limit = facts.half_limit(piece // 2, piece % 2) - first_row % HALF_WINDOW_ROWS

    @pl.when(step == 0)
    def _():
        bias_ref[...] = jnp.zeros_like(bias_ref)

    inside = lax.broadcasted_iota(jnp.int32, (rows, 1), 0) < limit
    block = jnp.where(inside, cot_ref[...], 0.0)
    bias_ref[...] = bias_ref[...] + jnp.sum(block, axis=0, keepdims=True)
    low = block.astype(jnp.bfloat16)
    low_ref[...] = low
    middle_ref[...] = lax.dot_general(
        low, weight_ref[...], (((1,), (1,)), ((), ())), preferred_element_type=jnp.float32
    )


def prepare(facts, cotangent, weight, slots, windows):
    total_rows, width = cotangent.shape
    inner = weight.shape[0]
    rows = 256
    return pl.pallas_call(
        functools.partial(prepare_body, slots, windows),
        grid=(total_rows // rows,),
        in_specs=[
            SMEM,
            pl.BlockSpec((rows, width), lambda i: (i, 0)),
            pl.BlockSpec((inner, width), lambda i: (0, 0)),
        ],
        out_specs=[
            pl.BlockSpec((rows, width), lambda i: (i, 0)),
            pl.BlockSpec((rows, inner), lambda i: (i, 0)),
            pl.BlockSpec((1, width), lambda i: (0, 0)),
        ],
        out_shape=[
            shape((total_rows, width), jnp.bfloat16),
            shape((total_rows, inner), jnp.float32),
            shape((1, width), jnp.float32),
        ],
        compiler_params=pltpu.CompilerParams(vmem_limit_bytes=16 << 20),
        cost_estimate=pl.CostEstimate(
            flops=2 * total_rows * width * inner,
            bytes_accessed=total_rows * (width * 6 + inner * 4),
            transcendentals=0,
        ),
        name="prepare_cotangent",
    )(facts, cotangent, weight)


def weights_body(dilated_ref, pointwise_ref, wide_ref, back_ref, low_ref):
    inner = dilated_ref.shape[2]
    for number, tap in enumerate((0, 2, 1)):
        values = dilated_ref[tap]
        wide_ref[:, tap * inner : (tap + 1) * inner] = values.astype(jnp.bfloat16)
        back_ref[number * inner : (number + 1) * inner, :] = values.T.astype(jnp.bfloat16)
    low_ref[...] = pointwise_ref[...].astype(jnp.bfloat16)


def prepare_weights(dilated_kernel, pointwise_kernel):
    taps, width, inner = dilated_kernel.shape
    return kernel_call(
        weights_body,
        "prepare_weights",
        (dilated_kernel, pointwise_kernel),
        [VMEM, VMEM],
        [
            shape((width, taps * inner), jnp.bfloat16),
            shape((taps * inner, width), jnp.bfloat16),
            shape(pointwise_kernel.shape, jnp.bfloat16),
        ],
        [VMEM, VMEM, VMEM],
        flops=4 * width * inner,
        bytes_moved=30 * width * inner,
        grant=16 << 20,
    )


def norm_terms(moments_ref, params_ref, rows_total):
    centre = moments_ref[0:1] / rows_total
    scale = lax.rsqrt(moments_ref[1:2] / rows_total + EPSILON)
    return centre, scale, params_ref[0:1] * scale, params_ref[1:2]


def half_terms(moments_ref, params_ref, rows_total):
    centre, _, slope, offset = norm_terms(moments_ref, params_ref, rows_total)
    return 0.5 * slope, 0.5 * (offset - centre * slope)


def bent(half):
    square = half * half
    return jnp.tanh(half * (2.0 * GELU_SLOPE + (8.0 * GELU_SLOPE * GELU_CUBE) * square)), square


def gelu_slope(half, bend, square):
    inner = GELU_SLOPE + (12.0 * GELU_SLOPE * GELU_CUBE) * square
    return (0.5 + 0.5 * bend) + (half - half * bend * bend) * inner


def activate_body(
    slots, windows, facts_ref, arrived_ref, moments_ref, params_ref, act_ref, border_ref
):
    blocks, rows, width = arrived_ref.shape
    facts = Facts(facts_ref, windows, slots)
    per_half = HALF_WINDOW_ROWS // rows
    slope, offset = half_terms(moments_ref, params_ref, facts.row_count())

    def work(block, carry):
        source, slot = block // slots, block % slots
        half, start = source // per_half, (source % per_half) * rows
        inside = lax.broadcasted_iota(jnp.int32, (rows, 1), 0) < (
            facts.half_limit(slot, half) - start
        )
        for lanes in column_slices(width):
            values = arrived_ref[block, :, lanes].astype(jnp.float32)
            half_pre = values * slope[:, lanes] + offset[:, lanes]
            bend, _ = bent(half_pre)
            act = jnp.where(inside, half_pre + half_pre * bend, 0.0)
            act_ref[slot * 2 + half, pl.ds(pl.multiple_of(start, rows), rows), lanes] = act.astype(
                jnp.bfloat16
            )
        return carry

    lax.fori_loop(0, blocks, work, 0)
    for piece in range(act_ref.shape[0]):
        start = 0 if piece % 2 else HALF_WINDOW_ROWS - BORDER
        border_ref[piece] = act_ref[piece, start : start + BORDER]


def activate(facts, arrived, moments, params, slots, windows):
    width = arrived.shape[2]
    return kernel_call(
        functools.partial(activate_body, slots, windows),
        "activate",
        (facts, arrived, moments, params),
        [SMEM, VMEM, VMEM, VMEM],
        [
            shape((2 * slots, HALF_WINDOW_ROWS, width), jnp.bfloat16),
            shape((2 * slots, BORDER, width), jnp.bfloat16),
        ],
        [VMEM, VMEM],
        flops=20 * arrived.size,
        bytes_moved=4 * arrived.size,
    )


def slope_body(slots, windows, piece, facts_ref, arrived_ref, moments_ref, params_ref, slope_ref):
    blocks, rows, width = arrived_ref.shape
    facts = Facts(facts_ref, windows, slots)
    per_half = HALF_WINDOW_ROWS // rows
    slope, offset = half_terms(moments_ref, params_ref, facts.row_count())
    slot, half = piece // 2, piece % 2
    limit = facts.half_limit(slot, half)

    def work(part, carry):
        start = part * rows
        inside = lax.broadcasted_iota(jnp.int32, (rows, 1), 0) < limit - start
        for lanes in column_slices(width):
            values = arrived_ref[(half * per_half + part) * slots + slot, :, lanes]
            half_pre = values.astype(jnp.float32) * slope[:, lanes] + offset[:, lanes]
            found = jnp.where(inside, gelu_slope(half_pre, *bent(half_pre)), 0.0)
            slope_ref[pl.ds(pl.multiple_of(start, rows), rows), lanes] = found
        return carry

    lax.fori_loop(0, per_half, work, 0)


def entry_slope(facts, arrived, moments, params, slots, windows, piece):
    width = arrived.shape[2]
    return kernel_call(
        functools.partial(slope_body, slots, windows, piece),
        "entry_slope",
        (facts, arrived, moments, params),
        [SMEM, VMEM, VMEM, VMEM],
        shape((HALF_WINDOW_ROWS, width), jnp.float32),
        VMEM,
        flops=25 * HALF_WINDOW_ROWS * width,
        bytes_moved=6 * HALF_WINDOW_ROWS * width,
    )


def block_moments(values, inside, count):
    block_sum = jnp.sum(jnp.where(inside, values, 0.0), axis=0, keepdims=True)
    deviation = jnp.where(inside, values - block_sum / jnp.maximum(count, 1.0), 0.0)
    return block_sum, jnp.sum(deviation * deviation, axis=0, keepdims=True), count


def convolve_body(slots, windows, facts_ref, act_ref, weight_ref, out_ref, moments_ref, wide):
    facts = Facts(facts_ref, windows, slots)
    pieces, rows, inner = out_ref.shape
    tiles = inner // LANES
    for tile in range(3 * tiles):
        wide[tile, 0:PAD] = jnp.zeros((PAD, LANES), jnp.float32)
        wide[tile, PAD + rows : PADDED_ROWS] = jnp.zeros((PAD, LANES), jnp.float32)
    moments_ref[...] = jnp.zeros_like(moments_ref)
    below, above = PAD - DILATION_STEP, PAD + DILATION_STEP

    def work(piece, carry):
        product = jnp.dot(act_ref[piece], weight_ref[...], preferred_element_type=jnp.float32)
        for tile, lanes in enumerate(column_slices(3 * inner)):
            wide[tile, PAD : PAD + rows] = product[:, lanes]
        half = piece % 2
        limit = facts.half_limit(piece // 2, half)
        start = half * STRIP
        row = lax.broadcasted_iota(jnp.int32, (rows, 1), 0)
        end = jnp.minimum(limit, rows - STRIP + start)
        inside = jnp.logical_and(row >= start, row < end)
        count = jnp.maximum(end - start, 0).astype(jnp.float32)
        for tile, lanes in enumerate(column_slices(inner)):
            out = (
                wide[tiles + tile, PAD : PAD + rows]
                + wide[tile, below : below + rows]
                + wide[2 * tiles + tile, above : above + rows]
            )
            out_ref[piece, :, lanes] = out
            held = (moments_ref[0:1, lanes], moments_ref[1:2, lanes], moments_ref[2:3, lanes])
            moments_ref[0:1, lanes], moments_ref[1:2, lanes], moments_ref[2:3, lanes] = merged(
                held, block_moments(out, inside, count)
            )
        return carry

    lax.fori_loop(0, pieces, work, 0)


def convolve(facts, act, weight, slots, windows):
    pieces, rows, width = act.shape
    inner = weight.shape[1] // 3
    return kernel_call(
        functools.partial(convolve_body, slots, windows),
        "convolve",
        (facts, act, weight),
        [SMEM, VMEM, VMEM],
        [shape((pieces, rows, inner), jnp.float32), shape((3, inner), jnp.float32)],
        [VMEM, VMEM],
        [pltpu.VMEM((3 * inner // LANES, PADDED_ROWS, LANES), jnp.float32)],
        flops=6 * pieces * rows * width * inner,
        bytes_moved=pieces * rows * (width * 2 + inner * 4),
    )


def join_body(
    slots, windows, facts_ref, out_ref, border_ref, weight_ref, held_ref, strip_ref, moments_ref,
    moved,
):
    facts = Facts(facts_ref, windows, slots)
    pieces, rows, inner = out_ref.shape
    found = (held_ref[0:1], held_ref[1:2], held_ref[2:3])
    gap = STRIP - DILATION_STEP
    skip = BORDER - DILATION_STEP
    for piece in range(pieces):
        half = piece % 2
        other = piece + 1 - 2 * half
        moved[...] = jnp.zeros_like(moved)
        if half == 0:
            moved[gap : gap + BORDER] = jnp.dot(
                border_ref[other], weight_ref[:, 2 * inner :], preferred_element_type=jnp.float32
            )
            strip = out_ref[piece, rows - STRIP : rows] + moved[0:STRIP]
        else:
            moved[0:BORDER] = jnp.dot(
                border_ref[other], weight_ref[:, :inner], preferred_element_type=jnp.float32
            )
            strip = out_ref[piece, 0:STRIP] + moved[skip : skip + STRIP]
        strip_ref[piece] = strip
        limit = facts.half_limit(piece // 2, half) - (1 - half) * (rows - STRIP)
        count = jnp.clip(limit, 0, STRIP)
        inside = lax.broadcasted_iota(jnp.int32, (STRIP, 1), 0) < count
        found = merged(found, block_moments(strip, inside, count.astype(jnp.float32)))
    for number, value in enumerate(found):
        moments_ref[number : number + 1] = jnp.broadcast_to(value, (1, inner))


def join(facts, out, border, weight, held, slots, windows):
    pieces, rows, inner = out.shape
    return kernel_call(
        functools.partial(join_body, slots, windows),
        "join_halves",
        (facts, out, border, weight, held),
        [SMEM, VMEM, VMEM, VMEM, VMEM],
        [shape((pieces, STRIP, inner), jnp.float32), shape((3, inner), jnp.float32)],
        [VMEM, VMEM],
        [pltpu.VMEM((2 * STRIP, inner), jnp.float32)],
        flops=2 * pieces * BORDER * border.shape[2] * inner,
        bytes_moved=pieces * STRIP * inner * 8,
    )


def middle_body(
    slots, windows, facts_ref, out_ref, strip_ref, moments_ref, params_ref, grad_ref,
    act_ref, slope_ref, norm_ref, sums_ref,
):
    facts = Facts(facts_ref, windows, slots)
    pieces, rows, inner = out_ref.shape
    centre, scale, _, _ = norm_terms(moments_ref, params_ref, facts.row_count())
    gain, offset = 0.5 * params_ref[0:1], 0.5 * params_ref[1:2]
    sums_ref[...] = jnp.zeros_like(sums_ref)

    def chunk(piece, start, values):
        size = values.shape[0]
        limit = facts.half_limit(piece // 2, piece % 2)
        inside = lax.broadcasted_iota(jnp.int32, (size, 1), 0) < limit - start
        here = pl.ds(start, size)
        for lanes in column_slices(inner):
            norm = (values[:, lanes] - centre[:, lanes]) * scale[:, lanes]
            half_pre = norm * gain[:, lanes] + offset[:, lanes]
            bend, square = bent(half_pre)
            act = jnp.where(inside, half_pre + half_pre * bend, 0.0)
            act_ref[piece, here, lanes] = act.astype(jnp.bfloat16)
            grad = grad_ref[piece, here, lanes] * gelu_slope(half_pre, bend, square)
            grad = jnp.where(inside, grad, 0.0)
            slope_ref[piece, here, lanes] = grad
            norm_ref[piece, here, lanes] = norm
            sums_ref[0:1, lanes] = sums_ref[0:1, lanes] + jnp.sum(
                grad * norm, axis=0, keepdims=True
            )
            sums_ref[1:2, lanes] = sums_ref[1:2, lanes] + jnp.sum(grad, axis=0, keepdims=True)

    size = 2 * STRIP
    steps = rows // size - 1

    def main(step, carry):
        piece = step // steps
        start = pl.multiple_of((step % steps + piece % 2) * size, size)
        chunk(piece, start, out_ref[piece, pl.ds(start, size), :])
        return carry

    lax.fori_loop(0, pieces * steps, main, 0)

    def edge(slot, carry):
        low, high = 2 * slot, 2 * slot + 1
        start = rows - size
        values = jnp.concatenate([out_ref[low, start : start + STRIP], strip_ref[low]], axis=0)
        chunk(low, start, values)
        chunk(high, 0, jnp.concatenate([strip_ref[high], out_ref[high, STRIP:size]], axis=0))
        return carry

    lax.fori_loop(0, slots, edge, 0)


def middle(facts, out, strip, moments, params, grad, slots, windows):
    dims = out.shape
    return kernel_call(
        functools.partial(middle_body, slots, windows),
        "middle_norm",
        (facts, out, strip, moments, params, grad),
        [SMEM] + [VMEM] * 5,
        [
            shape(dims, jnp.bfloat16),
            shape(dims, jnp.float32),
            shape(dims, jnp.float32),
            shape((2, dims[2]), jnp.float32),
        ],
        [VMEM] * 4,
        flops=40 * out.size,
        bytes_moved=18 * out.size,
    )


def middle_grad_body(
    slots, windows, facts_ref, grad_ref, norm_ref, moments_ref, params_ref, sums_ref,
    padded_ref, border_ref, centre_ref,
):
    facts = Facts(facts_ref, windows, slots)
    pieces, rows, inner = grad_ref.shape
    rows_total = facts.row_count()
    _, _, slope, _ = norm_terms(moments_ref, params_ref, rows_total)
    level, tilt = sums_ref[1:2] / rows_total, sums_ref[0:1] / rows_total
    tiles = inner // LANES
    for piece in range(pieces):
        for tile in range(tiles):
            padded_ref[piece, tile, 0:PAD] = jnp.zeros((PAD, LANES), jnp.float32)
            padded_ref[piece, tile, PAD + rows : PADDED_ROWS] = jnp.zeros(
                (PAD, LANES), jnp.float32
            )
    size = 2 * STRIP

    def work(step, carry):
        piece, part = step // (rows // size), step % (rows // size)
        start = pl.multiple_of(part * size, size)
        limit = facts.half_limit(piece // 2, piece % 2)
        inside = lax.broadcasted_iota(jnp.int32, (size, 1), 0) < limit - start
        for tile, lanes in enumerate(column_slices(inner)):
            norm = norm_ref[piece, pl.ds(start, size), lanes]
            grad = slope[:, lanes] * (
                grad_ref[piece, pl.ds(start, size), lanes]
                - (level[:, lanes] + norm * tilt[:, lanes])
            )
            low = jnp.where(inside, grad, 0.0).astype(jnp.bfloat16)
            centre_ref[piece, pl.ds(start, size), lanes] = low
            padded_ref[piece, tile, pl.ds(pl.multiple_of(start + PAD, 8), size), :] = low.astype(
                jnp.float32
            )
        return carry

    lax.fori_loop(0, pieces * (rows // size), work, 0)
    for piece in range(pieces):
        start = PAD + (0 if piece % 2 else rows - BORDER)
        for tile, lanes in enumerate(column_slices(inner)):
            border_ref[piece, :, lanes] = padded_ref[piece, tile, start : start + BORDER].astype(
                jnp.bfloat16
            )


def middle_grad(facts, grad, norm, moments, params, sums, slots, windows):
    pieces, _, inner = grad.shape
    return kernel_call(
        functools.partial(middle_grad_body, slots, windows),
        "middle_grad",
        (facts, grad, norm, moments, params, sums),
        [SMEM] + [VMEM] * 5,
        [
            shape((pieces, inner // LANES, PADDED_ROWS, LANES), jnp.float32),
            shape((pieces, BORDER, inner), jnp.bfloat16),
            shape(grad.shape, jnp.bfloat16),
        ],
        [VMEM, VMEM, VMEM],
        flops=8 * grad.size,
        bytes_moved=12 * grad.size,
    )


def output_body(
    slots, windows, facts_ref, act_ref, weight_ref, arrived_ref, params_ref, out_ref
):
    source, slot = pl.program_id(0), pl.program_id(1)
    rows = out_ref.shape[0]
    facts = Facts(facts_ref, windows, slots)
    per_half = HALF_WINDOW_ROWS // rows
    half, start = source // per_half, (source % per_half) * rows
    inside = lax.broadcasted_iota(jnp.int32, (rows, 1), 0) < facts.half_limit(slot, half) - start
    mixed = jnp.dot(act_ref[...], weight_ref[...], preferred_element_type=jnp.float32)
    block = arrived_ref[0].astype(jnp.float32) + mixed + params_ref[2:3]
    out_ref[...] = jnp.where(inside, block, 0.0)


def output_rows(facts, act, weight, arrived, params, slots, windows):
    blocks, rows, width = arrived.shape
    inner = act.shape[1]
    sources = blocks // slots
    place = lambda s, j: (j * sources + s, 0)
    return pl.pallas_call(
        functools.partial(output_body, slots, windows),
        grid=(sources, slots),
        in_specs=[
            SMEM,
            pl.BlockSpec((rows, inner), place),
            pl.BlockSpec((inner, width), lambda s, j: (0, 0)),
            pl.BlockSpec((1, rows, width), lambda s, j: (s * slots + j, 0, 0)),
            pl.BlockSpec((3, width), lambda s, j: (0, 0)),
        ],
        out_specs=pl.BlockSpec((rows, width), place),
        out_shape=shape((blocks * rows, width), jnp.float32),
        compiler_params=pltpu.CompilerParams(vmem_limit_bytes=16 << 20),
        cost_estimate=pl.CostEstimate(
            flops=2 * act.size * width * 8, bytes_accessed=8 * arrived.size * 8, transcendentals=0
        ),
        name="output_rows",
    )(facts, act, weight, arrived, params)


def entry_grad_body(
    slots, windows, slot, facts_ref, padded_ref, border_ref, weight_ref, *refs
):
    slope_refs, (arrived_ref, block_ref, moments_ref, params_ref) = refs[:2], refs[2:6]
    sent_ref, kept_ref, sums_ref, wide, packed, taps_ref, departures, kept = refs[-8:]
    facts = Facts(facts_ref, windows, slots)
    sources, rows, width = packed.shape
    tiles = padded_ref.shape[1]
    per_half = HALF_WINDOW_ROWS // rows
    centre, scale, slope, _ = norm_terms(moments_ref, params_ref, facts.row_count())
    skip = BORDER - DILATION_STEP
    sums_ref[...] = jnp.zeros_like(sums_ref)

    def departure(source):
        return pltpu.make_async_copy(
            packed.at[source], sent_ref.at[source], departures.at[source]
        )

    def keeping(half):
        return pltpu.make_async_copy(
            taps_ref.at[half, :, pl.ds(0, kept_ref.shape[2])],
            kept_ref.at[slot * 2 + half],
            kept.at[half],
        )

    for half in range(2):
        piece = slot * 2 + half
        other = slot * 2 + 1 - half
        for tile, lanes in enumerate(column_slices(tiles * LANES)):
            border = border_ref[other, :, lanes].astype(jnp.float32)
            wide[tile] = padded_ref[piece, tile]
            if half == 0:
                end = PAD + HALF_WINDOW_ROWS
                wide[tile, end : end + DILATION_STEP] = border[0:DILATION_STEP]
            else:
                wide[tile, PAD - DILATION_STEP : PAD] = border[skip:BORDER]
            for number, tap in enumerate((0, 2, 1)):
                start = PAD - (tap - 1) * DILATION_STEP
                first = (number * tiles + tile) * LANES
                taps_ref[half, :, first : first + LANES] = wide[
                    tile, start : start + HALF_WINDOW_ROWS
                ].astype(jnp.bfloat16)
        keeping(half).start()
        for column in range(0, width, 2 * LANES):
            grad = jnp.dot(
                taps_ref[half],
                weight_ref[:, column : column + 2 * LANES],
                preferred_element_type=jnp.float32,
            )
            for part in range(per_half):
                source = half * per_half + part
                here = slice(part * rows, (part + 1) * rows)
                for start in (column, column + LANES):
                    lanes = slice(start, start + LANES)
                    pre = grad[here, start - column : start - column + LANES]
                    pre = pre * slope_refs[half][here, lanes]
                    values = arrived_ref[source * slots + slot, :, lanes].astype(jnp.float32)
                    sums_ref[0:1, lanes] = sums_ref[0:1, lanes] + jnp.sum(
                        pre * values, axis=0, keepdims=True
                    )
                    sums_ref[1:2, lanes] = sums_ref[1:2, lanes] + jnp.sum(
                        pre, axis=0, keepdims=True
                    )
                    block = block_ref[piece, here, lanes].astype(jnp.float32)
                    packed[source, :, lanes] = (pre * slope[:, lanes] + block).astype(
                        jnp.bfloat16
                    )
        for part in range(per_half):
            departure(half * per_half + part).start()
    sums_ref[0:1] = (sums_ref[0:1] - centre * sums_ref[1:2]) * scale
    for half in range(2):
        keeping(half).wait()
    for source in range(sources):
        departure(source).wait()


def entry_grad(
    facts, padded, border, weight, slopes, arrived, block, moments, params, taps, slots, windows,
    slot,
):
    blocks, rows, width = arrived.shape
    inner, sources = border.shape[2], blocks // slots
    inputs = [facts, padded, border, weight, *slopes, arrived, block, moments, params]
    specs = [SMEM] + [VMEM] * 9
    aliases = {}
    if taps is not None:
        aliases = {len(inputs): 1}
        inputs.append(in_hbm(taps))
        specs.append(HBM)
    taps_shape = (HALF_WINDOW_ROWS, 3 * inner)
    return pl.pallas_call(
        functools.partial(entry_grad_body, slots, windows, slot),
        in_specs=specs,
        out_specs=[HBM, HBM, VMEM],
        out_shape=[
            pltpu.HBM((sources, rows, width), jnp.bfloat16),
            pltpu.HBM((2 * slots, HALF_WINDOW_ROWS, 2 * inner), jnp.bfloat16),
            shape((2, width), jnp.float32),
        ],
        input_output_aliases=aliases,
        scratch_shapes=[
            pltpu.VMEM((inner // LANES, PADDED_ROWS, LANES), jnp.float32),
            pltpu.VMEM((sources, rows, width), jnp.bfloat16),
            pltpu.VMEM((2, *taps_shape), jnp.bfloat16),
            pltpu.SemaphoreType.DMA((sources,)),
            pltpu.SemaphoreType.DMA((2,)),
        ],
        compiler_params=pltpu.CompilerParams(vmem_limit_bytes=10 << 20),
        cost_estimate=pl.CostEstimate(
            flops=2 * 2 * HALF_WINDOW_ROWS * 3 * inner * width,
            bytes_accessed=2 * HALF_WINDOW_ROWS * (width * 10 + inner * 10),
            transcendentals=0,
        ),
        name="entry_grad",
    )(*inputs)


def flat_mask(bits):
    return sum(mask * (lax.axis_size("seq") if axis == "grp" else 1) for axis, mask in bits)


def from_flat_partner(block, mask):
    count = lax.axis_size("grp") * lax.axis_size("seq")
    return lax.ppermute(
        block, ("grp", "seq"), [(place, place ^ mask) for place in range(count)]
    )


def bit_of(axis, mask):
    return (lax.axis_index(axis) // mask) % 2


def square_phases():
    steps = exchange_steps()[1:]
    outer = [step for step in steps if step[0] == "grp"]
    inner = [step for step in steps if step[0] == "seq"]
    ordered = []
    while outer and inner:
        ordered += [outer.pop(0), inner.pop(0)]
    ordered += outer + inner
    return [ordered[start : start + 2] for start in range(0, len(ordered), 2)]


def phase_place(phase):
    return sum(bit_of(*step) * 2**number for number, step in enumerate(phase))


def phase_parts(phase):
    parts = 2 ** len(phase)
    masks = [
        flat_mask([step for number, step in enumerate(phase) if part >> number & 1])
        for part in range(parts)
    ]
    return parts, masks


def exchange_parts(parts, phase):
    _, masks = phase_parts(phase)
    return [from_flat_partner(part, mask) for part, mask in zip(parts, masks[1:])]


def place_in(facts_ref, phase):
    bits = [
        (facts_ref[0 if axis == "grp" else 1] // mask) % 2 * 2**number
        for number, (axis, mask) in enumerate(phase)
    ]
    return sum(bits)


def encoded(sums, rows_ref):
    count = sums.shape[0]
    high = sums.astype(jnp.bfloat16).astype(jnp.float32)
    low = (sums - high).astype(jnp.bfloat16).astype(jnp.float32)
    rows_ref[...] = jnp.zeros_like(rows_ref)
    rows_ref[0:count] = high
    rows_ref[count : 2 * count] = low
    return rows_ref[...].astype(jnp.bfloat16), high + low


def decoded(found_ref, count, rows_ref):
    rows_ref[...] = found_ref[found_ref.shape[0] - EXTRA :, :].astype(jnp.float32)
    return rows_ref[0:count] + rows_ref[count : 2 * count]


def pair_sum(values):
    while len(values) > 1:
        values = [values[i] + values[i + 1] for i in range(0, len(values), 2)]
    return values[0]


def other_half_body(
    facts_ref, sides_ref, centre_ref, pointwise_ref, sums_ref, sent_ref, held_ref, rows_ref
):
    width, inner = pointwise_ref.shape
    sent_ref[width:, :], held_ref[...] = encoded(sums_ref[...], rows_ref)

    @pl.when(facts_ref[0] % 2 == 0)
    def _():
        sent_ref[:width, :inner] = sides_ref[:, inner:].astype(jnp.bfloat16)
        sent_ref[:width, inner:] = pointwise_ref[...].astype(jnp.bfloat16)

    @pl.when(facts_ref[0] % 2 == 1)
    def _():
        sent_ref[:width, :inner] = sides_ref[:, :inner].astype(jnp.bfloat16)
        sent_ref[:width, inner:] = centre_ref[...].astype(jnp.bfloat16)


def other_half(facts, sides, centre, pointwise, sums):
    width, inner = pointwise.shape
    return kernel_call(
        other_half_body,
        "other_half",
        (facts, sides, centre, pointwise, sums),
        [SMEM] + [VMEM] * 4,
        [shape((width + EXTRA, 2 * inner), jnp.bfloat16), shape(sums.shape, jnp.float32)],
        [VMEM, VMEM],
        [pltpu.VMEM((EXTRA, 2 * inner), jnp.float32)],
        flops=2 * width * inner,
        bytes_moved=12 * width * inner,
        grant=10 << 20,
    )


def part_rows(mine, part, rows):
    return pl.ds(pl.multiple_of(jnp.bitwise_xor(mine, part) * rows, rows), rows)


def own_half_body(
    phase, facts_ref, sides_ref, centre_ref, pointwise_ref, sums_ref, other_ref, total_ref, *refs
):
    part_refs, rows_ref = refs[:-1], refs[-1]
    inner = pointwise_ref.shape[1]
    rows = part_refs[0].shape[0]
    mine = place_in(facts_ref, phase)
    sums = sums_ref[...] + decoded(other_ref, sums_ref.shape[0], rows_ref)
    extra, total_ref[...] = encoded(sums, rows_ref)
    for part_ref in part_refs[1:]:
        part_ref[rows:, :] = extra

    def write(low, high):
        for part, part_ref in enumerate(part_refs):
            here = part_rows(mine, part, rows)
            for piece, lanes in ((low, slice(0, inner)), (high, slice(inner, 2 * inner))):
                value = piece(here) + other_ref[here, lanes].astype(jnp.float32)
                part_ref[:rows, lanes] = value.astype(part_ref.dtype)

    @pl.when(facts_ref[0] % 2 == 0)
    def _():
        write(
            lambda here: sides_ref[here, :inner],
            lambda here: centre_ref[here, :],
        )

    @pl.when(facts_ref[0] % 2 == 1)
    def _():
        write(lambda here: sides_ref[here, inner:], lambda here: pointwise_ref[here, :])


def part_shapes(sums, rows, columns, phase):
    parts = 2 ** len(phase)
    rows //= parts
    return [
        shape(sums.shape, jnp.float32),
        shape((rows, columns), jnp.float32),
        *[shape((rows + EXTRA, columns), jnp.bfloat16)] * (parts - 1),
    ]


def own_half(facts, sides, centre, pointwise, sums, other, phase):
    width, inner = pointwise.shape
    outputs = part_shapes(sums, width, 2 * inner, phase)
    return kernel_call(
        functools.partial(own_half_body, phase),
        "own_half",
        (facts, sides, centre, pointwise, sums, other),
        [SMEM] + [VMEM] * 5,
        outputs,
        [VMEM] * len(outputs),
        [pltpu.VMEM((EXTRA, 2 * inner), jnp.float32)],
        flops=2 * width * inner,
        bytes_moved=20 * width * inner,
        grant=12 << 20,
    )


def next_parts_body(count, phase, facts_ref, kept_ref, sums_ref, *refs):
    found_refs, total_ref, part_refs, rows_ref = (
        refs[:count],
        refs[count],
        refs[count + 1 : -1],
        refs[-1],
    )
    sums = pair_sum(
        [sums_ref[...]] + [decoded(ref, sums_ref.shape[0], rows_ref) for ref in found_refs]
    )
    total_ref[...] = sums
    rows = part_refs[0].shape[0]
    if phase:
        mine = place_in(facts_ref, phase)
        extra, total_ref[...] = encoded(sums, rows_ref)
        for part_ref in part_refs[1:]:
            part_ref[rows:, :] = extra
    for part, part_ref in enumerate(part_refs):
        here = part_rows(mine, part, rows) if phase else slice(0, rows)
        value = kept_ref[here, :]
        for found_ref in found_refs:
            value = value + found_ref[here, :].astype(jnp.float32)
        part_ref[:rows, :] = value.astype(part_ref.dtype)


def plain_parts(kept, sums, found, phase):
    rows, count = kept.shape[0], sums.shape[0]
    totals = [sums]
    for block in found:
        kept = kept + block[:rows].astype(jnp.float32)
        tail = block[rows:].astype(jnp.float32)
        totals.append(tail[:count] + tail[count : 2 * count])
    sums = pair_sum(totals)
    if not phase:
        return [sums, kept.astype(jnp.bfloat16)]
    high = lax.reduce_precision(sums, 8, 7)
    low = lax.reduce_precision(sums - high, 8, 7)
    rest = jnp.zeros((EXTRA - 2 * count, sums.shape[1]), jnp.float32)
    extra, sums = jnp.concatenate([high, low, rest]).astype(jnp.bfloat16), high + low
    parts = 2 ** len(phase)
    mine, rows = phase_place(phase), rows // parts
    slices = [
        lax.dynamic_slice_in_dim(kept, jnp.bitwise_xor(mine, part) * rows, rows)
        for part in range(parts)
    ]
    return [sums, slices[0]] + [
        jnp.concatenate([block.astype(jnp.bfloat16), extra]) for block in slices[1:]
    ]


def next_parts(facts, kept, sums, found, phase):
    rows, columns = kept.shape
    if rows // 2 ** len(phase) % 16:
        return plain_parts(kept, sums, found, phase)
    outputs = part_shapes(sums, rows, columns, phase)
    if not phase:
        outputs = [outputs[0], shape((rows, columns), jnp.bfloat16)]
    return kernel_call(
        functools.partial(next_parts_body, len(found), phase),
        "next_parts",
        (facts, kept, sums, *found),
        [SMEM] + [VMEM] * (2 + len(found)),
        outputs,
        [VMEM] * len(outputs),
        [pltpu.VMEM((EXTRA, columns), jnp.float32)],
        flops=4 * rows * columns,
        bytes_moved=16 * rows * columns,
    )


def gather_parts(buffer, phase):
    _, masks = phase_parts(phase)
    return [buffer] + [from_flat_partner(buffer, mask) for mask in masks[1:]]


def in_order(found, owners):
    parts = len(found)
    orders = [
        jnp.concatenate([found[place ^ own] for place in range(parts)], axis=0)
        for own in range(parts)
    ]
    result = orders[0]
    for own in range(1, parts):
        result = jnp.where(owners[own], orders[own], result)
    return result


def finish_body(facts_ref, mine_ref, other_ref, dilated_ref, pointwise_ref):
    inner = dilated_ref.shape[2]

    def write(low_ref, high_ref):
        dilated_ref[0] = low_ref[:, :inner].astype(jnp.float32)
        dilated_ref[1] = low_ref[:, inner:].astype(jnp.float32)
        dilated_ref[2] = high_ref[:, :inner].astype(jnp.float32)
        pointwise_ref[...] = high_ref[:, inner:].astype(jnp.float32).T

    upper = facts_ref[0] % 2

    @pl.when(upper == 0)
    def _():
        write(mine_ref, other_ref)

    @pl.when(upper == 1)
    def _():
        write(other_ref, mine_ref)


def finish_weights(facts, mine, other):
    width, both = mine.shape
    inner = both // 2
    return kernel_call(
        finish_body,
        "finish_weights",
        (facts, mine, other),
        [SMEM, VMEM, VMEM],
        [shape((3, width, inner), jnp.float32), shape((inner, width), jnp.float32)],
        [VMEM, VMEM],
        flops=width * both,
        bytes_moved=12 * width * both,
        grant=16 << 20,
    )


def per_device(
    signal,
    entry_gain,
    entry_shift,
    dilated_kernel,
    middle_gain,
    middle_shift,
    pointwise_kernel,
    pointwise_bias,
    lengths,
    assignment,
    cotangent,
):
    seq_count = lax.axis_size("seq")
    windows, segment, width = signal.shape
    inner = pointwise_kernel.shape[0]
    slots = windows // seq_count
    rows = segment // 2
    pieces = 2 * slots
    places = jnp.stack([lax.axis_index("grp"), lax.axis_index("seq"), jnp.int32(seq_count)])
    facts = jnp.concatenate([places.astype(jnp.int32), assignment[0], lengths])
    entry_params = jnp.stack([entry_gain, entry_shift, pointwise_bias])
    middle_params = jnp.stack([middle_gain, middle_shift])

    outgoing, entry_local = pool(facts, signal, slots)
    arrived = lax.all_to_all(outgoing, "seq", split_axis=0, concat_axis=0, tiled=True)

    late_facts, _ = lax.optimization_barrier((facts, entry_local))
    first_chosen = first_marks(late_facts, signal, slots)
    wide_kernel, back_kernel, pointwise_low = prepare_weights(dilated_kernel, pointwise_kernel)
    grad_block, grad_middle, bias_part = prepare(
        facts, cotangent, pointwise_low, slots, windows
    )
    entry_moments, prepared = total_moments(
        entry_local,
        [first_chosen, grad_block, grad_middle, wide_kernel, back_kernel, pointwise_low],
    )
    first_chosen, grad_block, grad_middle, wide_kernel, back_kernel, pointwise_low = prepared
    phases = square_phases()
    owners = [
        [phase_place(phase) == own for own in range(2 ** len(phase))] for phase in phases
    ]
    first_axis, first_mask = exchange_steps()[0]
    upper = bit_of(first_axis, first_mask) == 1
    (
        arrived,
        first_chosen,
        grad_block,
        grad_middle,
        wide_kernel,
        back_kernel,
        pointwise_low,
        owners,
        upper,
        middle_params,
        facts,
    ) = lax.optimization_barrier(
        (
            arrived,
            first_chosen,
            grad_block,
            grad_middle,
            wide_kernel,
            back_kernel,
            pointwise_low,
            owners,
            upper,
            middle_params,
            facts,
        )
    )

    act, act_border = activate(facts, arrived, entry_moments, entry_params, slots, windows)
    act_border = from_partner(act_border, "seq", 1)
    dilated, held_moments = convolve(facts, act, wide_kernel, slots, windows)
    strip, middle_moments = join(
        facts, dilated, act_border, wide_kernel, held_moments, slots, windows
    )
    slopes = []
    for number, (axis, mask) in enumerate(exchange_steps()):
        other = from_partner(middle_moments, axis, mask)
        if number and len(slopes) < pieces:
            tied, middle_moments = lax.optimization_barrier((arrived, middle_moments))
            found = entry_slope(
                facts, tied, entry_moments, entry_params, slots, windows, len(slopes)
            )
            other, found = lax.optimization_barrier((other, found))
            slopes.append(found)
        middle_moments = jnp.concatenate(
            merged(
                (middle_moments[0:1], middle_moments[1:2], middle_moments[2:3]),
                (other[0:1], other[1:2], other[2:3]),
            ),
            axis=0,
        )
    while len(slopes) < pieces:
        slopes.append(
            entry_slope(facts, arrived, entry_moments, entry_params, slots, windows, len(slopes))
        )
    middle_act, middle_slope, middle_norm, middle_sums = middle(
        facts,
        dilated,
        strip,
        middle_moments,
        middle_params,
        grad_middle.reshape(pieces, HALF_WINDOW_ROWS, inner),
        slots,
        windows,
    )
    flat_act = middle_act.reshape(-1, inner)
    for number, (axis, mask) in enumerate(exchange_steps()):
        other = from_partner(middle_sums, axis, mask)
        if number == 1:
            tied, middle_sums = lax.optimization_barrier((flat_act, middle_sums))
            pointwise_part = jnp.einsum(
                "rd,rf->df", grad_block, tied, preferred_element_type=jnp.float32
            )
            other, pointwise_part = lax.optimization_barrier((other, pointwise_part))
        middle_sums = middle_sums + other
    padded, grad_border, grad_centre = middle_grad(
        facts, middle_slope, middle_norm, middle_moments, middle_params, middle_sums, slots, windows
    )
    centre_part = jnp.einsum("hrc,hrf->cf", act, grad_centre, preferred_element_type=jnp.float32)
    grad_border = from_partner(grad_border, "seq", 1)
    grad_border, centre_part = lax.optimization_barrier((grad_border, centre_part))
    block_pieces = grad_block.reshape(pieces, HALF_WINDOW_ROWS, width)
    sent, taps, entry_part = [], None, jnp.concatenate([jnp.zeros_like(bias_part)] * 2)
    returned = []

    def send_back(block):
        return lax.all_to_all(block, "seq", split_axis=0, concat_axis=0, tiled=True)

    for slot in range(slots):
        block, taps, part = entry_grad(
            facts, padded, grad_border, back_kernel, slopes[2 * slot : 2 * slot + 2],
            arrived, block_pieces, entry_moments, entry_params, taps, slots, windows, slot,
        )
        sent.append(block)
        entry_part = entry_part + part
    entry_sums = jnp.concatenate([entry_part, bias_part])
    tied = lax.optimization_barrier((*sent, entry_sums))
    sent, entry_sums = list(tied[:-1]), tied[-1]
    returned = [send_back(sent[0])]
    side_parts = jnp.einsum("hrc,hrf->cf", act, taps, preferred_element_type=jnp.float32)
    other, entry_sums = other_half(facts, side_parts, centre_part, pointwise_part, entry_sums)
    other = from_partner(other, first_axis, first_mask)
    entry_sums, *parts = own_half(
        facts, side_parts, centre_part, pointwise_part, entry_sums, other, phases[0]
    )
    for held, phase in zip(phases, phases[1:] + [[]]):
        found = exchange_parts(parts[1:], held)
        entry_sums, *parts = next_parts(facts, parts[0], entry_sums, found, phase)
    buffer, signal_gradient, activations = parts[0], None, None
    for number, phase in reversed(list(enumerate(phases))):
        found = gather_parts(buffer, phase)
        if number == len(phases) - 1:
            found[1], flat_act, entry_sums, *later = lax.optimization_barrier(
                (found[1], flat_act, entry_sums, *sent[1:])
            )
            returned += [send_back(block) for block in later]
        if number == 0:
            signal_gradient = unpool(
                facts, returned[0], outgoing, first_chosen, entry_moments, entry_sums,
                entry_params, slots, 0, None,
            )
            activations = output_rows(
                facts, flat_act, pointwise_low, arrived, entry_params, slots, windows
            )
            vectors = [entry_sums[0], entry_sums[1], middle_sums[0], middle_sums[1], entry_sums[2]]
            tied = lax.optimization_barrier((signal_gradient, activations, *vectors, *found))
            signal_gradient, activations, vectors, found = tied[0], tied[1], tied[2:7], tied[7:]
        buffer = in_order(found, owners[number])
    other = from_partner(buffer, first_axis, first_mask)
    dilated_kernel_gradient, pointwise_kernel_gradient = finish_weights(facts, buffer, other)
    for slot in range(1, slots):
        signal_gradient = unpool(
            facts, returned[slot], outgoing, first_chosen, entry_moments, entry_sums,
            entry_params, slots, slot, signal_gradient,
        )
    return (
        activations,
        signal_gradient,
        vectors[0],
        vectors[1],
        dilated_kernel_gradient,
        vectors[2],
        vectors[3],
        pointwise_kernel_gradient,
        vectors[4],
    )


def solution(mesh):
    return jax.shard_map(
        per_device,
        mesh=mesh,
        in_specs=(
            P("grp", "seq", None),
            P(),
            P(),
            P(),
            P(),
            P(),
            P(),
            P(),
            P(),
            P("grp", None),
            P(("grp", "seq"), None),
        ),
        out_specs=(
            P(("grp", "seq"), None),
            P("grp", "seq", None),
            P(),
            P(),
            P(),
            P(),
            P(),
            P(),
            P(),
        ),
        check_vma=False,
    )
```

```python
import functools
import math

import jax
import jax.numpy as jnp
from jax import lax
from jax.experimental import pallas as pl
from jax.experimental.pallas import tpu as pltpu
from jax.sharding import PartitionSpec as P

DILATION_STEP = 38
WINDOW_SPAN = 1024
HALF_WINDOW_ROWS = 512


EPSILON = 0.001

LANES = 128
BORDER = 48
STRIP = 64
PAD = 40
PADDED_ROWS = HALF_WINDOW_ROWS + 2 * PAD
EXTRA = 8
GELU_SLOPE = math.sqrt(2.0 / math.pi)
GELU_CUBE = 0.044715

VMEM = pl.BlockSpec(memory_space=pltpu.VMEM)
SMEM = pl.BlockSpec(memory_space=pltpu.SMEM)
HBM = pl.BlockSpec(memory_space=pltpu.HBM)


def from_partner(block, axis, mask):
    count = lax.axis_size(axis)
    return lax.ppermute(block, axis, [(place, place ^ mask) for place in range(count)])


def exchange_steps():
    steps = []
    for axis in ("grp", "seq"):
        mask = 1
        while mask < lax.axis_size(axis):
            steps.append((axis, mask))
            mask *= 2
    return steps


def total(values):
    for axis, mask in exchange_steps():
        values = values + from_partner(values, axis, mask)
    return values


def merged(left, right):
    left_sum, left_spread, left_count = left
    right_sum, right_spread, right_count = right
    gap = left_sum / jnp.maximum(left_count, 1.0) - right_sum / jnp.maximum(right_count, 1.0)
    weight = left_count * right_count / jnp.maximum(left_count + right_count, 1.0)
    return (
        left_sum + right_sum,
        left_spread + right_spread + gap * gap * weight,
        left_count + right_count,
    )


def total_moments(packed, others):
    steps = exchange_steps()
    for number, (axis, mask) in enumerate(steps):
        if number == len(steps) - 1:
            packed, *others = lax.optimization_barrier((packed, *others))
        other = from_partner(packed, axis, mask)
        packed = jnp.concatenate(
            merged(
                (packed[0:1], packed[1:2], packed[2:3]), (other[0:1], other[1:2], other[2:3])
            ),
            axis=0,
        )
    return packed, others


class Facts:
    def __init__(self, ref, windows, slots):
        self.ref, self.windows, self.slots = ref, windows, slots

    def slot_window(self, slot):
        upper = (2 * self.ref[1]) // self.ref[2]
        target = jnp.bitwise_xor(slot // self.slots, upper)
        return self.ref[3 + target * self.slots + slot % self.slots]

    def length(self, window):
        return self.ref[3 + self.windows + self.ref[0] * self.windows + window]

    def slot_count(self, slot, rows):
        return jnp.clip(self.length(self.slot_window(slot)) - self.ref[1] * rows, 0, rows)

    def half_limit(self, slot, half):
        place = jnp.bitwise_xor(self.ref[1], half)
        window = self.ref[3 + place * self.slots + slot]
        return jnp.clip(self.length(window) - half * HALF_WINDOW_ROWS, 0, HALF_WINDOW_ROWS)

    def row_count(self):
        start = 3 + self.windows
        count = self.ref.shape[0] - start
        added = lax.fori_loop(0, count, lambda i, held: held + self.ref[start + i], jnp.int32(0))
        return added.astype(jnp.float32)


def kernel_call(body, name, inputs, specs, outputs, out_specs, scratch=(), flops=0, bytes_moved=0, grant=8 << 20):
    return pl.pallas_call(
        body,
        in_specs=specs,
        out_specs=out_specs,
        out_shape=outputs,
        scratch_shapes=list(scratch),
        compiler_params=pltpu.CompilerParams(vmem_limit_bytes=grant),
        cost_estimate=pl.CostEstimate(
            flops=flops, bytes_accessed=bytes_moved, transcendentals=0
        ),
        name=name,
    )(*inputs)


def shape(dims, dtype):
    return jax.ShapeDtypeStruct(dims, dtype)


def in_hbm(array):
    return pltpu.with_memory_space_constraint(array, pltpu.HBM)


def column_slices(width):
    return [slice(start, start + LANES) for start in range(0, width, LANES)]


def bin_copy(facts, signal_ref, held, arrivals, place, column):
    return pltpu.make_async_copy(
        signal_ref.at[facts.slot_window(place), :, pl.ds(column * LANES, LANES)],
        held.at[place, column],
        arrivals.at[place, column],
    )


def begin_bins(facts, signal_ref, held, arrivals):
    windows, columns = held.shape[:2]

    def begin(place, carry):
        for column in range(columns):
            bin_copy(facts, signal_ref, held, arrivals, place, column).start()
        return carry

    lax.fori_loop(0, windows, begin, 0)


def bins_of(facts, signal_ref, held, arrivals, place, rows):
    columns = held.shape[1]
    for column in range(columns):
        bin_copy(facts, signal_ref, held, arrivals, place, column).wait()
    return [
        (
            lanes,
            held[place, column, pl.ds(0, rows, stride=2), :],
            held[place, column, pl.ds(1, rows, stride=2), :],
        )
        for column, lanes in enumerate(column_slices(columns * LANES))
    ]


def finish_copies(copy_of, count):
    def finish(place, carry):
        copy_of(place).wait()
        return carry

    lax.fori_loop(0, count, finish, 0)


def pool_body(
    slots, order_ref, lengths_ref, signal_ref, pooled_ref, moments_ref,
    held, low, blocks, order, lengths, places, arrivals, departures, facts_copies,
):
    windows, columns = held.shape[:2]
    rows = low.shape[1]
    grp, seq = lax.axis_index("grp"), lax.axis_index("seq")
    upper = (2 * seq) // (windows // slots)

    def arrival(window, column):
        return pltpu.make_async_copy(
            signal_ref.at[window, :, pl.ds(column * LANES, LANES)],
            held.at[window, column],
            arrivals.at[window, column],
        )

    def departure(window):
        return pltpu.make_async_copy(
            low.at[window], pooled_ref.at[places[window]], departures.at[window]
        )

    fetches = [
        pltpu.make_async_copy(order_ref, order, facts_copies.at[0]),
        pltpu.make_async_copy(lengths_ref, lengths, facts_copies.at[1]),
    ]
    for fetch in fetches:
        fetch.start()

    def begin(window, carry):
        for column in range(columns):
            arrival(window, column).start()
        return carry

    lax.fori_loop(0, windows, begin, 0)
    moments_ref[...] = jnp.zeros_like(moments_ref)
    for fetch in fetches:
        fetch.wait()

    def note(place, carry):
        target = jnp.bitwise_xor(place // slots, upper)
        places[order[0, target * slots + place % slots]] = place
        return carry

    lax.fori_loop(0, windows, note, 0)

    def count_of(window):
        return jnp.clip(lengths[grp * windows + window] - seq * rows, 0, rows)

    def work(window, carry):
        count = count_of(window)
        inside = lax.broadcasted_iota(jnp.int32, (rows, LANES), 0) < count
        for column in range(columns):
            arrival(window, column).wait()
        for column, lanes in enumerate(column_slices(columns * LANES)):
            first_bin = held[window, column, pl.ds(0, rows, stride=2), :]
            second_bin = held[window, column, pl.ds(1, rows, stride=2), :]
            pooled = jnp.where(inside, jnp.maximum(first_bin, second_bin), 0.0)
            pooled = pooled.astype(jnp.bfloat16)
            low[window, :, lanes] = pooled
            found = block_moments(pooled.astype(jnp.float32), inside, count.astype(jnp.float32))
            blocks[window, 0:1, lanes] = found[0]
            blocks[window, 1:2, lanes] = found[1]
        departure(window).start()
        return carry

    lax.fori_loop(0, windows, work, 0)

    def join_blocks(window, carry):
        count = jnp.broadcast_to(count_of(window).astype(jnp.float32), (1, columns * LANES))
        held_moments = (moments_ref[0:1], moments_ref[1:2], moments_ref[2:3])
        moments_ref[0:1], moments_ref[1:2], moments_ref[2:3] = merged(
            held_moments, (blocks[window, 0:1], blocks[window, 1:2], count)
        )
        return carry

    lax.fori_loop(0, windows, join_blocks, 0)
    finish_copies(departure, windows)


def pool(order, lengths, signal, slots):
    windows, segment, width = signal.shape
    rows, columns = segment // 2, width // LANES
    block = (windows, rows, width)
    return kernel_call(
        functools.partial(pool_body, slots),
        "pool",
        (in_hbm(order), in_hbm(lengths), in_hbm(signal)),
        [HBM, HBM, HBM],
        [pltpu.HBM(block, jnp.bfloat16), shape((3, width), jnp.float32)],
        [HBM, VMEM],
        [
            pltpu.VMEM((windows, columns, segment, LANES), jnp.float32),
            pltpu.VMEM(block, jnp.bfloat16),
            pltpu.VMEM((windows, 2, width), jnp.float32),
            pltpu.SMEM(order.shape, jnp.int32),
            pltpu.SMEM(lengths.shape, jnp.int32),
            pltpu.SMEM((windows,), jnp.int32),
            pltpu.SemaphoreType.DMA((windows, columns)),
            pltpu.SemaphoreType.DMA((windows,)),
            pltpu.SemaphoreType.DMA((2,)),
        ],
        flops=10 * windows * rows * width,
        bytes_moved=windows * rows * width * 10,
        grant=24 << 20,
    )


def marks_body(slots, facts_ref, signal_ref, first_ref, held, mark, arrivals, departures):
    windows = held.shape[0]
    rows = mark.shape[1]
    facts = Facts(facts_ref, windows, slots)

    def departure(place):
        return pltpu.make_async_copy(mark.at[place], first_ref.at[place], departures.at[place])

    begin_bins(facts, signal_ref, held, arrivals)

    def work(place, carry):
        for lanes, first_bin, second_bin in bins_of(
            facts, signal_ref, held, arrivals, place, rows
        ):
            mark[place, :, lanes] = jnp.where(first_bin >= second_bin, 1.0, 0.0).astype(
                jnp.bfloat16
            )
        departure(place).start()
        return carry

    lax.fori_loop(0, windows, work, 0)
    finish_copies(departure, windows)


def first_marks(facts, signal, slots):
    windows, segment, width = signal.shape
    rows, columns = segment // 2, width // LANES
    block = (windows, rows, width)
    return kernel_call(
        functools.partial(marks_body, slots),
        "first_marks",
        (facts, in_hbm(signal)),
        [SMEM, HBM],
        pltpu.HBM(block, jnp.bfloat16),
        HBM,
        [
            pltpu.VMEM((windows, columns, segment, LANES), jnp.float32),
            pltpu.VMEM(block, jnp.bfloat16),
            pltpu.SemaphoreType.DMA((windows, columns)),
            pltpu.SemaphoreType.DMA((windows,)),
        ],
        flops=3 * windows * rows * width,
        bytes_moved=windows * rows * width * 10,
        grant=24 << 20,
    )


def unpool_body(
    slots, slot, windows, facts_ref, returned_ref, pooled_ref, first_ref, moments_ref, sums_ref,
    params_ref, *refs,
):
    out_ref, back, low, mark, held, arrivals, departures = refs[-7:]
    targets, rows, width = back.shape
    columns = held.shape[1]
    facts = Facts(facts_ref, windows, slots)

    def arrival(target):
        place = target * slots + slot
        return [
            pltpu.make_async_copy(returned_ref.at[target], back.at[target], arrivals.at[target, 0]),
            pltpu.make_async_copy(pooled_ref.at[place], low.at[target], arrivals.at[target, 1]),
            pltpu.make_async_copy(first_ref.at[place], mark.at[target], arrivals.at[target, 2]),
        ]

    def departure(target, column):
        window = facts.slot_window(target * slots + slot)
        return pltpu.make_async_copy(
            held.at[target, column],
            out_ref.at[window, :, pl.ds(column * LANES, LANES)],
            departures.at[target, column],
        )

    def begin(target, carry):
        for copy in arrival(target):
            copy.start()
        return carry

    lax.fori_loop(0, targets, begin, 0)
    rows_total = facts.row_count()
    centre = moments_ref[0:1] / rows_total
    scale = lax.rsqrt(moments_ref[1:2] / rows_total + EPSILON)
    factor = params_ref[0:1] * scale / rows_total
    level = factor * sums_ref[1:2]
    tilt = factor * scale * sums_ref[0:1]

    def work(target, carry):
        for copy in arrival(target):
            copy.wait()
        inside = lax.broadcasted_iota(jnp.int32, (rows, LANES), 0) < facts.slot_count(
            target * slots + slot, rows
        )
        for column, lanes in enumerate(column_slices(width)):
            centred = low[target, :, lanes].astype(jnp.float32) - centre[:, lanes]
            gradient = back[target, :, lanes].astype(jnp.float32) - (
                level[:, lanes] + centred * tilt[:, lanes]
            )
            gradient = jnp.where(inside, gradient, 0.0).astype(jnp.bfloat16).astype(jnp.float32)
            first = gradient * mark[target, :, lanes].astype(jnp.float32)
            held[target, column, pl.ds(0, rows, stride=2), :] = first
            held[target, column, pl.ds(1, rows, stride=2), :] = gradient - first
        for column in range(columns):
            departure(target, column).start()
        return carry

    lax.fori_loop(0, targets, work, 0)

    def finish(target, carry):
        for column in range(columns):
            departure(target, column).wait()
        return carry

    lax.fori_loop(0, targets, finish, 0)


def unpool(facts, returned, pooled, first, moments, sums, params, slots, slot, held_output):
    targets, rows, width = returned.shape
    windows, columns = targets * slots, width // LANES
    inputs = [facts, in_hbm(returned), in_hbm(pooled), in_hbm(first), moments, sums, params]
    specs = [SMEM, HBM, HBM, HBM, VMEM, VMEM, VMEM]
    aliases = {}
    if held_output is not None:
        aliases = {len(inputs): 0}
        inputs.append(in_hbm(held_output))
        specs.append(HBM)
    block = (targets, rows, width)
    return pl.pallas_call(
        functools.partial(unpool_body, slots, slot, windows),
        in_specs=specs,
        out_specs=HBM,
        out_shape=pltpu.HBM((windows, 2 * rows, width), jnp.float32),
        input_output_aliases=aliases,
        scratch_shapes=[
            pltpu.VMEM(block, jnp.bfloat16),
            pltpu.VMEM(block, jnp.bfloat16),
            pltpu.VMEM(block, jnp.bfloat16),
            pltpu.VMEM((targets, columns, 2 * rows, LANES), jnp.float32),
            pltpu.SemaphoreType.DMA((targets, 3)),
            pltpu.SemaphoreType.DMA((targets, columns)),
        ],
        compiler_params=pltpu.CompilerParams(vmem_limit_bytes=16 << 20),
        cost_estimate=pl.CostEstimate(
            flops=10 * targets * rows * width,
            bytes_accessed=targets * rows * width * 14,
            transcendentals=0,
        ),
        name="unpool",
    )(*inputs)


def prepare_body(slots, windows, facts_ref, cot_ref, weight_ref, low_ref, middle_ref, bias_ref):
    step = pl.program_id(0)
    rows = cot_ref.shape[0]
    facts = Facts(facts_ref, windows, slots)
    first_row = step * rows
    piece = first_row // HALF_WINDOW_ROWS
    limit = facts.half_limit(piece // 2, piece % 2) - first_row % HALF_WINDOW_ROWS

    @pl.when(step == 0)
    def _():
        bias_ref[...] = jnp.zeros_like(bias_ref)

    inside = lax.broadcasted_iota(jnp.int32, (rows, 1), 0) < limit
    block = jnp.where(inside, cot_ref[...], 0.0)
    bias_ref[...] = bias_ref[...] + jnp.sum(block, axis=0, keepdims=True)
    low = block.astype(jnp.bfloat16)
    low_ref[...] = low
    middle_ref[...] = lax.dot_general(
        low, weight_ref[...], (((1,), (1,)), ((), ())), preferred_element_type=jnp.float32
    )


def prepare(facts, cotangent, weight, slots, windows):
    total_rows, width = cotangent.shape
    inner = weight.shape[0]
    rows = 256
    return pl.pallas_call(
        functools.partial(prepare_body, slots, windows),
        grid=(total_rows // rows,),
        in_specs=[
            SMEM,
            pl.BlockSpec((rows, width), lambda i: (i, 0)),
            pl.BlockSpec((inner, width), lambda i: (0, 0)),
        ],
        out_specs=[
            pl.BlockSpec((rows, width), lambda i: (i, 0)),
            pl.BlockSpec((rows, inner), lambda i: (i, 0)),
            pl.BlockSpec((1, width), lambda i: (0, 0)),
        ],
        out_shape=[
            shape((total_rows, width), jnp.bfloat16),
            shape((total_rows, inner), jnp.float32),
            shape((1, width), jnp.float32),
        ],
        compiler_params=pltpu.CompilerParams(vmem_limit_bytes=16 << 20),
        cost_estimate=pl.CostEstimate(
            flops=2 * total_rows * width * inner,
            bytes_accessed=total_rows * (width * 6 + inner * 4),
            transcendentals=0,
        ),
        name="prepare_cotangent",
    )(facts, cotangent, weight)


def weights_body(dilated_ref, pointwise_ref, wide_ref, back_ref, low_ref):
    inner = dilated_ref.shape[2]
    for number, tap in enumerate((0, 2, 1)):
        values = dilated_ref[tap]
        wide_ref[:, tap * inner : (tap + 1) * inner] = values.astype(jnp.bfloat16)
        back_ref[number * inner : (number + 1) * inner, :] = values.T.astype(jnp.bfloat16)
    low_ref[...] = pointwise_ref[...].astype(jnp.bfloat16)


def prepare_weights(dilated_kernel, pointwise_kernel):
    taps, width, inner = dilated_kernel.shape
    return kernel_call(
        weights_body,
        "prepare_weights",
        (dilated_kernel, pointwise_kernel),
        [VMEM, VMEM],
        [
            shape((width, taps * inner), jnp.bfloat16),
            shape((taps * inner, width), jnp.bfloat16),
            shape(pointwise_kernel.shape, jnp.bfloat16),
        ],
        [VMEM, VMEM, VMEM],
        flops=4 * width * inner,
        bytes_moved=30 * width * inner,
        grant=16 << 20,
    )


def norm_terms(moments_ref, params_ref, rows_total):
    centre = moments_ref[0:1] / rows_total
    scale = lax.rsqrt(moments_ref[1:2] / rows_total + EPSILON)
    return centre, scale, params_ref[0:1] * scale, params_ref[1:2]


def half_terms(moments_ref, params_ref, rows_total):
    centre, _, slope, offset = norm_terms(moments_ref, params_ref, rows_total)
    return 0.5 * slope, 0.5 * (offset - centre * slope)


def bent(half):
    square = half * half
    return jnp.tanh(half * (2.0 * GELU_SLOPE + (8.0 * GELU_SLOPE * GELU_CUBE) * square)), square


def gelu_slope(half, bend, square):
    inner = GELU_SLOPE + (12.0 * GELU_SLOPE * GELU_CUBE) * square
    return (0.5 + 0.5 * bend) + (half - half * bend * bend) * inner


def activate_body(
    slots, windows, facts_ref, arrived_ref, moments_ref, params_ref, act_ref, border_ref
):
    blocks, rows, width = arrived_ref.shape
    facts = Facts(facts_ref, windows, slots)
    per_half = HALF_WINDOW_ROWS // rows
    slope, offset = half_terms(moments_ref, params_ref, facts.row_count())

    def work(block, carry):
        source, slot = block // slots, block % slots
        half, start = source // per_half, (source % per_half) * rows
        inside = lax.broadcasted_iota(jnp.int32, (rows, 1), 0) < (
            facts.half_limit(slot, half) - start
        )
        for lanes in column_slices(width):
            values = arrived_ref[block, :, lanes].astype(jnp.float32)
            half_pre = values * slope[:, lanes] + offset[:, lanes]
            bend, _ = bent(half_pre)
            act = jnp.where(inside, half_pre + half_pre * bend, 0.0)
            act_ref[slot * 2 + half, pl.ds(pl.multiple_of(start, rows), rows), lanes] = act.astype(
                jnp.bfloat16
            )
        return carry

    lax.fori_loop(0, blocks, work, 0)
    for piece in range(act_ref.shape[0]):
        start = 0 if piece % 2 else HALF_WINDOW_ROWS - BORDER
        border_ref[piece] = act_ref[piece, start : start + BORDER]


def activate(facts, arrived, moments, params, slots, windows):
    width = arrived.shape[2]
    return kernel_call(
        functools.partial(activate_body, slots, windows),
        "activate",
        (facts, arrived, moments, params),
        [SMEM, VMEM, VMEM, VMEM],
        [
            shape((2 * slots, HALF_WINDOW_ROWS, width), jnp.bfloat16),
            shape((2 * slots, BORDER, width), jnp.bfloat16),
        ],
        [VMEM, VMEM],
        flops=20 * arrived.size,
        bytes_moved=4 * arrived.size,
    )


def slope_body(slots, windows, piece, facts_ref, arrived_ref, moments_ref, params_ref, slope_ref):
    blocks, rows, width = arrived_ref.shape
    facts = Facts(facts_ref, windows, slots)
    per_half = HALF_WINDOW_ROWS // rows
    slope, offset = half_terms(moments_ref, params_ref, facts.row_count())
    slot, half = piece // 2, piece % 2
    limit = facts.half_limit(slot, half)

    def work(part, carry):
        start = part * rows
        inside = lax.broadcasted_iota(jnp.int32, (rows, 1), 0) < limit - start
        for lanes in column_slices(width):
            values = arrived_ref[(half * per_half + part) * slots + slot, :, lanes]
            half_pre = values.astype(jnp.float32) * slope[:, lanes] + offset[:, lanes]
            found = jnp.where(inside, gelu_slope(half_pre, *bent(half_pre)), 0.0)
            slope_ref[pl.ds(pl.multiple_of(start, rows), rows), lanes] = found
        return carry

    lax.fori_loop(0, per_half, work, 0)


def entry_slope(facts, arrived, moments, params, slots, windows, piece):
    width = arrived.shape[2]
    return kernel_call(
        functools.partial(slope_body, slots, windows, piece),
        "entry_slope",
        (facts, arrived, moments, params),
        [SMEM, VMEM, VMEM, VMEM],
        shape((HALF_WINDOW_ROWS, width), jnp.float32),
        VMEM,
        flops=25 * HALF_WINDOW_ROWS * width,
        bytes_moved=6 * HALF_WINDOW_ROWS * width,
    )


def block_moments(values, inside, count):
    block_sum = jnp.sum(jnp.where(inside, values, 0.0), axis=0, keepdims=True)
    deviation = jnp.where(inside, values - block_sum / jnp.maximum(count, 1.0), 0.0)
    return block_sum, jnp.sum(deviation * deviation, axis=0, keepdims=True), count


def convolve_body(slots, windows, facts_ref, act_ref, weight_ref, out_ref, moments_ref, wide):
    facts = Facts(facts_ref, windows, slots)
    pieces, rows, inner = out_ref.shape
    tiles = inner // LANES
    for tile in range(3 * tiles):
        wide[tile, 0:PAD] = jnp.zeros((PAD, LANES), jnp.float32)
        wide[tile, PAD + rows : PADDED_ROWS] = jnp.zeros((PAD, LANES), jnp.float32)
    moments_ref[...] = jnp.zeros_like(moments_ref)
    below, above = PAD - DILATION_STEP, PAD + DILATION_STEP

    def work(piece, carry):
        product = jnp.dot(act_ref[piece], weight_ref[...], preferred_element_type=jnp.float32)
        for tile, lanes in enumerate(column_slices(3 * inner)):
            wide[tile, PAD : PAD + rows] = product[:, lanes]
        half = piece % 2
        limit = facts.half_limit(piece // 2, half)
        start = half * STRIP
        row = lax.broadcasted_iota(jnp.int32, (rows, 1), 0)
        end = jnp.minimum(limit, rows - STRIP + start)
        inside = jnp.logical_and(row >= start, row < end)
        count = jnp.maximum(end - start, 0).astype(jnp.float32)
        for tile, lanes in enumerate(column_slices(inner)):
            out = (
                wide[tiles + tile, PAD : PAD + rows]
                + wide[tile, below : below + rows]
                + wide[2 * tiles + tile, above : above + rows]
            )
            out_ref[piece, :, lanes] = out
            held = (moments_ref[0:1, lanes], moments_ref[1:2, lanes], moments_ref[2:3, lanes])
            moments_ref[0:1, lanes], moments_ref[1:2, lanes], moments_ref[2:3, lanes] = merged(
                held, block_moments(out, inside, count)
            )
        return carry

    lax.fori_loop(0, pieces, work, 0)


def convolve(facts, act, weight, slots, windows):
    pieces, rows, width = act.shape
    inner = weight.shape[1] // 3
    return kernel_call(
        functools.partial(convolve_body, slots, windows),
        "convolve",
        (facts, act, weight),
        [SMEM, VMEM, VMEM],
        [shape((pieces, rows, inner), jnp.float32), shape((3, inner), jnp.float32)],
        [VMEM, VMEM],
        [pltpu.VMEM((3 * inner // LANES, PADDED_ROWS, LANES), jnp.float32)],
        flops=6 * pieces * rows * width * inner,
        bytes_moved=pieces * rows * (width * 2 + inner * 4),
    )


def join_body(
    slots, windows, facts_ref, out_ref, border_ref, weight_ref, held_ref, strip_ref, moments_ref,
    moved,
):
    facts = Facts(facts_ref, windows, slots)
    pieces, rows, inner = out_ref.shape
    found = (held_ref[0:1], held_ref[1:2], held_ref[2:3])
    gap = STRIP - DILATION_STEP
    skip = BORDER - DILATION_STEP
    for piece in range(pieces):
        half = piece % 2
        other = piece + 1 - 2 * half
        moved[...] = jnp.zeros_like(moved)
        if half == 0:
            moved[gap : gap + BORDER] = jnp.dot(
                border_ref[other], weight_ref[:, 2 * inner :], preferred_element_type=jnp.float32
            )
            strip = out_ref[piece, rows - STRIP : rows] + moved[0:STRIP]
        else:
            moved[0:BORDER] = jnp.dot(
                border_ref[other], weight_ref[:, :inner], preferred_element_type=jnp.float32
            )
            strip = out_ref[piece, 0:STRIP] + moved[skip : skip + STRIP]
        strip_ref[piece] = strip
        limit = facts.half_limit(piece // 2, half) - (1 - half) * (rows - STRIP)
        count = jnp.clip(limit, 0, STRIP)
        inside = lax.broadcasted_iota(jnp.int32, (STRIP, 1), 0) < count
        found = merged(found, block_moments(strip, inside, count.astype(jnp.float32)))
    for number, value in enumerate(found):
        moments_ref[number : number + 1] = jnp.broadcast_to(value, (1, inner))


def join(facts, out, border, weight, held, slots, windows):
    pieces, rows, inner = out.shape
    return kernel_call(
        functools.partial(join_body, slots, windows),
        "join_halves",
        (facts, out, border, weight, held),
        [SMEM, VMEM, VMEM, VMEM, VMEM],
        [shape((pieces, STRIP, inner), jnp.float32), shape((3, inner), jnp.float32)],
        [VMEM, VMEM],
        [pltpu.VMEM((2 * STRIP, inner), jnp.float32)],
        flops=2 * pieces * BORDER * border.shape[2] * inner,
        bytes_moved=pieces * STRIP * inner * 8,
    )


def middle_body(
    slots, windows, facts_ref, out_ref, strip_ref, moments_ref, params_ref, grad_ref,
    act_ref, slope_ref, norm_ref, sums_ref,
):
    facts = Facts(facts_ref, windows, slots)
    pieces, rows, inner = out_ref.shape
    centre, scale, _, _ = norm_terms(moments_ref, params_ref, facts.row_count())
    gain, offset = 0.5 * params_ref[0:1], 0.5 * params_ref[1:2]
    sums_ref[...] = jnp.zeros_like(sums_ref)

    def chunk(piece, start, values):
        size = values.shape[0]
        limit = facts.half_limit(piece // 2, piece % 2)
        inside = lax.broadcasted_iota(jnp.int32, (size, 1), 0) < limit - start
        here = pl.ds(start, size)
        for lanes in column_slices(inner):
            norm = (values[:, lanes] - centre[:, lanes]) * scale[:, lanes]
            half_pre = norm * gain[:, lanes] + offset[:, lanes]
            bend, square = bent(half_pre)
            act = jnp.where(inside, half_pre + half_pre * bend, 0.0)
            act_ref[piece, here, lanes] = act.astype(jnp.bfloat16)
            grad = grad_ref[piece, here, lanes] * gelu_slope(half_pre, bend, square)
            grad = jnp.where(inside, grad, 0.0)
            slope_ref[piece, here, lanes] = grad
            norm_ref[piece, here, lanes] = norm
            sums_ref[0:1, lanes] = sums_ref[0:1, lanes] + jnp.sum(
                grad * norm, axis=0, keepdims=True
            )
            sums_ref[1:2, lanes] = sums_ref[1:2, lanes] + jnp.sum(grad, axis=0, keepdims=True)

    size = 2 * STRIP
    steps = rows // size - 1

    def main(step, carry):
        piece = step // steps
        start = pl.multiple_of((step % steps + piece % 2) * size, size)
        chunk(piece, start, out_ref[piece, pl.ds(start, size), :])
        return carry

    lax.fori_loop(0, pieces * steps, main, 0)

    def edge(slot, carry):
        low, high = 2 * slot, 2 * slot + 1
        start = rows - size
        values = jnp.concatenate([out_ref[low, start : start + STRIP], strip_ref[low]], axis=0)
        chunk(low, start, values)
        chunk(high, 0, jnp.concatenate([strip_ref[high], out_ref[high, STRIP:size]], axis=0))
        return carry

    lax.fori_loop(0, slots, edge, 0)


def middle(facts, out, strip, moments, params, grad, slots, windows):
    dims = out.shape
    return kernel_call(
        functools.partial(middle_body, slots, windows),
        "middle_norm",
        (facts, out, strip, moments, params, grad),
        [SMEM] + [VMEM] * 5,
        [
            shape(dims, jnp.bfloat16),
            shape(dims, jnp.float32),
            shape(dims, jnp.float32),
            shape((2, dims[2]), jnp.float32),
        ],
        [VMEM] * 4,
        flops=40 * out.size,
        bytes_moved=18 * out.size,
    )


def middle_grad_body(
    slots, windows, facts_ref, grad_ref, norm_ref, moments_ref, params_ref, sums_ref,
    padded_ref, border_ref, centre_ref,
):
    facts = Facts(facts_ref, windows, slots)
    pieces, rows, inner = grad_ref.shape
    rows_total = facts.row_count()
    _, _, slope, _ = norm_terms(moments_ref, params_ref, rows_total)
    level, tilt = sums_ref[1:2] / rows_total, sums_ref[0:1] / rows_total
    tiles = inner // LANES
    for piece in range(pieces):
        for tile in range(tiles):
            padded_ref[piece, tile, 0:PAD] = jnp.zeros((PAD, LANES), jnp.float32)
            padded_ref[piece, tile, PAD + rows : PADDED_ROWS] = jnp.zeros(
                (PAD, LANES), jnp.float32
            )
    size = 2 * STRIP

    def work(step, carry):
        piece, part = step // (rows // size), step % (rows // size)
        start = pl.multiple_of(part * size, size)
        limit = facts.half_limit(piece // 2, piece % 2)
        inside = lax.broadcasted_iota(jnp.int32, (size, 1), 0) < limit - start
        for tile, lanes in enumerate(column_slices(inner)):
            norm = norm_ref[piece, pl.ds(start, size), lanes]
            grad = slope[:, lanes] * (
                grad_ref[piece, pl.ds(start, size), lanes]
                - (level[:, lanes] + norm * tilt[:, lanes])
            )
            low = jnp.where(inside, grad, 0.0).astype(jnp.bfloat16)
            centre_ref[piece, pl.ds(start, size), lanes] = low
            padded_ref[piece, tile, pl.ds(pl.multiple_of(start + PAD, 8), size), :] = low.astype(
                jnp.float32
            )
        return carry

    lax.fori_loop(0, pieces * (rows // size), work, 0)
    for piece in range(pieces):
        start = PAD + (0 if piece % 2 else rows - BORDER)
        for tile, lanes in enumerate(column_slices(inner)):
            border_ref[piece, :, lanes] = padded_ref[piece, tile, start : start + BORDER].astype(
                jnp.bfloat16
            )


def middle_grad(facts, grad, norm, moments, params, sums, slots, windows):
    pieces, _, inner = grad.shape
    return kernel_call(
        functools.partial(middle_grad_body, slots, windows),
        "middle_grad",
        (facts, grad, norm, moments, params, sums),
        [SMEM] + [VMEM] * 5,
        [
            shape((pieces, inner // LANES, PADDED_ROWS, LANES), jnp.float32),
            shape((pieces, BORDER, inner), jnp.bfloat16),
            shape(grad.shape, jnp.bfloat16),
        ],
        [VMEM, VMEM, VMEM],
        flops=8 * grad.size,
        bytes_moved=12 * grad.size,
    )


def output_body(
    slots, windows, facts_ref, act_ref, weight_ref, arrived_ref, params_ref, out_ref
):
    source, slot = pl.program_id(0), pl.program_id(1)
    rows = out_ref.shape[0]
    facts = Facts(facts_ref, windows, slots)
    per_half = HALF_WINDOW_ROWS // rows
    half, start = source // per_half, (source % per_half) * rows
    inside = lax.broadcasted_iota(jnp.int32, (rows, 1), 0) < facts.half_limit(slot, half) - start
    mixed = jnp.dot(act_ref[...], weight_ref[...], preferred_element_type=jnp.float32)
    block = arrived_ref[0].astype(jnp.float32) + mixed + params_ref[2:3]
    out_ref[...] = jnp.where(inside, block, 0.0)


def output_rows(facts, act, weight, arrived, params, slots, windows):
    blocks, rows, width = arrived.shape
    inner = act.shape[1]
    sources = blocks // slots
    place = lambda s, j: (j * sources + s, 0)
    return pl.pallas_call(
        functools.partial(output_body, slots, windows),
        grid=(sources, slots),
        in_specs=[
            SMEM,
            pl.BlockSpec((rows, inner), place),
            pl.BlockSpec((inner, width), lambda s, j: (0, 0)),
            pl.BlockSpec((1, rows, width), lambda s, j: (s * slots + j, 0, 0)),
            pl.BlockSpec((3, width), lambda s, j: (0, 0)),
        ],
        out_specs=pl.BlockSpec((rows, width), place),
        out_shape=shape((blocks * rows, width), jnp.float32),
        compiler_params=pltpu.CompilerParams(vmem_limit_bytes=16 << 20),
        cost_estimate=pl.CostEstimate(
            flops=2 * act.size * width * 7, bytes_accessed=8 * arrived.size * 7, transcendentals=0
        ),
        name="output_rows",
    )(facts, act, weight, arrived, params)


def entry_grad_body(slots, windows, facts_ref, padded_ref, border_ref, weight_ref, *refs):
    pieces = 2 * slots
    slope_refs, refs = refs[:pieces], refs[pieces:]
    (arrived_ref, block_ref, moments_ref, params_ref, bias_ref), refs = refs[:5], refs[5:]
    sent_refs, (kept_ref, sums_ref, wide, packed, taps_ref, departures, kept) = (
        refs[:slots],
        refs[slots:],
    )
    facts = Facts(facts_ref, windows, slots)
    _, sources, rows, width = packed.shape
    tiles = padded_ref.shape[1]
    per_half = HALF_WINDOW_ROWS // rows
    centre, scale, slope, _ = norm_terms(moments_ref, params_ref, facts.row_count())
    skip = BORDER - DILATION_STEP
    sums_ref[...] = jnp.zeros_like(sums_ref)

    def departure(slot, source):
        return pltpu.make_async_copy(
            packed.at[slot, source], sent_refs[slot].at[source], departures.at[slot, source]
        )

    def keeping(piece):
        return pltpu.make_async_copy(
            taps_ref.at[piece, :, pl.ds(0, kept_ref.shape[2])], kept_ref.at[piece], kept.at[piece]
        )

    def lay_taps(piece):
        half, turn = piece % 2, piece % 2
        for tile, lanes in enumerate(column_slices(tiles * LANES)):
            border = border_ref[piece + 1 - 2 * half, :, lanes].astype(jnp.float32)
            wide[turn, tile] = padded_ref[piece, tile]
            if half == 0:
                end = PAD + HALF_WINDOW_ROWS
                wide[turn, tile, end : end + DILATION_STEP] = border[0:DILATION_STEP]
            else:
                wide[turn, tile, PAD - DILATION_STEP : PAD] = border[skip:BORDER]
            for number, tap in enumerate((0, 2, 1)):
                start = PAD - (tap - 1) * DILATION_STEP
                first = (number * tiles + tile) * LANES
                taps_ref[piece, :, first : first + LANES] = wide[
                    turn, tile, start : start + HALF_WINDOW_ROWS
                ].astype(jnp.bfloat16)

    lay_taps(0)
    for piece in range(pieces):
        slot, half = piece // 2, piece % 2
        if piece + 1 < pieces:
            lay_taps(piece + 1)
        for column in range(0, width, 2 * LANES):
            grad = jnp.dot(
                taps_ref[piece],
                weight_ref[:, column : column + 2 * LANES],
                preferred_element_type=jnp.float32,
            )
            for part in range(per_half):
                source = half * per_half + part
                here = slice(part * rows, (part + 1) * rows)
                for start in (column, column + LANES):
                    lanes = slice(start, start + LANES)
                    pre = grad[here, start - column : start - column + LANES]
                    pre = pre * slope_refs[piece][here, lanes]
                    values = arrived_ref[source * slots + slot, :, lanes].astype(jnp.float32)
                    sums_ref[0:1, lanes] = sums_ref[0:1, lanes] + jnp.sum(
                        pre * values, axis=0, keepdims=True
                    )
                    sums_ref[1:2, lanes] = sums_ref[1:2, lanes] + jnp.sum(
                        pre, axis=0, keepdims=True
                    )
                    block = block_ref[piece, here, lanes].astype(jnp.float32)
                    packed[slot, source, :, lanes] = (pre * slope[:, lanes] + block).astype(
                        jnp.bfloat16
                    )
        for part in range(per_half):
            departure(slot, half * per_half + part).start()
        keeping(piece).start()
    sums_ref[0:1] = (sums_ref[0:1] - centre * sums_ref[1:2]) * scale
    sums_ref[2:3] = bias_ref[...]
    for piece in range(pieces):
        keeping(piece).wait()
    for slot in range(slots):
        for source in range(sources):
            departure(slot, source).wait()


def entry_grad(
    facts, padded, border, weight, slopes, arrived, block, moments, params, bias, slots, windows
):
    blocks, rows, width = arrived.shape
    inner, sources = border.shape[2], blocks // slots
    pieces = 2 * slots
    inputs = [facts, padded, border, weight, *slopes, arrived, block, moments, params, bias]
    taps_shape = (HALF_WINDOW_ROWS, 3 * inner)
    return kernel_call(
        functools.partial(entry_grad_body, slots, windows),
        "entry_grad",
        inputs,
        [SMEM] + [VMEM] * (len(inputs) - 1),
        [
            *[pltpu.HBM((sources, rows, width), jnp.bfloat16)] * slots,
            pltpu.HBM((pieces, HALF_WINDOW_ROWS, 2 * inner), jnp.bfloat16),
            shape((3, width), jnp.float32),
        ],
        [HBM] * (slots + 1) + [VMEM],
        [
            pltpu.VMEM((2, inner // LANES, PADDED_ROWS, LANES), jnp.float32),
            pltpu.VMEM((slots, sources, rows, width), jnp.bfloat16),
            pltpu.VMEM((pieces, *taps_shape), jnp.bfloat16),
            pltpu.SemaphoreType.DMA((slots, sources)),
            pltpu.SemaphoreType.DMA((pieces,)),
        ],
        flops=2 * pieces * HALF_WINDOW_ROWS * 3 * inner * width,
        bytes_moved=pieces * HALF_WINDOW_ROWS * (width * 10 + inner * 10),
        grant=16 << 20,
    )


def flat_mask(bits):
    return sum(mask * (lax.axis_size("seq") if axis == "grp" else 1) for axis, mask in bits)


def from_flat_partner(block, mask):
    count = lax.axis_size("grp") * lax.axis_size("seq")
    return lax.ppermute(
        block, ("grp", "seq"), [(place, place ^ mask) for place in range(count)]
    )


def bit_of(axis, mask):
    return (lax.axis_index(axis) // mask) % 2


def square_phases():
    steps = exchange_steps()[1:]
    outer = [step for step in steps if step[0] == "grp"]
    inner = [step for step in steps if step[0] == "seq"]
    ordered = []
    while outer and inner:
        ordered += [outer.pop(0), inner.pop(0)]
    ordered += outer + inner
    return [ordered[start : start + 2] for start in range(0, len(ordered), 2)]


def phase_place(phase):
    return sum(bit_of(*step) * 2**number for number, step in enumerate(phase))


def phase_parts(phase):
    parts = 2 ** len(phase)
    masks = [
        flat_mask([step for number, step in enumerate(phase) if part >> number & 1])
        for part in range(parts)
    ]
    return parts, masks


def exchange_parts(parts, phase):
    _, masks = phase_parts(phase)
    return [from_flat_partner(part, mask) for part, mask in zip(parts, masks[1:])]


def place_in(facts_ref, phase):
    bits = [
        (facts_ref[0 if axis == "grp" else 1] // mask) % 2 * 2**number
        for number, (axis, mask) in enumerate(phase)
    ]
    return sum(bits)


def encoded(sums, rows_ref):
    count = sums.shape[0]
    high = sums.astype(jnp.bfloat16).astype(jnp.float32)
    low = (sums - high).astype(jnp.bfloat16).astype(jnp.float32)
    rows_ref[...] = jnp.zeros_like(rows_ref)
    rows_ref[0:count] = high
    rows_ref[count : 2 * count] = low
    return rows_ref[...].astype(jnp.bfloat16), high + low


def decoded(found_ref, count, rows_ref):
    rows_ref[...] = found_ref[found_ref.shape[0] - EXTRA :, :].astype(jnp.float32)
    return rows_ref[0:count] + rows_ref[count : 2 * count]


def pair_sum(values):
    while len(values) > 1:
        values = [values[i] + values[i + 1] for i in range(0, len(values), 2)]
    return values[0]


def other_half_body(
    facts_ref, sides_ref, centre_ref, pointwise_ref, sums_ref, sent_ref, held_ref, rows_ref
):
    width, inner = pointwise_ref.shape
    sent_ref[width:, :], held_ref[...] = encoded(sums_ref[...], rows_ref)

    @pl.when(facts_ref[0] % 2 == 0)
    def _():
        sent_ref[:width, :inner] = sides_ref[:, inner:].astype(jnp.bfloat16)
        sent_ref[:width, inner:] = pointwise_ref[...].astype(jnp.bfloat16)

    @pl.when(facts_ref[0] % 2 == 1)
    def _():
        sent_ref[:width, :inner] = sides_ref[:, :inner].astype(jnp.bfloat16)
        sent_ref[:width, inner:] = centre_ref[...].astype(jnp.bfloat16)


def other_half(facts, sides, centre, pointwise, sums):
    width, inner = pointwise.shape
    return kernel_call(
        other_half_body,
        "other_half",
        (facts, sides, centre, pointwise, sums),
        [SMEM] + [VMEM] * 4,
        [shape((width + EXTRA, 2 * inner), jnp.bfloat16), shape(sums.shape, jnp.float32)],
        [VMEM, VMEM],
        [pltpu.VMEM((EXTRA, 2 * inner), jnp.float32)],
        flops=2 * width * inner,
        bytes_moved=12 * width * inner,
        grant=10 << 20,
    )


def part_rows(mine, part, rows):
    return pl.ds(pl.multiple_of(jnp.bitwise_xor(mine, part) * rows, rows), rows)


def own_half_body(
    phase, facts_ref, sides_ref, centre_ref, pointwise_ref, sums_ref, other_ref, total_ref, *refs
):
    part_refs, rows_ref = refs[:-1], refs[-1]
    inner = pointwise_ref.shape[1]
    rows = part_refs[0].shape[0]
    mine = place_in(facts_ref, phase)
    sums = sums_ref[...] + decoded(other_ref, sums_ref.shape[0], rows_ref)
    extra, total_ref[...] = encoded(sums, rows_ref)
    for part_ref in part_refs[1:]:
        part_ref[rows:, :] = extra

    def write(low, high):
        for part, part_ref in enumerate(part_refs):
            here = part_rows(mine, part, rows)
            for piece, lanes in ((low, slice(0, inner)), (high, slice(inner, 2 * inner))):
                value = piece(here) + other_ref[here, lanes].astype(jnp.float32)
                part_ref[:rows, lanes] = value.astype(part_ref.dtype)

    @pl.when(facts_ref[0] % 2 == 0)
    def _():
        write(
            lambda here: sides_ref[here, :inner],
            lambda here: centre_ref[here, :],
        )

    @pl.when(facts_ref[0] % 2 == 1)
    def _():
        write(lambda here: sides_ref[here, inner:], lambda here: pointwise_ref[here, :])


def part_shapes(sums, rows, columns, phase):
    parts = 2 ** len(phase)
    rows //= parts
    return [
        shape(sums.shape, jnp.float32),
        shape((rows, columns), jnp.float32),
        *[shape((rows + EXTRA, columns), jnp.bfloat16)] * (parts - 1),
    ]


def own_half(facts, sides, centre, pointwise, sums, other, phase):
    width, inner = pointwise.shape
    outputs = part_shapes(sums, width, 2 * inner, phase)
    return kernel_call(
        functools.partial(own_half_body, phase),
        "own_half",
        (facts, sides, centre, pointwise, sums, other),
        [SMEM] + [VMEM] * 5,
        outputs,
        [VMEM] * len(outputs),
        [pltpu.VMEM((EXTRA, 2 * inner), jnp.float32)],
        flops=2 * width * inner,
        bytes_moved=20 * width * inner,
        grant=12 << 20,
    )


def next_parts_body(count, phase, facts_ref, kept_ref, sums_ref, *refs):
    found_refs, total_ref, part_refs, rows_ref = (
        refs[:count],
        refs[count],
        refs[count + 1 : -1],
        refs[-1],
    )
    sums = pair_sum(
        [sums_ref[...]] + [decoded(ref, sums_ref.shape[0], rows_ref) for ref in found_refs]
    )
    total_ref[...] = sums
    rows = part_refs[0].shape[0]
    if phase:
        mine = place_in(facts_ref, phase)
        extra, total_ref[...] = encoded(sums, rows_ref)
        for part_ref in part_refs[1:]:
            part_ref[rows:, :] = extra
    for part, part_ref in enumerate(part_refs):
        here = part_rows(mine, part, rows) if phase else slice(0, rows)
        value = kept_ref[here, :]
        for found_ref in found_refs:
            value = value + found_ref[here, :].astype(jnp.float32)
        part_ref[:rows, :] = value.astype(part_ref.dtype)


def plain_parts(kept, sums, found, phase):
    rows, count = kept.shape[0], sums.shape[0]
    totals = [sums]
    for block in found:
        kept = kept + block[:rows].astype(jnp.float32)
        tail = block[rows:].astype(jnp.float32)
        totals.append(tail[:count] + tail[count : 2 * count])
    sums = pair_sum(totals)
    if not phase:
        return [sums, kept.astype(jnp.bfloat16)]
    high = lax.reduce_precision(sums, 8, 7)
    low = lax.reduce_precision(sums - high, 8, 7)
    rest = jnp.zeros((EXTRA - 2 * count, sums.shape[1]), jnp.float32)
    extra, sums = jnp.concatenate([high, low, rest]).astype(jnp.bfloat16), high + low
    parts = 2 ** len(phase)
    mine, rows = phase_place(phase), rows // parts
    slices = [
        lax.dynamic_slice_in_dim(kept, jnp.bitwise_xor(mine, part) * rows, rows)
        for part in range(parts)
    ]
    return [sums, slices[0]] + [
        jnp.concatenate([block.astype(jnp.bfloat16), extra]) for block in slices[1:]
    ]


def next_parts(facts, kept, sums, found, phase):
    rows, columns = kept.shape
    if rows // 2 ** len(phase) % 16:
        return plain_parts(kept, sums, found, phase)
    outputs = part_shapes(sums, rows, columns, phase)
    if not phase:
        outputs = [outputs[0], shape((rows, columns), jnp.bfloat16)]
    return kernel_call(
        functools.partial(next_parts_body, len(found), phase),
        "next_parts",
        (facts, kept, sums, *found),
        [SMEM] + [VMEM] * (2 + len(found)),
        outputs,
        [VMEM] * len(outputs),
        [pltpu.VMEM((EXTRA, columns), jnp.float32)],
        flops=4 * rows * columns,
        bytes_moved=16 * rows * columns,
    )


def gather_parts(buffer, phase):
    _, masks = phase_parts(phase)
    return [buffer] + [from_flat_partner(buffer, mask) for mask in masks[1:]]


def in_order(found, owners):
    parts = len(found)
    orders = [
        jnp.concatenate([found[place ^ own] for place in range(parts)], axis=0)
        for own in range(parts)
    ]
    result = orders[0]
    for own in range(1, parts):
        result = jnp.where(owners[own], orders[own], result)
    return result


def finish_body(own, facts_ref, half_ref, *refs):
    dilated_ref, pointwise_ref, held, turned, copies = refs[-5:]
    inner = dilated_ref.shape[2]

    def write(places):
        for number, place in enumerate(places):
            held[number] = half_ref[:, number * inner : (number + 1) * inner].astype(jnp.float32)
            pltpu.make_async_copy(
                held.at[number], dilated_ref.at[place], copies.at[number]
            ).start()
        if len(places) == 1:
            turned[...] = half_ref[:, inner:].astype(jnp.float32).T
            pltpu.make_async_copy(turned, pointwise_ref, copies.at[1]).start()
            pltpu.make_async_copy(turned, pointwise_ref, copies.at[1]).wait()
        for number, place in enumerate(places):
            pltpu.make_async_copy(
                held.at[number], dilated_ref.at[place], copies.at[number]
            ).wait()

    upper = facts_ref[0] % 2

    @pl.when(upper == 1 - own)
    def _():
        write((0, 1))

    @pl.when(upper == own)
    def _():
        write((2,))


def finish_weights(facts, half, own, begun):
    width, both = half.shape
    inner = both // 2
    inputs, specs, aliases = [facts, half], [SMEM, VMEM], {}
    if begun is not None:
        aliases = {2: 0, 3: 1}
        inputs += [in_hbm(array) for array in begun]
        specs += [HBM, HBM]
    return pl.pallas_call(
        functools.partial(finish_body, own),
        in_specs=specs,
        out_specs=[HBM, HBM],
        out_shape=[
            pltpu.HBM((3, width, inner), jnp.float32),
            pltpu.HBM((inner, width), jnp.float32),
        ],
        input_output_aliases=aliases,
        scratch_shapes=[
            pltpu.VMEM((2, width, inner), jnp.float32),
            pltpu.VMEM((inner, width), jnp.float32),
            pltpu.SemaphoreType.DMA((2,)),
        ],
        compiler_params=pltpu.CompilerParams(vmem_limit_bytes=12 << 20),
        cost_estimate=pl.CostEstimate(
            flops=width * both, bytes_accessed=6 * width * both, transcendentals=0
        ),
        name="finish_weights",
    )(*inputs)


def per_device(
    signal,
    entry_gain,
    entry_shift,
    dilated_kernel,
    middle_gain,
    middle_shift,
    pointwise_kernel,
    pointwise_bias,
    lengths,
    assignment,
    cotangent,
):
    seq_count = lax.axis_size("seq")
    windows, segment, width = signal.shape
    inner = pointwise_kernel.shape[0]
    slots = windows // seq_count
    rows = segment // 2
    pieces = 2 * slots
    places = jnp.stack([lax.axis_index("grp"), lax.axis_index("seq"), jnp.int32(seq_count)])
    facts = jnp.concatenate([places.astype(jnp.int32), assignment[0], lengths])
    entry_params = jnp.stack([entry_gain, entry_shift, pointwise_bias])
    middle_params = jnp.stack([middle_gain, middle_shift])

    outgoing, entry_local = pool(assignment, lengths, signal, slots)
    arrived = lax.all_to_all(outgoing, "seq", split_axis=0, concat_axis=0, tiled=True)

    late_facts, _ = lax.optimization_barrier((facts, entry_local))
    first_chosen = first_marks(late_facts, signal, slots)
    wide_kernel, back_kernel, pointwise_low = prepare_weights(dilated_kernel, pointwise_kernel)
    grad_block, grad_middle, bias_part = prepare(
        facts, cotangent, pointwise_low, slots, windows
    )
    entry_moments, prepared = total_moments(
        entry_local,
        [first_chosen, grad_block, grad_middle, wide_kernel, back_kernel, pointwise_low],
    )
    first_chosen, grad_block, grad_middle, wide_kernel, back_kernel, pointwise_low = prepared
    phases = square_phases()
    owners = [
        [phase_place(phase) == own for own in range(2 ** len(phase))] for phase in phases
    ]
    first_axis, first_mask = exchange_steps()[0]
    upper = bit_of(first_axis, first_mask) == 1
    (
        arrived,
        first_chosen,
        grad_block,
        grad_middle,
        wide_kernel,
        back_kernel,
        pointwise_low,
        owners,
        upper,
        middle_params,
        facts,
    ) = lax.optimization_barrier(
        (
            arrived,
            first_chosen,
            grad_block,
            grad_middle,
            wide_kernel,
            back_kernel,
            pointwise_low,
            owners,
            upper,
            middle_params,
            facts,
        )
    )

    act, act_border = activate(facts, arrived, entry_moments, entry_params, slots, windows)
    act_border = from_partner(act_border, "seq", 1)
    dilated, held_moments = convolve(facts, act, wide_kernel, slots, windows)
    strip, middle_moments = join(
        facts, dilated, act_border, wide_kernel, held_moments, slots, windows
    )
    slopes = []
    for number, (axis, mask) in enumerate(exchange_steps()):
        other = from_partner(middle_moments, axis, mask)
        if number and len(slopes) < pieces:
            tied, middle_moments = lax.optimization_barrier((arrived, middle_moments))
            found = entry_slope(
                facts, tied, entry_moments, entry_params, slots, windows, len(slopes)
            )
            other, found = lax.optimization_barrier((other, found))
            slopes.append(found)
        middle_moments = jnp.concatenate(
            merged(
                (middle_moments[0:1], middle_moments[1:2], middle_moments[2:3]),
                (other[0:1], other[1:2], other[2:3]),
            ),
            axis=0,
        )
    while len(slopes) < pieces:
        slopes.append(
            entry_slope(facts, arrived, entry_moments, entry_params, slots, windows, len(slopes))
        )
    middle_act, middle_slope, middle_norm, middle_sums = middle(
        facts,
        dilated,
        strip,
        middle_moments,
        middle_params,
        grad_middle.reshape(pieces, HALF_WINDOW_ROWS, inner),
        slots,
        windows,
    )
    flat_act = middle_act.reshape(-1, inner)
    for number, (axis, mask) in enumerate(exchange_steps()):
        other = from_partner(middle_sums, axis, mask)
        if number == 1:
            tied, middle_sums = lax.optimization_barrier((flat_act, middle_sums))
            pointwise_part = jnp.einsum(
                "rd,rf->df", grad_block, tied, preferred_element_type=jnp.float32
            )
            other, pointwise_part = lax.optimization_barrier((other, pointwise_part))
        middle_sums = middle_sums + other
    padded, grad_border, grad_centre = middle_grad(
        facts, middle_slope, middle_norm, middle_moments, middle_params, middle_sums, slots, windows
    )
    centre_part = jnp.einsum("hrc,hrf->cf", act, grad_centre, preferred_element_type=jnp.float32)
    grad_border = from_partner(grad_border, "seq", 1)
    grad_border, centre_part = lax.optimization_barrier((grad_border, centre_part))
    block_pieces = grad_block.reshape(pieces, HALF_WINDOW_ROWS, width)
    def send_back(block):
        return lax.all_to_all(block, "seq", split_axis=0, concat_axis=0, tiled=True)

    *sent, taps, entry_sums = entry_grad(
        facts, padded, grad_border, back_kernel, slopes, arrived, block_pieces, entry_moments,
        entry_params, bias_part, slots, windows,
    )
    tied = lax.optimization_barrier((*sent, entry_sums))
    sent, entry_sums = list(tied[:-1]), tied[-1]
    returned = [send_back(sent[0])]
    side_parts = jnp.einsum("hrc,hrf->cf", act, taps, preferred_element_type=jnp.float32)
    other, entry_sums = other_half(facts, side_parts, centre_part, pointwise_part, entry_sums)
    other = from_partner(other, first_axis, first_mask)
    entry_sums, *parts = own_half(
        facts, side_parts, centre_part, pointwise_part, entry_sums, other, phases[0]
    )
    for held, phase in zip(phases, phases[1:] + [[]]):
        found = exchange_parts(parts[1:], held)
        entry_sums, *parts = next_parts(facts, parts[0], entry_sums, found, phase)
    buffer, signal_gradient, activations = parts[0], None, None
    for number, phase in reversed(list(enumerate(phases))):
        found = gather_parts(buffer, phase)
        if number == len(phases) - 1:
            found[1], flat_act, entry_sums, *later = lax.optimization_barrier(
                (found[1], flat_act, entry_sums, *sent[1:])
            )
            returned += [send_back(block) for block in later]
        if number == 0:
            signal_gradient = unpool(
                facts, returned[0], outgoing, first_chosen, entry_moments, entry_sums,
                entry_params, slots, 0, None,
            )
            activations = output_rows(
                facts, flat_act, pointwise_low, arrived, entry_params, slots, windows
            )
            signal_gradient, middle_sums = lax.optimization_barrier((signal_gradient, middle_sums))
            vectors = [entry_sums[0], entry_sums[1], middle_sums[0], middle_sums[1], entry_sums[2]]
            tied = lax.optimization_barrier((signal_gradient, activations, *vectors, *found))
            signal_gradient, activations, vectors, found = tied[0], tied[1], tied[2:7], tied[7:]
        buffer = in_order(found, owners[number])
    other = from_partner(buffer, first_axis, first_mask)
    begun = finish_weights(facts, buffer, 1, None)
    other, *begun = lax.optimization_barrier((other, *begun))
    dilated_kernel_gradient, pointwise_kernel_gradient = finish_weights(facts, other, 0, begun)
    for slot in range(1, slots):
        signal_gradient = unpool(
            facts, returned[slot], outgoing, first_chosen, entry_moments, entry_sums,
            entry_params, slots, slot, signal_gradient,
        )
    return (
        activations,
        signal_gradient,
        vectors[0],
        vectors[1],
        dilated_kernel_gradient,
        vectors[2],
        vectors[3],
        pointwise_kernel_gradient,
        vectors[4],
    )


def solution(mesh):
    return jax.shard_map(
        per_device,
        mesh=mesh,
        in_specs=(
            P("grp", "seq", None),
            P(),
            P(),
            P(),
            P(),
            P(),
            P(),
            P(),
            P(),
            P("grp", None),
            P(("grp", "seq"), None),
        ),
        out_specs=(
            P(("grp", "seq"), None),
            P("grp", "seq", None),
            P(),
            P(),
            P(),
            P(),
            P(),
            P(),
            P(),
        ),
        check_vma=False,
    )
```

```python
import functools
import math

import jax
import jax.numpy as jnp
from jax import lax
from jax.experimental import pallas as pl
from jax.experimental.pallas import tpu as pltpu
from jax.sharding import PartitionSpec as P

DILATION_STEP = 38
WINDOW_SPAN = 1024
HALF_WINDOW_ROWS = 512


EPSILON = 0.001

LANES = 128
BORDER = 48
STRIP = 64
PAD = 40
PADDED_ROWS = HALF_WINDOW_ROWS + 2 * PAD
EXTRA = 8
GELU_SLOPE = math.sqrt(2.0 / math.pi)
GELU_CUBE = 0.044715

VMEM = pl.BlockSpec(memory_space=pltpu.VMEM)
SMEM = pl.BlockSpec(memory_space=pltpu.SMEM)
HBM = pl.BlockSpec(memory_space=pltpu.HBM)


def from_partner(block, axis, mask):
    count = lax.axis_size(axis)
    return lax.ppermute(block, axis, [(place, place ^ mask) for place in range(count)])


def exchange_steps():
    steps = []
    for axis in ("grp", "seq"):
        mask = 1
        while mask < lax.axis_size(axis):
            steps.append((axis, mask))
            mask *= 2
    return steps


def total(values):
    for axis, mask in exchange_steps():
        values = values + from_partner(values, axis, mask)
    return values


def merged(left, right):
    left_sum, left_spread, left_count = left
    right_sum, right_spread, right_count = right
    gap = left_sum / jnp.maximum(left_count, 1.0) - right_sum / jnp.maximum(right_count, 1.0)
    weight = left_count * right_count / jnp.maximum(left_count + right_count, 1.0)
    return (
        left_sum + right_sum,
        left_spread + right_spread + gap * gap * weight,
        left_count + right_count,
    )


def total_moments(packed, others):
    steps = exchange_steps()
    for number, (axis, mask) in enumerate(steps):
        if number == len(steps) - 1:
            packed, *others = lax.optimization_barrier((packed, *others))
        other = from_partner(packed, axis, mask)
        packed = jnp.concatenate(
            merged(
                (packed[0:1], packed[1:2], packed[2:3]), (other[0:1], other[1:2], other[2:3])
            ),
            axis=0,
        )
    return packed, others


class Facts:
    def __init__(self, ref, windows, slots):
        self.ref, self.windows, self.slots = ref, windows, slots

    def slot_window(self, slot):
        upper = (2 * self.ref[1]) // self.ref[2]
        target = jnp.bitwise_xor(slot // self.slots, upper)
        return self.ref[3 + target * self.slots + slot % self.slots]

    def length(self, window):
        return self.ref[3 + self.windows + self.ref[0] * self.windows + window]

    def slot_count(self, slot, rows):
        return jnp.clip(self.length(self.slot_window(slot)) - self.ref[1] * rows, 0, rows)

    def half_limit(self, slot, half):
        place = jnp.bitwise_xor(self.ref[1], half)
        window = self.ref[3 + place * self.slots + slot]
        return jnp.clip(self.length(window) - half * HALF_WINDOW_ROWS, 0, HALF_WINDOW_ROWS)

    def row_count(self):
        start = 3 + self.windows
        count = self.ref.shape[0] - start
        added = lax.fori_loop(0, count, lambda i, held: held + self.ref[start + i], jnp.int32(0))
        return added.astype(jnp.float32)


def kernel_call(body, name, inputs, specs, outputs, out_specs, scratch=(), flops=0, bytes_moved=0, grant=8 << 20):
    return pl.pallas_call(
        body,
        in_specs=specs,
        out_specs=out_specs,
        out_shape=outputs,
        scratch_shapes=list(scratch),
        compiler_params=pltpu.CompilerParams(vmem_limit_bytes=grant),
        cost_estimate=pl.CostEstimate(
            flops=flops, bytes_accessed=bytes_moved, transcendentals=0
        ),
        name=name,
    )(*inputs)


def shape(dims, dtype):
    return jax.ShapeDtypeStruct(dims, dtype)


def in_hbm(array):
    return pltpu.with_memory_space_constraint(array, pltpu.HBM)


def column_slices(width):
    return [slice(start, start + LANES) for start in range(0, width, LANES)]


def bin_copy(facts, signal_ref, held, arrivals, place, column):
    return pltpu.make_async_copy(
        signal_ref.at[facts.slot_window(place), :, pl.ds(column * LANES, LANES)],
        held.at[place, column],
        arrivals.at[place, column],
    )


def begin_bins(facts, signal_ref, held, arrivals):
    windows, columns = held.shape[:2]

    def begin(place, carry):
        for column in range(columns):
            bin_copy(facts, signal_ref, held, arrivals, place, column).start()
        return carry

    lax.fori_loop(0, windows, begin, 0)


def bins_of(facts, signal_ref, held, arrivals, place, rows):
    columns = held.shape[1]
    for column in range(columns):
        bin_copy(facts, signal_ref, held, arrivals, place, column).wait()
    return [
        (
            lanes,
            held[place, column, pl.ds(0, rows, stride=2), :],
            held[place, column, pl.ds(1, rows, stride=2), :],
        )
        for column, lanes in enumerate(column_slices(columns * LANES))
    ]


def finish_copies(copy_of, count):
    def finish(place, carry):
        copy_of(place).wait()
        return carry

    lax.fori_loop(0, count, finish, 0)


def pool_body(
    slots, order_ref, lengths_ref, signal_ref, pooled_ref, moments_ref,
    held, low, blocks, order, lengths, places, arrivals, departures, facts_copies,
):
    windows, columns = held.shape[:2]
    rows = low.shape[1]
    grp, seq = lax.axis_index("grp"), lax.axis_index("seq")
    upper = (2 * seq) // (windows // slots)

    def arrival(window, column):
        return pltpu.make_async_copy(
            signal_ref.at[window, :, pl.ds(column * LANES, LANES)],
            held.at[window, column],
            arrivals.at[window, column],
        )

    def departure(window):
        return pltpu.make_async_copy(
            low.at[window], pooled_ref.at[places[window]], departures.at[window]
        )

    fetches = [
        pltpu.make_async_copy(order_ref, order, facts_copies.at[0]),
        pltpu.make_async_copy(lengths_ref, lengths, facts_copies.at[1]),
    ]
    for fetch in fetches:
        fetch.start()

    def begin(window, carry):
        for column in range(columns):
            arrival(window, column).start()
        return carry

    lax.fori_loop(0, windows, begin, 0)
    moments_ref[...] = jnp.zeros_like(moments_ref)
    for fetch in fetches:
        fetch.wait()

    def note(place, carry):
        target = jnp.bitwise_xor(place // slots, upper)
        places[order[0, target * slots + place % slots]] = place
        return carry

    lax.fori_loop(0, windows, note, 0)

    def count_of(window):
        return jnp.clip(lengths[grp * windows + window] - seq * rows, 0, rows)

    def work(window, carry):
        count = count_of(window)
        inside = lax.broadcasted_iota(jnp.int32, (rows, LANES), 0) < count
        for column in range(columns):
            arrival(window, column).wait()
        for column, lanes in enumerate(column_slices(columns * LANES)):
            first_bin = held[window, column, pl.ds(0, rows, stride=2), :]
            second_bin = held[window, column, pl.ds(1, rows, stride=2), :]
            pooled = jnp.where(inside, jnp.maximum(first_bin, second_bin), 0.0)
            pooled = pooled.astype(jnp.bfloat16)
            low[window, :, lanes] = pooled
            found = block_moments(pooled.astype(jnp.float32), inside, count.astype(jnp.float32))
            blocks[window, 0:1, lanes] = found[0]
            blocks[window, 1:2, lanes] = found[1]
        departure(window).start()
        return carry

    lax.fori_loop(0, windows, work, 0)

    def join_blocks(window, carry):
        count = jnp.broadcast_to(count_of(window).astype(jnp.float32), (1, columns * LANES))
        held_moments = (moments_ref[0:1], moments_ref[1:2], moments_ref[2:3])
        moments_ref[0:1], moments_ref[1:2], moments_ref[2:3] = merged(
            held_moments, (blocks[window, 0:1], blocks[window, 1:2], count)
        )
        return carry

    lax.fori_loop(0, windows, join_blocks, 0)
    finish_copies(departure, windows)


def pool(order, lengths, signal, slots):
    windows, segment, width = signal.shape
    rows, columns = segment // 2, width // LANES
    block = (windows, rows, width)
    return kernel_call(
        functools.partial(pool_body, slots),
        "pool",
        (in_hbm(order), in_hbm(lengths), in_hbm(signal)),
        [HBM, HBM, HBM],
        [pltpu.HBM(block, jnp.bfloat16), shape((3, width), jnp.float32)],
        [HBM, VMEM],
        [
            pltpu.VMEM((windows, columns, segment, LANES), jnp.float32),
            pltpu.VMEM(block, jnp.bfloat16),
            pltpu.VMEM((windows, 2, width), jnp.float32),
            pltpu.SMEM(order.shape, jnp.int32),
            pltpu.SMEM(lengths.shape, jnp.int32),
            pltpu.SMEM((windows,), jnp.int32),
            pltpu.SemaphoreType.DMA((windows, columns)),
            pltpu.SemaphoreType.DMA((windows,)),
            pltpu.SemaphoreType.DMA((2,)),
        ],
        flops=10 * windows * rows * width,
        bytes_moved=windows * rows * width * 10,
        grant=24 << 20,
    )


def marks_body(slots, facts_ref, signal_ref, first_ref, held, mark, arrivals, departures):
    windows = held.shape[0]
    rows = mark.shape[1]
    facts = Facts(facts_ref, windows, slots)

    def departure(place):
        return pltpu.make_async_copy(mark.at[place], first_ref.at[place], departures.at[place])

    begin_bins(facts, signal_ref, held, arrivals)

    def work(place, carry):
        for lanes, first_bin, second_bin in bins_of(
            facts, signal_ref, held, arrivals, place, rows
        ):
            mark[place, :, lanes] = jnp.where(first_bin >= second_bin, 1.0, 0.0).astype(
                jnp.bfloat16
            )
        departure(place).start()
        return carry

    lax.fori_loop(0, windows, work, 0)
    finish_copies(departure, windows)


def first_marks(facts, signal, slots):
    windows, segment, width = signal.shape
    rows, columns = segment // 2, width // LANES
    block = (windows, rows, width)
    return kernel_call(
        functools.partial(marks_body, slots),
        "first_marks",
        (facts, in_hbm(signal)),
        [SMEM, HBM],
        pltpu.HBM(block, jnp.bfloat16),
        HBM,
        [
            pltpu.VMEM((windows, columns, segment, LANES), jnp.float32),
            pltpu.VMEM(block, jnp.bfloat16),
            pltpu.SemaphoreType.DMA((windows, columns)),
            pltpu.SemaphoreType.DMA((windows,)),
        ],
        flops=3 * windows * rows * width,
        bytes_moved=windows * rows * width * 10,
        grant=24 << 20,
    )


def unpool_body(
    slots, slot, windows, facts_ref, returned_ref, pooled_ref, first_ref, moments_ref, sums_ref,
    params_ref, *refs,
):
    out_ref, back, low, mark, held, arrivals, departures = refs[-7:]
    targets, rows, width = back.shape
    columns = held.shape[1]
    facts = Facts(facts_ref, windows, slots)

    def arrival(target):
        place = target * slots + slot
        return [
            pltpu.make_async_copy(returned_ref.at[target], back.at[target], arrivals.at[target, 0]),
            pltpu.make_async_copy(pooled_ref.at[place], low.at[target], arrivals.at[target, 1]),
            pltpu.make_async_copy(first_ref.at[place], mark.at[target], arrivals.at[target, 2]),
        ]

    def departure(target, column):
        window = facts.slot_window(target * slots + slot)
        return pltpu.make_async_copy(
            held.at[target, column],
            out_ref.at[window, :, pl.ds(column * LANES, LANES)],
            departures.at[target, column],
        )

    def begin(target, carry):
        for copy in arrival(target):
            copy.start()
        return carry

    lax.fori_loop(0, targets, begin, 0)
    rows_total = facts.row_count()
    centre = moments_ref[0:1] / rows_total
    scale = lax.rsqrt(moments_ref[1:2] / rows_total + EPSILON)
    factor = params_ref[0:1] * scale / rows_total
    level = factor * sums_ref[1:2]
    tilt = factor * scale * sums_ref[0:1]

    def work(target, carry):
        for copy in arrival(target):
            copy.wait()
        inside = lax.broadcasted_iota(jnp.int32, (rows, LANES), 0) < facts.slot_count(
            target * slots + slot, rows
        )
        for column, lanes in enumerate(column_slices(width)):
            centred = low[target, :, lanes].astype(jnp.float32) - centre[:, lanes]
            gradient = back[target, :, lanes].astype(jnp.float32) - (
                level[:, lanes] + centred * tilt[:, lanes]
            )
            gradient = jnp.where(inside, gradient, 0.0).astype(jnp.bfloat16).astype(jnp.float32)
            first = gradient * mark[target, :, lanes].astype(jnp.float32)
            held[target, column, pl.ds(0, rows, stride=2), :] = first
            held[target, column, pl.ds(1, rows, stride=2), :] = gradient - first
        for column in range(columns):
            departure(target, column).start()
        return carry

    lax.fori_loop(0, targets, work, 0)

    def finish(target, carry):
        for column in range(columns):
            departure(target, column).wait()
        return carry

    lax.fori_loop(0, targets, finish, 0)


def unpool(facts, returned, pooled, first, moments, sums, params, slots, slot, held_output):
    targets, rows, width = returned.shape
    windows, columns = targets * slots, width // LANES
    inputs = [facts, in_hbm(returned), in_hbm(pooled), in_hbm(first), moments, sums, params]
    specs = [SMEM, HBM, HBM, HBM, VMEM, VMEM, VMEM]
    aliases = {}
    if held_output is not None:
        aliases = {len(inputs): 0}
        inputs.append(in_hbm(held_output))
        specs.append(HBM)
    block = (targets, rows, width)
    return pl.pallas_call(
        functools.partial(unpool_body, slots, slot, windows),
        in_specs=specs,
        out_specs=HBM,
        out_shape=pltpu.HBM((windows, 2 * rows, width), jnp.float32),
        input_output_aliases=aliases,
        scratch_shapes=[
            pltpu.VMEM(block, jnp.bfloat16),
            pltpu.VMEM(block, jnp.bfloat16),
            pltpu.VMEM(block, jnp.bfloat16),
            pltpu.VMEM((targets, columns, 2 * rows, LANES), jnp.float32),
            pltpu.SemaphoreType.DMA((targets, 3)),
            pltpu.SemaphoreType.DMA((targets, columns)),
        ],
        compiler_params=pltpu.CompilerParams(vmem_limit_bytes=16 << 20),
        cost_estimate=pl.CostEstimate(
            flops=10 * targets * rows * width,
            bytes_accessed=targets * rows * width * 14,
            transcendentals=0,
        ),
        name="unpool",
    )(*inputs)


def prepare_body(slots, windows, facts_ref, cot_ref, weight_ref, low_ref, middle_ref, bias_ref):
    step = pl.program_id(0)
    rows = cot_ref.shape[0]
    facts = Facts(facts_ref, windows, slots)
    first_row = step * rows
    piece = first_row // HALF_WINDOW_ROWS
    limit = facts.half_limit(piece // 2, piece % 2) - first_row % HALF_WINDOW_ROWS

    @pl.when(step == 0)
    def _():
        bias_ref[...] = jnp.zeros_like(bias_ref)

    inside = lax.broadcasted_iota(jnp.int32, (rows, 1), 0) < limit
    block = jnp.where(inside, cot_ref[...], 0.0)
    bias_ref[...] = bias_ref[...] + jnp.sum(block, axis=0, keepdims=True)
    low = block.astype(jnp.bfloat16)
    low_ref[...] = low
    middle_ref[...] = lax.dot_general(
        low, weight_ref[...], (((1,), (1,)), ((), ())), preferred_element_type=jnp.float32
    )


def prepare(facts, cotangent, weight, slots, windows):
    total_rows, width = cotangent.shape
    inner = weight.shape[0]
    rows = 256
    return pl.pallas_call(
        functools.partial(prepare_body, slots, windows),
        grid=(total_rows // rows,),
        in_specs=[
            SMEM,
            pl.BlockSpec((rows, width), lambda i: (i, 0)),
            pl.BlockSpec((inner, width), lambda i: (0, 0)),
        ],
        out_specs=[
            pl.BlockSpec((rows, width), lambda i: (i, 0)),
            pl.BlockSpec((rows, inner), lambda i: (i, 0)),
            pl.BlockSpec((1, width), lambda i: (0, 0)),
        ],
        out_shape=[
            shape((total_rows, width), jnp.bfloat16),
            shape((total_rows, inner), jnp.float32),
            shape((1, width), jnp.float32),
        ],
        compiler_params=pltpu.CompilerParams(vmem_limit_bytes=16 << 20),
        cost_estimate=pl.CostEstimate(
            flops=2 * total_rows * width * inner,
            bytes_accessed=total_rows * (width * 6 + inner * 4),
            transcendentals=0,
        ),
        name="prepare_cotangent",
    )(facts, cotangent, weight)


def weights_body(dilated_ref, pointwise_ref, wide_ref, back_ref, low_ref):
    inner = dilated_ref.shape[2]
    for number, tap in enumerate((0, 2, 1)):
        values = dilated_ref[tap]
        wide_ref[:, tap * inner : (tap + 1) * inner] = values.astype(jnp.bfloat16)
        back_ref[number * inner : (number + 1) * inner, :] = values.T.astype(jnp.bfloat16)
    low_ref[...] = pointwise_ref[...].astype(jnp.bfloat16)


def prepare_weights(dilated_kernel, pointwise_kernel):
    taps, width, inner = dilated_kernel.shape
    return kernel_call(
        weights_body,
        "prepare_weights",
        (dilated_kernel, pointwise_kernel),
        [VMEM, VMEM],
        [
            shape((width, taps * inner), jnp.bfloat16),
            shape((taps * inner, width), jnp.bfloat16),
            shape(pointwise_kernel.shape, jnp.bfloat16),
        ],
        [VMEM, VMEM, VMEM],
        flops=4 * width * inner,
        bytes_moved=30 * width * inner,
        grant=16 << 20,
    )


def norm_terms(moments_ref, params_ref, rows_total):
    centre = moments_ref[0:1] / rows_total
    scale = lax.rsqrt(moments_ref[1:2] / rows_total + EPSILON)
    return centre, scale, params_ref[0:1] * scale, params_ref[1:2]


def half_terms(moments_ref, params_ref, rows_total):
    centre, _, slope, offset = norm_terms(moments_ref, params_ref, rows_total)
    return 0.5 * slope, 0.5 * (offset - centre * slope)


def bent(half):
    square = half * half
    return jnp.tanh(half * (2.0 * GELU_SLOPE + (8.0 * GELU_SLOPE * GELU_CUBE) * square)), square


def gelu_slope(half, bend, square):
    inner = GELU_SLOPE + (12.0 * GELU_SLOPE * GELU_CUBE) * square
    return (0.5 + 0.5 * bend) + (half - half * bend * bend) * inner


def activated(values, inside, slope, offset):
    half_pre = values.astype(jnp.float32) * slope + offset
    bend, _ = bent(half_pre)
    return jnp.where(inside, half_pre + half_pre * bend, 0.0).astype(jnp.bfloat16)


def edge_body(slots, windows, facts_ref, arrived_ref, moments_ref, params_ref, border_ref):
    _, rows, width = arrived_ref.shape
    facts = Facts(facts_ref, windows, slots)
    per_half = HALF_WINDOW_ROWS // rows
    slope, offset = half_terms(moments_ref, params_ref, facts.row_count())
    for piece in range(2 * slots):
        slot, half = piece // 2, piece % 2
        limit = facts.half_limit(slot, half)
        first = 0 if half else HALF_WINDOW_ROWS - BORDER
        row = first
        while row < first + BORDER:
            inner_row = row % rows
            size = min(rows - inner_row, first + BORDER - row)
            block = (half * per_half + row // rows) * slots + slot
            inside = lax.broadcasted_iota(jnp.int32, (size, 1), 0) < limit - row
            for lanes in column_slices(width):
                border_ref[piece, row - first : row - first + size, lanes] = activated(
                    arrived_ref[block, inner_row : inner_row + size, lanes],
                    inside,
                    slope[:, lanes],
                    offset[:, lanes],
                )
            row += size


def edge_rows(facts, arrived, moments, params, slots, windows):
    width = arrived.shape[2]
    return kernel_call(
        functools.partial(edge_body, slots, windows),
        "edge_rows",
        (facts, arrived, moments, params),
        [SMEM, VMEM, VMEM, VMEM],
        shape((2 * slots, BORDER, width), jnp.bfloat16),
        VMEM,
        flops=40 * slots * BORDER * width,
        bytes_moved=8 * slots * BORDER * width,
    )


def slope_body(slots, windows, piece, facts_ref, arrived_ref, moments_ref, params_ref, slope_ref):
    blocks, rows, width = arrived_ref.shape
    facts = Facts(facts_ref, windows, slots)
    per_half = HALF_WINDOW_ROWS // rows
    slope, offset = half_terms(moments_ref, params_ref, facts.row_count())
    slot, half = piece // 2, piece % 2
    limit = facts.half_limit(slot, half)

    def work(part, carry):
        start = part * rows
        inside = lax.broadcasted_iota(jnp.int32, (rows, 1), 0) < limit - start
        for lanes in column_slices(width):
            values = arrived_ref[(half * per_half + part) * slots + slot, :, lanes]
            half_pre = values.astype(jnp.float32) * slope[:, lanes] + offset[:, lanes]
            found = jnp.where(inside, gelu_slope(half_pre, *bent(half_pre)), 0.0)
            slope_ref[pl.ds(pl.multiple_of(start, rows), rows), lanes] = found
        return carry

    lax.fori_loop(0, per_half, work, 0)


def entry_slope(facts, arrived, moments, params, slots, windows, piece):
    width = arrived.shape[2]
    return kernel_call(
        functools.partial(slope_body, slots, windows, piece),
        "entry_slope",
        (facts, arrived, moments, params),
        [SMEM, VMEM, VMEM, VMEM],
        shape((HALF_WINDOW_ROWS, width), jnp.float32),
        VMEM,
        flops=25 * HALF_WINDOW_ROWS * width,
        bytes_moved=6 * HALF_WINDOW_ROWS * width,
    )


def block_moments(values, inside, count):
    block_sum = jnp.sum(jnp.where(inside, values, 0.0), axis=0, keepdims=True)
    deviation = jnp.where(inside, values - block_sum / jnp.maximum(count, 1.0), 0.0)
    return block_sum, jnp.sum(deviation * deviation, axis=0, keepdims=True), count


def convolve_body(
    slots, windows, facts_ref, arrived_ref, entry_ref, params_ref, weight_ref,
    act_ref, out_ref, moments_ref, wide,
):
    facts = Facts(facts_ref, windows, slots)
    pieces, rows, inner = out_ref.shape
    _, block_rows, width = arrived_ref.shape
    per_half = rows // block_rows
    slope, offset = half_terms(entry_ref, params_ref, facts.row_count())
    tiles = inner // LANES
    for turn in range(2):
        for tile in range(3 * tiles):
            wide[turn, tile, 0:PAD] = jnp.zeros((PAD, LANES), jnp.float32)
            wide[turn, tile, PAD + rows : PADDED_ROWS] = jnp.zeros((PAD, LANES), jnp.float32)
    moments_ref[...] = jnp.zeros_like(moments_ref)
    below, above = PAD - DILATION_STEP, PAD + DILATION_STEP

    def lay_act(piece):
        slot, half = piece // 2, piece % 2
        limit = facts.half_limit(slot, half)
        for part in range(per_half):
            start = part * block_rows
            inside = lax.broadcasted_iota(jnp.int32, (block_rows, 1), 0) < limit - start
            for lanes in column_slices(width):
                act_ref[piece, start : start + block_rows, lanes] = activated(
                    arrived_ref[(half * per_half + part) * slots + slot, :, lanes],
                    inside,
                    slope[:, lanes],
                    offset[:, lanes],
                )

    lay_act(0)
    for piece in range(pieces):
        turn, half = piece % 2, piece % 2
        if piece + 1 < pieces:
            lay_act(piece + 1)
        product = jnp.dot(act_ref[piece], weight_ref[...], preferred_element_type=jnp.float32)
        for tile, lanes in enumerate(column_slices(3 * inner)):
            wide[turn, tile, PAD : PAD + rows] = product[:, lanes]
        limit = facts.half_limit(piece // 2, half)
        start = half * STRIP
        row = lax.broadcasted_iota(jnp.int32, (rows, 1), 0)
        end = jnp.minimum(limit, rows - STRIP + start)
        inside = jnp.logical_and(row >= start, row < end)
        count = jnp.maximum(end - start, 0).astype(jnp.float32)
        for tile, lanes in enumerate(column_slices(inner)):
            out = (
                wide[turn, tiles + tile, PAD : PAD + rows]
                + wide[turn, tile, below : below + rows]
                + wide[turn, 2 * tiles + tile, above : above + rows]
            )
            out_ref[piece, :, lanes] = out
            held = (moments_ref[0:1, lanes], moments_ref[1:2, lanes], moments_ref[2:3, lanes])
            moments_ref[0:1, lanes], moments_ref[1:2, lanes], moments_ref[2:3, lanes] = merged(
                held, block_moments(out, inside, count)
            )


def convolve(facts, arrived, entry_moments, params, weight, slots, windows):
    width, inner = weight.shape[0], weight.shape[1] // 3
    pieces, rows = 2 * slots, HALF_WINDOW_ROWS
    return kernel_call(
        functools.partial(convolve_body, slots, windows),
        "convolve",
        (facts, arrived, entry_moments, params, weight),
        [SMEM] + [VMEM] * 4,
        [
            shape((pieces, rows, width), jnp.bfloat16),
            shape((pieces, rows, inner), jnp.float32),
            shape((3, inner), jnp.float32),
        ],
        [VMEM, VMEM, VMEM],
        [pltpu.VMEM((2, 3 * inner // LANES, PADDED_ROWS, LANES), jnp.float32)],
        flops=6 * pieces * rows * width * inner,
        bytes_moved=pieces * rows * (width * 2 + inner * 4),
        grant=16 << 20,
    )


def join_body(
    slots, windows, facts_ref, out_ref, border_ref, weight_ref, held_ref, strip_ref, moments_ref,
    moved,
):
    facts = Facts(facts_ref, windows, slots)
    pieces, rows, inner = out_ref.shape
    found = (held_ref[0:1], held_ref[1:2], held_ref[2:3])
    gap = STRIP - DILATION_STEP
    skip = BORDER - DILATION_STEP
    for piece in range(pieces):
        half = piece % 2
        other = piece + 1 - 2 * half
        moved[...] = jnp.zeros_like(moved)
        if half == 0:
            moved[gap : gap + BORDER] = jnp.dot(
                border_ref[other], weight_ref[:, 2 * inner :], preferred_element_type=jnp.float32
            )
            strip = out_ref[piece, rows - STRIP : rows] + moved[0:STRIP]
        else:
            moved[0:BORDER] = jnp.dot(
                border_ref[other], weight_ref[:, :inner], preferred_element_type=jnp.float32
            )
            strip = out_ref[piece, 0:STRIP] + moved[skip : skip + STRIP]
        strip_ref[piece] = strip
        limit = facts.half_limit(piece // 2, half) - (1 - half) * (rows - STRIP)
        count = jnp.clip(limit, 0, STRIP)
        inside = lax.broadcasted_iota(jnp.int32, (STRIP, 1), 0) < count
        found = merged(found, block_moments(strip, inside, count.astype(jnp.float32)))
    for number, value in enumerate(found):
        moments_ref[number : number + 1] = jnp.broadcast_to(value, (1, inner))


def join(facts, out, border, weight, held, slots, windows):
    pieces, rows, inner = out.shape
    return kernel_call(
        functools.partial(join_body, slots, windows),
        "join_halves",
        (facts, out, border, weight, held),
        [SMEM, VMEM, VMEM, VMEM, VMEM],
        [shape((pieces, STRIP, inner), jnp.float32), shape((3, inner), jnp.float32)],
        [VMEM, VMEM],
        [pltpu.VMEM((2 * STRIP, inner), jnp.float32)],
        flops=2 * pieces * BORDER * border.shape[2] * inner,
        bytes_moved=pieces * STRIP * inner * 8,
    )


def middle_body(
    slots, windows, facts_ref, out_ref, strip_ref, moments_ref, params_ref, grad_ref,
    act_ref, slope_ref, norm_ref, sums_ref,
):
    facts = Facts(facts_ref, windows, slots)
    pieces, rows, inner = out_ref.shape
    centre, scale, _, _ = norm_terms(moments_ref, params_ref, facts.row_count())
    gain, offset = 0.5 * params_ref[0:1], 0.5 * params_ref[1:2]
    sums_ref[...] = jnp.zeros_like(sums_ref)

    def chunk(piece, start, values):
        size = values.shape[0]
        limit = facts.half_limit(piece // 2, piece % 2)
        inside = lax.broadcasted_iota(jnp.int32, (size, 1), 0) < limit - start
        here = pl.ds(start, size)
        for lanes in column_slices(inner):
            norm = (values[:, lanes] - centre[:, lanes]) * scale[:, lanes]
            half_pre = norm * gain[:, lanes] + offset[:, lanes]
            bend, square = bent(half_pre)
            act = jnp.where(inside, half_pre + half_pre * bend, 0.0)
            act_ref[piece, here, lanes] = act.astype(jnp.bfloat16)
            grad = grad_ref[piece, here, lanes] * gelu_slope(half_pre, bend, square)
            grad = jnp.where(inside, grad, 0.0)
            slope_ref[piece, here, lanes] = grad
            norm_ref[piece, here, lanes] = norm
            sums_ref[0:1, lanes] = sums_ref[0:1, lanes] + jnp.sum(
                grad * norm, axis=0, keepdims=True
            )
            sums_ref[1:2, lanes] = sums_ref[1:2, lanes] + jnp.sum(grad, axis=0, keepdims=True)

    size = 2 * STRIP
    steps = rows // size - 1

    def main(step, carry):
        piece = step // steps
        start = pl.multiple_of((step % steps + piece % 2) * size, size)
        chunk(piece, start, out_ref[piece, pl.ds(start, size), :])
        return carry

    lax.fori_loop(0, pieces * steps, main, 0)

    def edge(slot, carry):
        low, high = 2 * slot, 2 * slot + 1
        start = rows - size
        values = jnp.concatenate([out_ref[low, start : start + STRIP], strip_ref[low]], axis=0)
        chunk(low, start, values)
        chunk(high, 0, jnp.concatenate([strip_ref[high], out_ref[high, STRIP:size]], axis=0))
        return carry

    lax.fori_loop(0, slots, edge, 0)


def middle(facts, out, strip, moments, params, grad, slots, windows):
    dims = out.shape
    return kernel_call(
        functools.partial(middle_body, slots, windows),
        "middle_norm",
        (facts, out, strip, moments, params, grad),
        [SMEM] + [VMEM] * 5,
        [
            shape(dims, jnp.bfloat16),
            shape(dims, jnp.float32),
            shape(dims, jnp.float32),
            shape((2, dims[2]), jnp.float32),
        ],
        [VMEM] * 4,
        flops=40 * out.size,
        bytes_moved=18 * out.size,
    )


def middle_grad_body(
    slots, windows, facts_ref, grad_ref, norm_ref, moments_ref, params_ref, sums_ref,
    padded_ref, border_ref, centre_ref,
):
    facts = Facts(facts_ref, windows, slots)
    pieces, rows, inner = grad_ref.shape
    rows_total = facts.row_count()
    _, _, slope, _ = norm_terms(moments_ref, params_ref, rows_total)
    level, tilt = sums_ref[1:2] / rows_total, sums_ref[0:1] / rows_total
    tiles = inner // LANES
    for piece in range(pieces):
        for tile in range(tiles):
            padded_ref[piece, tile, 0:PAD] = jnp.zeros((PAD, LANES), jnp.float32)
            padded_ref[piece, tile, PAD + rows : PADDED_ROWS] = jnp.zeros(
                (PAD, LANES), jnp.float32
            )
    size = 2 * STRIP

    def work(step, carry):
        piece, part = step // (rows // size), step % (rows // size)
        start = pl.multiple_of(part * size, size)
        limit = facts.half_limit(piece // 2, piece % 2)
        inside = lax.broadcasted_iota(jnp.int32, (size, 1), 0) < limit - start
        for tile, lanes in enumerate(column_slices(inner)):
            norm = norm_ref[piece, pl.ds(start, size), lanes]
            grad = slope[:, lanes] * (
                grad_ref[piece, pl.ds(start, size), lanes]
                - (level[:, lanes] + norm * tilt[:, lanes])
            )
            low = jnp.where(inside, grad, 0.0).astype(jnp.bfloat16)
            centre_ref[piece, pl.ds(start, size), lanes] = low
            padded_ref[piece, tile, pl.ds(pl.multiple_of(start + PAD, 8), size), :] = low.astype(
                jnp.float32
            )
        return carry

    lax.fori_loop(0, pieces * (rows // size), work, 0)
    for piece in range(pieces):
        start = PAD + (0 if piece % 2 else rows - BORDER)
        for tile, lanes in enumerate(column_slices(inner)):
            border_ref[piece, :, lanes] = padded_ref[piece, tile, start : start + BORDER].astype(
                jnp.bfloat16
            )


def middle_grad(facts, grad, norm, moments, params, sums, slots, windows):
    pieces, _, inner = grad.shape
    return kernel_call(
        functools.partial(middle_grad_body, slots, windows),
        "middle_grad",
        (facts, grad, norm, moments, params, sums),
        [SMEM] + [VMEM] * 5,
        [
            shape((pieces, inner // LANES, PADDED_ROWS, LANES), jnp.float32),
            shape((pieces, BORDER, inner), jnp.bfloat16),
            shape(grad.shape, jnp.bfloat16),
        ],
        [VMEM, VMEM, VMEM],
        flops=8 * grad.size,
        bytes_moved=12 * grad.size,
    )


def output_body(
    slots, windows, facts_ref, act_ref, weight_ref, arrived_ref, params_ref, out_ref
):
    source, slot = pl.program_id(0), pl.program_id(1)
    rows = out_ref.shape[0]
    facts = Facts(facts_ref, windows, slots)
    per_half = HALF_WINDOW_ROWS // rows
    half, start = source // per_half, (source % per_half) * rows
    inside = lax.broadcasted_iota(jnp.int32, (rows, 1), 0) < facts.half_limit(slot, half) - start
    mixed = jnp.dot(act_ref[...], weight_ref[...], preferred_element_type=jnp.float32)
    block = arrived_ref[0].astype(jnp.float32) + mixed + params_ref[2:3]
    out_ref[...] = jnp.where(inside, block, 0.0)


def output_rows(facts, act, weight, arrived, params, slots, windows):
    blocks, rows, width = arrived.shape
    inner = act.shape[1]
    sources = blocks // slots
    place = lambda s, j: (j * sources + s, 0)
    return pl.pallas_call(
        functools.partial(output_body, slots, windows),
        grid=(sources, slots),
        in_specs=[
            SMEM,
            pl.BlockSpec((rows, inner), place),
            pl.BlockSpec((inner, width), lambda s, j: (0, 0)),
            pl.BlockSpec((1, rows, width), lambda s, j: (s * slots + j, 0, 0)),
            pl.BlockSpec((3, width), lambda s, j: (0, 0)),
        ],
        out_specs=pl.BlockSpec((rows, width), place),
        out_shape=shape((blocks * rows, width), jnp.float32),
        compiler_params=pltpu.CompilerParams(vmem_limit_bytes=16 << 20),
        cost_estimate=pl.CostEstimate(
            flops=2 * act.size * width * 7, bytes_accessed=8 * arrived.size * 7, transcendentals=0
        ),
        name="output_rows",
    )(facts, act, weight, arrived, params)


def entry_grad_body(slots, windows, facts_ref, padded_ref, border_ref, weight_ref, *refs):
    pieces = 2 * slots
    slope_refs, refs = refs[:pieces], refs[pieces:]
    (arrived_ref, block_ref, moments_ref, params_ref, bias_ref), refs = refs[:5], refs[5:]
    sent_refs, (kept_ref, sums_ref, wide, packed, taps_ref, departures, kept) = (
        refs[:slots],
        refs[slots:],
    )
    facts = Facts(facts_ref, windows, slots)
    _, sources, rows, width = packed.shape
    tiles = padded_ref.shape[1]
    per_half = HALF_WINDOW_ROWS // rows
    centre, scale, slope, _ = norm_terms(moments_ref, params_ref, facts.row_count())
    skip = BORDER - DILATION_STEP
    sums_ref[...] = jnp.zeros_like(sums_ref)

    def departure(slot, source):
        return pltpu.make_async_copy(
            packed.at[slot, source], sent_refs[slot].at[source], departures.at[slot, source]
        )

    def keeping(piece):
        return pltpu.make_async_copy(
            taps_ref.at[piece, :, pl.ds(0, kept_ref.shape[2])], kept_ref.at[piece], kept.at[piece]
        )

    def lay_taps(piece):
        half, turn = piece % 2, piece % 2
        for tile, lanes in enumerate(column_slices(tiles * LANES)):
            border = border_ref[piece + 1 - 2 * half, :, lanes].astype(jnp.float32)
            wide[turn, tile] = padded_ref[piece, tile]
            if half == 0:
                end = PAD + HALF_WINDOW_ROWS
                wide[turn, tile, end : end + DILATION_STEP] = border[0:DILATION_STEP]
            else:
                wide[turn, tile, PAD - DILATION_STEP : PAD] = border[skip:BORDER]
            for number, tap in enumerate((0, 2, 1)):
                start = PAD - (tap - 1) * DILATION_STEP
                first = (number * tiles + tile) * LANES
                taps_ref[piece, :, first : first + LANES] = wide[
                    turn, tile, start : start + HALF_WINDOW_ROWS
                ].astype(jnp.bfloat16)

    lay_taps(0)
    for piece in range(pieces):
        slot, half = piece // 2, piece % 2
        if piece + 1 < pieces:
            lay_taps(piece + 1)
        for column in range(0, width, 2 * LANES):
            grad = jnp.dot(
                taps_ref[piece],
                weight_ref[:, column : column + 2 * LANES],
                preferred_element_type=jnp.float32,
            )
            for part in range(per_half):
                source = half * per_half + part
                here = slice(part * rows, (part + 1) * rows)
                for start in (column, column + LANES):
                    lanes = slice(start, start + LANES)
                    pre = grad[here, start - column : start - column + LANES]
                    pre = pre * slope_refs[piece][here, lanes]
                    values = arrived_ref[source * slots + slot, :, lanes].astype(jnp.float32)
                    sums_ref[0:1, lanes] = sums_ref[0:1, lanes] + jnp.sum(
                        pre * values, axis=0, keepdims=True
                    )
                    sums_ref[1:2, lanes] = sums_ref[1:2, lanes] + jnp.sum(
                        pre, axis=0, keepdims=True
                    )
                    block = block_ref[piece, here, lanes].astype(jnp.float32)
                    packed[slot, source, :, lanes] = (pre * slope[:, lanes] + block).astype(
                        jnp.bfloat16
                    )
        if piece == 0:
            keeping(piece).start()
        for part in range(per_half):
            departure(slot, half * per_half + part).start()
        if piece + 1 < pieces:
            keeping(piece + 1).start()
    sums_ref[0:1] = (sums_ref[0:1] - centre * sums_ref[1:2]) * scale
    sums_ref[2:3] = bias_ref[...]
    for piece in range(pieces):
        keeping(piece).wait()
    for slot in range(slots):
        for source in range(sources):
            departure(slot, source).wait()


def entry_grad(
    facts, padded, border, weight, slopes, arrived, block, moments, params, bias, slots, windows
):
    blocks, rows, width = arrived.shape
    inner, sources = border.shape[2], blocks // slots
    pieces = 2 * slots
    inputs = [facts, padded, border, weight, *slopes, arrived, block, moments, params, bias]
    taps_shape = (HALF_WINDOW_ROWS, 3 * inner)
    return kernel_call(
        functools.partial(entry_grad_body, slots, windows),
        "entry_grad",
        inputs,
        [SMEM] + [VMEM] * (len(inputs) - 1),
        [
            *[pltpu.HBM((sources, rows, width), jnp.bfloat16)] * slots,
            pltpu.HBM((pieces, HALF_WINDOW_ROWS, 2 * inner), jnp.bfloat16),
            shape((3, width), jnp.float32),
        ],
        [HBM] * (slots + 1) + [VMEM],
        [
            pltpu.VMEM((2, inner // LANES, PADDED_ROWS, LANES), jnp.float32),
            pltpu.VMEM((slots, sources, rows, width), jnp.bfloat16),
            pltpu.VMEM((pieces, *taps_shape), jnp.bfloat16),
            pltpu.SemaphoreType.DMA((slots, sources)),
            pltpu.SemaphoreType.DMA((pieces,)),
        ],
        flops=2 * pieces * HALF_WINDOW_ROWS * 3 * inner * width,
        bytes_moved=pieces * HALF_WINDOW_ROWS * (width * 10 + inner * 10),
        grant=16 << 20,
    )


def flat_mask(bits):
    return sum(mask * (lax.axis_size("seq") if axis == "grp" else 1) for axis, mask in bits)


def from_flat_partner(block, mask):
    count = lax.axis_size("grp") * lax.axis_size("seq")
    return lax.ppermute(
        block, ("grp", "seq"), [(place, place ^ mask) for place in range(count)]
    )


def bit_of(axis, mask):
    return (lax.axis_index(axis) // mask) % 2


def square_phases():
    steps = exchange_steps()[1:]
    outer = [step for step in steps if step[0] == "grp"]
    inner = [step for step in steps if step[0] == "seq"]
    ordered = []
    while outer and inner:
        ordered += [outer.pop(0), inner.pop(0)]
    ordered += outer + inner
    return [ordered[start : start + 2] for start in range(0, len(ordered), 2)]


def phase_place(phase):
    return sum(bit_of(*step) * 2**number for number, step in enumerate(phase))


def phase_parts(phase):
    parts = 2 ** len(phase)
    masks = [
        flat_mask([step for number, step in enumerate(phase) if part >> number & 1])
        for part in range(parts)
    ]
    return parts, masks


def exchange_parts(parts, phase):
    _, masks = phase_parts(phase)
    return [from_flat_partner(part, mask) for part, mask in zip(parts, masks[1:])]


def place_in(facts_ref, phase):
    bits = [
        (facts_ref[0 if axis == "grp" else 1] // mask) % 2 * 2**number
        for number, (axis, mask) in enumerate(phase)
    ]
    return sum(bits)


def encoded(sums, rows_ref):
    count = sums.shape[0]
    high = sums.astype(jnp.bfloat16).astype(jnp.float32)
    low = (sums - high).astype(jnp.bfloat16).astype(jnp.float32)
    rows_ref[...] = jnp.zeros_like(rows_ref)
    rows_ref[0:count] = high
    rows_ref[count : 2 * count] = low
    return rows_ref[...].astype(jnp.bfloat16), high + low


def decoded(found_ref, count, rows_ref):
    rows_ref[...] = found_ref[found_ref.shape[0] - EXTRA :, :].astype(jnp.float32)
    return rows_ref[0:count] + rows_ref[count : 2 * count]


def pair_sum(values):
    while len(values) > 1:
        values = [values[i] + values[i + 1] for i in range(0, len(values), 2)]
    return values[0]


def other_half_body(
    facts_ref, sides_ref, centre_ref, pointwise_ref, sums_ref, sent_ref, held_ref, rows_ref
):
    width, inner = pointwise_ref.shape
    sent_ref[width:, :], held_ref[...] = encoded(sums_ref[...], rows_ref)

    @pl.when(facts_ref[0] % 2 == 0)
    def _():
        sent_ref[:width, :inner] = sides_ref[:, inner:].astype(jnp.bfloat16)
        sent_ref[:width, inner:] = pointwise_ref[...].astype(jnp.bfloat16)

    @pl.when(facts_ref[0] % 2 == 1)
    def _():
        sent_ref[:width, :inner] = sides_ref[:, :inner].astype(jnp.bfloat16)
        sent_ref[:width, inner:] = centre_ref[...].astype(jnp.bfloat16)


def other_half(facts, sides, centre, pointwise, sums):
    width, inner = pointwise.shape
    return kernel_call(
        other_half_body,
        "other_half",
        (facts, sides, centre, pointwise, sums),
        [SMEM] + [VMEM] * 4,
        [shape((width + EXTRA, 2 * inner), jnp.bfloat16), shape(sums.shape, jnp.float32)],
        [VMEM, VMEM],
        [pltpu.VMEM((EXTRA, 2 * inner), jnp.float32)],
        flops=2 * width * inner,
        bytes_moved=12 * width * inner,
        grant=10 << 20,
    )


def part_rows(mine, part, rows):
    return pl.ds(pl.multiple_of(jnp.bitwise_xor(mine, part) * rows, rows), rows)


def own_half_body(
    phase, facts_ref, sides_ref, centre_ref, pointwise_ref, sums_ref, other_ref, total_ref, *refs
):
    part_refs, rows_ref = refs[:-1], refs[-1]
    inner = pointwise_ref.shape[1]
    rows = part_refs[0].shape[0]
    mine = place_in(facts_ref, phase)
    sums = sums_ref[...] + decoded(other_ref, sums_ref.shape[0], rows_ref)
    extra, total_ref[...] = encoded(sums, rows_ref)
    for part_ref in part_refs[1:]:
        part_ref[rows:, :] = extra

    def write(low, high):
        for part, part_ref in enumerate(part_refs):
            here = part_rows(mine, part, rows)
            for piece, lanes in ((low, slice(0, inner)), (high, slice(inner, 2 * inner))):
                value = piece(here) + other_ref[here, lanes].astype(jnp.float32)
                part_ref[:rows, lanes] = value.astype(part_ref.dtype)

    @pl.when(facts_ref[0] % 2 == 0)
    def _():
        write(
            lambda here: sides_ref[here, :inner],
            lambda here: centre_ref[here, :],
        )

    @pl.when(facts_ref[0] % 2 == 1)
    def _():
        write(lambda here: sides_ref[here, inner:], lambda here: pointwise_ref[here, :])


def part_shapes(sums, rows, columns, phase):
    parts = 2 ** len(phase)
    rows //= parts
    return [
        shape(sums.shape, jnp.float32),
        shape((rows, columns), jnp.float32),
        *[shape((rows + EXTRA, columns), jnp.bfloat16)] * (parts - 1),
    ]


def own_half(facts, sides, centre, pointwise, sums, other, phase):
    width, inner = pointwise.shape
    outputs = part_shapes(sums, width, 2 * inner, phase)
    return kernel_call(
        functools.partial(own_half_body, phase),
        "own_half",
        (facts, sides, centre, pointwise, sums, other),
        [SMEM] + [VMEM] * 5,
        outputs,
        [VMEM] * len(outputs),
        [pltpu.VMEM((EXTRA, 2 * inner), jnp.float32)],
        flops=2 * width * inner,
        bytes_moved=20 * width * inner,
        grant=12 << 20,
    )


def next_parts_body(count, phase, facts_ref, kept_ref, sums_ref, *refs):
    found_refs, total_ref, part_refs, rows_ref = (
        refs[:count],
        refs[count],
        refs[count + 1 : -1],
        refs[-1],
    )
    sums = pair_sum(
        [sums_ref[...]] + [decoded(ref, sums_ref.shape[0], rows_ref) for ref in found_refs]
    )
    total_ref[...] = sums
    rows = part_refs[0].shape[0]
    if phase:
        mine = place_in(facts_ref, phase)
        extra, total_ref[...] = encoded(sums, rows_ref)
        for part_ref in part_refs[1:]:
            part_ref[rows:, :] = extra
    for part, part_ref in enumerate(part_refs):
        here = part_rows(mine, part, rows) if phase else slice(0, rows)
        value = kept_ref[here, :]
        for found_ref in found_refs:
            value = value + found_ref[here, :].astype(jnp.float32)
        part_ref[:rows, :] = value.astype(part_ref.dtype)


def plain_parts(kept, sums, found, phase):
    rows, count = kept.shape[0], sums.shape[0]
    totals = [sums]
    for block in found:
        kept = kept + block[:rows].astype(jnp.float32)
        tail = block[rows:].astype(jnp.float32)
        totals.append(tail[:count] + tail[count : 2 * count])
    sums = pair_sum(totals)
    if not phase:
        return [sums, kept.astype(jnp.bfloat16)]
    high = lax.reduce_precision(sums, 8, 7)
    low = lax.reduce_precision(sums - high, 8, 7)
    rest = jnp.zeros((EXTRA - 2 * count, sums.shape[1]), jnp.float32)
    extra, sums = jnp.concatenate([high, low, rest]).astype(jnp.bfloat16), high + low
    parts = 2 ** len(phase)
    mine, rows = phase_place(phase), rows // parts
    slices = [
        lax.dynamic_slice_in_dim(kept, jnp.bitwise_xor(mine, part) * rows, rows)
        for part in range(parts)
    ]
    return [sums, slices[0]] + [
        jnp.concatenate([block.astype(jnp.bfloat16), extra]) for block in slices[1:]
    ]


def next_parts(facts, kept, sums, found, phase):
    rows, columns = kept.shape
    if rows // 2 ** len(phase) % 16:
        return plain_parts(kept, sums, found, phase)
    outputs = part_shapes(sums, rows, columns, phase)
    if not phase:
        outputs = [outputs[0], shape((rows, columns), jnp.bfloat16)]
    return kernel_call(
        functools.partial(next_parts_body, len(found), phase),
        "next_parts",
        (facts, kept, sums, *found),
        [SMEM] + [VMEM] * (2 + len(found)),
        outputs,
        [VMEM] * len(outputs),
        [pltpu.VMEM((EXTRA, columns), jnp.float32)],
        flops=4 * rows * columns,
        bytes_moved=16 * rows * columns,
    )


def gather_parts(buffer, phase):
    _, masks = phase_parts(phase)
    return [buffer] + [from_flat_partner(buffer, mask) for mask in masks[1:]]


def in_order(found, owners):
    parts = len(found)
    orders = [
        jnp.concatenate([found[place ^ own] for place in range(parts)], axis=0)
        for own in range(parts)
    ]
    result = orders[0]
    for own in range(1, parts):
        result = jnp.where(owners[own], orders[own], result)
    return result


def finish_body(own, facts_ref, half_ref, *refs):
    dilated_ref, pointwise_ref, held, turned, copies = refs[-5:]
    inner = dilated_ref.shape[2]

    def write(places):
        for number, place in enumerate(places):
            held[number] = half_ref[:, number * inner : (number + 1) * inner].astype(jnp.float32)
            pltpu.make_async_copy(
                held.at[number], dilated_ref.at[place], copies.at[number]
            ).start()
        if len(places) == 1:
            turned[...] = half_ref[:, inner:].astype(jnp.float32).T
            pltpu.make_async_copy(turned, pointwise_ref, copies.at[1]).start()
            pltpu.make_async_copy(turned, pointwise_ref, copies.at[1]).wait()
        for number, place in enumerate(places):
            pltpu.make_async_copy(
                held.at[number], dilated_ref.at[place], copies.at[number]
            ).wait()

    upper = facts_ref[0] % 2

    @pl.when(upper == 1 - own)
    def _():
        write((0, 1))

    @pl.when(upper == own)
    def _():
        write((2,))


def finish_weights(facts, half, own, begun):
    width, both = half.shape
    inner = both // 2
    inputs, specs, aliases = [facts, half], [SMEM, VMEM], {}
    if begun is not None:
        aliases = {2: 0, 3: 1}
        inputs += [in_hbm(array) for array in begun]
        specs += [HBM, HBM]
    return pl.pallas_call(
        functools.partial(finish_body, own),
        in_specs=specs,
        out_specs=[HBM, HBM],
        out_shape=[
            pltpu.HBM((3, width, inner), jnp.float32),
            pltpu.HBM((inner, width), jnp.float32),
        ],
        input_output_aliases=aliases,
        scratch_shapes=[
            pltpu.VMEM((2, width, inner), jnp.float32),
            pltpu.VMEM((inner, width), jnp.float32),
            pltpu.SemaphoreType.DMA((2,)),
        ],
        compiler_params=pltpu.CompilerParams(vmem_limit_bytes=12 << 20),
        cost_estimate=pl.CostEstimate(
            flops=width * both, bytes_accessed=6 * width * both, transcendentals=0
        ),
        name="finish_weights",
    )(*inputs)


def per_device(
    signal,
    entry_gain,
    entry_shift,
    dilated_kernel,
    middle_gain,
    middle_shift,
    pointwise_kernel,
    pointwise_bias,
    lengths,
    assignment,
    cotangent,
):
    seq_count = lax.axis_size("seq")
    windows, segment, width = signal.shape
    inner = pointwise_kernel.shape[0]
    slots = windows // seq_count
    rows = segment // 2
    pieces = 2 * slots
    places = jnp.stack([lax.axis_index("grp"), lax.axis_index("seq"), jnp.int32(seq_count)])
    facts = jnp.concatenate([places.astype(jnp.int32), assignment[0], lengths])
    entry_params = jnp.stack([entry_gain, entry_shift, pointwise_bias])
    middle_params = jnp.stack([middle_gain, middle_shift])

    outgoing, entry_local = pool(assignment, lengths, signal, slots)
    arrived = lax.all_to_all(outgoing, "seq", split_axis=0, concat_axis=0, tiled=True)

    late_facts, _ = lax.optimization_barrier((facts, entry_local))
    first_chosen = first_marks(late_facts, signal, slots)
    wide_kernel, back_kernel, pointwise_low = prepare_weights(dilated_kernel, pointwise_kernel)
    grad_block, grad_middle, bias_part = prepare(
        facts, cotangent, pointwise_low, slots, windows
    )
    entry_moments, prepared = total_moments(
        entry_local,
        [first_chosen, grad_block, grad_middle, wide_kernel, back_kernel, pointwise_low],
    )
    first_chosen, grad_block, grad_middle, wide_kernel, back_kernel, pointwise_low = prepared
    phases = square_phases()
    owners = [
        [phase_place(phase) == own for own in range(2 ** len(phase))] for phase in phases
    ]
    first_axis, first_mask = exchange_steps()[0]
    upper = bit_of(first_axis, first_mask) == 1
    (
        arrived,
        first_chosen,
        grad_block,
        grad_middle,
        wide_kernel,
        back_kernel,
        pointwise_low,
        owners,
        upper,
        middle_params,
        facts,
    ) = lax.optimization_barrier(
        (
            arrived,
            first_chosen,
            grad_block,
            grad_middle,
            wide_kernel,
            back_kernel,
            pointwise_low,
            owners,
            upper,
            middle_params,
            facts,
        )
    )

    act_border = edge_rows(facts, arrived, entry_moments, entry_params, slots, windows)
    tied, act_border = lax.optimization_barrier((arrived, act_border))
    act_border = from_partner(act_border, "seq", 1)
    act, dilated, held_moments = convolve(
        facts, tied, entry_moments, entry_params, wide_kernel, slots, windows
    )
    strip, middle_moments = join(
        facts, dilated, act_border, wide_kernel, held_moments, slots, windows
    )
    slopes = []
    for number, (axis, mask) in enumerate(exchange_steps()):
        other = from_partner(middle_moments, axis, mask)
        if number and len(slopes) < pieces:
            tied, middle_moments = lax.optimization_barrier((arrived, middle_moments))
            found = entry_slope(
                facts, tied, entry_moments, entry_params, slots, windows, len(slopes)
            )
            other, found = lax.optimization_barrier((other, found))
            slopes.append(found)
        middle_moments = jnp.concatenate(
            merged(
                (middle_moments[0:1], middle_moments[1:2], middle_moments[2:3]),
                (other[0:1], other[1:2], other[2:3]),
            ),
            axis=0,
        )
    while len(slopes) < pieces:
        slopes.append(
            entry_slope(facts, arrived, entry_moments, entry_params, slots, windows, len(slopes))
        )
    middle_act, middle_slope, middle_norm, middle_sums = middle(
        facts,
        dilated,
        strip,
        middle_moments,
        middle_params,
        grad_middle.reshape(pieces, HALF_WINDOW_ROWS, inner),
        slots,
        windows,
    )
    flat_act = middle_act.reshape(-1, inner)
    for number, (axis, mask) in enumerate(exchange_steps()):
        other = from_partner(middle_sums, axis, mask)
        if number == len(exchange_steps()) - 1:
            tied, middle_sums = lax.optimization_barrier((flat_act, middle_sums))
            pointwise_part = jnp.einsum(
                "rd,rf->df", grad_block, tied, preferred_element_type=jnp.float32
            )
            other, pointwise_part = lax.optimization_barrier((other, pointwise_part))
        middle_sums = middle_sums + other
    padded, grad_border, grad_centre = middle_grad(
        facts, middle_slope, middle_norm, middle_moments, middle_params, middle_sums, slots, windows
    )
    centre_part = jnp.einsum("hrc,hrf->cf", act, grad_centre, preferred_element_type=jnp.float32)
    grad_border = from_partner(grad_border, "seq", 1)
    grad_border, centre_part = lax.optimization_barrier((grad_border, centre_part))
    block_pieces = grad_block.reshape(pieces, HALF_WINDOW_ROWS, width)
    def send_back(block):
        return lax.all_to_all(block, "seq", split_axis=0, concat_axis=0, tiled=True)

    *sent, taps, entry_sums = entry_grad(
        facts, padded, grad_border, back_kernel, slopes, arrived, block_pieces, entry_moments,
        entry_params, bias_part, slots, windows,
    )
    tied = lax.optimization_barrier((*sent, entry_sums))
    sent, entry_sums = list(tied[:-1]), tied[-1]
    returned = [send_back(sent[0])]
    side_parts = jnp.einsum("hrc,hrf->cf", act, taps, preferred_element_type=jnp.float32)
    other, entry_sums = other_half(facts, side_parts, centre_part, pointwise_part, entry_sums)
    other = from_partner(other, first_axis, first_mask)
    entry_sums, *parts = own_half(
        facts, side_parts, centre_part, pointwise_part, entry_sums, other, phases[0]
    )
    for held, phase in zip(phases, phases[1:] + [[]]):
        found = exchange_parts(parts[1:], held)
        entry_sums, *parts = next_parts(facts, parts[0], entry_sums, found, phase)
    buffer, signal_gradient, activations = parts[0], None, None
    for number, phase in reversed(list(enumerate(phases))):
        found = gather_parts(buffer, phase)
        if number == len(phases) - 1:
            found[1], flat_act, entry_sums, *later = lax.optimization_barrier(
                (found[1], flat_act, entry_sums, *sent[1:])
            )
            returned += [send_back(block) for block in later]
        if number == 0:
            signal_gradient = unpool(
                facts, returned[0], outgoing, first_chosen, entry_moments, entry_sums,
                entry_params, slots, 0, None,
            )
            activations = output_rows(
                facts, flat_act, pointwise_low, arrived, entry_params, slots, windows
            )
            signal_gradient, middle_sums = lax.optimization_barrier((signal_gradient, middle_sums))
            vectors = [entry_sums[0], entry_sums[1], middle_sums[0], middle_sums[1], entry_sums[2]]
            tied = lax.optimization_barrier((signal_gradient, activations, *vectors, *found))
            signal_gradient, activations, vectors, found = tied[0], tied[1], tied[2:7], tied[7:]
        buffer = in_order(found, owners[number])
    other = from_partner(buffer, first_axis, first_mask)
    begun = finish_weights(facts, buffer, 1, None)
    other, *begun = lax.optimization_barrier((other, *begun))
    dilated_kernel_gradient, pointwise_kernel_gradient = finish_weights(facts, other, 0, begun)
    for slot in range(1, slots):
        signal_gradient = unpool(
            facts, returned[slot], outgoing, first_chosen, entry_moments, entry_sums,
            entry_params, slots, slot, signal_gradient,
        )
    return (
        activations,
        signal_gradient,
        vectors[0],
        vectors[1],
        dilated_kernel_gradient,
        vectors[2],
        vectors[3],
        pointwise_kernel_gradient,
        vectors[4],
    )


def solution(mesh):
    return jax.shard_map(
        per_device,
        mesh=mesh,
        in_specs=(
            P("grp", "seq", None),
            P(),
            P(),
            P(),
            P(),
            P(),
            P(),
            P(),
            P(),
            P("grp", None),
            P(("grp", "seq"), None),
        ),
        out_specs=(
            P(("grp", "seq"), None),
            P("grp", "seq", None),
            P(),
            P(),
            P(),
            P(),
            P(),
            P(),
            P(),
        ),
        check_vma=False,
    )
```

```python
import functools
import math

import jax
import jax.numpy as jnp
from jax import lax
from jax.experimental import pallas as pl
from jax.experimental.pallas import tpu as pltpu
from jax.sharding import PartitionSpec as P

DILATION_STEP = 38
WINDOW_SPAN = 1024
HALF_WINDOW_ROWS = 512


EPSILON = 0.001

LANES = 128
BORDER = 48
STRIP = 64
PAD = 40
PADDED_ROWS = HALF_WINDOW_ROWS + 2 * PAD
EXTRA = 8
GELU_SLOPE = math.sqrt(2.0 / math.pi)
GELU_CUBE = 0.044715

VMEM = pl.BlockSpec(memory_space=pltpu.VMEM)
SMEM = pl.BlockSpec(memory_space=pltpu.SMEM)
HBM = pl.BlockSpec(memory_space=pltpu.HBM)


def from_partner(block, axis, mask):
    count = lax.axis_size(axis)
    return lax.ppermute(block, axis, [(place, place ^ mask) for place in range(count)])


def exchange_steps():
    steps = []
    for axis in ("grp", "seq"):
        mask = 1
        while mask < lax.axis_size(axis):
            steps.append((axis, mask))
            mask *= 2
    return steps


def total(values):
    for axis, mask in exchange_steps():
        values = values + from_partner(values, axis, mask)
    return values


def merged(left, right):
    left_sum, left_spread, left_count = left
    right_sum, right_spread, right_count = right
    gap = left_sum / jnp.maximum(left_count, 1.0) - right_sum / jnp.maximum(right_count, 1.0)
    weight = left_count * right_count / jnp.maximum(left_count + right_count, 1.0)
    return (
        left_sum + right_sum,
        left_spread + right_spread + gap * gap * weight,
        left_count + right_count,
    )


def total_moments(packed, others):
    steps = exchange_steps()
    for number, (axis, mask) in enumerate(steps):
        if number == len(steps) - 1:
            packed, *others = lax.optimization_barrier((packed, *others))
        other = from_partner(packed, axis, mask)
        packed = jnp.concatenate(
            merged(
                (packed[0:1], packed[1:2], packed[2:3]), (other[0:1], other[1:2], other[2:3])
            ),
            axis=0,
        )
    return packed, others


class Facts:
    def __init__(self, ref, windows, slots):
        self.ref, self.windows, self.slots = ref, windows, slots

    def slot_window(self, slot):
        upper = (2 * self.ref[1]) // self.ref[2]
        target = jnp.bitwise_xor(slot // self.slots, upper)
        return self.ref[4 + target * self.slots + slot % self.slots]

    def length(self, window):
        return self.ref[4 + self.windows + self.ref[0] * self.windows + window]

    def slot_count(self, slot, rows):
        return jnp.clip(self.length(self.slot_window(slot)) - self.ref[1] * rows, 0, rows)

    def half_limit(self, slot, half):
        place = jnp.bitwise_xor(self.ref[1], half)
        window = self.ref[4 + place * self.slots + slot]
        return jnp.clip(self.length(window) - half * HALF_WINDOW_ROWS, 0, HALF_WINDOW_ROWS)

    def row_count(self):
        return self.ref[3].astype(jnp.float32)


def kernel_call(body, name, inputs, specs, outputs, out_specs, scratch=(), flops=0, bytes_moved=0, grant=8 << 20):
    return pl.pallas_call(
        body,
        in_specs=specs,
        out_specs=out_specs,
        out_shape=outputs,
        scratch_shapes=list(scratch),
        compiler_params=pltpu.CompilerParams(vmem_limit_bytes=grant),
        cost_estimate=pl.CostEstimate(
            flops=flops, bytes_accessed=bytes_moved, transcendentals=0
        ),
        name=name,
    )(*inputs)


def shape(dims, dtype):
    return jax.ShapeDtypeStruct(dims, dtype)


def in_hbm(array):
    return pltpu.with_memory_space_constraint(array, pltpu.HBM)


def column_slices(width):
    return [slice(start, start + LANES) for start in range(0, width, LANES)]


def bin_copy(facts, signal_ref, held, arrivals, place, column):
    return pltpu.make_async_copy(
        signal_ref.at[facts.slot_window(place), :, pl.ds(column * LANES, LANES)],
        held.at[place, column],
        arrivals.at[place, column],
    )


def begin_bins(facts, signal_ref, held, arrivals):
    windows, columns = held.shape[:2]

    def begin(place, carry):
        for column in range(columns):
            bin_copy(facts, signal_ref, held, arrivals, place, column).start()
        return carry

    lax.fori_loop(0, windows, begin, 0)


def bins_of(facts, signal_ref, held, arrivals, place, rows):
    columns = held.shape[1]
    for column in range(columns):
        bin_copy(facts, signal_ref, held, arrivals, place, column).wait()
    return [
        (
            lanes,
            held[place, column, pl.ds(0, rows, stride=2), :],
            held[place, column, pl.ds(1, rows, stride=2), :],
        )
        for column, lanes in enumerate(column_slices(columns * LANES))
    ]


def finish_copies(copy_of, count):
    def finish(place, carry):
        copy_of(place).wait()
        return carry

    lax.fori_loop(0, count, finish, 0)


def pool_body(
    slots, order_ref, lengths_ref, signal_ref, pooled_ref, moments_ref,
    held, low, blocks, order, lengths, places, arrivals, departures, facts_copies,
):
    windows, columns = held.shape[:2]
    rows = low.shape[1]
    grp, seq = lax.axis_index("grp"), lax.axis_index("seq")
    upper = (2 * seq) // (windows // slots)

    def arrival(window, column):
        return pltpu.make_async_copy(
            signal_ref.at[window, :, pl.ds(column * LANES, LANES)],
            held.at[window, column],
            arrivals.at[window, column],
        )

    def departure(window):
        return pltpu.make_async_copy(
            low.at[window], pooled_ref.at[places[window]], departures.at[window]
        )

    fetches = [
        pltpu.make_async_copy(order_ref, order, facts_copies.at[0]),
        pltpu.make_async_copy(lengths_ref, lengths, facts_copies.at[1]),
    ]
    for fetch in fetches:
        fetch.start()

    def begin(window, carry):
        for column in range(columns):
            arrival(window, column).start()
        return carry

    lax.fori_loop(0, windows, begin, 0)
    moments_ref[...] = jnp.zeros_like(moments_ref)
    for fetch in fetches:
        fetch.wait()

    def note(place, carry):
        target = jnp.bitwise_xor(place // slots, upper)
        places[order[0, target * slots + place % slots]] = place
        return carry

    lax.fori_loop(0, windows, note, 0)

    def count_of(window):
        return jnp.clip(lengths[grp * windows + window] - seq * rows, 0, rows)

    def work(window, carry):
        count = count_of(window)
        inside = lax.broadcasted_iota(jnp.int32, (rows, LANES), 0) < count
        for column in range(columns):
            arrival(window, column).wait()
        for column, lanes in enumerate(column_slices(columns * LANES)):
            first_bin = held[window, column, pl.ds(0, rows, stride=2), :]
            second_bin = held[window, column, pl.ds(1, rows, stride=2), :]
            pooled = jnp.where(inside, jnp.maximum(first_bin, second_bin), 0.0)
            pooled = pooled.astype(jnp.bfloat16)
            low[window, :, lanes] = pooled
            found = block_moments(pooled.astype(jnp.float32), inside, count.astype(jnp.float32))
            blocks[window, 0:1, lanes] = found[0]
            blocks[window, 1:2, lanes] = found[1]
        departure(window).start()
        return carry

    lax.fori_loop(0, windows, work, 0)

    def join_blocks(window, carry):
        count = jnp.broadcast_to(count_of(window).astype(jnp.float32), (1, columns * LANES))
        held_moments = (moments_ref[0:1], moments_ref[1:2], moments_ref[2:3])
        moments_ref[0:1], moments_ref[1:2], moments_ref[2:3] = merged(
            held_moments, (blocks[window, 0:1], blocks[window, 1:2], count)
        )
        return carry

    lax.fori_loop(0, windows, join_blocks, 0)
    finish_copies(departure, windows)


def pool(order, lengths, signal, slots):
    windows, segment, width = signal.shape
    rows, columns = segment // 2, width // LANES
    block = (windows, rows, width)
    return kernel_call(
        functools.partial(pool_body, slots),
        "pool",
        (in_hbm(order), in_hbm(lengths), in_hbm(signal)),
        [HBM, HBM, HBM],
        [pltpu.HBM(block, jnp.bfloat16), shape((3, width), jnp.float32)],
        [HBM, VMEM],
        [
            pltpu.VMEM((windows, columns, segment, LANES), jnp.float32),
            pltpu.VMEM(block, jnp.bfloat16),
            pltpu.VMEM((windows, 2, width), jnp.float32),
            pltpu.SMEM(order.shape, jnp.int32),
            pltpu.SMEM(lengths.shape, jnp.int32),
            pltpu.SMEM((windows,), jnp.int32),
            pltpu.SemaphoreType.DMA((windows, columns)),
            pltpu.SemaphoreType.DMA((windows,)),
            pltpu.SemaphoreType.DMA((2,)),
        ],
        flops=10 * windows * rows * width,
        bytes_moved=windows * rows * width * 10,
        grant=24 << 20,
    )


def marks_body(slots, facts_ref, signal_ref, first_ref, held, mark, arrivals, departures):
    windows = held.shape[0]
    rows = mark.shape[1]
    facts = Facts(facts_ref, windows, slots)

    def departure(place):
        return pltpu.make_async_copy(mark.at[place], first_ref.at[place], departures.at[place])

    begin_bins(facts, signal_ref, held, arrivals)

    def work(place, carry):
        for lanes, first_bin, second_bin in bins_of(
            facts, signal_ref, held, arrivals, place, rows
        ):
            mark[place, :, lanes] = jnp.where(first_bin >= second_bin, 1.0, 0.0).astype(
                jnp.bfloat16
            )
        departure(place).start()
        return carry

    lax.fori_loop(0, windows, work, 0)
    finish_copies(departure, windows)


def first_marks(facts, signal, slots):
    windows, segment, width = signal.shape
    rows, columns = segment // 2, width // LANES
    block = (windows, rows, width)
    return kernel_call(
        functools.partial(marks_body, slots),
        "first_marks",
        (facts, in_hbm(signal)),
        [SMEM, HBM],
        pltpu.HBM(block, jnp.bfloat16),
        HBM,
        [
            pltpu.VMEM((windows, columns, segment, LANES), jnp.float32),
            pltpu.VMEM(block, jnp.bfloat16),
            pltpu.SemaphoreType.DMA((windows, columns)),
            pltpu.SemaphoreType.DMA((windows,)),
        ],
        flops=3 * windows * rows * width,
        bytes_moved=windows * rows * width * 10,
        grant=24 << 20,
    )


def unpool_body(
    slots, slot, windows, facts_ref, returned_ref, pooled_ref, first_ref, moments_ref, sums_ref,
    params_ref, *refs,
):
    out_ref, back, low, mark, held, arrivals, departures = refs[-7:]
    targets, rows, width = back.shape
    columns = held.shape[1]
    facts = Facts(facts_ref, windows, slots)

    def arrival(target):
        place = target * slots + slot
        return [
            pltpu.make_async_copy(returned_ref.at[target], back.at[target], arrivals.at[target, 0]),
            pltpu.make_async_copy(pooled_ref.at[place], low.at[target], arrivals.at[target, 1]),
            pltpu.make_async_copy(first_ref.at[place], mark.at[target], arrivals.at[target, 2]),
        ]

    def departure(target, column):
        window = facts.slot_window(target * slots + slot)
        return pltpu.make_async_copy(
            held.at[target, column],
            out_ref.at[window, :, pl.ds(column * LANES, LANES)],
            departures.at[target, column],
        )

    def begin(target, carry):
        for copy in arrival(target):
            copy.start()
        return carry

    lax.fori_loop(0, targets, begin, 0)
    rows_total = facts.row_count()
    centre = moments_ref[0:1] / rows_total
    scale = lax.rsqrt(moments_ref[1:2] / rows_total + EPSILON)
    factor = params_ref[0:1] * scale / rows_total
    level = factor * sums_ref[1:2]
    tilt = factor * scale * sums_ref[0:1]

    def work(target, carry):
        for copy in arrival(target):
            copy.wait()
        inside = lax.broadcasted_iota(jnp.int32, (rows, LANES), 0) < facts.slot_count(
            target * slots + slot, rows
        )
        for column, lanes in enumerate(column_slices(width)):
            centred = low[target, :, lanes].astype(jnp.float32) - centre[:, lanes]
            gradient = back[target, :, lanes].astype(jnp.float32) - (
                level[:, lanes] + centred * tilt[:, lanes]
            )
            gradient = jnp.where(inside, gradient, 0.0).astype(jnp.bfloat16).astype(jnp.float32)
            first = gradient * mark[target, :, lanes].astype(jnp.float32)
            held[target, column, pl.ds(0, rows, stride=2), :] = first
            held[target, column, pl.ds(1, rows, stride=2), :] = gradient - first
        for column in range(columns):
            departure(target, column).start()
        return carry

    lax.fori_loop(0, targets, work, 0)

    def finish(target, carry):
        for column in range(columns):
            departure(target, column).wait()
        return carry

    lax.fori_loop(0, targets, finish, 0)


def unpool(facts, returned, pooled, first, moments, sums, params, slots, slot, held_output):
    targets, rows, width = returned.shape
    windows, columns = targets * slots, width // LANES
    inputs = [facts, in_hbm(returned), in_hbm(pooled), in_hbm(first), moments, sums, params]
    specs = [SMEM, HBM, HBM, HBM, VMEM, VMEM, VMEM]
    aliases = {}
    if held_output is not None:
        aliases = {len(inputs): 0}
        inputs.append(in_hbm(held_output))
        specs.append(HBM)
    block = (targets, rows, width)
    return pl.pallas_call(
        functools.partial(unpool_body, slots, slot, windows),
        in_specs=specs,
        out_specs=HBM,
        out_shape=pltpu.HBM((windows, 2 * rows, width), jnp.float32),
        input_output_aliases=aliases,
        scratch_shapes=[
            pltpu.VMEM(block, jnp.bfloat16),
            pltpu.VMEM(block, jnp.bfloat16),
            pltpu.VMEM(block, jnp.bfloat16),
            pltpu.VMEM((targets, columns, 2 * rows, LANES), jnp.float32),
            pltpu.SemaphoreType.DMA((targets, 3)),
            pltpu.SemaphoreType.DMA((targets, columns)),
        ],
        compiler_params=pltpu.CompilerParams(vmem_limit_bytes=16 << 20),
        cost_estimate=pl.CostEstimate(
            flops=10 * targets * rows * width,
            bytes_accessed=targets * rows * width * 14,
            transcendentals=0,
        ),
        name="unpool",
    )(*inputs)


def prepare_body(slots, windows, facts_ref, cot_ref, weight_ref, low_ref, middle_ref, bias_ref):
    step = pl.program_id(0)
    rows = cot_ref.shape[0]
    facts = Facts(facts_ref, windows, slots)
    first_row = step * rows
    piece = first_row // HALF_WINDOW_ROWS
    limit = facts.half_limit(piece // 2, piece % 2) - first_row % HALF_WINDOW_ROWS

    @pl.when(step == 0)
    def _():
        bias_ref[...] = jnp.zeros_like(bias_ref)

    inside = lax.broadcasted_iota(jnp.int32, (rows, 1), 0) < limit
    block = jnp.where(inside, cot_ref[...], 0.0)
    bias_ref[...] = bias_ref[...] + jnp.sum(block, axis=0, keepdims=True)
    low = block.astype(jnp.bfloat16)
    low_ref[...] = low
    middle_ref[...] = lax.dot_general(
        low, weight_ref[...], (((1,), (1,)), ((), ())), preferred_element_type=jnp.float32
    )


def prepare(facts, cotangent, weight, slots, windows):
    total_rows, width = cotangent.shape
    inner = weight.shape[0]
    rows = 256
    return pl.pallas_call(
        functools.partial(prepare_body, slots, windows),
        grid=(total_rows // rows,),
        in_specs=[
            SMEM,
            pl.BlockSpec((rows, width), lambda i: (i, 0)),
            pl.BlockSpec((inner, width), lambda i: (0, 0)),
        ],
        out_specs=[
            pl.BlockSpec((rows, width), lambda i: (i, 0)),
            pl.BlockSpec((rows, inner), lambda i: (i, 0)),
            pl.BlockSpec((1, width), lambda i: (0, 0)),
        ],
        out_shape=[
            shape((total_rows, width), jnp.bfloat16),
            shape((total_rows, inner), jnp.float32),
            shape((1, width), jnp.float32),
        ],
        compiler_params=pltpu.CompilerParams(vmem_limit_bytes=16 << 20),
        cost_estimate=pl.CostEstimate(
            flops=2 * total_rows * width * inner,
            bytes_accessed=total_rows * (width * 6 + inner * 4),
            transcendentals=0,
        ),
        name="prepare_cotangent",
    )(facts, cotangent, weight)


def weights_body(dilated_ref, pointwise_ref, wide_ref, back_ref, low_ref):
    inner = dilated_ref.shape[2]
    for number, tap in enumerate((0, 2, 1)):
        values = dilated_ref[tap]
        wide_ref[:, tap * inner : (tap + 1) * inner] = values.astype(jnp.bfloat16)
        back_ref[number * inner : (number + 1) * inner, :] = values.T.astype(jnp.bfloat16)
    low_ref[...] = pointwise_ref[...].astype(jnp.bfloat16)


def prepare_weights(dilated_kernel, pointwise_kernel):
    taps, width, inner = dilated_kernel.shape
    return kernel_call(
        weights_body,
        "prepare_weights",
        (dilated_kernel, pointwise_kernel),
        [VMEM, VMEM],
        [
            shape((width, taps * inner), jnp.bfloat16),
            shape((taps * inner, width), jnp.bfloat16),
            shape(pointwise_kernel.shape, jnp.bfloat16),
        ],
        [VMEM, VMEM, VMEM],
        flops=4 * width * inner,
        bytes_moved=30 * width * inner,
        grant=16 << 20,
    )


def norm_terms(moments_ref, params_ref, rows_total):
    centre = moments_ref[0:1] / rows_total
    scale = lax.rsqrt(moments_ref[1:2] / rows_total + EPSILON)
    return centre, scale, params_ref[0:1] * scale, params_ref[1:2]


def half_terms(moments_ref, params_ref, rows_total):
    centre, _, slope, offset = norm_terms(moments_ref, params_ref, rows_total)
    return 0.5 * slope, 0.5 * (offset - centre * slope)


def bent(half):
    square = half * half
    return jnp.tanh(half * (2.0 * GELU_SLOPE + (8.0 * GELU_SLOPE * GELU_CUBE) * square)), square


def gelu_slope(half, bend, square):
    rise = 1.0 + bend
    inner = GELU_SLOPE + (12.0 * GELU_SLOPE * GELU_CUBE) * square
    return rise * (0.5 + (half * inner) * (2.0 - rise))


def activated(values, inside, slope, offset):
    half_pre = values.astype(jnp.float32) * slope + offset
    bend, _ = bent(half_pre)
    return jnp.where(inside, half_pre + half_pre * bend, 0.0).astype(jnp.bfloat16)


def edge_body(slots, windows, facts_ref, arrived_ref, moments_ref, params_ref, border_ref):
    _, rows, width = arrived_ref.shape
    facts = Facts(facts_ref, windows, slots)
    per_half = HALF_WINDOW_ROWS // rows
    slope, offset = half_terms(moments_ref, params_ref, facts.row_count())
    for piece in range(2 * slots):
        slot, half = piece // 2, piece % 2
        limit = facts.half_limit(slot, half)
        first = 0 if half else HALF_WINDOW_ROWS - BORDER
        row = first
        while row < first + BORDER:
            inner_row = row % rows
            size = min(rows - inner_row, first + BORDER - row)
            block = (half * per_half + row // rows) * slots + slot
            inside = lax.broadcasted_iota(jnp.int32, (size, 1), 0) < limit - row
            for lanes in column_slices(width):
                border_ref[piece, row - first : row - first + size, lanes] = activated(
                    arrived_ref[block, inner_row : inner_row + size, lanes],
                    inside,
                    slope[:, lanes],
                    offset[:, lanes],
                )
            row += size


def edge_rows(facts, arrived, moments, params, slots, windows):
    width = arrived.shape[2]
    return kernel_call(
        functools.partial(edge_body, slots, windows),
        "edge_rows",
        (facts, arrived, moments, params),
        [SMEM, VMEM, VMEM, VMEM],
        shape((2 * slots, BORDER, width), jnp.bfloat16),
        VMEM,
        flops=40 * slots * BORDER * width,
        bytes_moved=8 * slots * BORDER * width,
    )


def slope_body(slots, windows, piece, facts_ref, arrived_ref, moments_ref, params_ref, slope_ref):
    blocks, rows, width = arrived_ref.shape
    facts = Facts(facts_ref, windows, slots)
    per_half = HALF_WINDOW_ROWS // rows
    slope, offset = half_terms(moments_ref, params_ref, facts.row_count())
    slot, half = piece // 2, piece % 2
    limit = facts.half_limit(slot, half)

    def work(part, carry):
        start = part * rows
        inside = lax.broadcasted_iota(jnp.int32, (rows, 1), 0) < limit - start
        for lanes in column_slices(width):
            values = arrived_ref[(half * per_half + part) * slots + slot, :, lanes]
            half_pre = values.astype(jnp.float32) * slope[:, lanes] + offset[:, lanes]
            found = jnp.where(inside, gelu_slope(half_pre, *bent(half_pre)), 0.0)
            slope_ref[pl.ds(pl.multiple_of(start, rows), rows), lanes] = found
        return carry

    lax.fori_loop(0, per_half, work, 0)


def entry_slope(facts, arrived, moments, params, slots, windows, piece):
    width = arrived.shape[2]
    return kernel_call(
        functools.partial(slope_body, slots, windows, piece),
        "entry_slope",
        (facts, arrived, moments, params),
        [SMEM, VMEM, VMEM, VMEM],
        shape((HALF_WINDOW_ROWS, width), jnp.float32),
        VMEM,
        flops=25 * HALF_WINDOW_ROWS * width,
        bytes_moved=6 * HALF_WINDOW_ROWS * width,
    )


def block_moments(values, inside, count):
    block_sum = jnp.sum(jnp.where(inside, values, 0.0), axis=0, keepdims=True)
    deviation = jnp.where(inside, values - block_sum / jnp.maximum(count, 1.0), 0.0)
    return block_sum, jnp.sum(deviation * deviation, axis=0, keepdims=True), count


def convolve_body(
    slots, windows, facts_ref, arrived_ref, entry_ref, params_ref, weight_ref,
    act_ref, out_ref, moments_ref, wide,
):
    facts = Facts(facts_ref, windows, slots)
    pieces, rows, inner = out_ref.shape
    _, block_rows, width = arrived_ref.shape
    per_half = rows // block_rows
    slope, offset = half_terms(entry_ref, params_ref, facts.row_count())
    tiles = inner // LANES
    for turn in range(2):
        for tile in range(3 * tiles):
            wide[turn, tile, 0:PAD] = jnp.zeros((PAD, LANES), jnp.float32)
            wide[turn, tile, PAD + rows : PADDED_ROWS] = jnp.zeros((PAD, LANES), jnp.float32)
    moments_ref[...] = jnp.zeros_like(moments_ref)
    below, above = PAD - DILATION_STEP, PAD + DILATION_STEP

    def lay_act(piece):
        slot, half = piece // 2, piece % 2
        limit = facts.half_limit(slot, half)
        for part in range(per_half):
            start = part * block_rows
            inside = lax.broadcasted_iota(jnp.int32, (block_rows, 1), 0) < limit - start
            for lanes in column_slices(width):
                act_ref[piece, start : start + block_rows, lanes] = activated(
                    arrived_ref[(half * per_half + part) * slots + slot, :, lanes],
                    inside,
                    slope[:, lanes],
                    offset[:, lanes],
                )

    lay_act(0)
    for piece in range(pieces):
        turn, half = piece % 2, piece % 2
        if piece + 1 < pieces:
            lay_act(piece + 1)
        product = jnp.dot(act_ref[piece], weight_ref[...], preferred_element_type=jnp.float32)
        for tile, lanes in enumerate(column_slices(3 * inner)):
            wide[turn, tile, PAD : PAD + rows] = product[:, lanes]
        limit = facts.half_limit(piece // 2, half)
        start = half * STRIP
        row = lax.broadcasted_iota(jnp.int32, (rows, 1), 0)
        end = jnp.minimum(limit, rows - STRIP + start)
        inside = jnp.logical_and(row >= start, row < end)
        count = jnp.maximum(end - start, 0).astype(jnp.float32)
        for tile, lanes in enumerate(column_slices(inner)):
            out = (
                wide[turn, tiles + tile, PAD : PAD + rows]
                + wide[turn, tile, below : below + rows]
                + wide[turn, 2 * tiles + tile, above : above + rows]
            )
            out_ref[piece, :, lanes] = out
            held = (moments_ref[0:1, lanes], moments_ref[1:2, lanes], moments_ref[2:3, lanes])
            moments_ref[0:1, lanes], moments_ref[1:2, lanes], moments_ref[2:3, lanes] = merged(
                held, block_moments(out, inside, count)
            )


def convolve(facts, arrived, entry_moments, params, weight, slots, windows):
    width, inner = weight.shape[0], weight.shape[1] // 3
    pieces, rows = 2 * slots, HALF_WINDOW_ROWS
    return kernel_call(
        functools.partial(convolve_body, slots, windows),
        "convolve",
        (facts, arrived, entry_moments, params, weight),
        [SMEM] + [VMEM] * 4,
        [
            shape((pieces, rows, width), jnp.bfloat16),
            shape((pieces, rows, inner), jnp.float32),
            shape((3, inner), jnp.float32),
        ],
        [VMEM, VMEM, VMEM],
        [pltpu.VMEM((2, 3 * inner // LANES, PADDED_ROWS, LANES), jnp.float32)],
        flops=6 * pieces * rows * width * inner,
        bytes_moved=pieces * rows * (width * 2 + inner * 4),
        grant=16 << 20,
    )


def join_body(
    slots, windows, facts_ref, out_ref, border_ref, weight_ref, held_ref, strip_ref, moments_ref,
    moved,
):
    facts = Facts(facts_ref, windows, slots)
    pieces, rows, inner = out_ref.shape
    found = (held_ref[0:1], held_ref[1:2], held_ref[2:3])
    gap = STRIP - DILATION_STEP
    skip = BORDER - DILATION_STEP
    for piece in range(pieces):
        half = piece % 2
        other = piece + 1 - 2 * half
        moved[...] = jnp.zeros_like(moved)
        if half == 0:
            moved[gap : gap + BORDER] = jnp.dot(
                border_ref[other], weight_ref[:, 2 * inner :], preferred_element_type=jnp.float32
            )
            strip = out_ref[piece, rows - STRIP : rows] + moved[0:STRIP]
        else:
            moved[0:BORDER] = jnp.dot(
                border_ref[other], weight_ref[:, :inner], preferred_element_type=jnp.float32
            )
            strip = out_ref[piece, 0:STRIP] + moved[skip : skip + STRIP]
        strip_ref[piece] = strip
        limit = facts.half_limit(piece // 2, half) - (1 - half) * (rows - STRIP)
        count = jnp.clip(limit, 0, STRIP)
        inside = lax.broadcasted_iota(jnp.int32, (STRIP, 1), 0) < count
        found = merged(found, block_moments(strip, inside, count.astype(jnp.float32)))
    for number, value in enumerate(found):
        moments_ref[number : number + 1] = jnp.broadcast_to(value, (1, inner))


def join(facts, out, border, weight, held, slots, windows):
    pieces, rows, inner = out.shape
    return kernel_call(
        functools.partial(join_body, slots, windows),
        "join_halves",
        (facts, out, border, weight, held),
        [SMEM, VMEM, VMEM, VMEM, VMEM],
        [shape((pieces, STRIP, inner), jnp.float32), shape((3, inner), jnp.float32)],
        [VMEM, VMEM],
        [pltpu.VMEM((2 * STRIP, inner), jnp.float32)],
        flops=2 * pieces * BORDER * border.shape[2] * inner,
        bytes_moved=pieces * STRIP * inner * 8,
    )


def middle_body(
    slots, windows, facts_ref, out_ref, strip_ref, moments_ref, params_ref, grad_ref,
    act_ref, slope_ref, norm_ref, sums_ref,
):
    facts = Facts(facts_ref, windows, slots)
    pieces, rows, inner = out_ref.shape
    centre, scale, _, _ = norm_terms(moments_ref, params_ref, facts.row_count())
    gain, offset = 0.5 * params_ref[0:1], 0.5 * params_ref[1:2]
    sums_ref[...] = jnp.zeros_like(sums_ref)

    def chunk(piece, start, values):
        size = values.shape[0]
        limit = facts.half_limit(piece // 2, piece % 2)
        inside = lax.broadcasted_iota(jnp.int32, (size, 1), 0) < limit - start
        here = pl.ds(start, size)
        for lanes in column_slices(inner):
            norm = (values[:, lanes] - centre[:, lanes]) * scale[:, lanes]
            half_pre = norm * gain[:, lanes] + offset[:, lanes]
            bend, square = bent(half_pre)
            act = jnp.where(inside, half_pre * (1.0 + bend), 0.0)
            act_ref[piece, here, lanes] = act.astype(jnp.bfloat16)
            grad = grad_ref[piece, here, lanes] * gelu_slope(half_pre, bend, square)
            grad = jnp.where(inside, grad, 0.0)
            slope_ref[piece, here, lanes] = grad
            norm_ref[piece, here, lanes] = norm
            sums_ref[0:1, lanes] = sums_ref[0:1, lanes] + jnp.sum(
                grad * norm, axis=0, keepdims=True
            )
            sums_ref[1:2, lanes] = sums_ref[1:2, lanes] + jnp.sum(grad, axis=0, keepdims=True)

    size = 2 * STRIP
    steps = rows // size - 1

    def main(step, carry):
        piece = step // steps
        start = pl.multiple_of((step % steps + piece % 2) * size, size)
        chunk(piece, start, out_ref[piece, pl.ds(start, size), :])
        return carry

    lax.fori_loop(0, pieces * steps, main, 0)

    def edge(slot, carry):
        low, high = 2 * slot, 2 * slot + 1
        start = rows - size
        values = jnp.concatenate([out_ref[low, start : start + STRIP], strip_ref[low]], axis=0)
        chunk(low, start, values)
        chunk(high, 0, jnp.concatenate([strip_ref[high], out_ref[high, STRIP:size]], axis=0))
        return carry

    lax.fori_loop(0, slots, edge, 0)


def middle(facts, out, strip, moments, params, grad, slots, windows):
    dims = out.shape
    return kernel_call(
        functools.partial(middle_body, slots, windows),
        "middle_norm",
        (facts, out, strip, moments, params, grad),
        [SMEM] + [VMEM] * 5,
        [
            shape(dims, jnp.bfloat16),
            shape(dims, jnp.float32),
            shape(dims, jnp.float32),
            shape((2, dims[2]), jnp.float32),
        ],
        [VMEM] * 4,
        flops=40 * out.size,
        bytes_moved=18 * out.size,
    )


def middle_grad_body(
    slots, windows, facts_ref, grad_ref, norm_ref, moments_ref, params_ref, sums_ref,
    padded_ref, border_ref, centre_ref,
):
    facts = Facts(facts_ref, windows, slots)
    pieces, rows, inner = grad_ref.shape
    rows_total = facts.row_count()
    _, _, slope, _ = norm_terms(moments_ref, params_ref, rows_total)
    level, tilt = sums_ref[1:2] / rows_total, sums_ref[0:1] / rows_total
    tiles = inner // LANES
    for piece in range(pieces):
        for tile in range(tiles):
            padded_ref[piece, tile, 0:PAD] = jnp.zeros((PAD, LANES), jnp.float32)
            padded_ref[piece, tile, PAD + rows : PADDED_ROWS] = jnp.zeros(
                (PAD, LANES), jnp.float32
            )
    size = 2 * STRIP

    def work(step, carry):
        piece, part = step // (rows // size), step % (rows // size)
        start = pl.multiple_of(part * size, size)
        limit = facts.half_limit(piece // 2, piece % 2)
        inside = lax.broadcasted_iota(jnp.int32, (size, 1), 0) < limit - start
        for tile, lanes in enumerate(column_slices(inner)):
            norm = norm_ref[piece, pl.ds(start, size), lanes]
            grad = slope[:, lanes] * (
                grad_ref[piece, pl.ds(start, size), lanes]
                - (level[:, lanes] + norm * tilt[:, lanes])
            )
            low = jnp.where(inside, grad, 0.0).astype(jnp.bfloat16)
            centre_ref[piece, pl.ds(start, size), lanes] = low
            padded_ref[piece, tile, pl.ds(pl.multiple_of(start + PAD, 8), size), :] = low.astype(
                jnp.float32
            )
        return carry

    lax.fori_loop(0, pieces * (rows // size), work, 0)
    for piece in range(pieces):
        start = PAD + (0 if piece % 2 else rows - BORDER)
        for tile, lanes in enumerate(column_slices(inner)):
            border_ref[piece, :, lanes] = padded_ref[piece, tile, start : start + BORDER].astype(
                jnp.bfloat16
            )


def middle_grad(facts, grad, norm, moments, params, sums, slots, windows):
    pieces, _, inner = grad.shape
    return kernel_call(
        functools.partial(middle_grad_body, slots, windows),
        "middle_grad",
        (facts, grad, norm, moments, params, sums),
        [SMEM] + [VMEM] * 5,
        [
            shape((pieces, inner // LANES, PADDED_ROWS, LANES), jnp.float32),
            shape((pieces, BORDER, inner), jnp.bfloat16),
            shape(grad.shape, jnp.bfloat16),
        ],
        [VMEM, VMEM, VMEM],
        flops=8 * grad.size,
        bytes_moved=12 * grad.size,
    )


def output_body(
    slots, windows, facts_ref, act_ref, weight_ref, arrived_ref, params_ref, out_ref
):
    source, slot = pl.program_id(0), pl.program_id(1)
    rows = out_ref.shape[0]
    facts = Facts(facts_ref, windows, slots)
    per_half = HALF_WINDOW_ROWS // rows
    half, start = source // per_half, (source % per_half) * rows
    inside = lax.broadcasted_iota(jnp.int32, (rows, 1), 0) < facts.half_limit(slot, half) - start
    mixed = jnp.dot(act_ref[...], weight_ref[...], preferred_element_type=jnp.float32)
    block = arrived_ref[0].astype(jnp.float32) + mixed + params_ref[2:3]
    out_ref[...] = jnp.where(inside, block, 0.0)


def output_rows(facts, act, weight, arrived, params, slots, windows):
    blocks, rows, width = arrived.shape
    inner = act.shape[1]
    sources = blocks // slots
    place = lambda s, j: (j * sources + s, 0)
    return pl.pallas_call(
        functools.partial(output_body, slots, windows),
        grid=(sources, slots),
        in_specs=[
            SMEM,
            pl.BlockSpec((rows, inner), place),
            pl.BlockSpec((inner, width), lambda s, j: (0, 0)),
            pl.BlockSpec((1, rows, width), lambda s, j: (s * slots + j, 0, 0)),
            pl.BlockSpec((3, width), lambda s, j: (0, 0)),
        ],
        out_specs=pl.BlockSpec((rows, width), place),
        out_shape=shape((blocks * rows, width), jnp.float32),
        compiler_params=pltpu.CompilerParams(vmem_limit_bytes=16 << 20),
        cost_estimate=pl.CostEstimate(
            flops=2 * act.size * width * 7, bytes_accessed=8 * arrived.size * 7, transcendentals=0
        ),
        name="output_rows",
    )(facts, act, weight, arrived, params)


def entry_grad_body(slots, windows, facts_ref, padded_ref, border_ref, weight_ref, *refs):
    pieces = 2 * slots
    slope_refs, refs = refs[:pieces], refs[pieces:]
    (arrived_ref, block_ref, moments_ref, params_ref, bias_ref), refs = refs[:5], refs[5:]
    sent_refs, (kept_ref, sums_ref, wide, packed, taps_ref, departures, kept) = (
        refs[:slots],
        refs[slots:],
    )
    facts = Facts(facts_ref, windows, slots)
    _, sources, rows, width = packed.shape
    tiles = padded_ref.shape[1]
    per_half = HALF_WINDOW_ROWS // rows
    centre, scale, slope, _ = norm_terms(moments_ref, params_ref, facts.row_count())
    skip = BORDER - DILATION_STEP
    sums_ref[...] = jnp.zeros_like(sums_ref)

    def departure(slot, source):
        return pltpu.make_async_copy(
            packed.at[slot, source], sent_refs[slot].at[source], departures.at[slot, source]
        )

    def keeping(piece):
        return pltpu.make_async_copy(
            taps_ref.at[piece, :, pl.ds(0, kept_ref.shape[2])], kept_ref.at[piece], kept.at[piece]
        )

    def lay_taps(piece):
        half, turn = piece % 2, piece % 2
        for tile, lanes in enumerate(column_slices(tiles * LANES)):
            border = border_ref[piece + 1 - 2 * half, :, lanes].astype(jnp.float32)
            wide[turn, tile] = padded_ref[piece, tile]
            if half == 0:
                end = PAD + HALF_WINDOW_ROWS
                wide[turn, tile, end : end + DILATION_STEP] = border[0:DILATION_STEP]
            else:
                wide[turn, tile, PAD - DILATION_STEP : PAD] = border[skip:BORDER]
            for number, tap in enumerate((0, 2, 1)):
                start = PAD - (tap - 1) * DILATION_STEP
                first = (number * tiles + tile) * LANES
                taps_ref[piece, :, first : first + LANES] = wide[
                    turn, tile, start : start + HALF_WINDOW_ROWS
                ].astype(jnp.bfloat16)

    lay_taps(0)
    for piece in range(pieces):
        slot, half = piece // 2, piece % 2
        if piece + 1 < pieces:
            lay_taps(piece + 1)
        for column in range(0, width, 2 * LANES):
            grad = jnp.dot(
                taps_ref[piece],
                weight_ref[:, column : column + 2 * LANES],
                preferred_element_type=jnp.float32,
            )
            for part in range(per_half):
                source = half * per_half + part
                here = slice(part * rows, (part + 1) * rows)
                for start in (column, column + LANES):
                    lanes = slice(start, start + LANES)
                    pre = grad[here, start - column : start - column + LANES]
                    pre = pre * slope_refs[piece][here, lanes]
                    values = arrived_ref[source * slots + slot, :, lanes].astype(jnp.float32)
                    sums_ref[0:1, lanes] = sums_ref[0:1, lanes] + jnp.sum(
                        pre * values, axis=0, keepdims=True
                    )
                    sums_ref[1:2, lanes] = sums_ref[1:2, lanes] + jnp.sum(
                        pre, axis=0, keepdims=True
                    )
                    block = block_ref[piece, here, lanes].astype(jnp.float32)
                    packed[slot, source, :, lanes] = (pre * slope[:, lanes] + block).astype(
                        jnp.bfloat16
                    )
        if piece == 0:
            keeping(piece).start()
        for part in range(per_half):
            departure(slot, half * per_half + part).start()
        if piece + 1 < pieces:
            keeping(piece + 1).start()
    sums_ref[0:1] = (sums_ref[0:1] - centre * sums_ref[1:2]) * scale
    sums_ref[2:3] = bias_ref[...]
    for piece in range(pieces):
        keeping(piece).wait()
    for slot in range(slots):
        for source in range(sources):
            departure(slot, source).wait()


def entry_grad(
    facts, padded, border, weight, slopes, arrived, block, moments, params, bias, slots, windows
):
    blocks, rows, width = arrived.shape
    inner, sources = border.shape[2], blocks // slots
    pieces = 2 * slots
    inputs = [facts, padded, border, weight, *slopes, arrived, block, moments, params, bias]
    taps_shape = (HALF_WINDOW_ROWS, 3 * inner)
    return kernel_call(
        functools.partial(entry_grad_body, slots, windows),
        "entry_grad",
        inputs,
        [SMEM] + [VMEM] * (len(inputs) - 1),
        [
            *[pltpu.HBM((sources, rows, width), jnp.bfloat16)] * slots,
            pltpu.HBM((pieces, HALF_WINDOW_ROWS, 2 * inner), jnp.bfloat16),
            shape((3, width), jnp.float32),
        ],
        [HBM] * (slots + 1) + [VMEM],
        [
            pltpu.VMEM((2, inner // LANES, PADDED_ROWS, LANES), jnp.float32),
            pltpu.VMEM((slots, sources, rows, width), jnp.bfloat16),
            pltpu.VMEM((pieces, *taps_shape), jnp.bfloat16),
            pltpu.SemaphoreType.DMA((slots, sources)),
            pltpu.SemaphoreType.DMA((pieces,)),
        ],
        flops=2 * pieces * HALF_WINDOW_ROWS * 3 * inner * width,
        bytes_moved=pieces * HALF_WINDOW_ROWS * (width * 10 + inner * 10),
        grant=16 << 20,
    )


def flat_mask(bits):
    return sum(mask * (lax.axis_size("seq") if axis == "grp" else 1) for axis, mask in bits)


def from_flat_partner(block, mask):
    count = lax.axis_size("grp") * lax.axis_size("seq")
    return lax.ppermute(
        block, ("grp", "seq"), [(place, place ^ mask) for place in range(count)]
    )


def bit_of(axis, mask):
    return (lax.axis_index(axis) // mask) % 2


def square_phases():
    steps = exchange_steps()[1:]
    outer = [step for step in steps if step[0] == "grp"]
    inner = [step for step in steps if step[0] == "seq"]
    ordered = []
    while outer and inner:
        ordered += [outer.pop(0), inner.pop(0)]
    ordered += outer + inner
    return [ordered[start : start + 2] for start in range(0, len(ordered), 2)]


def phase_place(phase):
    return sum(bit_of(*step) * 2**number for number, step in enumerate(phase))


def phase_parts(phase):
    parts = 2 ** len(phase)
    masks = [
        flat_mask([step for number, step in enumerate(phase) if part >> number & 1])
        for part in range(parts)
    ]
    return parts, masks


def exchange_parts(parts, phase):
    _, masks = phase_parts(phase)
    return [from_flat_partner(part, mask) for part, mask in zip(parts, masks[1:])]


def place_in(facts_ref, phase):
    bits = [
        (facts_ref[0 if axis == "grp" else 1] // mask) % 2 * 2**number
        for number, (axis, mask) in enumerate(phase)
    ]
    return sum(bits)


def encoded(sums, rows_ref):
    count = sums.shape[0]
    high = sums.astype(jnp.bfloat16).astype(jnp.float32)
    low = (sums - high).astype(jnp.bfloat16).astype(jnp.float32)
    rows_ref[...] = jnp.zeros_like(rows_ref)
    rows_ref[0:count] = high
    rows_ref[count : 2 * count] = low
    return rows_ref[...].astype(jnp.bfloat16), high + low


def decoded(found_ref, count, rows_ref):
    rows_ref[...] = found_ref[found_ref.shape[0] - EXTRA :, :].astype(jnp.float32)
    return rows_ref[0:count] + rows_ref[count : 2 * count]


def pair_sum(values):
    while len(values) > 1:
        values = [values[i] + values[i + 1] for i in range(0, len(values), 2)]
    return values[0]


def other_half_body(
    facts_ref, sides_ref, centre_ref, pointwise_ref, sums_ref, sent_ref, held_ref, rows_ref
):
    width, inner = pointwise_ref.shape
    sent_ref[width:, :], held_ref[...] = encoded(sums_ref[...], rows_ref)

    @pl.when(facts_ref[0] % 2 == 0)
    def _():
        sent_ref[:width, :inner] = sides_ref[:, inner:].astype(jnp.bfloat16)
        sent_ref[:width, inner:] = pointwise_ref[...].astype(jnp.bfloat16)

    @pl.when(facts_ref[0] % 2 == 1)
    def _():
        sent_ref[:width, :inner] = sides_ref[:, :inner].astype(jnp.bfloat16)
        sent_ref[:width, inner:] = centre_ref[...].astype(jnp.bfloat16)


def other_half(facts, sides, centre, pointwise, sums):
    width, inner = pointwise.shape
    return kernel_call(
        other_half_body,
        "other_half",
        (facts, sides, centre, pointwise, sums),
        [SMEM] + [VMEM] * 4,
        [shape((width + EXTRA, 2 * inner), jnp.bfloat16), shape(sums.shape, jnp.float32)],
        [VMEM, VMEM],
        [pltpu.VMEM((EXTRA, 2 * inner), jnp.float32)],
        flops=2 * width * inner,
        bytes_moved=12 * width * inner,
        grant=10 << 20,
    )


def part_rows(mine, part, rows):
    return pl.ds(pl.multiple_of(jnp.bitwise_xor(mine, part) * rows, rows), rows)


def own_half_body(
    phase, facts_ref, sides_ref, centre_ref, pointwise_ref, sums_ref, other_ref, total_ref, *refs
):
    part_refs, rows_ref = refs[:-1], refs[-1]
    inner = pointwise_ref.shape[1]
    rows = part_refs[0].shape[0]
    mine = place_in(facts_ref, phase)
    sums = sums_ref[...] + decoded(other_ref, sums_ref.shape[0], rows_ref)
    extra, total_ref[...] = encoded(sums, rows_ref)
    for part_ref in part_refs[1:]:
        part_ref[rows:, :] = extra

    def write(low, high):
        for part, part_ref in enumerate(part_refs):
            here = part_rows(mine, part, rows)
            for piece, lanes in ((low, slice(0, inner)), (high, slice(inner, 2 * inner))):
                value = piece(here) + other_ref[here, lanes].astype(jnp.float32)
                part_ref[:rows, lanes] = value.astype(part_ref.dtype)

    @pl.when(facts_ref[0] % 2 == 0)
    def _():
        write(
            lambda here: sides_ref[here, :inner],
            lambda here: centre_ref[here, :],
        )

    @pl.when(facts_ref[0] % 2 == 1)
    def _():
        write(lambda here: sides_ref[here, inner:], lambda here: pointwise_ref[here, :])


def part_shapes(sums, rows, columns, phase):
    parts = 2 ** len(phase)
    rows //= parts
    return [
        shape(sums.shape, jnp.float32),
        shape((rows, columns), jnp.float32),
        *[shape((rows + EXTRA, columns), jnp.bfloat16)] * (parts - 1),
    ]


def own_half(facts, sides, centre, pointwise, sums, other, phase):
    width, inner = pointwise.shape
    outputs = part_shapes(sums, width, 2 * inner, phase)
    return kernel_call(
        functools.partial(own_half_body, phase),
        "own_half",
        (facts, sides, centre, pointwise, sums, other),
        [SMEM] + [VMEM] * 5,
        outputs,
        [VMEM] * len(outputs),
        [pltpu.VMEM((EXTRA, 2 * inner), jnp.float32)],
        flops=2 * width * inner,
        bytes_moved=20 * width * inner,
        grant=12 << 20,
    )


def next_parts_body(count, phase, facts_ref, kept_ref, sums_ref, *refs):
    found_refs, total_ref, part_refs, rows_ref = (
        refs[:count],
        refs[count],
        refs[count + 1 : -1],
        refs[-1],
    )
    sums = pair_sum(
        [sums_ref[...]] + [decoded(ref, sums_ref.shape[0], rows_ref) for ref in found_refs]
    )
    total_ref[...] = sums
    rows = part_refs[0].shape[0]
    if phase:
        mine = place_in(facts_ref, phase)
        extra, total_ref[...] = encoded(sums, rows_ref)
        for part_ref in part_refs[1:]:
            part_ref[rows:, :] = extra
    for part, part_ref in enumerate(part_refs):
        here = part_rows(mine, part, rows) if phase else slice(0, rows)
        value = kept_ref[here, :]
        for found_ref in found_refs:
            value = value + found_ref[here, :].astype(jnp.float32)
        part_ref[:rows, :] = value.astype(part_ref.dtype)


def plain_parts(kept, sums, found, phase):
    rows, count = kept.shape[0], sums.shape[0]
    totals = [sums]
    for block in found:
        kept = kept + block[:rows].astype(jnp.float32)
        tail = block[rows:].astype(jnp.float32)
        totals.append(tail[:count] + tail[count : 2 * count])
    sums = pair_sum(totals)
    if not phase:
        return [sums, kept.astype(jnp.bfloat16)]
    high = lax.reduce_precision(sums, 8, 7)
    low = lax.reduce_precision(sums - high, 8, 7)
    rest = jnp.zeros((EXTRA - 2 * count, sums.shape[1]), jnp.float32)
    extra, sums = jnp.concatenate([high, low, rest]).astype(jnp.bfloat16), high + low
    parts = 2 ** len(phase)
    mine, rows = phase_place(phase), rows // parts
    slices = [
        lax.dynamic_slice_in_dim(kept, jnp.bitwise_xor(mine, part) * rows, rows)
        for part in range(parts)
    ]
    return [sums, slices[0]] + [
        jnp.concatenate([block.astype(jnp.bfloat16), extra]) for block in slices[1:]
    ]


def next_parts(facts, kept, sums, found, phase):
    rows, columns = kept.shape
    if rows // 2 ** len(phase) % 16:
        return plain_parts(kept, sums, found, phase)
    outputs = part_shapes(sums, rows, columns, phase)
    if not phase:
        outputs = [outputs[0], shape((rows, columns), jnp.bfloat16)]
    return kernel_call(
        functools.partial(next_parts_body, len(found), phase),
        "next_parts",
        (facts, kept, sums, *found),
        [SMEM] + [VMEM] * (2 + len(found)),
        outputs,
        [VMEM] * len(outputs),
        [pltpu.VMEM((EXTRA, columns), jnp.float32)],
        flops=4 * rows * columns,
        bytes_moved=16 * rows * columns,
    )


def gather_parts(buffer, phase):
    _, masks = phase_parts(phase)
    return [buffer] + [from_flat_partner(buffer, mask) for mask in masks[1:]]


def in_order(found, owners):
    parts = len(found)
    orders = [
        jnp.concatenate([found[place ^ own] for place in range(parts)], axis=0)
        for own in range(parts)
    ]
    result = orders[0]
    for own in range(1, parts):
        result = jnp.where(owners[own], orders[own], result)
    return result


def finish_body(own, facts_ref, half_ref, *refs):
    dilated_ref, pointwise_ref, held, turned, copies = refs[-5:]
    inner = dilated_ref.shape[2]

    def write(places):
        for number, place in enumerate(places):
            held[number] = half_ref[:, number * inner : (number + 1) * inner].astype(jnp.float32)
            pltpu.make_async_copy(
                held.at[number], dilated_ref.at[place], copies.at[number]
            ).start()
        if len(places) == 1:
            turned[...] = half_ref[:, inner:].astype(jnp.float32).T
            pltpu.make_async_copy(turned, pointwise_ref, copies.at[1]).start()
            pltpu.make_async_copy(turned, pointwise_ref, copies.at[1]).wait()
        for number, place in enumerate(places):
            pltpu.make_async_copy(
                held.at[number], dilated_ref.at[place], copies.at[number]
            ).wait()

    upper = facts_ref[0] % 2

    @pl.when(upper == 1 - own)
    def _():
        write((0, 1))

    @pl.when(upper == own)
    def _():
        write((2,))


def finish_weights(facts, half, own, begun):
    width, both = half.shape
    inner = both // 2
    inputs, specs, aliases = [facts, half], [SMEM, VMEM], {}
    if begun is not None:
        aliases = {2: 0, 3: 1}
        inputs += [in_hbm(array) for array in begun]
        specs += [HBM, HBM]
    return pl.pallas_call(
        functools.partial(finish_body, own),
        in_specs=specs,
        out_specs=[HBM, HBM],
        out_shape=[
            pltpu.HBM((3, width, inner), jnp.float32),
            pltpu.HBM((inner, width), jnp.float32),
        ],
        input_output_aliases=aliases,
        scratch_shapes=[
            pltpu.VMEM((2, width, inner), jnp.float32),
            pltpu.VMEM((inner, width), jnp.float32),
            pltpu.SemaphoreType.DMA((2,)),
        ],
        compiler_params=pltpu.CompilerParams(vmem_limit_bytes=12 << 20),
        cost_estimate=pl.CostEstimate(
            flops=width * both, bytes_accessed=6 * width * both, transcendentals=0
        ),
        name="finish_weights",
    )(*inputs)


def per_device(
    signal,
    entry_gain,
    entry_shift,
    dilated_kernel,
    middle_gain,
    middle_shift,
    pointwise_kernel,
    pointwise_bias,
    lengths,
    assignment,
    cotangent,
):
    seq_count = lax.axis_size("seq")
    windows, segment, width = signal.shape
    inner = pointwise_kernel.shape[0]
    slots = windows // seq_count
    rows = segment // 2
    pieces = 2 * slots
    places = jnp.stack([lax.axis_index("grp"), lax.axis_index("seq"), jnp.int32(seq_count)])
    row_count = jnp.sum(lengths, keepdims=True)
    facts = jnp.concatenate([places.astype(jnp.int32), row_count, assignment[0], lengths])
    entry_params = jnp.stack([entry_gain, entry_shift, pointwise_bias])
    middle_params = jnp.stack([middle_gain, middle_shift])

    outgoing, entry_local = pool(assignment, lengths, signal, slots)
    arrived = lax.all_to_all(outgoing, "seq", split_axis=0, concat_axis=0, tiled=True)

    late_facts, _ = lax.optimization_barrier((facts, entry_local))
    first_chosen = first_marks(late_facts, signal, slots)
    wide_kernel, back_kernel, pointwise_low = prepare_weights(dilated_kernel, pointwise_kernel)
    grad_block, grad_middle, bias_part = prepare(
        facts, cotangent, pointwise_low, slots, windows
    )
    entry_moments, prepared = total_moments(
        entry_local,
        [first_chosen, grad_block, grad_middle, wide_kernel, back_kernel, pointwise_low],
    )
    first_chosen, grad_block, grad_middle, wide_kernel, back_kernel, pointwise_low = prepared
    phases = square_phases()
    owners = [
        [phase_place(phase) == own for own in range(2 ** len(phase))] for phase in phases
    ]
    first_axis, first_mask = exchange_steps()[0]
    upper = bit_of(first_axis, first_mask) == 1
    (
        arrived,
        first_chosen,
        grad_block,
        grad_middle,
        wide_kernel,
        back_kernel,
        pointwise_low,
        owners,
        upper,
        middle_params,
        facts,
    ) = lax.optimization_barrier(
        (
            arrived,
            first_chosen,
            grad_block,
            grad_middle,
            wide_kernel,
            back_kernel,
            pointwise_low,
            owners,
            upper,
            middle_params,
            facts,
        )
    )

    act_border = edge_rows(facts, arrived, entry_moments, entry_params, slots, windows)
    tied, act_border = lax.optimization_barrier((arrived, act_border))
    act_border = from_partner(act_border, "seq", 1)
    act, dilated, held_moments = convolve(
        facts, tied, entry_moments, entry_params, wide_kernel, slots, windows
    )
    strip, middle_moments = join(
        facts, dilated, act_border, wide_kernel, held_moments, slots, windows
    )
    slopes = []
    for number, (axis, mask) in enumerate(exchange_steps()):
        other = from_partner(middle_moments, axis, mask)
        if number and len(slopes) < pieces:
            tied, middle_moments = lax.optimization_barrier((arrived, middle_moments))
            found = entry_slope(
                facts, tied, entry_moments, entry_params, slots, windows, len(slopes)
            )
            other, found = lax.optimization_barrier((other, found))
            slopes.append(found)
        middle_moments = jnp.concatenate(
            merged(
                (middle_moments[0:1], middle_moments[1:2], middle_moments[2:3]),
                (other[0:1], other[1:2], other[2:3]),
            ),
            axis=0,
        )
    while len(slopes) < pieces:
        slopes.append(
            entry_slope(facts, arrived, entry_moments, entry_params, slots, windows, len(slopes))
        )
    middle_act, middle_slope, middle_norm, middle_sums = middle(
        facts,
        dilated,
        strip,
        middle_moments,
        middle_params,
        grad_middle.reshape(pieces, HALF_WINDOW_ROWS, inner),
        slots,
        windows,
    )
    flat_act = middle_act.reshape(-1, inner)
    for number, (axis, mask) in enumerate(exchange_steps()):
        other = from_partner(middle_sums, axis, mask)
        if number == len(exchange_steps()) - 1:
            tied, middle_sums = lax.optimization_barrier((flat_act, middle_sums))
            pointwise_part = jnp.einsum(
                "rd,rf->df", grad_block, tied, preferred_element_type=jnp.float32
            )
            other, pointwise_part = lax.optimization_barrier((other, pointwise_part))
        middle_sums = middle_sums + other
    padded, grad_border, grad_centre = middle_grad(
        facts, middle_slope, middle_norm, middle_moments, middle_params, middle_sums, slots, windows
    )
    centre_part = jnp.einsum("hrc,hrf->cf", act, grad_centre, preferred_element_type=jnp.float32)
    grad_border = from_partner(grad_border, "seq", 1)
    grad_border, centre_part = lax.optimization_barrier((grad_border, centre_part))
    block_pieces = grad_block.reshape(pieces, HALF_WINDOW_ROWS, width)
    def send_back(block):
        return lax.all_to_all(block, "seq", split_axis=0, concat_axis=0, tiled=True)

    *sent, taps, entry_sums = entry_grad(
        facts, padded, grad_border, back_kernel, slopes, arrived, block_pieces, entry_moments,
        entry_params, bias_part, slots, windows,
    )
    tied = lax.optimization_barrier((*sent, entry_sums))
    sent, entry_sums = list(tied[:-1]), tied[-1]
    returned = [send_back(sent[0])]
    side_parts = jnp.einsum("hrc,hrf->cf", act, taps, preferred_element_type=jnp.float32)
    other, entry_sums = other_half(facts, side_parts, centre_part, pointwise_part, entry_sums)
    other = from_partner(other, first_axis, first_mask)
    entry_sums, *parts = own_half(
        facts, side_parts, centre_part, pointwise_part, entry_sums, other, phases[0]
    )
    for held, phase in zip(phases, phases[1:] + [[]]):
        found = exchange_parts(parts[1:], held)
        entry_sums, *parts = next_parts(facts, parts[0], entry_sums, found, phase)
    buffer, signal_gradient, activations = parts[0], None, None
    for number, phase in reversed(list(enumerate(phases))):
        found = gather_parts(buffer, phase)
        if number == len(phases) - 1:
            found[1], flat_act, entry_sums, *later = lax.optimization_barrier(
                (found[1], flat_act, entry_sums, *sent[1:])
            )
            returned += [send_back(block) for block in later]
        if number == 0:
            signal_gradient = unpool(
                facts, returned[0], outgoing, first_chosen, entry_moments, entry_sums,
                entry_params, slots, 0, None,
            )
            activations = output_rows(
                facts, flat_act, pointwise_low, arrived, entry_params, slots, windows
            )
            signal_gradient, middle_sums = lax.optimization_barrier((signal_gradient, middle_sums))
            vectors = [entry_sums[0], entry_sums[1], middle_sums[0], middle_sums[1], entry_sums[2]]
            tied = lax.optimization_barrier((signal_gradient, activations, *vectors, *found))
            signal_gradient, activations, vectors, found = tied[0], tied[1], tied[2:7], tied[7:]
        buffer = in_order(found, owners[number])
    other = from_partner(buffer, first_axis, first_mask)
    begun = finish_weights(facts, buffer, 1, None)
    other, *begun = lax.optimization_barrier((other, *begun))
    dilated_kernel_gradient, pointwise_kernel_gradient = finish_weights(facts, other, 0, begun)
    for slot in range(1, slots):
        signal_gradient = unpool(
            facts, returned[slot], outgoing, first_chosen, entry_moments, entry_sums,
            entry_params, slots, slot, signal_gradient,
        )
    return (
        activations,
        signal_gradient,
        vectors[0],
        vectors[1],
        dilated_kernel_gradient,
        vectors[2],
        vectors[3],
        pointwise_kernel_gradient,
        vectors[4],
    )


def solution(mesh):
    return jax.shard_map(
        per_device,
        mesh=mesh,
        in_specs=(
            P("grp", "seq", None),
            P(),
            P(),
            P(),
            P(),
            P(),
            P(),
            P(),
            P(),
            P("grp", None),
            P(("grp", "seq"), None),
        ),
        out_specs=(
            P(("grp", "seq"), None),
            P("grp", "seq", None),
            P(),
            P(),
            P(),
            P(),
            P(),
            P(),
            P(),
        ),
        check_vma=False,
    )
```

```python
import functools
import math

import jax
import jax.numpy as jnp
from jax import lax
from jax.experimental import pallas as pl
from jax.experimental.pallas import tpu as pltpu
from jax.sharding import PartitionSpec as P

DILATION_STEP = 38
WINDOW_SPAN = 1024
HALF_WINDOW_ROWS = 512


EPSILON = 0.001

LANES = 128
BORDER = 48
STRIP = 64
PAD = 40
PADDED_ROWS = HALF_WINDOW_ROWS + 2 * PAD
EXTRA = 8
EARLY_SHARE = 8
GELU_SLOPE = math.sqrt(2.0 / math.pi)
GELU_CUBE = 0.044715

VMEM = pl.BlockSpec(memory_space=pltpu.VMEM)
SMEM = pl.BlockSpec(memory_space=pltpu.SMEM)
HBM = pl.BlockSpec(memory_space=pltpu.HBM)


def from_partner(block, axis, mask):
    count = lax.axis_size(axis)
    return lax.ppermute(block, axis, [(place, place ^ mask) for place in range(count)])


def exchange_steps():
    steps = []
    for axis in ("grp", "seq"):
        mask = 1
        while mask < lax.axis_size(axis):
            steps.append((axis, mask))
            mask *= 2
    return steps


def total(values):
    for axis, mask in exchange_steps():
        values = values + from_partner(values, axis, mask)
    return values


def merged(left, right):
    left_sum, left_spread, left_count = left
    right_sum, right_spread, right_count = right
    gap = left_sum / jnp.maximum(left_count, 1.0) - right_sum / jnp.maximum(right_count, 1.0)
    weight = left_count * right_count / jnp.maximum(left_count + right_count, 1.0)
    return (
        left_sum + right_sum,
        left_spread + right_spread + gap * gap * weight,
        left_count + right_count,
    )


def total_moments(packed, others):
    steps = exchange_steps()
    for number, (axis, mask) in enumerate(steps):
        if number == len(steps) - 1:
            packed, *others = lax.optimization_barrier((packed, *others))
        other = from_partner(packed, axis, mask)
        packed = jnp.concatenate(
            merged(
                (packed[0:1], packed[1:2], packed[2:3]), (other[0:1], other[1:2], other[2:3])
            ),
            axis=0,
        )
    return packed, others


class Facts:
    def __init__(self, ref, windows, slots):
        self.ref, self.windows, self.slots = ref, windows, slots

    def slot_window(self, slot):
        upper = (2 * self.ref[1]) // self.ref[2]
        target = jnp.bitwise_xor(slot // self.slots, upper)
        return self.ref[4 + target * self.slots + slot % self.slots]

    def length(self, window):
        return self.ref[4 + self.windows + self.ref[0] * self.windows + window]

    def slot_count(self, slot, rows):
        return jnp.clip(self.length(self.slot_window(slot)) - self.ref[1] * rows, 0, rows)

    def half_limit(self, slot, half):
        place = jnp.bitwise_xor(self.ref[1], half)
        window = self.ref[4 + place * self.slots + slot]
        return jnp.clip(self.length(window) - half * HALF_WINDOW_ROWS, 0, HALF_WINDOW_ROWS)

    def row_count(self):
        return self.ref[3].astype(jnp.float32)


def kernel_call(body, name, inputs, specs, outputs, out_specs, scratch=(), flops=0, bytes_moved=0, grant=8 << 20):
    return pl.pallas_call(
        body,
        in_specs=specs,
        out_specs=out_specs,
        out_shape=outputs,
        scratch_shapes=list(scratch),
        compiler_params=pltpu.CompilerParams(vmem_limit_bytes=grant),
        cost_estimate=pl.CostEstimate(
            flops=flops, bytes_accessed=bytes_moved, transcendentals=0
        ),
        name=name,
    )(*inputs)


def shape(dims, dtype):
    return jax.ShapeDtypeStruct(dims, dtype)


def in_hbm(array):
    return pltpu.with_memory_space_constraint(array, pltpu.HBM)


def column_slices(width):
    return [slice(start, start + LANES) for start in range(0, width, LANES)]


def bin_copy(facts, signal_ref, held, arrivals, place, column):
    return pltpu.make_async_copy(
        signal_ref.at[facts.slot_window(place), :, pl.ds(column * LANES, LANES)],
        held.at[place, column],
        arrivals.at[place, column],
    )


def begin_bins(facts, signal_ref, held, arrivals):
    windows, columns = held.shape[:2]

    def begin(place, carry):
        for column in range(columns):
            bin_copy(facts, signal_ref, held, arrivals, place, column).start()
        return carry

    lax.fori_loop(0, windows, begin, 0)


def bins_of(facts, signal_ref, held, arrivals, place, rows):
    columns = held.shape[1]
    for column in range(columns):
        bin_copy(facts, signal_ref, held, arrivals, place, column).wait()
    return [
        (
            lanes,
            held[place, column, pl.ds(0, rows, stride=2), :],
            held[place, column, pl.ds(1, rows, stride=2), :],
        )
        for column, lanes in enumerate(column_slices(columns * LANES))
    ]


def finish_copies(copy_of, count):
    def finish(place, carry):
        copy_of(place).wait()
        return carry

    lax.fori_loop(0, count, finish, 0)


def pool_body(
    slots, order_ref, lengths_ref, signal_ref, pooled_ref, moments_ref,
    held, low, blocks, order, lengths, places, arrivals, departures, facts_copies,
):
    windows, columns = held.shape[:2]
    rows = low.shape[1]
    grp, seq = lax.axis_index("grp"), lax.axis_index("seq")
    upper = (2 * seq) // (windows // slots)

    def arrival(window, column):
        return pltpu.make_async_copy(
            signal_ref.at[window, :, pl.ds(column * LANES, LANES)],
            held.at[window, column],
            arrivals.at[window, column],
        )

    def departure(window):
        return pltpu.make_async_copy(
            low.at[window], pooled_ref.at[places[window]], departures.at[window]
        )

    fetches = [
        pltpu.make_async_copy(order_ref, order, facts_copies.at[0]),
        pltpu.make_async_copy(lengths_ref, lengths, facts_copies.at[1]),
    ]
    for fetch in fetches:
        fetch.start()

    def begin(window, carry):
        for column in range(columns):
            arrival(window, column).start()
        return carry

    lax.fori_loop(0, windows, begin, 0)
    moments_ref[...] = jnp.zeros_like(moments_ref)
    for fetch in fetches:
        fetch.wait()

    def note(place, carry):
        target = jnp.bitwise_xor(place // slots, upper)
        places[order[0, target * slots + place % slots]] = place
        return carry

    lax.fori_loop(0, windows, note, 0)

    def count_of(window):
        return jnp.clip(lengths[grp * windows + window] - seq * rows, 0, rows)

    def work(window, carry):
        count = count_of(window)
        inside = lax.broadcasted_iota(jnp.int32, (rows, LANES), 0) < count
        for column in range(columns):
            arrival(window, column).wait()
        for column, lanes in enumerate(column_slices(columns * LANES)):
            first_bin = held[window, column, pl.ds(0, rows, stride=2), :]
            second_bin = held[window, column, pl.ds(1, rows, stride=2), :]
            pooled = jnp.where(inside, jnp.maximum(first_bin, second_bin), 0.0)
            pooled = pooled.astype(jnp.bfloat16)
            low[window, :, lanes] = pooled
            found = block_moments(pooled.astype(jnp.float32), inside, count.astype(jnp.float32))
            blocks[window, 0:1, lanes] = found[0]
            blocks[window, 1:2, lanes] = found[1]
        departure(window).start()
        return carry

    lax.fori_loop(0, windows, work, 0)

    def join_blocks(window, carry):
        count = jnp.broadcast_to(count_of(window).astype(jnp.float32), (1, columns * LANES))
        held_moments = (moments_ref[0:1], moments_ref[1:2], moments_ref[2:3])
        moments_ref[0:1], moments_ref[1:2], moments_ref[2:3] = merged(
            held_moments, (blocks[window, 0:1], blocks[window, 1:2], count)
        )
        return carry

    lax.fori_loop(0, windows, join_blocks, 0)
    finish_copies(departure, windows)


def pool(order, lengths, signal, slots):
    windows, segment, width = signal.shape
    rows, columns = segment // 2, width // LANES
    block = (windows, rows, width)
    return kernel_call(
        functools.partial(pool_body, slots),
        "pool",
        (in_hbm(order), in_hbm(lengths), in_hbm(signal)),
        [HBM, HBM, HBM],
        [pltpu.HBM(block, jnp.bfloat16), shape((3, width), jnp.float32)],
        [HBM, VMEM],
        [
            pltpu.VMEM((windows, columns, segment, LANES), jnp.float32),
            pltpu.VMEM(block, jnp.bfloat16),
            pltpu.VMEM((windows, 2, width), jnp.float32),
            pltpu.SMEM(order.shape, jnp.int32),
            pltpu.SMEM(lengths.shape, jnp.int32),
            pltpu.SMEM((windows,), jnp.int32),
            pltpu.SemaphoreType.DMA((windows, columns)),
            pltpu.SemaphoreType.DMA((windows,)),
            pltpu.SemaphoreType.DMA((2,)),
        ],
        flops=10 * windows * rows * width,
        bytes_moved=windows * rows * width * 10,
        grant=24 << 20,
    )


def marks_body(slots, facts_ref, signal_ref, first_ref, held, mark, arrivals, departures):
    windows = held.shape[0]
    rows = mark.shape[1]
    facts = Facts(facts_ref, windows, slots)

    def departure(place):
        return pltpu.make_async_copy(mark.at[place], first_ref.at[place], departures.at[place])

    begin_bins(facts, signal_ref, held, arrivals)

    def work(place, carry):
        for lanes, first_bin, second_bin in bins_of(
            facts, signal_ref, held, arrivals, place, rows
        ):
            mark[place, :, lanes] = jnp.where(first_bin >= second_bin, 1.0, 0.0).astype(
                jnp.bfloat16
            )
        departure(place).start()
        return carry

    lax.fori_loop(0, windows, work, 0)
    finish_copies(departure, windows)


def first_marks(facts, signal, slots):
    windows, segment, width = signal.shape
    rows, columns = segment // 2, width // LANES
    block = (windows, rows, width)
    return kernel_call(
        functools.partial(marks_body, slots),
        "first_marks",
        (facts, in_hbm(signal)),
        [SMEM, HBM],
        pltpu.HBM(block, jnp.bfloat16),
        HBM,
        [
            pltpu.VMEM((windows, columns, segment, LANES), jnp.float32),
            pltpu.VMEM(block, jnp.bfloat16),
            pltpu.SemaphoreType.DMA((windows, columns)),
            pltpu.SemaphoreType.DMA((windows,)),
        ],
        flops=3 * windows * rows * width,
        bytes_moved=windows * rows * width * 10,
        grant=24 << 20,
    )


def unpool_body(
    slots, slot, windows, span, segment_rows, facts_ref, returned_ref, pooled_ref, first_ref,
    moments_ref, sums_ref, params_ref, *refs,
):
    start, row, size = span
    out_ref, back, low, mark, held, arrivals, departures = refs[-7:]
    targets, rows, width = back.shape
    columns = held.shape[1]
    facts = Facts(facts_ref, windows, slots)

    def arrival(target):
        place = target * slots + slot
        return [
            pltpu.make_async_copy(
                returned_ref.at[target, pl.ds(start, size)], back.at[target], arrivals.at[target, 0]
            ),
            pltpu.make_async_copy(
                pooled_ref.at[place, pl.ds(row, size)], low.at[target], arrivals.at[target, 1]
            ),
            pltpu.make_async_copy(
                first_ref.at[place, pl.ds(row, size)], mark.at[target], arrivals.at[target, 2]
            ),
        ]

    def departure(target, column):
        window = facts.slot_window(target * slots + slot)
        return pltpu.make_async_copy(
            held.at[target, column],
            out_ref.at[window, pl.ds(2 * row, 2 * size), pl.ds(column * LANES, LANES)],
            departures.at[target, column],
        )

    def begin(target, carry):
        for copy in arrival(target):
            copy.start()
        return carry

    lax.fori_loop(0, targets, begin, 0)
    rows_total = facts.row_count()
    centre = moments_ref[0:1] / rows_total
    scale = lax.rsqrt(moments_ref[1:2] / rows_total + EPSILON)
    factor = params_ref[0:1] * scale / rows_total
    level = factor * sums_ref[1:2]
    tilt = factor * scale * sums_ref[0:1]

    def work(target, carry):
        for copy in arrival(target):
            copy.wait()
        inside = lax.broadcasted_iota(jnp.int32, (rows, LANES), 0) < (
            facts.slot_count(target * slots + slot, segment_rows) - row
        )
        for column, lanes in enumerate(column_slices(width)):
            centred = low[target, :, lanes].astype(jnp.float32) - centre[:, lanes]
            gradient = back[target, :, lanes].astype(jnp.float32) - (
                level[:, lanes] + centred * tilt[:, lanes]
            )
            gradient = jnp.where(inside, gradient, 0.0).astype(jnp.bfloat16).astype(jnp.float32)
            first = gradient * mark[target, :, lanes].astype(jnp.float32)
            held[target, column, pl.ds(0, rows, stride=2), :] = first
            held[target, column, pl.ds(1, rows, stride=2), :] = gradient - first
        for column in range(columns):
            departure(target, column).start()
        return carry

    lax.fori_loop(0, targets, work, 0)

    def finish(target, carry):
        for column in range(columns):
            departure(target, column).wait()
        return carry

    lax.fori_loop(0, targets, finish, 0)


def unpool(
    facts, returned, pooled, first, moments, sums, params, slots, slot, span, held_output
):
    windows, all_rows, width = pooled.shape
    targets, rows = windows // slots, span[2]
    columns = width // LANES
    inputs = [facts, in_hbm(returned), in_hbm(pooled), in_hbm(first), moments, sums, params]
    specs = [SMEM, HBM, HBM, HBM, VMEM, VMEM, VMEM]
    aliases = {}
    if held_output is not None:
        aliases = {len(inputs): 0}
        inputs.append(in_hbm(held_output))
        specs.append(HBM)
    block = (targets, rows, width)
    return pl.pallas_call(
        functools.partial(unpool_body, slots, slot, windows, span, all_rows),
        in_specs=specs,
        out_specs=HBM,
        out_shape=pltpu.HBM((windows, 2 * all_rows, width), jnp.float32),
        input_output_aliases=aliases,
        scratch_shapes=[
            pltpu.VMEM(block, jnp.bfloat16),
            pltpu.VMEM(block, jnp.bfloat16),
            pltpu.VMEM(block, jnp.bfloat16),
            pltpu.VMEM((targets, columns, 2 * rows, LANES), jnp.float32),
            pltpu.SemaphoreType.DMA((targets, 3)),
            pltpu.SemaphoreType.DMA((targets, columns)),
        ],
        compiler_params=pltpu.CompilerParams(vmem_limit_bytes=16 << 20),
        cost_estimate=pl.CostEstimate(
            flops=10 * targets * rows * width,
            bytes_accessed=targets * rows * width * 14,
            transcendentals=0,
        ),
        name="unpool",
    )(*inputs)


def prepare_body(slots, windows, facts_ref, cot_ref, weight_ref, low_ref, middle_ref, bias_ref):
    step = pl.program_id(0)
    rows = cot_ref.shape[0]
    facts = Facts(facts_ref, windows, slots)
    first_row = step * rows
    piece = first_row // HALF_WINDOW_ROWS
    limit = facts.half_limit(piece // 2, piece % 2) - first_row % HALF_WINDOW_ROWS

    @pl.when(step == 0)
    def _():
        bias_ref[...] = jnp.zeros_like(bias_ref)

    inside = lax.broadcasted_iota(jnp.int32, (rows, 1), 0) < limit
    block = jnp.where(inside, cot_ref[...], 0.0)
    bias_ref[...] = bias_ref[...] + jnp.sum(block, axis=0, keepdims=True)
    low = block.astype(jnp.bfloat16)
    low_ref[...] = low
    middle_ref[...] = lax.dot_general(
        low, weight_ref[...], (((1,), (1,)), ((), ())), preferred_element_type=jnp.float32
    )


def prepare(facts, cotangent, weight, slots, windows):
    total_rows, width = cotangent.shape
    inner = weight.shape[0]
    rows = 256
    return pl.pallas_call(
        functools.partial(prepare_body, slots, windows),
        grid=(total_rows // rows,),
        in_specs=[
            SMEM,
            pl.BlockSpec((rows, width), lambda i: (i, 0)),
            pl.BlockSpec((inner, width), lambda i: (0, 0)),
        ],
        out_specs=[
            pl.BlockSpec((rows, width), lambda i: (i, 0)),
            pl.BlockSpec((rows, inner), lambda i: (i, 0)),
            pl.BlockSpec((1, width), lambda i: (0, 0)),
        ],
        out_shape=[
            shape((total_rows, width), jnp.bfloat16),
            shape((total_rows, inner), jnp.float32),
            shape((1, width), jnp.float32),
        ],
        compiler_params=pltpu.CompilerParams(vmem_limit_bytes=16 << 20),
        cost_estimate=pl.CostEstimate(
            flops=2 * total_rows * width * inner,
            bytes_accessed=total_rows * (width * 6 + inner * 4),
            transcendentals=0,
        ),
        name="prepare_cotangent",
    )(facts, cotangent, weight)


def weights_body(dilated_ref, pointwise_ref, wide_ref, back_ref, low_ref):
    inner = dilated_ref.shape[2]
    for number, tap in enumerate((0, 2, 1)):
        values = dilated_ref[tap]
        wide_ref[:, tap * inner : (tap + 1) * inner] = values.astype(jnp.bfloat16)
        back_ref[number * inner : (number + 1) * inner, :] = values.T.astype(jnp.bfloat16)
    low_ref[...] = pointwise_ref[...].astype(jnp.bfloat16)


def prepare_weights(dilated_kernel, pointwise_kernel):
    taps, width, inner = dilated_kernel.shape
    return kernel_call(
        weights_body,
        "prepare_weights",
        (dilated_kernel, pointwise_kernel),
        [VMEM, VMEM],
        [
            shape((width, taps * inner), jnp.bfloat16),
            shape((taps * inner, width), jnp.bfloat16),
            shape(pointwise_kernel.shape, jnp.bfloat16),
        ],
        [VMEM, VMEM, VMEM],
        flops=4 * width * inner,
        bytes_moved=30 * width * inner,
        grant=16 << 20,
    )


def norm_terms(moments_ref, params_ref, rows_total):
    centre = moments_ref[0:1] / rows_total
    scale = lax.rsqrt(moments_ref[1:2] / rows_total + EPSILON)
    return centre, scale, params_ref[0:1] * scale, params_ref[1:2]


def half_terms(moments_ref, params_ref, rows_total):
    centre, _, slope, offset = norm_terms(moments_ref, params_ref, rows_total)
    return 0.5 * slope, 0.5 * (offset - centre * slope)


def bent(half):
    square = half * half
    return jnp.tanh(half * (2.0 * GELU_SLOPE + (8.0 * GELU_SLOPE * GELU_CUBE) * square)), square


def gelu_slope(half, bend, square):
    rise = 1.0 + bend
    inner = GELU_SLOPE + (12.0 * GELU_SLOPE * GELU_CUBE) * square
    return rise * (0.5 + (half * inner) * (2.0 - rise))


def activated(values, inside, slope, offset):
    half_pre = values.astype(jnp.float32) * slope + offset
    bend, _ = bent(half_pre)
    return jnp.where(inside, half_pre + half_pre * bend, 0.0).astype(jnp.bfloat16)


def edge_body(slots, windows, facts_ref, arrived_ref, moments_ref, params_ref, border_ref):
    _, rows, width = arrived_ref.shape
    facts = Facts(facts_ref, windows, slots)
    per_half = HALF_WINDOW_ROWS // rows
    slope, offset = half_terms(moments_ref, params_ref, facts.row_count())
    for piece in range(2 * slots):
        slot, half = piece // 2, piece % 2
        limit = facts.half_limit(slot, half)
        first = 0 if half else HALF_WINDOW_ROWS - BORDER
        row = first
        while row < first + BORDER:
            inner_row = row % rows
            size = min(rows - inner_row, first + BORDER - row)
            block = (half * per_half + row // rows) * slots + slot
            inside = lax.broadcasted_iota(jnp.int32, (size, 1), 0) < limit - row
            for lanes in column_slices(width):
                border_ref[piece, row - first : row - first + size, lanes] = activated(
                    arrived_ref[block, inner_row : inner_row + size, lanes],
                    inside,
                    slope[:, lanes],
                    offset[:, lanes],
                )
            row += size


def edge_rows(facts, arrived, moments, params, slots, windows):
    width = arrived.shape[2]
    return kernel_call(
        functools.partial(edge_body, slots, windows),
        "edge_rows",
        (facts, arrived, moments, params),
        [SMEM, VMEM, VMEM, VMEM],
        shape((2 * slots, BORDER, width), jnp.bfloat16),
        VMEM,
        flops=40 * slots * BORDER * width,
        bytes_moved=8 * slots * BORDER * width,
    )


def slope_body(slots, windows, piece, facts_ref, arrived_ref, moments_ref, params_ref, slope_ref):
    blocks, rows, width = arrived_ref.shape
    facts = Facts(facts_ref, windows, slots)
    per_half = HALF_WINDOW_ROWS // rows
    slope, offset = half_terms(moments_ref, params_ref, facts.row_count())
    slot, half = piece // 2, piece % 2
    limit = facts.half_limit(slot, half)

    def work(part, carry):
        start = part * rows
        inside = lax.broadcasted_iota(jnp.int32, (rows, 1), 0) < limit - start
        for lanes in column_slices(width):
            values = arrived_ref[(half * per_half + part) * slots + slot, :, lanes]
            half_pre = values.astype(jnp.float32) * slope[:, lanes] + offset[:, lanes]
            found = jnp.where(inside, gelu_slope(half_pre, *bent(half_pre)), 0.0)
            slope_ref[pl.ds(pl.multiple_of(start, rows), rows), lanes] = found
        return carry

    lax.fori_loop(0, per_half, work, 0)


def entry_slope(facts, arrived, moments, params, slots, windows, piece):
    width = arrived.shape[2]
    return kernel_call(
        functools.partial(slope_body, slots, windows, piece),
        "entry_slope",
        (facts, arrived, moments, params),
        [SMEM, VMEM, VMEM, VMEM],
        shape((HALF_WINDOW_ROWS, width), jnp.float32),
        VMEM,
        flops=25 * HALF_WINDOW_ROWS * width,
        bytes_moved=6 * HALF_WINDOW_ROWS * width,
    )


def block_moments(values, inside, count):
    block_sum = jnp.sum(jnp.where(inside, values, 0.0), axis=0, keepdims=True)
    deviation = jnp.where(inside, values - block_sum / jnp.maximum(count, 1.0), 0.0)
    return block_sum, jnp.sum(deviation * deviation, axis=0, keepdims=True), count


def convolve_body(
    slots, windows, facts_ref, arrived_ref, entry_ref, params_ref, weight_ref,
    act_ref, out_ref, moments_ref, wide,
):
    facts = Facts(facts_ref, windows, slots)
    pieces, rows, inner = out_ref.shape
    _, block_rows, width = arrived_ref.shape
    per_half = rows // block_rows
    slope, offset = half_terms(entry_ref, params_ref, facts.row_count())
    tiles = inner // LANES
    for turn in range(2):
        for tile in range(3 * tiles):
            wide[turn, tile, 0:PAD] = jnp.zeros((PAD, LANES), jnp.float32)
            wide[turn, tile, PAD + rows : PADDED_ROWS] = jnp.zeros((PAD, LANES), jnp.float32)
    moments_ref[...] = jnp.zeros_like(moments_ref)
    below, above = PAD - DILATION_STEP, PAD + DILATION_STEP

    def lay_act(piece):
        slot, half = piece // 2, piece % 2
        limit = facts.half_limit(slot, half)
        for part in range(per_half):
            start = part * block_rows
            inside = lax.broadcasted_iota(jnp.int32, (block_rows, 1), 0) < limit - start
            for lanes in column_slices(width):
                act_ref[piece, start : start + block_rows, lanes] = activated(
                    arrived_ref[(half * per_half + part) * slots + slot, :, lanes],
                    inside,
                    slope[:, lanes],
                    offset[:, lanes],
                )

    lay_act(0)
    for piece in range(pieces):
        turn, half = piece % 2, piece % 2
        if piece + 1 < pieces:
            lay_act(piece + 1)
        product = jnp.dot(act_ref[piece], weight_ref[...], preferred_element_type=jnp.float32)
        for tile, lanes in enumerate(column_slices(3 * inner)):
            wide[turn, tile, PAD : PAD + rows] = product[:, lanes]
        limit = facts.half_limit(piece // 2, half)
        start = half * STRIP
        row = lax.broadcasted_iota(jnp.int32, (rows, 1), 0)
        end = jnp.minimum(limit, rows - STRIP + start)
        inside = jnp.logical_and(row >= start, row < end)
        count = jnp.maximum(end - start, 0).astype(jnp.float32)
        for tile, lanes in enumerate(column_slices(inner)):
            out = (
                wide[turn, tiles + tile, PAD : PAD + rows]
                + wide[turn, tile, below : below + rows]
                + wide[turn, 2 * tiles + tile, above : above + rows]
            )
            out_ref[piece, :, lanes] = out
            held = (moments_ref[0:1, lanes], moments_ref[1:2, lanes], moments_ref[2:3, lanes])
            moments_ref[0:1, lanes], moments_ref[1:2, lanes], moments_ref[2:3, lanes] = merged(
                held, block_moments(out, inside, count)
            )


def convolve(facts, arrived, entry_moments, params, weight, slots, windows):
    width, inner = weight.shape[0], weight.shape[1] // 3
    pieces, rows = 2 * slots, HALF_WINDOW_ROWS
    return kernel_call(
        functools.partial(convolve_body, slots, windows),
        "convolve",
        (facts, arrived, entry_moments, params, weight),
        [SMEM] + [VMEM] * 4,
        [
            shape((pieces, rows, width), jnp.bfloat16),
            shape((pieces, rows, inner), jnp.float32),
            shape((3, inner), jnp.float32),
        ],
        [VMEM, VMEM, VMEM],
        [pltpu.VMEM((2, 3 * inner // LANES, PADDED_ROWS, LANES), jnp.float32)],
        flops=6 * pieces * rows * width * inner,
        bytes_moved=pieces * rows * (width * 2 + inner * 4),
        grant=16 << 20,
    )


def join_body(
    slots, windows, facts_ref, out_ref, border_ref, weight_ref, held_ref, strip_ref, moments_ref,
    moved,
):
    facts = Facts(facts_ref, windows, slots)
    pieces, rows, inner = out_ref.shape
    found = (held_ref[0:1], held_ref[1:2], held_ref[2:3])
    gap = STRIP - DILATION_STEP
    skip = BORDER - DILATION_STEP
    for piece in range(pieces):
        half = piece % 2
        other = piece + 1 - 2 * half
        moved[...] = jnp.zeros_like(moved)
        if half == 0:
            moved[gap : gap + BORDER] = jnp.dot(
                border_ref[other], weight_ref[:, 2 * inner :], preferred_element_type=jnp.float32
            )
            strip = out_ref[piece, rows - STRIP : rows] + moved[0:STRIP]
        else:
            moved[0:BORDER] = jnp.dot(
                border_ref[other], weight_ref[:, :inner], preferred_element_type=jnp.float32
            )
            strip = out_ref[piece, 0:STRIP] + moved[skip : skip + STRIP]
        strip_ref[piece] = strip
        limit = facts.half_limit(piece // 2, half) - (1 - half) * (rows - STRIP)
        count = jnp.clip(limit, 0, STRIP)
        inside = lax.broadcasted_iota(jnp.int32, (STRIP, 1), 0) < count
        found = merged(found, block_moments(strip, inside, count.astype(jnp.float32)))
    for number, value in enumerate(found):
        moments_ref[number : number + 1] = jnp.broadcast_to(value, (1, inner))


def join(facts, out, border, weight, held, slots, windows):
    pieces, rows, inner = out.shape
    return kernel_call(
        functools.partial(join_body, slots, windows),
        "join_halves",
        (facts, out, border, weight, held),
        [SMEM, VMEM, VMEM, VMEM, VMEM],
        [shape((pieces, STRIP, inner), jnp.float32), shape((3, inner), jnp.float32)],
        [VMEM, VMEM],
        [pltpu.VMEM((2 * STRIP, inner), jnp.float32)],
        flops=2 * pieces * BORDER * border.shape[2] * inner,
        bytes_moved=pieces * STRIP * inner * 8,
    )


def middle_body(
    slots, windows, facts_ref, out_ref, strip_ref, moments_ref, params_ref, grad_ref,
    act_ref, slope_ref, norm_ref, sums_ref,
):
    facts = Facts(facts_ref, windows, slots)
    pieces, rows, inner = out_ref.shape
    centre, scale, _, _ = norm_terms(moments_ref, params_ref, facts.row_count())
    gain, offset = 0.5 * params_ref[0:1], 0.5 * params_ref[1:2]
    sums_ref[...] = jnp.zeros_like(sums_ref)

    def chunk(piece, start, values):
        size = values.shape[0]
        limit = facts.half_limit(piece // 2, piece % 2)
        inside = lax.broadcasted_iota(jnp.int32, (size, 1), 0) < limit - start
        here = pl.ds(start, size)
        for lanes in column_slices(inner):
            norm = (values[:, lanes] - centre[:, lanes]) * scale[:, lanes]
            half_pre = norm * gain[:, lanes] + offset[:, lanes]
            bend, square = bent(half_pre)
            act = jnp.where(inside, half_pre * (1.0 + bend), 0.0)
            act_ref[piece, here, lanes] = act.astype(jnp.bfloat16)
            grad = grad_ref[piece, here, lanes] * gelu_slope(half_pre, bend, square)
            grad = jnp.where(inside, grad, 0.0)
            slope_ref[piece, here, lanes] = grad
            norm_ref[piece, here, lanes] = norm
            sums_ref[0:1, lanes] = sums_ref[0:1, lanes] + jnp.sum(
                grad * norm, axis=0, keepdims=True
            )
            sums_ref[1:2, lanes] = sums_ref[1:2, lanes] + jnp.sum(grad, axis=0, keepdims=True)

    size = 2 * STRIP
    steps = rows // size - 1

    def main(step, carry):
        piece = step // steps
        start = pl.multiple_of((step % steps + piece % 2) * size, size)
        chunk(piece, start, out_ref[piece, pl.ds(start, size), :])
        return carry

    lax.fori_loop(0, pieces * steps, main, 0)

    def edge(slot, carry):
        low, high = 2 * slot, 2 * slot + 1
        start = rows - size
        values = jnp.concatenate([out_ref[low, start : start + STRIP], strip_ref[low]], axis=0)
        chunk(low, start, values)
        chunk(high, 0, jnp.concatenate([strip_ref[high], out_ref[high, STRIP:size]], axis=0))
        return carry

    lax.fori_loop(0, slots, edge, 0)


def middle(facts, out, strip, moments, params, grad, slots, windows):
    dims = out.shape
    return kernel_call(
        functools.partial(middle_body, slots, windows),
        "middle_norm",
        (facts, out, strip, moments, params, grad),
        [SMEM] + [VMEM] * 5,
        [
            shape(dims, jnp.bfloat16),
            shape(dims, jnp.float32),
            shape(dims, jnp.float32),
            shape((2, dims[2]), jnp.float32),
        ],
        [VMEM] * 4,
        flops=40 * out.size,
        bytes_moved=18 * out.size,
    )


def middle_grad_body(
    slots, windows, facts_ref, grad_ref, norm_ref, moments_ref, params_ref, sums_ref,
    padded_ref, border_ref, centre_ref,
):
    facts = Facts(facts_ref, windows, slots)
    pieces, rows, inner = grad_ref.shape
    rows_total = facts.row_count()
    _, _, slope, _ = norm_terms(moments_ref, params_ref, rows_total)
    level, tilt = sums_ref[1:2] / rows_total, sums_ref[0:1] / rows_total
    tiles = inner // LANES
    for piece in range(pieces):
        for tile in range(tiles):
            padded_ref[piece, tile, 0:PAD] = jnp.zeros((PAD, LANES), jnp.float32)
            padded_ref[piece, tile, PAD + rows : PADDED_ROWS] = jnp.zeros(
                (PAD, LANES), jnp.float32
            )
    size = 2 * STRIP

    def work(step, carry):
        piece, part = step // (rows // size), step % (rows // size)
        start = pl.multiple_of(part * size, size)
        limit = facts.half_limit(piece // 2, piece % 2)
        inside = lax.broadcasted_iota(jnp.int32, (size, 1), 0) < limit - start
        for tile, lanes in enumerate(column_slices(inner)):
            norm = norm_ref[piece, pl.ds(start, size), lanes]
            grad = slope[:, lanes] * (
                grad_ref[piece, pl.ds(start, size), lanes]
                - (level[:, lanes] + norm * tilt[:, lanes])
            )
            low = jnp.where(inside, grad, 0.0).astype(jnp.bfloat16)
            centre_ref[piece, pl.ds(start, size), lanes] = low
            padded_ref[piece, tile, pl.ds(pl.multiple_of(start + PAD, 8), size), :] = low.astype(
                jnp.float32
            )
        return carry

    lax.fori_loop(0, pieces * (rows // size), work, 0)
    for piece in range(pieces):
        start = PAD + (0 if piece % 2 else rows - BORDER)
        for tile, lanes in enumerate(column_slices(inner)):
            border_ref[piece, :, lanes] = padded_ref[piece, tile, start : start + BORDER].astype(
                jnp.bfloat16
            )


def middle_grad(facts, grad, norm, moments, params, sums, slots, windows):
    pieces, _, inner = grad.shape
    return kernel_call(
        functools.partial(middle_grad_body, slots, windows),
        "middle_grad",
        (facts, grad, norm, moments, params, sums),
        [SMEM] + [VMEM] * 5,
        [
            shape((pieces, inner // LANES, PADDED_ROWS, LANES), jnp.float32),
            shape((pieces, BORDER, inner), jnp.bfloat16),
            shape(grad.shape, jnp.bfloat16),
        ],
        [VMEM, VMEM, VMEM],
        flops=8 * grad.size,
        bytes_moved=12 * grad.size,
    )


def output_body(
    slots, windows, facts_ref, act_ref, weight_ref, arrived_ref, params_ref, out_ref
):
    source, slot = pl.program_id(0), pl.program_id(1)
    rows = out_ref.shape[0]
    facts = Facts(facts_ref, windows, slots)
    per_half = HALF_WINDOW_ROWS // rows
    half, start = source // per_half, (source % per_half) * rows
    inside = lax.broadcasted_iota(jnp.int32, (rows, 1), 0) < facts.half_limit(slot, half) - start
    mixed = jnp.dot(act_ref[...], weight_ref[...], preferred_element_type=jnp.float32)
    block = arrived_ref[0].astype(jnp.float32) + mixed + params_ref[2:3]
    out_ref[...] = jnp.where(inside, block, 0.0)


def output_rows(facts, act, weight, arrived, params, slots, windows):
    blocks, rows, width = arrived.shape
    inner = act.shape[1]
    sources = blocks // slots
    place = lambda s, j: (j * sources + s, 0)
    return pl.pallas_call(
        functools.partial(output_body, slots, windows),
        grid=(sources, slots),
        in_specs=[
            SMEM,
            pl.BlockSpec((rows, inner), place),
            pl.BlockSpec((inner, width), lambda s, j: (0, 0)),
            pl.BlockSpec((1, rows, width), lambda s, j: (s * slots + j, 0, 0)),
            pl.BlockSpec((3, width), lambda s, j: (0, 0)),
        ],
        out_specs=pl.BlockSpec((rows, width), place),
        out_shape=shape((blocks * rows, width), jnp.float32),
        compiler_params=pltpu.CompilerParams(vmem_limit_bytes=16 << 20),
        cost_estimate=pl.CostEstimate(
            flops=2 * act.size * width * 40 // 10, bytes_accessed=8 * arrived.size * 40 // 10, transcendentals=0
        ),
        name="output_rows",
    )(facts, act, weight, arrived, params)


def transfer_rows(rows, slots):
    early = -(-rows // EARLY_SHARE // 8) * 8
    return [rows + early, rows - early] + [rows] * (slots - 2)


def entry_grad_body(slots, windows, facts_ref, padded_ref, border_ref, weight_ref, *refs):
    pieces = 2 * slots
    slope_refs, refs = refs[:pieces], refs[pieces:]
    (arrived_ref, block_ref, moments_ref, params_ref, bias_ref), refs = refs[:5], refs[5:]
    sent_refs, (kept_ref, sums_ref, wide, packed, taps_ref, departures, kept) = (
        refs[:slots],
        refs[slots:],
    )
    facts = Facts(facts_ref, windows, slots)
    _, sources, rows, width = packed.shape
    tiles = padded_ref.shape[1]
    per_half = HALF_WINDOW_ROWS // rows
    centre, scale, slope, _ = norm_terms(moments_ref, params_ref, facts.row_count())
    skip = BORDER - DILATION_STEP
    sums_ref[...] = jnp.zeros_like(sums_ref)

    early = sent_refs[0].shape[1] - rows

    def departure(slot, source):
        if slot != 1:
            target = sent_refs[slot].at[source, pl.ds(0, rows)]
            return [
                pltpu.make_async_copy(packed.at[slot, source], target, departures.at[slot, source])
            ]
        return [
            pltpu.make_async_copy(
                packed.at[1, source, pl.ds(0, early)],
                sent_refs[0].at[source, pl.ds(rows, early)],
                departures.at[1, source],
            ),
            pltpu.make_async_copy(
                packed.at[1, source, pl.ds(early, rows - early)],
                sent_refs[1].at[source],
                departures.at[slots, source],
            ),
        ]

    def keeping(piece):
        return pltpu.make_async_copy(
            taps_ref.at[piece, :, pl.ds(0, kept_ref.shape[2])], kept_ref.at[piece], kept.at[piece]
        )

    def lay_taps(piece):
        half, turn = piece % 2, piece % 2
        for tile, lanes in enumerate(column_slices(tiles * LANES)):
            border = border_ref[piece + 1 - 2 * half, :, lanes].astype(jnp.float32)
            wide[turn, tile] = padded_ref[piece, tile]
            if half == 0:
                end = PAD + HALF_WINDOW_ROWS
                wide[turn, tile, end : end + DILATION_STEP] = border[0:DILATION_STEP]
            else:
                wide[turn, tile, PAD - DILATION_STEP : PAD] = border[skip:BORDER]
            for number, tap in enumerate((0, 2, 1)):
                start = PAD - (tap - 1) * DILATION_STEP
                first = (number * tiles + tile) * LANES
                taps_ref[piece, :, first : first + LANES] = wide[
                    turn, tile, start : start + HALF_WINDOW_ROWS
                ].astype(jnp.bfloat16)

    lay_taps(0)
    for piece in range(pieces):
        slot, half = piece // 2, piece % 2
        if piece + 1 < pieces:
            lay_taps(piece + 1)
        for column in range(0, width, 2 * LANES):
            grad = jnp.dot(
                taps_ref[piece],
                weight_ref[:, column : column + 2 * LANES],
                preferred_element_type=jnp.float32,
            )
            for part in range(per_half):
                source = half * per_half + part
                here = slice(part * rows, (part + 1) * rows)
                for start in (column, column + LANES):
                    lanes = slice(start, start + LANES)
                    pre = grad[here, start - column : start - column + LANES]
                    pre = pre * slope_refs[piece][here, lanes]
                    values = arrived_ref[source * slots + slot, :, lanes].astype(jnp.float32)
                    sums_ref[0:1, lanes] = sums_ref[0:1, lanes] + jnp.sum(
                        pre * values, axis=0, keepdims=True
                    )
                    sums_ref[1:2, lanes] = sums_ref[1:2, lanes] + jnp.sum(
                        pre, axis=0, keepdims=True
                    )
                    block = block_ref[piece, here, lanes].astype(jnp.float32)
                    packed[slot, source, :, lanes] = (pre * slope[:, lanes] + block).astype(
                        jnp.bfloat16
                    )
        if piece == 0:
            keeping(piece).start()
        for part in range(per_half):
            for copy in departure(slot, half * per_half + part):
                copy.start()
        if piece + 1 < pieces:
            keeping(piece + 1).start()
    sums_ref[0:1] = (sums_ref[0:1] - centre * sums_ref[1:2]) * scale
    sums_ref[2:3] = bias_ref[...]
    for piece in range(pieces):
        keeping(piece).wait()
    for slot in range(slots):
        for source in range(sources):
            for copy in departure(slot, source):
                copy.wait()


def entry_grad(
    facts, padded, border, weight, slopes, arrived, block, moments, params, bias, slots, windows
):
    blocks, rows, width = arrived.shape
    inner, sources = border.shape[2], blocks // slots
    pieces = 2 * slots
    inputs = [facts, padded, border, weight, *slopes, arrived, block, moments, params, bias]
    taps_shape = (HALF_WINDOW_ROWS, 3 * inner)
    return kernel_call(
        functools.partial(entry_grad_body, slots, windows),
        "entry_grad",
        inputs,
        [SMEM] + [VMEM] * (len(inputs) - 1),
        [
            *[
                pltpu.HBM((sources, size, width), jnp.bfloat16)
                for size in transfer_rows(rows, slots)
            ],
            pltpu.HBM((pieces, HALF_WINDOW_ROWS, 2 * inner), jnp.bfloat16),
            shape((3, width), jnp.float32),
        ],
        [HBM] * (slots + 1) + [VMEM],
        [
            pltpu.VMEM((2, inner // LANES, PADDED_ROWS, LANES), jnp.float32),
            pltpu.VMEM((slots, sources, rows, width), jnp.bfloat16),
            pltpu.VMEM((pieces, *taps_shape), jnp.bfloat16),
            pltpu.SemaphoreType.DMA((slots + 1, sources)),
            pltpu.SemaphoreType.DMA((pieces,)),
        ],
        flops=2 * pieces * HALF_WINDOW_ROWS * 3 * inner * width,
        bytes_moved=pieces * HALF_WINDOW_ROWS * (width * 10 + inner * 10),
        grant=16 << 20,
    )


def flat_mask(bits):
    return sum(mask * (lax.axis_size("seq") if axis == "grp" else 1) for axis, mask in bits)


def from_flat_partner(block, mask):
    count = lax.axis_size("grp") * lax.axis_size("seq")
    return lax.ppermute(
        block, ("grp", "seq"), [(place, place ^ mask) for place in range(count)]
    )


def bit_of(axis, mask):
    return (lax.axis_index(axis) // mask) % 2


def square_phases():
    steps = exchange_steps()[1:]
    outer = [step for step in steps if step[0] == "grp"]
    inner = [step for step in steps if step[0] == "seq"]
    ordered = []
    while outer and inner:
        ordered += [outer.pop(0), inner.pop(0)]
    ordered += outer + inner
    return [ordered[start : start + 2] for start in range(0, len(ordered), 2)]


def phase_place(phase):
    return sum(bit_of(*step) * 2**number for number, step in enumerate(phase))


def phase_parts(phase):
    parts = 2 ** len(phase)
    masks = [
        flat_mask([step for number, step in enumerate(phase) if part >> number & 1])
        for part in range(parts)
    ]
    return parts, masks


def exchange_parts(parts, phase):
    _, masks = phase_parts(phase)
    return [from_flat_partner(part, mask) for part, mask in zip(parts, masks[1:])]


def place_in(facts_ref, phase):
    bits = [
        (facts_ref[0 if axis == "grp" else 1] // mask) % 2 * 2**number
        for number, (axis, mask) in enumerate(phase)
    ]
    return sum(bits)


def encoded(sums, rows_ref):
    count = sums.shape[0]
    high = sums.astype(jnp.bfloat16).astype(jnp.float32)
    low = (sums - high).astype(jnp.bfloat16).astype(jnp.float32)
    rows_ref[...] = jnp.zeros_like(rows_ref)
    rows_ref[0:count] = high
    rows_ref[count : 2 * count] = low
    return rows_ref[...].astype(jnp.bfloat16), high + low


def decoded(found_ref, count, rows_ref):
    rows_ref[...] = found_ref[found_ref.shape[0] - EXTRA :, :].astype(jnp.float32)
    return rows_ref[0:count] + rows_ref[count : 2 * count]


def pair_sum(values):
    while len(values) > 1:
        values = [values[i] + values[i + 1] for i in range(0, len(values), 2)]
    return values[0]


def other_half_body(
    facts_ref, sides_ref, centre_ref, pointwise_ref, sums_ref, sent_ref, held_ref, rows_ref
):
    width, inner = pointwise_ref.shape
    sent_ref[width:, :], held_ref[...] = encoded(sums_ref[...], rows_ref)

    @pl.when(facts_ref[0] % 2 == 0)
    def _():
        sent_ref[:width, :inner] = sides_ref[:, inner:].astype(jnp.bfloat16)
        sent_ref[:width, inner:] = pointwise_ref[...].astype(jnp.bfloat16)

    @pl.when(facts_ref[0] % 2 == 1)
    def _():
        sent_ref[:width, :inner] = sides_ref[:, :inner].astype(jnp.bfloat16)
        sent_ref[:width, inner:] = centre_ref[...].astype(jnp.bfloat16)


def other_half(facts, sides, centre, pointwise, sums):
    width, inner = pointwise.shape
    return kernel_call(
        other_half_body,
        "other_half",
        (facts, sides, centre, pointwise, sums),
        [SMEM] + [VMEM] * 4,
        [shape((width + EXTRA, 2 * inner), jnp.bfloat16), shape(sums.shape, jnp.float32)],
        [VMEM, VMEM],
        [pltpu.VMEM((EXTRA, 2 * inner), jnp.float32)],
        flops=2 * width * inner,
        bytes_moved=12 * width * inner,
        grant=10 << 20,
    )


def part_rows(mine, part, rows):
    return pl.ds(pl.multiple_of(jnp.bitwise_xor(mine, part) * rows, rows), rows)


def own_half_body(
    phase, facts_ref, sides_ref, centre_ref, pointwise_ref, sums_ref, other_ref, total_ref, *refs
):
    part_refs, rows_ref = refs[:-1], refs[-1]
    inner = pointwise_ref.shape[1]
    rows = part_refs[0].shape[0]
    mine = place_in(facts_ref, phase)
    sums = sums_ref[...] + decoded(other_ref, sums_ref.shape[0], rows_ref)
    extra, total_ref[...] = encoded(sums, rows_ref)
    for part_ref in part_refs[1:]:
        part_ref[rows:, :] = extra

    def write(low, high):
        for part, part_ref in enumerate(part_refs):
            here = part_rows(mine, part, rows)
            for piece, lanes in ((low, slice(0, inner)), (high, slice(inner, 2 * inner))):
                value = piece(here) + other_ref[here, lanes].astype(jnp.float32)
                part_ref[:rows, lanes] = value.astype(part_ref.dtype)

    @pl.when(facts_ref[0] % 2 == 0)
    def _():
        write(
            lambda here: sides_ref[here, :inner],
            lambda here: centre_ref[here, :],
        )

    @pl.when(facts_ref[0] % 2 == 1)
    def _():
        write(lambda here: sides_ref[here, inner:], lambda here: pointwise_ref[here, :])


def part_shapes(sums, rows, columns, phase):
    parts = 2 ** len(phase)
    rows //= parts
    return [
        shape(sums.shape, jnp.float32),
        shape((rows, columns), jnp.float32),
        *[shape((rows + EXTRA, columns), jnp.bfloat16)] * (parts - 1),
    ]


def own_half(facts, sides, centre, pointwise, sums, other, phase):
    width, inner = pointwise.shape
    outputs = part_shapes(sums, width, 2 * inner, phase)
    return kernel_call(
        functools.partial(own_half_body, phase),
        "own_half",
        (facts, sides, centre, pointwise, sums, other),
        [SMEM] + [VMEM] * 5,
        outputs,
        [VMEM] * len(outputs),
        [pltpu.VMEM((EXTRA, 2 * inner), jnp.float32)],
        flops=2 * width * inner,
        bytes_moved=20 * width * inner,
        grant=12 << 20,
    )


def next_parts_body(count, phase, facts_ref, kept_ref, sums_ref, *refs):
    found_refs, total_ref, part_refs, rows_ref = (
        refs[:count],
        refs[count],
        refs[count + 1 : -1],
        refs[-1],
    )
    sums = pair_sum(
        [sums_ref[...]] + [decoded(ref, sums_ref.shape[0], rows_ref) for ref in found_refs]
    )
    total_ref[...] = sums
    rows = part_refs[0].shape[0]
    if phase:
        mine = place_in(facts_ref, phase)
        extra, total_ref[...] = encoded(sums, rows_ref)
        for part_ref in part_refs[1:]:
            part_ref[rows:, :] = extra
    for part, part_ref in enumerate(part_refs):
        here = part_rows(mine, part, rows) if phase else slice(0, rows)
        value = kept_ref[here, :]
        for found_ref in found_refs:
            value = value + found_ref[here, :].astype(jnp.float32)
        part_ref[:rows, :] = value.astype(part_ref.dtype)


def plain_parts(kept, sums, found, phase):
    rows, count = kept.shape[0], sums.shape[0]
    totals = [sums]
    for block in found:
        kept = kept + block[:rows].astype(jnp.float32)
        tail = block[rows:].astype(jnp.float32)
        totals.append(tail[:count] + tail[count : 2 * count])
    sums = pair_sum(totals)
    if not phase:
        return [sums, kept.astype(jnp.bfloat16)]
    high = lax.reduce_precision(sums, 8, 7)
    low = lax.reduce_precision(sums - high, 8, 7)
    rest = jnp.zeros((EXTRA - 2 * count, sums.shape[1]), jnp.float32)
    extra, sums = jnp.concatenate([high, low, rest]).astype(jnp.bfloat16), high + low
    parts = 2 ** len(phase)
    mine, rows = phase_place(phase), rows // parts
    slices = [
        lax.dynamic_slice_in_dim(kept, jnp.bitwise_xor(mine, part) * rows, rows)
        for part in range(parts)
    ]
    return [sums, slices[0]] + [
        jnp.concatenate([block.astype(jnp.bfloat16), extra]) for block in slices[1:]
    ]


def next_parts(facts, kept, sums, found, phase):
    rows, columns = kept.shape
    if rows // 2 ** len(phase) % 16:
        return plain_parts(kept, sums, found, phase)
    outputs = part_shapes(sums, rows, columns, phase)
    if not phase:
        outputs = [outputs[0], shape((rows, columns), jnp.bfloat16)]
    return kernel_call(
        functools.partial(next_parts_body, len(found), phase),
        "next_parts",
        (facts, kept, sums, *found),
        [SMEM] + [VMEM] * (2 + len(found)),
        outputs,
        [VMEM] * len(outputs),
        [pltpu.VMEM((EXTRA, columns), jnp.float32)],
        flops=4 * rows * columns,
        bytes_moved=16 * rows * columns,
    )


def gather_parts(buffer, phase):
    _, masks = phase_parts(phase)
    return [buffer] + [from_flat_partner(buffer, mask) for mask in masks[1:]]


def in_order(found, owners):
    parts = len(found)
    orders = [
        jnp.concatenate([found[place ^ own] for place in range(parts)], axis=0)
        for own in range(parts)
    ]
    result = orders[0]
    for own in range(1, parts):
        result = jnp.where(owners[own], orders[own], result)
    return result


def finish_body(own, facts_ref, half_ref, *refs):
    dilated_ref, pointwise_ref, held, turned, copies = refs[-5:]
    inner = dilated_ref.shape[2]

    def write(places):
        for number, place in enumerate(places):
            held[number] = half_ref[:, number * inner : (number + 1) * inner].astype(jnp.float32)
            pltpu.make_async_copy(
                held.at[number], dilated_ref.at[place], copies.at[number]
            ).start()
        if len(places) == 1:
            turned[...] = half_ref[:, inner:].astype(jnp.float32).T
            pltpu.make_async_copy(turned, pointwise_ref, copies.at[1]).start()
            pltpu.make_async_copy(turned, pointwise_ref, copies.at[1]).wait()
        for number, place in enumerate(places):
            pltpu.make_async_copy(
                held.at[number], dilated_ref.at[place], copies.at[number]
            ).wait()

    upper = facts_ref[0] % 2

    @pl.when(upper == 1 - own)
    def _():
        write((0, 1))

    @pl.when(upper == own)
    def _():
        write((2,))


def finish_weights(facts, half, own, begun):
    width, both = half.shape
    inner = both // 2
    inputs, specs, aliases = [facts, half], [SMEM, VMEM], {}
    if begun is not None:
        aliases = {2: 0, 3: 1}
        inputs += [in_hbm(array) for array in begun]
        specs += [HBM, HBM]
    return pl.pallas_call(
        functools.partial(finish_body, own),
        in_specs=specs,
        out_specs=[HBM, HBM],
        out_shape=[
            pltpu.HBM((3, width, inner), jnp.float32),
            pltpu.HBM((inner, width), jnp.float32),
        ],
        input_output_aliases=aliases,
        scratch_shapes=[
            pltpu.VMEM((2, width, inner), jnp.float32),
            pltpu.VMEM((inner, width), jnp.float32),
            pltpu.SemaphoreType.DMA((2,)),
        ],
        compiler_params=pltpu.CompilerParams(vmem_limit_bytes=12 << 20),
        cost_estimate=pl.CostEstimate(
            flops=width * both, bytes_accessed=6 * width * both, transcendentals=0
        ),
        name="finish_weights",
    )(*inputs)


def per_device(
    signal,
    entry_gain,
    entry_shift,
    dilated_kernel,
    middle_gain,
    middle_shift,
    pointwise_kernel,
    pointwise_bias,
    lengths,
    assignment,
    cotangent,
):
    seq_count = lax.axis_size("seq")
    windows, segment, width = signal.shape
    inner = pointwise_kernel.shape[0]
    slots = windows // seq_count
    rows = segment // 2
    pieces = 2 * slots
    places = jnp.stack([lax.axis_index("grp"), lax.axis_index("seq"), jnp.int32(seq_count)])
    row_count = jnp.sum(lengths, keepdims=True)
    facts = jnp.concatenate([places.astype(jnp.int32), row_count, assignment[0], lengths])
    entry_params = jnp.stack([entry_gain, entry_shift, pointwise_bias])
    middle_params = jnp.stack([middle_gain, middle_shift])

    outgoing, entry_local = pool(assignment, lengths, signal, slots)
    arrived = lax.all_to_all(outgoing, "seq", split_axis=0, concat_axis=0, tiled=True)

    late_facts, _ = lax.optimization_barrier((facts, entry_local))
    first_chosen = first_marks(late_facts, signal, slots)
    wide_kernel, back_kernel, pointwise_low = prepare_weights(dilated_kernel, pointwise_kernel)
    grad_block, grad_middle, bias_part = prepare(
        facts, cotangent, pointwise_low, slots, windows
    )
    entry_moments, prepared = total_moments(
        entry_local,
        [first_chosen, grad_block, grad_middle, wide_kernel, back_kernel, pointwise_low],
    )
    first_chosen, grad_block, grad_middle, wide_kernel, back_kernel, pointwise_low = prepared
    phases = square_phases()
    owners = [
        [phase_place(phase) == own for own in range(2 ** len(phase))] for phase in phases
    ]
    first_axis, first_mask = exchange_steps()[0]
    upper = bit_of(first_axis, first_mask) == 1
    (
        arrived,
        first_chosen,
        grad_block,
        grad_middle,
        wide_kernel,
        back_kernel,
        pointwise_low,
        owners,
        upper,
        middle_params,
        facts,
    ) = lax.optimization_barrier(
        (
            arrived,
            first_chosen,
            grad_block,
            grad_middle,
            wide_kernel,
            back_kernel,
            pointwise_low,
            owners,
            upper,
            middle_params,
            facts,
        )
    )

    act_border = edge_rows(facts, arrived, entry_moments, entry_params, slots, windows)
    tied, act_border = lax.optimization_barrier((arrived, act_border))
    act_border = from_partner(act_border, "seq", 1)
    act, dilated, held_moments = convolve(
        facts, tied, entry_moments, entry_params, wide_kernel, slots, windows
    )
    strip, middle_moments = join(
        facts, dilated, act_border, wide_kernel, held_moments, slots, windows
    )
    slopes = []
    for number, (axis, mask) in enumerate(exchange_steps()):
        other = from_partner(middle_moments, axis, mask)
        if number and len(slopes) < pieces:
            tied, middle_moments = lax.optimization_barrier((arrived, middle_moments))
            found = entry_slope(
                facts, tied, entry_moments, entry_params, slots, windows, len(slopes)
            )
            other, found = lax.optimization_barrier((other, found))
            slopes.append(found)
        middle_moments = jnp.concatenate(
            merged(
                (middle_moments[0:1], middle_moments[1:2], middle_moments[2:3]),
                (other[0:1], other[1:2], other[2:3]),
            ),
            axis=0,
        )
    while len(slopes) < pieces:
        slopes.append(
            entry_slope(facts, arrived, entry_moments, entry_params, slots, windows, len(slopes))
        )
    middle_act, middle_slope, middle_norm, middle_sums = middle(
        facts,
        dilated,
        strip,
        middle_moments,
        middle_params,
        grad_middle.reshape(pieces, HALF_WINDOW_ROWS, inner),
        slots,
        windows,
    )
    flat_act = middle_act.reshape(-1, inner)
    for number, (axis, mask) in enumerate(exchange_steps()):
        other = from_partner(middle_sums, axis, mask)
        if number == len(exchange_steps()) - 1:
            tied, middle_sums = lax.optimization_barrier((flat_act, middle_sums))
            pointwise_part = jnp.einsum(
                "rd,rf->df", grad_block, tied, preferred_element_type=jnp.float32
            )
            other, pointwise_part = lax.optimization_barrier((other, pointwise_part))
        middle_sums = middle_sums + other
    padded, grad_border, grad_centre = middle_grad(
        facts, middle_slope, middle_norm, middle_moments, middle_params, middle_sums, slots, windows
    )
    centre_part = jnp.einsum("hrc,hrf->cf", act, grad_centre, preferred_element_type=jnp.float32)
    grad_border = from_partner(grad_border, "seq", 1)
    grad_border, centre_part = lax.optimization_barrier((grad_border, centre_part))
    block_pieces = grad_block.reshape(pieces, HALF_WINDOW_ROWS, width)
    def send_back(block):
        return lax.all_to_all(block, "seq", split_axis=0, concat_axis=0, tiled=True)

    *sent, taps, entry_sums = entry_grad(
        facts, padded, grad_border, back_kernel, slopes, arrived, block_pieces, entry_moments,
        entry_params, bias_part, slots, windows,
    )
    tied = lax.optimization_barrier((*sent, entry_sums))
    sent, entry_sums = list(tied[:-1]), tied[-1]
    returned = [send_back(sent[0])]
    side_parts = jnp.einsum("hrc,hrf->cf", act, taps, preferred_element_type=jnp.float32)
    other, entry_sums = other_half(facts, side_parts, centre_part, pointwise_part, entry_sums)
    other = from_partner(other, first_axis, first_mask)
    entry_sums, *parts = own_half(
        facts, side_parts, centre_part, pointwise_part, entry_sums, other, phases[0]
    )
    for held, phase in zip(phases, phases[1:] + [[]]):
        found = exchange_parts(parts[1:], held)
        entry_sums, *parts = next_parts(facts, parts[0], entry_sums, found, phase)
    buffer, signal_gradient, activations = parts[0], None, None
    for number, phase in reversed(list(enumerate(phases))):
        found = gather_parts(buffer, phase)
        if number == len(phases) - 1:
            found[1], flat_act, entry_sums, *later = lax.optimization_barrier(
                (found[1], flat_act, entry_sums, *sent[1:])
            )
            returned += [send_back(block) for block in later]
        if number == 0:
            early = returned[0].shape[1] - rows
            for slot, span in ((0, (0, 0, rows)), (1, (rows, 0, early))):
                signal_gradient = unpool(
                    facts, returned[0], outgoing, first_chosen, entry_moments, entry_sums,
                    entry_params, slots, slot, span, signal_gradient,
                )
            activations = output_rows(
                facts, flat_act, pointwise_low, arrived, entry_params, slots, windows
            )
            signal_gradient, middle_sums = lax.optimization_barrier((signal_gradient, middle_sums))
            vectors = [entry_sums[0], entry_sums[1], middle_sums[0], middle_sums[1], entry_sums[2]]
            tied = lax.optimization_barrier((signal_gradient, activations, *vectors, *found))
            signal_gradient, activations, vectors, found = tied[0], tied[1], tied[2:7], tied[7:]
        buffer = in_order(found, owners[number])
    other = from_partner(buffer, first_axis, first_mask)
    begun = finish_weights(facts, buffer, 1, None)
    other, *begun = lax.optimization_barrier((other, *begun))
    dilated_kernel_gradient, pointwise_kernel_gradient = finish_weights(facts, other, 0, begun)
    signal_gradient, dilated_kernel_gradient, pointwise_kernel_gradient = (
        lax.optimization_barrier(
            (signal_gradient, dilated_kernel_gradient, pointwise_kernel_gradient)
        )
    )
    for slot in range(1, slots):
        span = (0, early, rows - early) if slot == 1 else (0, 0, rows)
        signal_gradient = unpool(
            facts, returned[slot], outgoing, first_chosen, entry_moments, entry_sums,
            entry_params, slots, slot, span, signal_gradient,
        )
    return (
        activations,
        signal_gradient,
        vectors[0],
        vectors[1],
        dilated_kernel_gradient,
        vectors[2],
        vectors[3],
        pointwise_kernel_gradient,
        vectors[4],
    )


def solution(mesh):
    return jax.shard_map(
        per_device,
        mesh=mesh,
        in_specs=(
            P("grp", "seq", None),
            P(),
            P(),
            P(),
            P(),
            P(),
            P(),
            P(),
            P(),
            P("grp", None),
            P(("grp", "seq"), None),
        ),
        out_specs=(
            P(("grp", "seq"), None),
            P("grp", "seq", None),
            P(),
            P(),
            P(),
            P(),
            P(),
            P(),
            P(),
        ),
        check_vma=False,
    )
```
